32 devices in a mesh: dp: 4 (over y, x), expert: 8 (over z, core).
Axes of the slice: x: 2, y: 2, z: 4, core: 2. Of those that a mesh axis runs over, the one named last changes fastest.
Arguments:
- inputs: bfloat16 [32768, 768], P(('dp', 'expert')), may hold values from -6 to 6
- cotangent: bfloat16 [32768, 768], P(('dp', 'expert')), may hold values from -6 to 6
- seq_group: int32 [32], P(('dp', 'expert')), may hold values from 0 to 7
- domain_counts: int32 [8], replicated, may hold values from 1 to 8
- sort_order: int32 [32, 1024], P(('dp', 'expert')), may hold values from 0 to 1023, each once within a row
- send_counts: int32 [32, 8], P(('dp', 'expert')), may hold values from 0 to 256, as said below
- gain_one: float32 [768], replicated, may hold values from 0.5 to 1.5
- shift_one: float32 [768], replicated, may hold values from -1.2 to 1.2
- gain_two: float32 [768], replicated, may hold values from 0.5 to 1.5
- shift_two: float32 [768], replicated, may hold values from -1.2 to 1.2
- w_query: bfloat16 [768, 768], replicated, may hold values from -0.3125 to 0.3125
- w_key: bfloat16 [768, 768], replicated, may hold values from -0.3125 to 0.3125
- w_value: bfloat16 [768, 768], replicated, may hold values from -0.21875 to 0.21875
- w_out: bfloat16 [768, 768], replicated, may hold values from -0.875 to 0.875
- router: bfloat16 [768, 8], replicated, may hold values from -0.15625 to 0.15625
- expert_in: bfloat16 [8, 768, 3072], P('expert'), may hold values from -0.21875 to 0.21875
- expert_out: bfloat16 [8, 3072, 768], P('expert'), may hold values from -0.3125 to 0.3125
Outputs:
- output: bfloat16 [32768, 768], P(('dp', 'expert'))
- grad_inputs: bfloat16 [32768, 768], P(('dp', 'expert'))
- grad_gain_one: float32 [768], replicated
- grad_shift_one: float32 [768], replicated
- grad_gain_two: float32 [768], replicated
- grad_shift_two: float32 [768], replicated
- grad_w_query: float32 [768, 768], replicated
- grad_w_key: float32 [768, 768], replicated
- grad_w_value: float32 [768, 768], replicated
- grad_w_out: float32 [768, 768], replicated
- grad_expert_in: float32 [8, 768, 3072], P('expert')
- grad_expert_out: float32 [8, 3072, 768], P('expert')
The draws below stay inside these ranges and needn't reach their ends.
Inputs may be any that keep to these rules, and one draw needn't show every extreme that they name: `send_counts`: each row sums to 1024. One expert, the same in every row, gets exactly 256 tokens from every device; in each row one other expert gets none and the rest get between 64 and 192. `sort_order`: each row is a permutation of the local token indices.
All inputs are finite; a program needn't handle non-finite values.
Results may differ from the reference program's by a relative error of at most 0.015.
The reference program's roundings to bfloat16 on the way count: a program that leaves them out, or rounds other values in their place, can miss the bound.
Values may be sent and summed in bfloat16 or wider, within the bound.
A program may use at most 256 MiB of HBM per device.

```python
import jax
import jax.numpy as jnp
from jax import lax

D = 768
HEADS = 12
HEAD_DIM = 64
FF = 3072
LEN = 1024
DOMAINS = 8
EXPERTS = 8
TOK_DEV = 1024
SEQS = 32
TOKENS = 32768
CAP = 256
DEVICES = 32


def draw_send_counts(key, part):
    mean_rows = TOK_DEV // EXPERTS
    hot_key, rest_key = jax.random.split(key)
    hottest = jax.random.randint(hot_key, (), 0, EXPERTS)
    device_keys = jax.random.split(rest_key, DEVICES)

    def one_row(row_key):
        perm_key, pair_key = jax.random.split(row_key)
        others = (hottest + 1 + jax.random.permutation(perm_key, EXPERTS - 1)) % EXPERTS
        shifts = jax.random.randint(pair_key, ((EXPERTS - 2) // 2,), -(mean_rows // 2), mean_rows // 2 + 1)
        counts = jnp.zeros((EXPERTS,), jnp.int32).at[hottest].set(2 * mean_rows)
        counts = counts.at[others[0]].set(0)
        counts = counts.at[others[1::2]].set(mean_rows + shifts)
        counts = counts.at[others[2::2]].set(mean_rows - shifts)
        return counts
    return jax.vmap(one_row)(device_keys).astype(jnp.int32)


def with_ends(drawn, own_key, least, high):
    longest = drawn.shape.index(max(drawn.shape))
    spots = []
    for shift in (0, 1):
        where = [jax.random.randint(jax.random.fold_in(own_key, axis), (), 0, length) for axis, length in enumerate(drawn.shape)]
        where[longest] = (where[longest] + shift) % drawn.shape[longest]
        spots.append(tuple(where))
    return drawn.at[spots[0]].set(least).at[spots[1]].set(high)


def levels(stream_key, dims, cuts, low, high):
    factor_of = 1.0
    for axis_at, blocks in cuts:
        draws = jax.random.uniform(jax.random.fold_in(jax.random.fold_in(stream_key, 6), axis_at), (blocks,), jnp.float32, low / len(cuts), high / len(cuts))
        factor_of = factor_of * jnp.repeat(jnp.exp(draws), dims[axis_at] // blocks).reshape((-1,) + (1,) * (len(dims) - 1 - axis_at))
    return factor_of


def bell_draw(key, dims, deviation, most, cuts=(), kind=jnp.bfloat16):
    values = jax.random.normal(key, dims, jnp.float32) * deviation
    if len(cuts) > 0:
        values = levels(key, dims, cuts, -0.22, 0.18) * values
    return jnp.clip(values, min=-most, max=most).astype(kind)


def setup_inputs(seed: int = 0) -> dict:
    keys = jax.random.split(jax.random.key(seed), 18)
    return {
        "inputs": bell_draw(keys[0], (TOKENS, D), 1.0, 6.0, ((0, 32),)),
        "cotangent": bell_draw(keys[1], (TOKENS, D), 1.0, 6.0, ((0, 32),)),
        "seq_group": with_ends(jax.random.randint(keys[2], (SEQS,), 0, DOMAINS), jax.random.fold_in(keys[2], 1), 0, DOMAINS - 1).astype(jnp.int32),
        "domain_counts": with_ends(jax.random.randint(keys[3], (DOMAINS,), 1, 9), jax.random.fold_in(keys[3], 1), 1, 8).astype(jnp.int32),
        "sort_order": jax.vmap(lambda own: jax.random.permutation(own, TOK_DEV))(jax.random.split(keys[4], DEVICES)).reshape((DEVICES, TOK_DEV)).astype(jnp.int32),
        "send_counts": draw_send_counts(jax.random.fold_in(keys[17], 71), 0),
        "gain_one": jnp.clip(1.0 + 0.1 * jax.random.normal(keys[6], (D,), jnp.float32), 0.5, 1.5),
        "shift_one": bell_draw(keys[7], (D,), 0.2, 1.2, (), jnp.float32),
        "gain_two": jnp.clip(1.0 + 0.1 * jax.random.normal(keys[8], (D,), jnp.float32), 0.5, 1.5),
        "shift_two": bell_draw(keys[9], (D,), 0.2, 1.2, (), jnp.float32),
        "w_query": bell_draw(keys[10], (D, D), (D // 2) ** -0.5, 0.3125),
        "w_key": bell_draw(keys[11], (D, D), (D // 2) ** -0.5, 0.3125),
        "w_value": bell_draw(keys[12], (D, D), D ** -0.5, 0.21875),
        "w_out": bell_draw(keys[13], (D, D), (D // 16) ** -0.5, 0.875),
        "router": bell_draw(keys[14], (D, EXPERTS), (D * 2) ** -0.5, 0.15625),
        "expert_in": bell_draw(keys[15], (EXPERTS, D, FF), D ** -0.5, 0.21875, ((0, 8),)),
        "expert_out": bell_draw(keys[16], (EXPERTS, FF, D), (FF // 8) ** -0.5, 0.3125, ((0, 8),)),
    }


@jax.custom_vjp
def low(v):
    return lax.optimization_barrier(v.astype(jnp.bfloat16)).astype(jnp.float32)

@jax.custom_vjp
def low_back(v):
    return v

def low_keep(v):
    return (low(v), None)

def low_pass(kept, grad):
    return (grad,)

def back_keep(v):
    return (v, None)

def back_low(kept, grad):
    return (low(grad),)
low.defvjp(low_keep, low_pass)
low_back.defvjp(back_keep, back_low)
epsilon = 1e-05
precise = lax.Precision.HIGHEST

def layer_norm(values_in, scales, offsets):
    center = values_in - lax.optimization_barrier(jnp.mean(values_in, axis=-1, keepdims=True))
    spread = lax.optimization_barrier(jnp.mean(center * center, axis=-1, keepdims=True))
    return center * lax.rsqrt(spread + epsilon) * scales + offsets

def route_tables(sort_order, send_counts):
    count_ends = jnp.cumsum(send_counts, axis=1).astype(jnp.int32)
    count_starts = (count_ends - send_counts).astype(jnp.int32)
    places = jnp.arange(TOK_DEV, dtype=jnp.int32)
    expert_at = lax.optimization_barrier(jnp.sum((places[None, :, None] >= count_ends[:, None, :]).astype(jnp.int32), axis=-1)).astype(jnp.int32)
    slot_at = places[None, :] - jnp.take_along_axis(count_starts, expert_at, axis=1)
    device_ids = jnp.arange(DEVICES, dtype=jnp.int32)[:, None]
    flat_index = ((expert_at * DEVICES + device_ids) * CAP + slot_at).astype(jnp.int32).reshape(-1)
    token_index = (device_ids * TOK_DEV + sort_order).astype(jnp.int32).reshape(-1)
    expert_of = jnp.zeros((TOKENS,), jnp.int32).at[token_index].set(expert_at.reshape(-1))
    return (flat_index, token_index, expert_of)

def attend_one(pieces):
    query_seq, key_seq, value_seq = pieces
    query_h = query_seq.reshape(LEN, HEADS, HEAD_DIM)
    key_h = key_seq.reshape(LEN, HEADS, HEAD_DIM)
    value_h = value_seq.reshape(LEN, HEADS, HEAD_DIM)
    scores = jnp.einsum('qhd,khd->hqk', query_h, key_h, precision=precise) * HEAD_DIM ** (-0.5)
    scores = low_back(scores)
    positions = jnp.arange(LEN, dtype=jnp.int32)
    causal = positions[:, None] >= positions[None, :]
    scores = jnp.where(causal[None], scores, -1000000000.0)
    attention = low(jax.nn.softmax(scores, axis=-1))
    mixed_h = jnp.einsum('hqk,khd->qhd', attention, value_h, precision=precise)
    return mixed_h.reshape(LEN, D)

def expert_apply(pieces):
    rows_in, first_weight, second_weight = pieces
    pre_act = low_back(jnp.dot(rows_in, first_weight, precision=precise))
    act_rows = low(jax.nn.gelu(pre_act, approximate=False))
    return low_back(low(jnp.dot(act_rows, second_weight, precision=precise)))

def reference(inputs, cotangent, seq_group, domain_counts, sort_order, send_counts, gain_one, shift_one, gain_two, shift_two, w_query, w_key, w_value, w_out, router, expert_in, expert_out):
    flat_index, token_index, expert_of = route_tables(sort_order, send_counts)
    router_rows = router.astype(jnp.float32)[:, expert_of].T

    def forward(inputs_f, gain_a, shift_a, gain_b, shift_b, query_w, key_w, value_w, out_w, first_all, second_all):
        normed = low(layer_norm(inputs_f, gain_a, shift_a))
        queries = low_back(low(jnp.dot(normed, query_w, precision=precise)))
        keys_all = low_back(low(jnp.dot(normed, key_w, precision=precise)))
        values_all = low_back(low(jnp.dot(normed, value_w, precision=precise)))
        mixed = lax.map(jax.checkpoint(attend_one), (queries.reshape(SEQS, LEN, D), keys_all.reshape(SEQS, LEN, D), values_all.reshape(SEQS, LEN, D)))
        mixed = low_back(low(mixed.reshape(TOKENS, D)))
        branch = low_back(jnp.dot(mixed, out_w, precision=precise))
        hidden = inputs_f + branch
        routed = layer_norm(hidden, gain_b, shift_b)
        routed_sent = low_back(low(routed))
        gate_vals = jax.nn.sigmoid(lax.optimization_barrier(jnp.sum(routed * router_rows, axis=1)))
        slot_rows = jnp.zeros((EXPERTS * DEVICES * CAP, D), jnp.float32).at[flat_index].set(routed_sent[token_index])
        grouped = slot_rows.reshape(EXPERTS, DEVICES * CAP, D)
        results = lax.map(jax.checkpoint(expert_apply), (grouped, first_all, second_all)).reshape(EXPERTS * DEVICES * CAP, D)
        returned = jnp.zeros((TOKENS, D), jnp.float32).at[token_index].set(results[flat_index])
        return hidden + gate_vals[:, None] * returned
    params = (inputs.astype(jnp.float32), gain_one, shift_one, gain_two, shift_two, w_query.astype(jnp.float32), w_key.astype(jnp.float32), w_value.astype(jnp.float32), w_out.astype(jnp.float32), expert_in.astype(jnp.float32), expert_out.astype(jnp.float32))
    result, pullback = jax.vjp(forward, *params)
    inverse = 1.0 / domain_counts.astype(jnp.float32)
    domain_weights = inverse / jnp.mean(inverse)
    row_weight = jnp.repeat(domain_weights[seq_group], LEN)
    grads = pullback(cotangent.astype(jnp.float32) * row_weight[:, None])
    return (result.astype(jnp.bfloat16), grads[0].astype(jnp.bfloat16), grads[1], grads[2], grads[3], grads[4], grads[5], grads[6], grads[7], grads[8], grads[9], grads[10])
```

```python
import functools

import jax
import jax.numpy as jnp
from jax import lax
from jax.experimental import pallas as pl
from jax.experimental.pallas import tpu as pltpu
from jax.sharding import PartitionSpec as P

HEADS = 12
HEAD_DIM = 64
LEN = 1024
EPS = 1e-05
F32 = jnp.float32
BF16 = jnp.bfloat16
BLK = 256
LIMIT = 60 * 1024 * 1024

VMEM = pl.BlockSpec(memory_space=pltpu.VMEM)
SMEM = pl.BlockSpec(memory_space=pltpu.SMEM)


def dot(left, right, contract):
    return lax.dot_general(left, right, ((contract[0:1], contract[1:2]), ((), ())), preferred_element_type=F32)


def nn(left, right):
    return dot(left, right, (1, 0))


def nt(left, right):
    return dot(left, right, (1, 1))


def tn(left, right):
    return dot(left, right, (0, 0))


def iota(shape, axis):
    return lax.broadcasted_iota(jnp.int32, shape, axis)


def norm_stats(rows):
    center = rows - jnp.mean(rows, axis=-1, keepdims=True)
    rstd = lax.rsqrt(jnp.mean(center * center, axis=-1, keepdims=True) + EPS)
    return center * rstd, rstd


def pack_rows(slot_row, rows_ref, send_ref):
    slots = send_ref.shape[0]
    tokens = rows_ref.shape[0]

    def step(block, carry):
        base = pl.multiple_of(block * BLK, BLK)
        slot = iota((BLK, tokens), 0) + base
        pick = jnp.where(slot == slot_row, 1.0, 0.0).astype(BF16)
        send_ref[pl.ds(base, BLK), :] = nn(pick, rows_ref[...]).astype(BF16)
        return carry

    lax.fori_loop(0, slots // BLK, step, 0)


def table_kernel(experts, capacity, counts_ref, weight_ref, sort_ref, cot_ref, send_ref, slot_col_ref, slot_row_ref, scaled):
    tokens = cot_ref.shape[0]
    place = iota((1, tokens), 1)
    expert_at = jnp.zeros((1, tokens), jnp.int32)
    start_at = jnp.zeros((1, tokens), jnp.int32)
    end = jnp.int32(0)
    for expert in range(experts):
        count = counts_ref[0, expert]
        end = end + count
        past = place >= end
        expert_at = expert_at + jnp.where(past, 1, 0)
        start_at = start_at + jnp.where(past, count, 0)
    dest = (expert_at * capacity + place - start_at).astype(F32)
    sort_row = sort_ref[...]
    scaled[...] = (cot_ref[...].astype(F32) * weight_ref[0, 0]).astype(BF16)
    for block in range(tokens // BLK):
        token = iota((BLK, tokens), 0) + block * BLK
        col = jnp.sum(jnp.where(token == sort_row, dest, 0.0), axis=1, keepdims=True)
        wide = jnp.broadcast_to(col, (BLK, 128))
        slot_col_ref[pl.ds(block * BLK, BLK), :] = wide.astype(jnp.int32)
        slot_row_ref[:, pl.ds(block * BLK, BLK)] = wide.T[0:8].astype(jnp.int32)
    pack_rows(slot_row_ref[0:1, :], scaled, send_ref)


def forward_kernel(
    capacity,
    x_ref,
    gain_one_ref,
    shift_one_ref,
    gain_two_ref,
    shift_two_ref,
    wq_ref,
    wk_ref,
    wv_ref,
    wo_ref,
    router_ref,
    slot_col_ref,
    slot_row_ref,
    normed_ref,
    q_ref,
    k_ref,
    v_ref,
    mixed_ref,
    lse_ref,
    hidden_ref,
    gate_ref,
    send_ref,
    routed,
):
    tokens, width = x_ref.shape
    blocks = tokens // BLK
    lane = iota((1, 128), 1)

    def project(block, carry):
        rows = pl.ds(pl.multiple_of(block * BLK, BLK), BLK)
        hat, _ = norm_stats(x_ref[rows, :].astype(F32))
        normed = (hat * gain_one_ref[...] + shift_one_ref[...]).astype(BF16)
        normed_ref[rows, :] = normed
        q_ref[rows, :] = (nn(normed, wq_ref[...]).astype(BF16) * (HEAD_DIM ** (-0.5))).astype(BF16)
        k_ref[rows, :] = nn(normed, wk_ref[...]).astype(BF16)
        v_ref[rows, :] = nn(normed, wv_ref[...]).astype(BF16)
        return carry

    lax.fori_loop(0, blocks, project, 0)

    keep = iota((BLK, BLK), 0) <= iota((BLK, BLK), 1)

    def attend(pair, carry):
        cols = pl.ds(pl.multiple_of(pair * 128, 128), 128)
        k_pair = k_ref[:, cols]
        v_t = v_ref[:, cols].astype(F32).T.astype(BF16)
        k_head = [jnp.where(lane < 64, k_pair, 0), jnp.where(lane >= 64, k_pair, 0)]
        for block in range(blocks):
            span = (block + 1) * BLK
            query = q_ref[pl.ds(block * BLK, BLK), cols]
            outs = []
            for half in range(2):
                scores = nt(k_head[half][:span], query)
                diag = jnp.where(keep, scores[block * BLK :], -1000000000.0)
                scores = jnp.concatenate([scores[: block * BLK], diag], axis=0) if block else diag
                peak = jnp.max(scores, axis=0, keepdims=True)
                exps = jnp.exp(scores - peak)
                total = jnp.sum(exps, axis=0, keepdims=True)
                out = nn(v_t[half * 64 : half * 64 + 64, :span], exps.astype(BF16))
                outs.append(out * (1.0 / total))
                lse_ref[pair, half : half + 1, pl.ds(block * BLK, BLK)] = peak + jnp.log(total)
            mixed_ref[pl.ds(block * BLK, BLK), cols] = jnp.concatenate(outs, axis=0).T.astype(BF16)
        return carry

    lax.fori_loop(0, HEADS // 2, attend, 0)

    experts = router_ref.shape[1]

    def finish(block, carry):
        rows = pl.ds(pl.multiple_of(block * BLK, BLK), BLK)
        hidden = x_ref[rows, :].astype(F32) + nn(mixed_ref[rows, :], wo_ref[...])
        hidden_ref[rows, :] = hidden
        hat, _ = norm_stats(hidden)
        low = (hat * gain_two_ref[...] + shift_two_ref[...]).astype(BF16)
        routed[rows, :] = low
        logits = nn(low, router_ref[...])
        slot = slot_col_ref[rows, 0:1]
        first = iota((BLK, experts), 1) * capacity
        mine = (slot >= first) & (slot < first + capacity)
        logit = jnp.sum(jnp.where(mine, logits, 0.0), axis=1, keepdims=True)
        gate_ref[rows, :] = jnp.broadcast_to(jax.nn.sigmoid(logit), (BLK, 128))
        return carry

    lax.fori_loop(0, blocks, finish, 0)
    pack_rows(slot_row_ref[0:1, :], routed, send_ref)


def gelu_parts(v):
    size = jnp.abs(v)
    t = 1.0 / (1.0 + (0.3275911 * 0.7071067811865476) * size)
    bell = jnp.exp(-0.5 * (v * v))
    poly = ((((1.061405429 * t - 1.453152027) * t + 1.421413741) * t - 0.284496736) * t + 0.254829592) * t
    tail = 0.5 * poly * bell
    return jnp.where(v >= 0.0, 1.0 - tail, tail), bell * 0.3989422804014327


def expert_kernel(
    chunk,
    x_ref,
    g_ref,
    router_ref,
    w1_ref,
    w2_ref,
    y_ref,
    dx_ref,
    gw1_ref,
    gw2_ref,
    acc1,
    acc2,
):
    step = pl.program_id(0)
    hidden = w1_ref.shape[1]
    width = w1_ref.shape[0]

    @pl.when(step == 0)
    def _():
        acc1[...] = jnp.zeros_like(acc1)
        acc2[...] = jnp.zeros_like(acc2)

    x = x_ref[...]
    router = router_ref[...]
    logit = jnp.sum(x.astype(F32) * router, axis=1, keepdims=True)
    gate = jax.nn.sigmoid(logit)
    go = g_ref[...].astype(F32)
    g = (gate * go).astype(BF16)
    x_t = x.astype(F32).T.astype(BF16)
    y = jnp.zeros(x.shape, F32)
    dx = jnp.zeros(x.shape, F32)
    for first in range(0, hidden, chunk):
        cols = pl.ds(first, chunk)
        w1 = w1_ref[:, cols]
        w2 = w2_ref[cols, :]
        pre = nn(x, w1)
        cdf, pdf = gelu_parts(pre)
        act = (pre * cdf).astype(BF16)
        slope = cdf + pre * pdf
        y = y + nn(act, w2)
        grad = (nt(g, w2) * slope).astype(BF16)
        dx = dx + nt(grad, w1)
        acc1[:, cols] += nn(x_t, grad)
        acc2[cols, :] += tn(act, g)
    y_low = y.astype(BF16)
    y_ref[...] = y_low
    dlogit = jnp.sum(y_low.astype(F32) * go, axis=1, keepdims=True) * gate * (1.0 - gate)
    dx_ref[...] = (dx + dlogit * router).astype(BF16)

    @pl.when(step == pl.num_programs(0) - 1)
    def _():
        gw1_ref[...] = acc1[...].astype(BF16)
        gw2_ref[...] = acc2[...].astype(BF16)


def backward_kernel(
    weight_ref,
    x_ref,
    cot_ref,
    gain_one_ref,
    gain_two_ref,
    wq_ref,
    wk_ref,
    wv_ref,
    wo_ref,
    slot_col_ref,
    normed_ref,
    q_ref,
    k_ref,
    v_ref,
    mixed_ref,
    lse_ref,
    hidden_ref,
    dx_ref,
    grad_ref,
    dense_ref,
    ghid,
    gmix,
    branch,
    normed_t,
    dqkv,
    sums,
):
    tokens, width = x_ref.shape
    slots = dx_ref.shape[0]
    blocks = tokens // BLK
    lane = iota((1, 128), 1)
    sums[...] = jnp.zeros_like(sums)

    def open_block(block, carry):
        rows = pl.ds(pl.multiple_of(block * BLK, BLK), BLK)
        slot = slot_col_ref[rows, 0:1]
        pick = jnp.where(iota((BLK, slots), 1) == slot, 1.0, 0.0).astype(BF16)
        grad = nn(pick, dx_ref[...])
        hat, rstd = norm_stats(hidden_ref[rows, :])
        sums[2:3, :] += jnp.sum(grad * hat, axis=0, keepdims=True)
        sums[3:4, :] += jnp.sum(grad, axis=0, keepdims=True)
        gg = grad * gain_two_ref[...]
        inner = gg - jnp.mean(gg, axis=1, keepdims=True) - hat * jnp.mean(gg * hat, axis=1, keepdims=True)
        total = cot_ref[rows, :].astype(F32) * weight_ref[0, 0] + rstd * inner
        ghid[rows, :] = total
        low = total.astype(BF16)
        branch[rows, :] = low
        gmix[rows, :] = nt(low, wo_ref[...]).astype(BF16)
        normed_t[:, rows] = normed_ref[rows, :].astype(F32).T.astype(BF16)
        return carry

    lax.fori_loop(0, blocks, open_block, 0)
    dense_ref[pl.ds(3 * width, width), :] = tn(mixed_ref[...], branch[...]).astype(BF16)

    keep = iota((BLK, BLK), 0) <= iota((BLK, BLK), 1)

    def attend(pair, carry):
        base = pl.multiple_of(pair * 128, 128)
        cols = pl.ds(base, 128)
        q_pair = q_ref[:, cols]
        k_pair = k_ref[:, cols]
        v_pair = v_ref[:, cols]
        o_pair = gmix[:, cols]
        low = lane < 64
        q_head = [jnp.where(low, q_pair, 0), jnp.where(low, 0, q_pair)]
        k_head = [jnp.where(low, k_pair, 0), jnp.where(low, 0, k_pair)]
        v_head = [jnp.where(low, v_pair, 0), jnp.where(low, 0, v_pair)]
        o_head = [jnp.where(low, o_pair, 0), jnp.where(low, 0, o_pair)]
        k_t = k_pair.astype(F32).T.astype(BF16)
        prod_t = (o_pair.astype(F32) * mixed_ref[:, cols].astype(F32)).T
        delta = [jnp.sum(prod_t[:64], axis=0, keepdims=True), jnp.sum(prod_t[64:], axis=0, keepdims=True)]
        dq_t = [[None] * blocks, [None] * blocks]
        for block in range(blocks):
            start = block * BLK
            dk = None
            dv = None
            for half in range(2):
                scores = nt(k_head[half][start : start + BLK], q_pair[start:])
                diag = jnp.where(keep, scores[:, :BLK], -1000000000.0)
                scores = jnp.concatenate([diag, scores[:, BLK:]], axis=1) if block < blocks - 1 else diag
                probs = jnp.exp(scores - lse_ref[pair, half : half + 1, pl.ds(start, tokens - start)])
                grad_p = nt(v_head[half][start : start + BLK], o_pair[start:])
                grad_s = (probs * (grad_p - delta[half][:, start:])).astype(BF16)
                dv_part = nn(probs.astype(BF16), o_head[half][start:])
                dk_part = nn(grad_s, q_head[half][start:])
                dv = dv_part if dv is None else dv + dv_part
                dk = dk_part if dk is None else dk + dk_part
                dq_part = nn(k_t[half * 64 : half * 64 + 64, start : start + BLK], grad_s)
                for later in range(block, blocks):
                    piece = dq_part[:, (later - block) * BLK : (later - block + 1) * BLK]
                    dq_t[half][later] = piece if dq_t[half][later] is None else dq_t[half][later] + piece
            rows = pl.ds(start, BLK)
            dqkv[rows, pl.ds(pl.multiple_of(base + width, 128), 128)] = dk.astype(BF16)
            dqkv[rows, pl.ds(pl.multiple_of(base + 2 * width, 128), 128)] = dv.astype(BF16)
        for block in range(blocks):
            both = jnp.concatenate([dq_t[0][block], dq_t[1][block]], axis=0) * (HEAD_DIM ** (-0.5))
            dqkv[pl.ds(block * BLK, BLK), cols] = both.T.astype(BF16)
        return carry

    lax.fori_loop(0, HEADS // 2, attend, 0)

    for part in range(3):
        dense_ref[pl.ds(part * width, width), :] = nn(normed_t[...], dqkv[:, pl.ds(part * width, width)]).astype(BF16)

    def close_block(block, carry):
        rows = pl.ds(pl.multiple_of(block * BLK, BLK), BLK)
        grad = nt(dqkv[rows, 0:width], wq_ref[...])
        grad = grad + nt(dqkv[rows, width : 2 * width], wk_ref[...])
        grad = grad + nt(dqkv[rows, 2 * width : 3 * width], wv_ref[...])
        hat, rstd = norm_stats(x_ref[rows, :].astype(F32))
        sums[0:1, :] += jnp.sum(grad * hat, axis=0, keepdims=True)
        sums[1:2, :] += jnp.sum(grad, axis=0, keepdims=True)
        gg = grad * gain_one_ref[...]
        inner = gg - jnp.mean(gg, axis=1, keepdims=True) - hat * jnp.mean(gg * hat, axis=1, keepdims=True)
        grad_ref[rows, :] = (ghid[rows, :] + rstd * inner).astype(BF16)
        return carry

    lax.fori_loop(0, blocks, close_block, 0)
    dense_ref[pl.ds(4 * width, 16), :] = sums[...].astype(BF16)


def output_kernel(slot_col_ref, hidden_ref, gate_ref, y_ref, out_ref):
    tokens, _ = hidden_ref.shape
    slots = y_ref.shape[0]

    def step(block, carry):
        rows = pl.ds(pl.multiple_of(block * BLK, BLK), BLK)
        slot = slot_col_ref[rows, 0:1]
        pick = jnp.where(iota((BLK, slots), 1) == slot, 1.0, 0.0).astype(BF16)
        back = nn(pick, y_ref[...])
        out_ref[rows, :] = (hidden_ref[rows, :] + gate_ref[rows, 0:1] * back).astype(BF16)
        return carry

    lax.fori_loop(0, tokens // BLK, step, 0)


def call(kernel, outs, in_specs, scratch, name):
    return pl.pallas_call(
        kernel,
        out_shape=outs,
        in_specs=in_specs,
        out_specs=[VMEM] * len(outs),
        scratch_shapes=scratch,
        compiler_params=pltpu.CompilerParams(vmem_limit_bytes=LIMIT),
        name=name,
    )


def shape(dims, kind):
    return jax.ShapeDtypeStruct(dims, kind)


def tables(experts, capacity, counts, weight, sort_order, cotangent):
    tokens, width = cotangent.shape
    slots = experts * capacity
    return call(
        functools.partial(table_kernel, experts, capacity),
        [shape((slots, width), BF16), shape((tokens, 128), jnp.int32), shape((8, tokens), jnp.int32)],
        [SMEM, SMEM, VMEM, VMEM],
        [pltpu.VMEM((tokens, width), BF16)],
        "tables",
    )(counts, weight, sort_order, cotangent)


def forward(capacity, slots, inputs, g1, s1, g2, s2, wq, wk, wv, wo, router, slot_col, slot_row):
    tokens, width = inputs.shape
    rows_low = shape((tokens, width), BF16)
    return call(
        functools.partial(forward_kernel, capacity),
        [
            rows_low,
            rows_low,
            rows_low,
            rows_low,
            rows_low,
            shape((HEADS // 2, 8, tokens), F32),
            shape((tokens, width), F32),
            shape((tokens, 128), F32),
            shape((slots, width), BF16),
        ],
        [VMEM] * 12,
        [pltpu.VMEM((tokens, width), BF16)],
        "dense_forward",
    )(inputs, g1, s1, g2, s2, wq, wk, wv, wo, router, slot_col, slot_row)


def expert_block(x, g, router_row, w1, w2, rows=BLK, chunk=768):
    slots, width = x.shape
    hidden = w1.shape[1]
    row_spec = pl.BlockSpec((rows, width), lambda i: (i, 0))
    one = pl.Buffered(1)

    def whole(dims):
        return pl.BlockSpec(dims, lambda i: (0, 0), pipeline_mode=one)

    return pl.pallas_call(
        functools.partial(expert_kernel, chunk),
        out_shape=[
            shape((slots, width), BF16),
            shape((slots, width), BF16),
            shape((width, hidden), BF16),
            shape((hidden, width), BF16),
        ],
        grid=(slots // rows,),
        in_specs=[row_spec, row_spec, whole((1, width)), whole((width, hidden)), whole((hidden, width))],
        out_specs=[row_spec, row_spec, whole((width, hidden)), whole((hidden, width))],
        scratch_shapes=[pltpu.VMEM((width, hidden), F32), pltpu.VMEM((hidden, width), F32)],
        compiler_params=pltpu.CompilerParams(vmem_limit_bytes=LIMIT),
        name="expert",
    )(x, g, router_row, w1, w2)


def backward(weight, inputs, cotangent, g1, g2, wq, wk, wv, wo, slot_col, normed, q, k, v, mixed, lse, hidden, dx):
    tokens, width = inputs.shape
    return call(
        backward_kernel,
        [shape((tokens, width), BF16), shape((4 * width + 16, width), BF16)],
        [SMEM] + [VMEM] * 17,
        [
            pltpu.VMEM((tokens, width), F32),
            pltpu.VMEM((tokens, width), BF16),
            pltpu.VMEM((tokens, width), BF16),
            pltpu.VMEM((width, tokens), BF16),
            pltpu.VMEM((tokens, 3 * width), BF16),
            pltpu.VMEM((16, width), F32),
        ],
        "dense_backward",
    )(weight, inputs, cotangent, g1, g2, wq, wk, wv, wo, slot_col, normed, q, k, v, mixed, lse, hidden, dx)


def combine(slot_col, hidden, gate, y):
    return call(output_kernel, [shape(hidden.shape, BF16)], [VMEM] * 4, [], "combine")(slot_col, hidden, gate, y)[0]


def local(
    inputs,
    cotangent,
    seq_group,
    domain_counts,
    sort_order,
    send_counts,
    gain_one,
    shift_one,
    gain_two,
    shift_two,
    w_query,
    w_key,
    w_value,
    w_out,
    router,
    expert_in,
    expert_out,
):
    tokens, width = inputs.shape
    experts = send_counts.shape[1]
    capacity = 2 * tokens // experts
    slots = experts * capacity
    inverse = 1.0 / domain_counts.astype(F32)
    domain_weights = inverse / jnp.mean(inverse)
    ids = jnp.arange(domain_counts.shape[0], dtype=jnp.int32)
    weight = jnp.sum(jnp.where(seq_group[:, None] == ids[None, :], domain_weights[None, :], 0.0), axis=1).reshape(1, 1)
    mine = lax.axis_index("expert")
    router_row = lax.dynamic_slice_in_dim(router.T, mine, 1, axis=0).astype(F32)

    def exchange(rows):
        return lax.all_to_all(
            rows.reshape(experts, capacity, width), "expert", split_axis=0, concat_axis=0, tiled=True
        ).reshape(slots, width)

    g1, s1, g2, s2 = (v.reshape(1, width) for v in (gain_one, shift_one, gain_two, shift_two))
    cot_send, slot_col, slot_row = tables(experts, capacity, send_counts, weight, sort_order, cotangent)
    cot_rows = exchange(cot_send)
    normed, q, k, v, mixed, lse, hidden, gate, send = forward(
        capacity, slots, inputs, g1, s1, g2, s2, w_query, w_key, w_value, w_out, router, slot_col, slot_row
    )
    arrived = exchange(send)
    y_rows, dx_rows, grad_first, grad_second = expert_block(arrived, cot_rows, router_row, expert_in[0], expert_out[0])
    dx_back = exchange(dx_rows)
    y_back = exchange(y_rows)
    expert_sums = (lax.psum(grad_first, "dp").astype(F32), lax.psum(grad_second, "dp").astype(F32))
    grad_inputs, dense = backward(
        weight, inputs, cotangent, g1, g2, w_query, w_key, w_value, w_out, slot_col, normed, q, k, v, mixed, lse, hidden, dx_back
    )
    output = combine(slot_col, hidden, gate, y_back)
    dense = lax.psum(dense, ("dp", "expert")).astype(F32)
    parts = [dense[i * width : (i + 1) * width] for i in range(4)]
    vecs = [dense[4 * width + i] for i in range(4)]
    return (
        output,
        grad_inputs,
        *vecs,
        *parts,
        expert_sums[0][None],
        expert_sums[1][None],
    )


def solution(mesh):
    rows = P(("dp", "expert"), None)
    split = P("expert", None, None)
    return jax.shard_map(
        local,
        mesh=mesh,
        in_specs=(rows, rows, P(("dp", "expert")), P(), rows, rows) + (P(),) * 9 + (split, split),
        out_specs=(rows, rows) + (P(),) * 8 + (split, split),
        check_vma=False,
    )
```

```python
import functools

import jax
import jax.numpy as jnp
from jax import lax
from jax.experimental import pallas as pl
from jax.experimental.pallas import tpu as pltpu
from jax.sharding import PartitionSpec as P

HEADS = 12
HEAD_DIM = 64
LEN = 1024
EPS = 1e-05
F32 = jnp.float32
BF16 = jnp.bfloat16
BLK = 256
LIMIT = 60 * 1024 * 1024

VMEM = pl.BlockSpec(memory_space=pltpu.VMEM)
SMEM = pl.BlockSpec(memory_space=pltpu.SMEM)
ANY = pl.BlockSpec(memory_space=pl.ANY)
MESH = pl.DeviceIdType.MESH


def dot(left, right, contract):
    return lax.dot_general(left, right, ((contract[0:1], contract[1:2]), ((), ())), preferred_element_type=F32)


def nn(left, right):
    return dot(left, right, (1, 0))


def nt(left, right):
    return dot(left, right, (1, 1))


def tn(left, right):
    return dot(left, right, (0, 0))


def iota(shape, axis):
    return lax.broadcasted_iota(jnp.int32, shape, axis)


def flip(index, mask, count):
    bit, out = 1, 0
    while bit < count:
        out = out + ((index // bit + mask // bit) % 2) * bit
        bit *= 2
    return out


def greet(axis, me, count):
    barrier = pltpu.get_barrier_semaphore()
    for mask in range(1, count):
        pl.semaphore_signal(barrier, inc=1, device_id={axis: flip(me, mask, count)}, device_id_type=MESH)
    pl.semaphore_wait(barrier, count - 1)


def send_block(me, count, capacity, mask, source, target, sends, recvs):
    peer = flip(me, mask, count)
    return pltpu.make_async_remote_copy(
        src_ref=source.at[pl.ds(pl.multiple_of(peer * capacity, capacity), capacity)],
        dst_ref=target.at[pl.ds(pl.multiple_of(mask * capacity, capacity), capacity)],
        send_sem=sends.at[mask],
        recv_sem=recvs.at[mask],
        device_id={"expert": peer},
        device_id_type=MESH,
    )


def return_block(me, count, capacity, mask, source, target, sends, recvs):
    return pltpu.make_async_remote_copy(
        src_ref=source.at[pl.ds(pl.multiple_of(mask * capacity, capacity), capacity)],
        dst_ref=target.at[pl.ds(pl.multiple_of(me * capacity, capacity), capacity)],
        send_sem=sends.at[mask],
        recv_sem=recvs.at[mask],
        device_id={"expert": flip(me, mask, count)},
        device_id_type=MESH,
    )


def norm_stats(rows):
    center = rows - jnp.mean(rows, axis=-1, keepdims=True)
    rstd = lax.rsqrt(jnp.mean(center * center, axis=-1, keepdims=True) + EPS)
    return center * rstd, rstd


def pack_rows(slot_row, rows_ref, send_ref):
    slots = send_ref.shape[0]
    tokens = rows_ref.shape[0]

    def step(block, carry):
        base = pl.multiple_of(block * BLK, BLK)
        slot = iota((BLK, tokens), 0) + base
        pick = jnp.where(slot == slot_row, 1.0, 0.0).astype(BF16)
        send_ref[pl.ds(base, BLK), :] = nn(pick, rows_ref[...]).astype(BF16)
        return carry

    lax.fori_loop(0, slots // BLK, step, 0)


def table_kernel(experts, capacity, counts_ref, weight_ref, sort_ref, cot_ref, send_ref, slot_col_ref, slot_row_ref, scaled):
    tokens = cot_ref.shape[0]
    place = iota((1, tokens), 1)
    expert_at = jnp.zeros((1, tokens), jnp.int32)
    start_at = jnp.zeros((1, tokens), jnp.int32)
    end = jnp.int32(0)
    for expert in range(experts):
        count = counts_ref[0, expert]
        end = end + count
        past = place >= end
        expert_at = expert_at + jnp.where(past, 1, 0)
        start_at = start_at + jnp.where(past, count, 0)
    dest = (expert_at * capacity + place - start_at).astype(F32)
    sort_row = sort_ref[...]
    scaled[...] = (cot_ref[...].astype(F32) * weight_ref[0, 0]).astype(BF16)
    for block in range(tokens // BLK):
        token = iota((BLK, tokens), 0) + block * BLK
        col = jnp.sum(jnp.where(token == sort_row, dest, 0.0), axis=1, keepdims=True)
        wide = jnp.broadcast_to(col, (BLK, 128))
        slot_col_ref[pl.ds(block * BLK, BLK), :] = wide.astype(jnp.int32)
        slot_row_ref[:, pl.ds(block * BLK, BLK)] = wide.T[0:8].astype(jnp.int32)
    pack_rows(slot_row_ref[0:1, :], scaled, send_ref)


def forward_kernel(
    count,
    capacity,
    x_ref,
    gain_one_ref,
    shift_one_ref,
    gain_two_ref,
    shift_two_ref,
    wq_ref,
    wk_ref,
    wv_ref,
    wo_ref,
    router_ref,
    slot_col_ref,
    slot_row_ref,
    cot_send_ref,
    normed_ref,
    q_ref,
    k_ref,
    v_ref,
    mixed_ref,
    lse_ref,
    hidden_ref,
    gate_ref,
    send_ref,
    cot_rows_ref,
    routed,
    sends,
    recvs,
    own,
):
    tokens, width = x_ref.shape
    blocks = tokens // BLK
    me = lax.axis_index("expert")
    greet("expert", me, count)
    copies = [send_block(me, count, capacity, mask, cot_send_ref, cot_rows_ref, sends, recvs) for mask in range(1, count)]
    for copy in reversed(copies):
        copy.start()
    mine = pltpu.make_async_copy(
        cot_send_ref.at[pl.ds(pl.multiple_of(me * capacity, capacity), capacity)], cot_rows_ref.at[pl.ds(0, capacity)], own
    )
    mine.start()
    lane = iota((1, 128), 1)

    def project(block, carry):
        rows = pl.ds(pl.multiple_of(block * BLK, BLK), BLK)
        hat, _ = norm_stats(x_ref[rows, :].astype(F32))
        normed = (hat * gain_one_ref[...] + shift_one_ref[...]).astype(BF16)
        normed_ref[rows, :] = normed
        q_ref[rows, :] = (nn(normed, wq_ref[...]).astype(BF16) * (HEAD_DIM ** (-0.5))).astype(BF16)
        k_ref[rows, :] = nn(normed, wk_ref[...]).astype(BF16)
        v_ref[rows, :] = nn(normed, wv_ref[...]).astype(BF16)
        return carry

    lax.fori_loop(0, blocks, project, 0)

    keep = iota((BLK, BLK), 0) <= iota((BLK, BLK), 1)

    def attend(pair, carry):
        cols = pl.ds(pl.multiple_of(pair * 128, 128), 128)
        k_pair = k_ref[:, cols]
        v_t = v_ref[:, cols].astype(F32).T.astype(BF16)
        k_head = [jnp.where(lane < 64, k_pair, 0), jnp.where(lane >= 64, k_pair, 0)]
        for block in range(blocks):
            span = (block + 1) * BLK
            query = q_ref[pl.ds(block * BLK, BLK), cols]
            outs = []
            for half in range(2):
                scores = nt(k_head[half][:span], query)
                diag = jnp.where(keep, scores[block * BLK :], -1000000000.0)
                scores = jnp.concatenate([scores[: block * BLK], diag], axis=0) if block else diag
                peak = jnp.max(scores, axis=0, keepdims=True)
                exps = jnp.exp(scores - peak)
                total = jnp.sum(exps, axis=0, keepdims=True)
                out = nn(v_t[half * 64 : half * 64 + 64, :span], exps.astype(BF16))
                outs.append(out * (1.0 / total))
                lse_ref[pair, half : half + 1, pl.ds(block * BLK, BLK)] = peak + jnp.log(total)
            mixed_ref[pl.ds(block * BLK, BLK), cols] = jnp.concatenate(outs, axis=0).T.astype(BF16)
        return carry

    lax.fori_loop(0, HEADS // 2, attend, 0)

    experts = router_ref.shape[1]

    def finish(block, carry):
        rows = pl.ds(pl.multiple_of(block * BLK, BLK), BLK)
        hidden = x_ref[rows, :].astype(F32) + nn(mixed_ref[rows, :], wo_ref[...])
        hidden_ref[rows, :] = hidden
        hat, _ = norm_stats(hidden)
        low = (hat * gain_two_ref[...] + shift_two_ref[...]).astype(BF16)
        routed[rows, :] = low
        logits = nn(low, router_ref[...])
        slot = slot_col_ref[rows, 0:1]
        first = iota((BLK, experts), 1) * capacity
        mine = (slot >= first) & (slot < first + capacity)
        logit = jnp.sum(jnp.where(mine, logits, 0.0), axis=1, keepdims=True)
        gate_ref[rows, :] = jnp.broadcast_to(jax.nn.sigmoid(logit), (BLK, 128))
        return carry

    lax.fori_loop(0, blocks, finish, 0)
    pack_rows(slot_row_ref[0:1, :], routed, send_ref)
    mine.wait()
    for copy in copies:
        copy.wait()


def gelu_parts(v):
    size = jnp.abs(v)
    t = 1.0 / (1.0 + (0.3275911 * 0.7071067811865476) * size)
    bell = jnp.exp(-0.5 * (v * v))
    poly = ((((1.061405429 * t - 1.453152027) * t + 1.421413741) * t - 0.284496736) * t + 0.254829592) * t
    tail = 0.5 * poly * bell
    return jnp.where(v >= 0.0, 1.0 - tail, tail), bell * 0.3989422804014327


def expert_kernel(
    count,
    capacity,
    chunk,
    send_ref,
    g_ref,
    router_ref,
    w1_hbm,
    w2_hbm,
    y_ref,
    back_ref,
    gw1_ref,
    gw2_ref,
    w1_ref,
    w2_ref,
    acc1,
    acc2,
    x_rows,
    dx_rows,
    y_rows,
    stage,
    load_sems,
    sends,
    recvs,
    back_sends,
    back_recvs,
    own,
    y_sems,
    stage_sems,
):
    width, hidden = w1_ref.shape
    slots = x_rows.shape[0]
    group = BLK // capacity
    me = lax.axis_index("expert")
    loads = [pltpu.make_async_copy(w1_hbm, w1_ref, load_sems.at[0]), pltpu.make_async_copy(w2_hbm, w2_ref, load_sems.at[1])]
    for load in loads:
        load.start()
    greet("expert", me, count)
    mine_in = pltpu.make_async_copy(
        send_ref.at[pl.ds(pl.multiple_of(me * capacity, capacity), capacity)], x_rows.at[pl.ds(0, capacity)], own.at[0]
    )
    mine_in.start()
    for mask in range(1, count):
        send_block(me, count, capacity, mask, send_ref, x_rows, sends, recvs).start()
    acc1[...] = jnp.zeros_like(acc1)
    acc2[...] = jnp.zeros_like(acc2)
    for load in loads:
        load.wait()
    mine_in.wait()
    router = router_ref[...]

    def store_y(block):
        rows = pl.ds(pl.multiple_of(block * BLK, BLK), BLK)
        return pltpu.make_async_copy(y_rows.at[rows], y_ref.at[rows], y_sems.at[block])

    def mine_out():
        return pltpu.make_async_copy(
            dx_rows.at[pl.ds(0, capacity)], back_ref.at[pl.ds(pl.multiple_of(me * capacity, capacity), capacity)], own.at[1]
        )

    def run(block, carry):
        for item in range(group):
            mask = block * group + item

            @pl.when(mask > 0)
            def _():
                send_block(me, count, capacity, mask, send_ref, x_rows, sends, recvs).wait_recv()

        rows = pl.ds(pl.multiple_of(block * BLK, BLK), BLK)
        x = x_rows[rows, :]
        logit = jnp.sum(x.astype(F32) * router, axis=1, keepdims=True)
        gate = jax.nn.sigmoid(logit)
        go = g_ref[rows, :].astype(F32)
        g = (gate * go).astype(BF16)
        x_t = x.astype(F32).T.astype(BF16)
        y = jnp.zeros(x.shape, F32)
        dx = jnp.zeros(x.shape, F32)
        for first in range(0, hidden, chunk):
            cols = pl.ds(first, chunk)
            w1 = w1_ref[:, cols]
            w2 = w2_ref[cols, :]
            pre = nn(x, w1)
            cdf, pdf = gelu_parts(pre)
            act = (pre * cdf).astype(BF16)
            slope = cdf + pre * pdf
            y = y + nn(act, w2)
            grad = (nt(g, w2) * slope).astype(BF16)
            dx = dx + nt(grad, w1)
            acc1[:, cols] += nn(x_t, grad)
            acc2[cols, :] += tn(act, g)
        y_low = y.astype(BF16)
        y_rows[rows, :] = y_low
        dlogit = jnp.sum(y_low.astype(F32) * go, axis=1, keepdims=True) * gate * (1.0 - gate)
        dx_rows[rows, :] = (dx + dlogit * router).astype(BF16)
        store_y(block).start()
        for item in range(group):
            mask = block * group + item

            @pl.when(mask > 0)
            def _():
                return_block(me, count, capacity, mask, dx_rows, back_ref, back_sends, back_recvs).start()

            @pl.when(mask == 0)
            def _():
                mine_out().start()

        return carry

    lax.fori_loop(0, slots // BLK, run, 0)

    pieces = []
    for first in range(0, hidden, stage.shape[1]):
        pieces.append((acc1.at[:, pl.ds(first, stage.shape[1])], gw1_ref.at[:, pl.ds(first, stage.shape[1])]))
    for first in range(0, hidden, stage.shape[1]):
        pieces.append((acc2.at[pl.ds(first, stage.shape[1]), :], gw2_ref.at[pl.ds(first, stage.shape[1]), :]))
    writes = []
    for index, (piece, target) in enumerate(pieces):
        slot = index % 2
        if index >= 2:
            writes[index - 2].wait()
        stage[slot] = piece[...].astype(BF16)
        write = pltpu.make_async_copy(stage.at[slot], target, stage_sems.at[slot])
        write.start()
        writes.append(write)
    for write in writes[-2:]:
        write.wait()
    mine_out().wait()

    def settle(block, carry):
        store_y(block).wait()
        return carry

    lax.fori_loop(0, slots // BLK, settle, 0)
    for mask in range(1, count):
        send_block(me, count, capacity, mask, send_ref, x_rows, sends, recvs).wait_send()
        return_block(me, count, capacity, mask, dx_rows, back_ref, back_sends, back_recvs).wait()


def backward_kernel(
    count,
    capacity,
    weight_ref,
    x_ref,
    cot_ref,
    gain_one_ref,
    gain_two_ref,
    wq_ref,
    wk_ref,
    wv_ref,
    wo_ref,
    slot_col_ref,
    normed_ref,
    q_ref,
    k_ref,
    v_ref,
    mixed_ref,
    lse_ref,
    hidden_ref,
    dx_ref,
    y_ref,
    grad_ref,
    dense_ref,
    y_back_ref,
    ghid,
    gmix,
    branch,
    normed_t,
    dqkv,
    sums,
    sends,
    recvs,
    own,
):
    tokens, width = x_ref.shape
    me = lax.axis_index("expert")
    greet("expert", me, count)
    copies = [return_block(me, count, capacity, mask, y_ref, y_back_ref, sends, recvs) for mask in range(1, count)]
    for copy in reversed(copies):
        copy.start()
    mine = pltpu.make_async_copy(
        y_ref.at[pl.ds(0, capacity)], y_back_ref.at[pl.ds(pl.multiple_of(me * capacity, capacity), capacity)], own
    )
    mine.start()
    slots = dx_ref.shape[0]
    blocks = tokens // BLK
    lane = iota((1, 128), 1)
    sums[...] = jnp.zeros_like(sums)

    def open_block(block, carry):
        rows = pl.ds(pl.multiple_of(block * BLK, BLK), BLK)
        slot = slot_col_ref[rows, 0:1]
        pick = jnp.where(iota((BLK, slots), 1) == slot, 1.0, 0.0).astype(BF16)
        grad = nn(pick, dx_ref[...])
        hat, rstd = norm_stats(hidden_ref[rows, :])
        sums[2:3, :] += jnp.sum(grad * hat, axis=0, keepdims=True)
        sums[3:4, :] += jnp.sum(grad, axis=0, keepdims=True)
        gg = grad * gain_two_ref[...]
        inner = gg - jnp.mean(gg, axis=1, keepdims=True) - hat * jnp.mean(gg * hat, axis=1, keepdims=True)
        total = cot_ref[rows, :].astype(F32) * weight_ref[0, 0] + rstd * inner
        ghid[rows, :] = total
        low = total.astype(BF16)
        branch[rows, :] = low
        gmix[rows, :] = nt(low, wo_ref[...]).astype(BF16)
        normed_t[:, rows] = normed_ref[rows, :].astype(F32).T.astype(BF16)
        return carry

    lax.fori_loop(0, blocks, open_block, 0)
    dense_ref[pl.ds(3 * width, width), :] = tn(mixed_ref[...], branch[...]).astype(BF16)

    keep = iota((BLK, BLK), 0) <= iota((BLK, BLK), 1)

    def attend(pair, carry):
        base = pl.multiple_of(pair * 128, 128)
        cols = pl.ds(base, 128)
        q_pair = q_ref[:, cols]
        k_pair = k_ref[:, cols]
        v_pair = v_ref[:, cols]
        o_pair = gmix[:, cols]
        low = lane < 64
        q_head = [jnp.where(low, q_pair, 0), jnp.where(low, 0, q_pair)]
        k_head = [jnp.where(low, k_pair, 0), jnp.where(low, 0, k_pair)]
        v_head = [jnp.where(low, v_pair, 0), jnp.where(low, 0, v_pair)]
        o_head = [jnp.where(low, o_pair, 0), jnp.where(low, 0, o_pair)]
        k_t = k_pair.astype(F32).T.astype(BF16)
        prod_t = (o_pair.astype(F32) * mixed_ref[:, cols].astype(F32)).T
        delta = [jnp.sum(prod_t[:64], axis=0, keepdims=True), jnp.sum(prod_t[64:], axis=0, keepdims=True)]
        dq_t = [[None] * blocks, [None] * blocks]
        for block in range(blocks):
            start = block * BLK
            dk = None
            dv = None
            for half in range(2):
                scores = nt(k_head[half][start : start + BLK], q_pair[start:])
                diag = jnp.where(keep, scores[:, :BLK], -1000000000.0)
                scores = jnp.concatenate([diag, scores[:, BLK:]], axis=1) if block < blocks - 1 else diag
                probs = jnp.exp(scores - lse_ref[pair, half : half + 1, pl.ds(start, tokens - start)])
                grad_p = nt(v_head[half][start : start + BLK], o_pair[start:])
                grad_s = (probs * (grad_p - delta[half][:, start:])).astype(BF16)
                dv_part = nn(probs.astype(BF16), o_head[half][start:])
                dk_part = nn(grad_s, q_head[half][start:])
                dv = dv_part if dv is None else dv + dv_part
                dk = dk_part if dk is None else dk + dk_part
                dq_part = nn(k_t[half * 64 : half * 64 + 64, start : start + BLK], grad_s)
                for later in range(block, blocks):
                    piece = dq_part[:, (later - block) * BLK : (later - block + 1) * BLK]
                    dq_t[half][later] = piece if dq_t[half][later] is None else dq_t[half][later] + piece
            rows = pl.ds(start, BLK)
            dqkv[rows, pl.ds(pl.multiple_of(base + width, 128), 128)] = dk.astype(BF16)
            dqkv[rows, pl.ds(pl.multiple_of(base + 2 * width, 128), 128)] = dv.astype(BF16)
        for block in range(blocks):
            both = jnp.concatenate([dq_t[0][block], dq_t[1][block]], axis=0) * (HEAD_DIM ** (-0.5))
            dqkv[pl.ds(block * BLK, BLK), cols] = both.T.astype(BF16)
        return carry

    lax.fori_loop(0, HEADS // 2, attend, 0)

    for part in range(3):
        dense_ref[pl.ds(part * width, width), :] = nn(normed_t[...], dqkv[:, pl.ds(part * width, width)]).astype(BF16)

    def close_block(block, carry):
        rows = pl.ds(pl.multiple_of(block * BLK, BLK), BLK)
        grad = nt(dqkv[rows, 0:width], wq_ref[...])
        grad = grad + nt(dqkv[rows, width : 2 * width], wk_ref[...])
        grad = grad + nt(dqkv[rows, 2 * width : 3 * width], wv_ref[...])
        hat, rstd = norm_stats(x_ref[rows, :].astype(F32))
        sums[0:1, :] += jnp.sum(grad * hat, axis=0, keepdims=True)
        sums[1:2, :] += jnp.sum(grad, axis=0, keepdims=True)
        gg = grad * gain_one_ref[...]
        inner = gg - jnp.mean(gg, axis=1, keepdims=True) - hat * jnp.mean(gg * hat, axis=1, keepdims=True)
        grad_ref[rows, :] = (ghid[rows, :] + rstd * inner).astype(BF16)
        return carry

    lax.fori_loop(0, blocks, close_block, 0)
    dense_ref[pl.ds(4 * width, 16), :] = sums[...].astype(BF16)
    mine.wait()
    for copy in copies:
        copy.wait()


def output_kernel(slot_col_ref, hidden_ref, gate_ref, y_ref, out_ref):
    tokens, _ = hidden_ref.shape
    slots = y_ref.shape[0]

    def step(block, carry):
        rows = pl.ds(pl.multiple_of(block * BLK, BLK), BLK)
        slot = slot_col_ref[rows, 0:1]
        pick = jnp.where(iota((BLK, slots), 1) == slot, 1.0, 0.0).astype(BF16)
        back = nn(pick, y_ref[...])
        out_ref[rows, :] = (hidden_ref[rows, :] + gate_ref[rows, 0:1] * back).astype(BF16)
        return carry

    lax.fori_loop(0, tokens // BLK, step, 0)


def call(kernel, outs, in_specs, scratch, name, out_specs=None, collective=None, flops=10**9):
    remote = {} if collective is None else {"collective_id": collective, "has_side_effects": True}
    return pl.pallas_call(
        kernel,
        out_shape=outs,
        in_specs=in_specs,
        out_specs=out_specs or [VMEM] * len(outs),
        scratch_shapes=scratch,
        compiler_params=pltpu.CompilerParams(vmem_limit_bytes=LIMIT, **remote),
        cost_estimate=pl.CostEstimate(flops=flops, bytes_accessed=10**7, transcendentals=0),
        name=name,
    )


def dma(*dims):
    return pltpu.SemaphoreType.DMA(dims)


def shape(dims, kind):
    return jax.ShapeDtypeStruct(dims, kind)


def tables(experts, capacity, counts, weight, sort_order, cotangent):
    tokens, width = cotangent.shape
    slots = experts * capacity
    return call(
        functools.partial(table_kernel, experts, capacity),
        [shape((slots, width), BF16), shape((tokens, 128), jnp.int32), shape((8, tokens), jnp.int32)],
        [SMEM, SMEM, VMEM, VMEM],
        [pltpu.VMEM((tokens, width), BF16)],
        "tables",
    )(counts, weight, sort_order, cotangent)


def forward(count, capacity, slots, inputs, g1, s1, g2, s2, wq, wk, wv, wo, router, slot_col, slot_row, cot_send):
    tokens, width = inputs.shape
    rows_low = shape((tokens, width), BF16)
    return call(
        functools.partial(forward_kernel, count, capacity),
        [
            rows_low,
            rows_low,
            rows_low,
            rows_low,
            rows_low,
            shape((HEADS // 2, 8, tokens), F32),
            shape((tokens, width), F32),
            shape((tokens, 128), F32),
            shape((slots, width), BF16),
            shape((slots, width), BF16),
        ],
        [VMEM] * 12 + [ANY],
        [pltpu.VMEM((tokens, width), BF16), dma(count), dma(count), dma()],
        "dense_forward",
        [VMEM] * 9 + [ANY],
        1,
    )(inputs, g1, s1, g2, s2, wq, wk, wv, wo, router, slot_col, slot_row, cot_send)


def expert_block(count, capacity, send, g, router_row, w1, w2, chunk=768):
    slots, width = send.shape
    hidden = w1.shape[1]
    rows = shape((slots, width), BF16)
    keep = pltpu.VMEM((slots, width), BF16)
    return call(
        functools.partial(expert_kernel, count, capacity, chunk),
        [rows, rows, shape((width, hidden), BF16), shape((hidden, width), BF16)],
        [ANY, VMEM, VMEM, ANY, ANY],
        [
            pltpu.VMEM((width, hidden), BF16),
            pltpu.VMEM((hidden, width), BF16),
            pltpu.VMEM((width, hidden), F32),
            pltpu.VMEM((hidden, width), F32),
            keep,
            keep,
            keep,
            pltpu.VMEM((2, width, width), BF16),
            dma(2),
            dma(count),
            dma(count),
            dma(count),
            dma(count),
            dma(2),
            dma(slots // BLK),
            dma(2),
        ],
        "expert",
        [ANY] * 4,
        2,
    )(send, g, router_row, w1, w2)


def backward(
    count, capacity, weight, inputs, cotangent, g1, g2, wq, wk, wv, wo, slot_col, normed, q, k, v, mixed, lse, hidden, dx, y
):
    tokens, width = inputs.shape
    return call(
        functools.partial(backward_kernel, count, capacity),
        [shape((tokens, width), BF16), shape((4 * width + 16, width), BF16), shape(y.shape, BF16)],
        [SMEM] + [VMEM] * 17 + [ANY],
        [
            pltpu.VMEM((tokens, width), F32),
            pltpu.VMEM((tokens, width), BF16),
            pltpu.VMEM((tokens, width), BF16),
            pltpu.VMEM((width, tokens), BF16),
            pltpu.VMEM((tokens, 3 * width), BF16),
            pltpu.VMEM((16, width), F32),
            dma(count),
            dma(count),
            dma(),
        ],
        "dense_backward",
        [VMEM, VMEM, ANY],
        3,
        5 * 10**10,
    )(weight, inputs, cotangent, g1, g2, wq, wk, wv, wo, slot_col, normed, q, k, v, mixed, lse, hidden, dx, y)


def combine(slot_col, hidden, gate, y):
    return call(output_kernel, [shape(hidden.shape, BF16)], [VMEM] * 4, [], "combine")(slot_col, hidden, gate, y)[0]


def local(
    inputs,
    cotangent,
    seq_group,
    domain_counts,
    sort_order,
    send_counts,
    gain_one,
    shift_one,
    gain_two,
    shift_two,
    w_query,
    w_key,
    w_value,
    w_out,
    router,
    expert_in,
    expert_out,
):
    tokens, width = inputs.shape
    experts = send_counts.shape[1]
    capacity = 2 * tokens // experts
    slots = experts * capacity
    inverse = 1.0 / domain_counts.astype(F32)
    domain_weights = inverse / jnp.mean(inverse)
    ids = jnp.arange(domain_counts.shape[0], dtype=jnp.int32)
    weight = jnp.sum(jnp.where(seq_group[:, None] == ids[None, :], domain_weights[None, :], 0.0), axis=1).reshape(1, 1)
    mine = lax.axis_index("expert")
    router_row = lax.dynamic_slice_in_dim(router.T, mine, 1, axis=0).astype(F32)

    count = lax.axis_size("expert")
    g1, s1, g2, s2 = (v.reshape(1, width) for v in (gain_one, shift_one, gain_two, shift_two))
    cot_send, slot_col, slot_row = tables(experts, capacity, send_counts, weight, sort_order, cotangent)
    normed, q, k, v, mixed, lse, hidden, gate, send, cot_rows = forward(
        count, capacity, slots, inputs, g1, s1, g2, s2, w_query, w_key, w_value, w_out, router, slot_col, slot_row, cot_send
    )
    y_rows, dx_back, grad_first, grad_second = expert_block(
        count, capacity, send, cot_rows, router_row, expert_in[0], expert_out[0]
    )
    expert_sums = (lax.psum(grad_first, "dp").astype(F32), lax.psum(grad_second, "dp").astype(F32))
    grad_inputs, dense, y_back = backward(
        count, capacity, weight, inputs, cotangent, g1, g2, w_query, w_key, w_value, w_out, slot_col,
        normed, q, k, v, mixed, lse, hidden, dx_back, y_rows,
    )
    output = combine(slot_col, hidden, gate, y_back)
    dense = lax.psum(dense, ("dp", "expert")).astype(F32)
    parts = [dense[i * width : (i + 1) * width] for i in range(4)]
    vecs = [dense[4 * width + i] for i in range(4)]
    return (
        output,
        grad_inputs,
        *vecs,
        *parts,
        expert_sums[0][None],
        expert_sums[1][None],
    )


def solution(mesh):
    rows = P(("dp", "expert"), None)
    split = P("expert", None, None)
    return jax.shard_map(
        local,
        mesh=mesh,
        in_specs=(rows, rows, P(("dp", "expert")), P(), rows, rows) + (P(),) * 9 + (split, split),
        out_specs=(rows, rows) + (P(),) * 8 + (split, split),
        check_vma=False,
    )
```

```python
import functools

import jax
import jax.numpy as jnp
from jax import lax
from jax.experimental import pallas as pl
from jax.experimental.pallas import tpu as pltpu
from jax.sharding import PartitionSpec as P

HEADS = 12
HEAD_DIM = 64
LEN = 1024
EPS = 1e-05
F32 = jnp.float32
BF16 = jnp.bfloat16
BLK = 256
LIMIT = 60 * 1024 * 1024

VMEM = pl.BlockSpec(memory_space=pltpu.VMEM)
SMEM = pl.BlockSpec(memory_space=pltpu.SMEM)
ANY = pl.BlockSpec(memory_space=pl.ANY)
MESH = pl.DeviceIdType.MESH


def dot(left, right, contract):
    return lax.dot_general(left, right, ((contract[0:1], contract[1:2]), ((), ())), preferred_element_type=F32)


def nn(left, right):
    return dot(left, right, (1, 0))


def nt(left, right):
    return dot(left, right, (1, 1))


def tn(left, right):
    return dot(left, right, (0, 0))


def iota(shape, axis):
    return lax.broadcasted_iota(jnp.int32, shape, axis)


def flip(index, mask, count):
    bit, out = 1, 0
    while bit < count:
        out = out + ((index // bit + mask // bit) % 2) * bit
        bit *= 2
    return out


def greet(axis, me, count):
    barrier = pltpu.get_barrier_semaphore()
    for mask in range(1, count):
        pl.semaphore_signal(barrier, inc=1, device_id={axis: flip(me, mask, count)}, device_id_type=MESH)
    pl.semaphore_wait(barrier, count - 1)


def send_block(me, count, capacity, mask, source, target, sends, recvs):
    peer = flip(me, mask, count)
    return pltpu.make_async_remote_copy(
        src_ref=source.at[pl.ds(pl.multiple_of(peer * capacity, capacity), capacity)],
        dst_ref=target.at[pl.ds(pl.multiple_of(mask * capacity, capacity), capacity)],
        send_sem=sends.at[mask],
        recv_sem=recvs.at[mask],
        device_id={"expert": peer},
        device_id_type=MESH,
    )


def return_block(me, count, capacity, mask, source, target, sends, recvs, shift=0):
    return pltpu.make_async_remote_copy(
        src_ref=source.at[pl.ds(pl.multiple_of((mask - shift) * capacity, capacity), capacity)],
        dst_ref=target.at[pl.ds(pl.multiple_of(me * capacity, capacity), capacity)],
        send_sem=sends.at[mask],
        recv_sem=recvs.at[mask],
        device_id={"expert": flip(me, mask, count)},
        device_id_type=MESH,
    )


def norm_stats(rows):
    center = rows - jnp.mean(rows, axis=-1, keepdims=True)
    rstd = lax.rsqrt(jnp.mean(center * center, axis=-1, keepdims=True) + EPS)
    return center * rstd, rstd


def pack_rows(slot_row, rows_ref, send_ref):
    slots = send_ref.shape[0]
    tokens = rows_ref.shape[0]

    def step(block, carry):
        base = pl.multiple_of(block * BLK, BLK)
        slot = iota((BLK, tokens), 0) + base
        pick = jnp.where(slot == slot_row, 1.0, 0.0).astype(BF16)
        send_ref[pl.ds(base, BLK), :] = nn(pick, rows_ref[...]).astype(BF16)
        return carry

    lax.fori_loop(0, slots // BLK, step, 0)


def table_kernel(experts, capacity, counts_ref, weight_ref, sort_ref, cot_ref, send_ref, slot_col_ref, slot_row_ref, scaled):
    tokens = cot_ref.shape[0]
    place = iota((1, tokens), 1)
    expert_at = jnp.zeros((1, tokens), jnp.int32)
    start_at = jnp.zeros((1, tokens), jnp.int32)
    end = jnp.int32(0)
    for expert in range(experts):
        count = counts_ref[0, expert]
        end = end + count
        past = place >= end
        expert_at = expert_at + jnp.where(past, 1, 0)
        start_at = start_at + jnp.where(past, count, 0)
    dest = (expert_at * capacity + place - start_at).astype(F32)
    sort_row = sort_ref[...]
    scaled[...] = (cot_ref[...].astype(F32) * weight_ref[0, 0]).astype(BF16)
    for block in range(tokens // BLK):
        token = iota((BLK, tokens), 0) + block * BLK
        col = jnp.sum(jnp.where(token == sort_row, dest, 0.0), axis=1, keepdims=True)
        wide = jnp.broadcast_to(col, (BLK, 128))
        slot_col_ref[pl.ds(block * BLK, BLK), :] = wide.astype(jnp.int32)
        slot_row_ref[:, pl.ds(block * BLK, BLK)] = wide.T[0:8].astype(jnp.int32)
    pack_rows(slot_row_ref[0:1, :], scaled, send_ref)


def forward_kernel(
    count,
    capacity,
    x_ref,
    gain_one_ref,
    shift_one_ref,
    gain_two_ref,
    shift_two_ref,
    wq_ref,
    wk_ref,
    wv_ref,
    wo_ref,
    router_ref,
    slot_col_ref,
    slot_row_ref,
    cot_send_ref,
    normed_ref,
    q_ref,
    k_ref,
    v_ref,
    mixed_ref,
    lse_ref,
    hidden_ref,
    gate_ref,
    send_ref,
    cot_rows_ref,
    routed,
    sends,
    recvs,
    own,
):
    tokens, width = x_ref.shape
    blocks = tokens // BLK
    me = lax.axis_index("expert")
    greet("expert", me, count)
    copies = [send_block(me, count, capacity, mask, cot_send_ref, cot_rows_ref, sends, recvs) for mask in range(1, count)]
    for copy in reversed(copies):
        copy.start()
    mine = pltpu.make_async_copy(
        cot_send_ref.at[pl.ds(pl.multiple_of(me * capacity, capacity), capacity)], cot_rows_ref.at[pl.ds(0, capacity)], own
    )
    mine.start()
    lane = iota((1, 128), 1)

    def project(block, carry):
        rows = pl.ds(pl.multiple_of(block * BLK, BLK), BLK)
        hat, _ = norm_stats(x_ref[rows, :].astype(F32))
        normed = (hat * gain_one_ref[...] + shift_one_ref[...]).astype(BF16)
        normed_ref[rows, :] = normed
        q_ref[rows, :] = (nn(normed, wq_ref[...]).astype(BF16) * (HEAD_DIM ** (-0.5))).astype(BF16)
        k_ref[rows, :] = nn(normed, wk_ref[...]).astype(BF16)
        v_ref[rows, :] = nn(normed, wv_ref[...]).astype(BF16)
        return carry

    lax.fori_loop(0, blocks, project, 0)

    keep = iota((BLK, BLK), 0) <= iota((BLK, BLK), 1)

    def attend(pair, carry):
        cols = pl.ds(pl.multiple_of(pair * 128, 128), 128)
        k_pair = k_ref[:, cols]
        v_t = v_ref[:, cols].astype(F32).T.astype(BF16)
        k_head = [jnp.where(lane < 64, k_pair, 0), jnp.where(lane >= 64, k_pair, 0)]
        for block in range(blocks):
            span = (block + 1) * BLK
            query = q_ref[pl.ds(block * BLK, BLK), cols]
            outs = []
            for half in range(2):
                scores = nt(k_head[half][:span], query)
                diag = jnp.where(keep, scores[block * BLK :], -1000000000.0)
                scores = jnp.concatenate([scores[: block * BLK], diag], axis=0) if block else diag
                peak = jnp.max(scores, axis=0, keepdims=True)
                exps = jnp.exp(scores - peak)
                total = jnp.sum(exps, axis=0, keepdims=True)
                out = nn(v_t[half * 64 : half * 64 + 64, :span], exps.astype(BF16))
                outs.append(out * (1.0 / total))
                lse_ref[pair, half : half + 1, pl.ds(block * BLK, BLK)] = peak + jnp.log(total)
            mixed_ref[pl.ds(block * BLK, BLK), cols] = jnp.concatenate(outs, axis=0).T.astype(BF16)
        return carry

    lax.fori_loop(0, HEADS // 2, attend, 0)

    experts = router_ref.shape[1]

    def finish(block, carry):
        rows = pl.ds(pl.multiple_of(block * BLK, BLK), BLK)
        hidden = x_ref[rows, :].astype(F32) + nn(mixed_ref[rows, :], wo_ref[...])
        hidden_ref[rows, :] = hidden
        hat, _ = norm_stats(hidden)
        low = (hat * gain_two_ref[...] + shift_two_ref[...]).astype(BF16)
        routed[rows, :] = low
        logits = nn(low, router_ref[...])
        slot = slot_col_ref[rows, 0:1]
        first = iota((BLK, experts), 1) * capacity
        mine = (slot >= first) & (slot < first + capacity)
        logit = jnp.sum(jnp.where(mine, logits, 0.0), axis=1, keepdims=True)
        gate_ref[rows, :] = jnp.broadcast_to(jax.nn.sigmoid(logit), (BLK, 128))
        return carry

    lax.fori_loop(0, blocks, finish, 0)
    pack_rows(slot_row_ref[0:1, :], routed, send_ref)
    mine.wait()
    for copy in copies:
        copy.wait()


def gelu_parts(v):
    size = jnp.abs(v)
    t = 1.0 / (1.0 + (0.3275911 * 0.7071067811865476) * size)
    bell = jnp.exp(-0.5 * (v * v))
    poly = ((((1.061405429 * t - 1.453152027) * t + 1.421413741) * t - 0.284496736) * t + 0.254829592) * t
    tail = 0.5 * poly * bell
    return jnp.where(v >= 0.0, 1.0 - tail, tail), bell * 0.3989422804014327


def expert_kernel(
    count,
    capacity,
    chunk,
    send_ref,
    g_ref,
    router_ref,
    w1_hbm,
    w2_hbm,
    y_ref,
    back_ref,
    late_ref,
    gw1_ref,
    gw2_ref,
    w1_ref,
    w2_ref,
    acc1,
    acc2,
    x_rows,
    dx_rows,
    y_rows,
    stage,
    load_sems,
    sends,
    recvs,
    back_sends,
    back_recvs,
    own,
    y_sems,
    stage_sems,
):
    width, hidden = w1_ref.shape
    slots = x_rows.shape[0]
    group = BLK // capacity
    early = count - count // 4
    me = lax.axis_index("expert")
    loads = [pltpu.make_async_copy(w1_hbm, w1_ref, load_sems.at[0]), pltpu.make_async_copy(w2_hbm, w2_ref, load_sems.at[1])]
    for load in loads:
        load.start()
    greet("expert", me, count)
    mine_in = pltpu.make_async_copy(
        send_ref.at[pl.ds(pl.multiple_of(me * capacity, capacity), capacity)], x_rows.at[pl.ds(0, capacity)], own.at[0]
    )
    mine_in.start()
    for mask in range(1, count):
        send_block(me, count, capacity, mask, send_ref, x_rows, sends, recvs).start()
    acc1[...] = jnp.zeros_like(acc1)
    acc2[...] = jnp.zeros_like(acc2)
    for load in loads:
        load.wait()
    mine_in.wait()
    router = router_ref[...]

    def store_y(block):
        rows = pl.ds(pl.multiple_of(block * BLK, BLK), BLK)
        return pltpu.make_async_copy(y_rows.at[rows], y_ref.at[rows], y_sems.at[block])

    def mine_out():
        return pltpu.make_async_copy(
            dx_rows.at[pl.ds(0, capacity)], back_ref.at[pl.ds(pl.multiple_of(me * capacity, capacity), capacity)], own.at[1]
        )

    def run(block, carry):
        for item in range(group):
            mask = block * group + item

            @pl.when(mask > 0)
            def _():
                send_block(me, count, capacity, mask, send_ref, x_rows, sends, recvs).wait_recv()

        rows = pl.ds(pl.multiple_of(block * BLK, BLK), BLK)
        x = x_rows[rows, :]
        logit = jnp.sum(x.astype(F32) * router, axis=1, keepdims=True)
        gate = jax.nn.sigmoid(logit)
        go = g_ref[rows, :].astype(F32)
        g = (gate * go).astype(BF16)
        x_t = x.astype(F32).T.astype(BF16)
        y = jnp.zeros(x.shape, F32)
        dx = jnp.zeros(x.shape, F32)
        for first in range(0, hidden, chunk):
            cols = pl.ds(first, chunk)
            w1 = w1_ref[:, cols]
            w2 = w2_ref[cols, :]
            pre = nn(x, w1)
            cdf, pdf = gelu_parts(pre)
            act = (pre * cdf).astype(BF16)
            slope = cdf + pre * pdf
            y = y + nn(act, w2)
            grad = (nt(g, w2) * slope).astype(BF16)
            dx = dx + nt(grad, w1)
            acc1[:, cols] += nn(x_t, grad)
            acc2[cols, :] += tn(act, g)
        y_low = y.astype(BF16)
        y_rows[rows, :] = y_low
        dlogit = jnp.sum(y_low.astype(F32) * go, axis=1, keepdims=True) * gate * (1.0 - gate)
        dx_rows[rows, :] = (dx + dlogit * router).astype(BF16)
        store_y(block).start()
        for item in range(group):
            mask = block * group + item

            @pl.when((mask > 0) & (mask < early))
            def _():
                return_block(me, count, capacity, mask, dx_rows, back_ref, back_sends, back_recvs).start()

            @pl.when(mask == 0)
            def _():
                mine_out().start()

        return carry

    lax.fori_loop(0, slots // BLK, run, 0)

    pieces = []
    for first in range(0, hidden, stage.shape[1]):
        pieces.append((acc1.at[:, pl.ds(first, stage.shape[1])], gw1_ref.at[:, pl.ds(first, stage.shape[1])]))
    for first in range(0, hidden, stage.shape[1]):
        pieces.append((acc2.at[pl.ds(first, stage.shape[1]), :], gw2_ref.at[pl.ds(first, stage.shape[1]), :]))
    writes = []
    for index, (piece, target) in enumerate(pieces):
        slot = index % 2
        if index >= 2:
            writes[index - 2].wait()
        stage[slot] = piece[...].astype(BF16)
        write = pltpu.make_async_copy(stage.at[slot], target, stage_sems.at[slot])
        write.start()
        writes.append(write)
    for write in writes[-2:]:
        write.wait()
    mine_out().wait()
    tail = pltpu.make_async_copy(dx_rows.at[pl.ds(early * capacity, (count - early) * capacity)], late_ref, own.at[0])
    tail.start()

    def settle(block, carry):
        store_y(block).wait()
        return carry

    lax.fori_loop(0, slots // BLK, settle, 0)
    tail.wait()
    for mask in range(1, count):
        send_block(me, count, capacity, mask, send_ref, x_rows, sends, recvs).wait_send()
    for mask in range(1, early):
        return_block(me, count, capacity, mask, dx_rows, back_ref, back_sends, back_recvs).wait()


def backward_kernel(
    count,
    capacity,
    weight_ref,
    x_ref,
    cot_ref,
    gain_one_ref,
    gain_two_ref,
    wq_ref,
    wk_ref,
    wv_ref,
    wo_ref,
    slot_col_ref,
    normed_ref,
    q_ref,
    k_ref,
    v_ref,
    mixed_ref,
    lse_ref,
    hidden_ref,
    dx_hbm,
    late_ref,
    y_ref,
    grad_ref,
    dense_ref,
    vec_ref,
    y_back_ref,
    dx_ref,
    ghid,
    gmix,
    branch,
    normed_t,
    dqkv,
    sums,
    sends,
    recvs,
    late_sends,
    late_recvs,
    own,
    gets,
):
    tokens, width = x_ref.shape
    me = lax.axis_index("expert")
    early = count - count // 4
    greet("expert", me, count)
    lates = [return_block(me, count, capacity, mask, late_ref, dx_ref, late_sends, late_recvs, early) for mask in range(early, count)]
    for copy in lates:
        copy.start()
    copies = [return_block(me, count, capacity, mask, y_ref, y_back_ref, sends, recvs) for mask in range(1, early)]
    for copy in reversed(copies):
        copy.start()
    mine = pltpu.make_async_copy(
        y_ref.at[pl.ds(0, capacity)], y_back_ref.at[pl.ds(pl.multiple_of(me * capacity, capacity), capacity)], own
    )
    mine.start()
    loads = []
    for mask in range(early):
        part = pl.ds(pl.multiple_of(flip(me, mask, count) * capacity, capacity), capacity)
        loads.append(pltpu.make_async_copy(dx_hbm.at[part], dx_ref.at[part], gets.at[mask]))
        loads[-1].start()
    for load in loads:
        load.wait()
    for copy in lates:
        copy.wait()
    slots = dx_ref.shape[0]
    blocks = tokens // BLK
    lane = iota((1, 128), 1)
    sums[...] = jnp.zeros_like(sums)

    def open_block(block, carry):
        rows = pl.ds(pl.multiple_of(block * BLK, BLK), BLK)
        slot = slot_col_ref[rows, 0:1]
        pick = jnp.where(iota((BLK, slots), 1) == slot, 1.0, 0.0).astype(BF16)
        grad = nn(pick, dx_ref[...])
        hat, rstd = norm_stats(hidden_ref[rows, :])
        sums[2:3, :] += jnp.sum(grad * hat, axis=0, keepdims=True)
        sums[3:4, :] += jnp.sum(grad, axis=0, keepdims=True)
        gg = grad * gain_two_ref[...]
        inner = gg - jnp.mean(gg, axis=1, keepdims=True) - hat * jnp.mean(gg * hat, axis=1, keepdims=True)
        total = cot_ref[rows, :].astype(F32) * weight_ref[0, 0] + rstd * inner
        ghid[rows, :] = total
        low = total.astype(BF16)
        branch[rows, :] = low
        gmix[rows, :] = nt(low, wo_ref[...]).astype(BF16)
        normed_t[:, rows] = normed_ref[rows, :].astype(F32).T.astype(BF16)
        return carry

    lax.fori_loop(0, blocks, open_block, 0)
    dense_ref[pl.ds(3 * width, width), :] = tn(mixed_ref[...], branch[...]).astype(BF16)

    keep = iota((BLK, BLK), 0) <= iota((BLK, BLK), 1)

    def attend(pair, carry):
        base = pl.multiple_of(pair * 128, 128)
        cols = pl.ds(base, 128)
        q_pair = q_ref[:, cols]
        k_pair = k_ref[:, cols]
        v_pair = v_ref[:, cols]
        o_pair = gmix[:, cols]
        low = lane < 64
        q_head = [jnp.where(low, q_pair, 0), jnp.where(low, 0, q_pair)]
        k_head = [jnp.where(low, k_pair, 0), jnp.where(low, 0, k_pair)]
        v_head = [jnp.where(low, v_pair, 0), jnp.where(low, 0, v_pair)]
        o_head = [jnp.where(low, o_pair, 0), jnp.where(low, 0, o_pair)]
        k_t = k_pair.astype(F32).T.astype(BF16)
        prod_t = (o_pair.astype(F32) * mixed_ref[:, cols].astype(F32)).T
        delta = [jnp.sum(prod_t[:64], axis=0, keepdims=True), jnp.sum(prod_t[64:], axis=0, keepdims=True)]
        dq_t = [[None] * blocks, [None] * blocks]
        for block in range(blocks):
            start = block * BLK
            dk = None
            dv = None
            for half in range(2):
                scores = nt(k_head[half][start : start + BLK], q_pair[start:])
                diag = jnp.where(keep, scores[:, :BLK], -1000000000.0)
                scores = jnp.concatenate([diag, scores[:, BLK:]], axis=1) if block < blocks - 1 else diag
                probs = jnp.exp(scores - lse_ref[pair, half : half + 1, pl.ds(start, tokens - start)])
                grad_p = nt(v_head[half][start : start + BLK], o_pair[start:])
                grad_s = (probs * (grad_p - delta[half][:, start:])).astype(BF16)
                dv_part = nn(probs.astype(BF16), o_head[half][start:])
                dk_part = nn(grad_s, q_head[half][start:])
                dv = dv_part if dv is None else dv + dv_part
                dk = dk_part if dk is None else dk + dk_part
                dq_part = nn(k_t[half * 64 : half * 64 + 64, start : start + BLK], grad_s)
                for later in range(block, blocks):
                    piece = dq_part[:, (later - block) * BLK : (later - block + 1) * BLK]
                    dq_t[half][later] = piece if dq_t[half][later] is None else dq_t[half][later] + piece
            rows = pl.ds(start, BLK)
            dqkv[rows, pl.ds(pl.multiple_of(base + width, 128), 128)] = dk.astype(BF16)
            dqkv[rows, pl.ds(pl.multiple_of(base + 2 * width, 128), 128)] = dv.astype(BF16)
        for block in range(blocks):
            both = jnp.concatenate([dq_t[0][block], dq_t[1][block]], axis=0) * (HEAD_DIM ** (-0.5))
            dqkv[pl.ds(block * BLK, BLK), cols] = both.T.astype(BF16)
        return carry

    lax.fori_loop(0, HEADS // 2, attend, 0)

    for part in range(3):
        dense_ref[pl.ds(part * width, width), :] = nn(normed_t[...], dqkv[:, pl.ds(part * width, width)]).astype(BF16)

    def close_block(block, carry):
        rows = pl.ds(pl.multiple_of(block * BLK, BLK), BLK)
        grad = nt(dqkv[rows, 0:width], wq_ref[...])
        grad = grad + nt(dqkv[rows, width : 2 * width], wk_ref[...])
        grad = grad + nt(dqkv[rows, 2 * width : 3 * width], wv_ref[...])
        hat, rstd = norm_stats(x_ref[rows, :].astype(F32))
        sums[0:1, :] += jnp.sum(grad * hat, axis=0, keepdims=True)
        sums[1:2, :] += jnp.sum(grad, axis=0, keepdims=True)
        gg = grad * gain_one_ref[...]
        inner = gg - jnp.mean(gg, axis=1, keepdims=True) - hat * jnp.mean(gg * hat, axis=1, keepdims=True)
        grad_ref[rows, :] = (ghid[rows, :] + rstd * inner).astype(BF16)
        return carry

    lax.fori_loop(0, blocks, close_block, 0)
    vec_ref[...] = sums[...]
    mine.wait()
    for copy in copies:
        copy.wait()


def bits_of(count):
    return [1 << bit for bit in range(count.bit_length() - 1)]


def halving_plan(dp, count, rows):
    experts = [("expert", mask) for mask in bits_of(count)]
    groups = [("dp", mask) for mask in bits_of(dp)]
    plans = [experts[:1] + groups + experts[1:], experts[:1] + experts[1:] + groups]
    halvings = 0
    while halvings < len(plans[0]) and (rows >> halvings) % 32 == 0:
        halvings += 1
    return plans, halvings


def finish_kernel(
    dp,
    count,
    capacity,
    dense_ref,
    vec_ref,
    slot_col_ref,
    hidden_ref,
    gate_ref,
    y_hbm,
    y_ref,
    out_ref,
    full_ref,
    total_ref,
    y_all,
    acc,
    landing,
    full,
    vec_acc,
    vec_land,
    sends,
    recvs,
    back_sends,
    back_recvs,
    vec_sends,
    vec_recvs,
    y_sends,
    y_recvs,
    gets,
    put,
):
    tokens, width = hidden_ref.shape
    slots = y_all.shape[0]
    rows = dense_ref.shape[0] // 2
    early = count - count // 4
    place = {"dp": lax.axis_index("dp"), "expert": lax.axis_index("expert")}
    size = {"dp": dp, "expert": count}
    me = place["expert"]
    plans, halvings = halving_plan(dp, count, rows)
    steps = len(plans[0])

    barrier = pltpu.get_barrier_semaphore()
    for mask in range(1, count):
        pl.semaphore_signal(barrier, inc=1, device_id={"expert": flip(me, mask, count)}, device_id_type=MESH)
    for mask in bits_of(dp):
        pl.semaphore_signal(barrier, inc=1, device_id={"dp": flip(place["dp"], mask, dp)}, device_id_type=MESH)
    pl.semaphore_wait(barrier, count - 1 + len(bits_of(dp)))

    def partner(axis, mask):
        return {axis: flip(place[axis], mask, size[axis])}

    def bit(axis, mask):
        return (place[axis] // mask) % 2

    def aligned(start):
        return pl.multiple_of(start, 16)

    def remote(source, target, send, recv, device):
        return pltpu.make_async_remote_copy(
            src_ref=source, dst_ref=target, send_sem=send, recv_sem=recv, device_id=device, device_id_type=MESH
        )

    low = [jnp.int32(stream * rows) for stream in range(2)]
    extent = rows
    offset = 0
    trail = []
    pending = []
    y_copies = [return_block(me, count, capacity, mask, y_ref, y_all, y_sends, y_recvs) for mask in range(early, count)]
    loads = []
    for step in range(steps):
        halve = step < halvings
        part = extent // 2 if halve else extent
        copies = []
        for stream in range(2):
            axis, mask = plans[stream][step]
            mine = low[stream] + bit(axis, mask) * part if halve else low[stream]
            other = low[stream] + (1 - bit(axis, mask)) * part if halve else low[stream]
            source = dense_ref if step == 0 else acc.at[(step - 1) % 2]
            land = landing.at[stream, pl.ds(offset, part)]
            copy = remote(
                source.at[pl.ds(aligned(other), part)], land, sends.at[stream, step], recvs.at[stream, step], partner(axis, mask)
            )
            copy.start()
            copies.append((copy, mine, source))
        axis, mask = plans[0][step]
        vec_source = vec_ref if step == 0 else vec_acc.at[step - 1]
        vec_copy = remote(vec_source, vec_land.at[step], vec_sends.at[step], vec_recvs.at[step], partner(axis, mask))
        vec_copy.start()
        if step == 0:
            for copy in y_copies:
                copy.start()
            for mask in range(early):
                span = pl.ds(pl.multiple_of(flip(me, mask, count) * capacity, capacity), capacity)
                loads.append(pltpu.make_async_copy(y_hbm.at[span], y_all.at[span], gets.at[mask]))
                loads[-1].start()
        trail.append((list(low), extent, halve))
        for stream in range(2):
            copy, mine, source = copies[stream]
            copy.wait()
            span = pl.ds(aligned(mine), part)
            kept = source[span, :].astype(F32) + landing[stream, pl.ds(offset, part), :].astype(F32)
            if step < steps - 1:
                acc[step % 2, span, :] = kept.astype(BF16)
            else:
                full[span, :] = kept.astype(BF16)
            low[stream] = mine
        vec_copy.wait()
        vec_sum = vec_source[...] + vec_land[step]
        if step < steps - 1:
            vec_acc[step] = vec_sum
        else:
            total_ref[...] = vec_sum
        extent = part
        offset += part

    for load in loads:
        load.wait()

    back = []
    for step in reversed(range(halvings)):
        starts, whole, _ = trail[step]
        copies = []
        for stream in range(2):
            axis, mask = plans[stream][step]
            span = pl.ds(aligned(low[stream]), extent)
            copy = remote(
                full.at[span], full.at[span], back_sends.at[stream, step], back_recvs.at[stream, step], partner(axis, mask)
            )
            copy.start()
            copies.append(copy)
        for stream in range(2):
            copies[stream].wait()
            low[stream] = starts[stream]
        extent = whole
        if step == halvings - 1:
            for copy in y_copies:
                copy.wait()

            def combine(block, carry):
                span = pl.ds(pl.multiple_of(block * BLK, BLK), BLK)
                slot = slot_col_ref[span, 0:1]
                pick = jnp.where(iota((BLK, slots), 1) == slot, 1.0, 0.0).astype(BF16)
                returned = nn(pick, y_all[...])
                out_ref[span, :] = (hidden_ref[span, :] + gate_ref[span, 0:1] * returned).astype(BF16)
                return carry

    lax.fori_loop(0, tokens // BLK, combine, 0)
    write = pltpu.make_async_copy(full, full_ref, put)
    write.start()
    write.wait()


def call(kernel, outs, in_specs, scratch, name, out_specs=None, collective=None, flops=10**9):
    remote = {} if collective is None else {"collective_id": collective, "has_side_effects": True}
    return pl.pallas_call(
        kernel,
        out_shape=outs,
        in_specs=in_specs,
        out_specs=out_specs or [VMEM] * len(outs),
        scratch_shapes=scratch,
        compiler_params=pltpu.CompilerParams(vmem_limit_bytes=LIMIT, **remote),
        cost_estimate=pl.CostEstimate(flops=flops, bytes_accessed=10**7, transcendentals=0),
        name=name,
    )


def dma(*dims):
    return pltpu.SemaphoreType.DMA(dims)


def shape(dims, kind):
    return jax.ShapeDtypeStruct(dims, kind)


def tables(experts, capacity, counts, weight, sort_order, cotangent):
    tokens, width = cotangent.shape
    slots = experts * capacity
    return call(
        functools.partial(table_kernel, experts, capacity),
        [shape((slots, width), BF16), shape((tokens, 128), jnp.int32), shape((8, tokens), jnp.int32)],
        [SMEM, SMEM, VMEM, VMEM],
        [pltpu.VMEM((tokens, width), BF16)],
        "tables",
    )(counts, weight, sort_order, cotangent)


def forward(count, capacity, slots, inputs, g1, s1, g2, s2, wq, wk, wv, wo, router, slot_col, slot_row, cot_send):
    tokens, width = inputs.shape
    rows_low = shape((tokens, width), BF16)
    return call(
        functools.partial(forward_kernel, count, capacity),
        [
            rows_low,
            rows_low,
            rows_low,
            rows_low,
            rows_low,
            shape((HEADS // 2, 8, tokens), F32),
            shape((tokens, width), F32),
            shape((tokens, 128), F32),
            shape((slots, width), BF16),
            shape((slots, width), BF16),
        ],
        [VMEM] * 12 + [ANY],
        [pltpu.VMEM((tokens, width), BF16), dma(count), dma(count), dma()],
        "dense_forward",
        [VMEM] * 9 + [ANY],
        1,
    )(inputs, g1, s1, g2, s2, wq, wk, wv, wo, router, slot_col, slot_row, cot_send)


def expert_block(count, capacity, send, g, router_row, w1, w2, chunk=768):
    slots, width = send.shape
    hidden = w1.shape[1]
    rows = shape((slots, width), BF16)
    keep = pltpu.VMEM((slots, width), BF16)
    return call(
        functools.partial(expert_kernel, count, capacity, chunk),
        [rows, rows, shape((slots // 4, width), BF16), shape((width, hidden), BF16), shape((hidden, width), BF16)],
        [ANY, VMEM, VMEM, ANY, ANY],
        [
            pltpu.VMEM((width, hidden), BF16),
            pltpu.VMEM((hidden, width), BF16),
            pltpu.VMEM((width, hidden), F32),
            pltpu.VMEM((hidden, width), F32),
            keep,
            keep,
            keep,
            pltpu.VMEM((2, width, width), BF16),
            dma(2),
            dma(count),
            dma(count),
            dma(count),
            dma(count),
            dma(2),
            dma(slots // BLK),
            dma(2),
        ],
        "expert",
        [ANY] * 5,
        2,
    )(send, g, router_row, w1, w2)


def backward(
    count, capacity, weight, inputs, cotangent, g1, g2, wq, wk, wv, wo, slot_col, normed, q, k, v, mixed, lse, hidden, dx, late, y
):
    tokens, width = inputs.shape
    return call(
        functools.partial(backward_kernel, count, capacity),
        [shape((tokens, width), BF16), shape((4 * width, width), BF16), shape((8, width), F32), shape(y.shape, BF16)],
        [SMEM] + [VMEM] * 16 + [ANY] * 3,
        [
            pltpu.VMEM(dx.shape, BF16),
            pltpu.VMEM((tokens, width), F32),
            pltpu.VMEM((tokens, width), BF16),
            pltpu.VMEM((tokens, width), BF16),
            pltpu.VMEM((width, tokens), BF16),
            pltpu.VMEM((tokens, 3 * width), BF16),
            pltpu.VMEM((8, width), F32),
            dma(count),
            dma(count),
            dma(count),
            dma(count),
            dma(),
            dma(count),
        ],
        "dense_backward",
        [VMEM, VMEM, VMEM, ANY],
        3,
        5 * 10**10,
    )(weight, inputs, cotangent, g1, g2, wq, wk, wv, wo, slot_col, normed, q, k, v, mixed, lse, hidden, dx, late, y)


def finish(dp, count, capacity, dense, vec, slot_col, hidden, gate, y_back, y):
    tokens, width = hidden.shape
    rows = dense.shape[0]
    steps = len(bits_of(dp)) + len(bits_of(count))
    return call(
        functools.partial(finish_kernel, dp, count, capacity),
        [shape(hidden.shape, BF16), shape(dense.shape, BF16), shape(vec.shape, F32)],
        [VMEM] * 5 + [ANY] * 2,
        [
            pltpu.VMEM(y.shape, BF16),
            pltpu.VMEM((2, rows, width), BF16),
            pltpu.VMEM((2, rows, width), BF16),
            pltpu.VMEM((rows, width), BF16),
            pltpu.VMEM((steps,) + vec.shape, F32),
            pltpu.VMEM((steps,) + vec.shape, F32),
            dma(2, steps),
            dma(2, steps),
            dma(2, steps),
            dma(2, steps),
            dma(steps),
            dma(steps),
            dma(count),
            dma(count),
            dma(count),
            dma(),
        ],
        "finish",
        [VMEM, ANY, VMEM],
        4,
    )(dense, vec, slot_col, hidden, gate, y_back, y)


def local(
    inputs,
    cotangent,
    seq_group,
    domain_counts,
    sort_order,
    send_counts,
    gain_one,
    shift_one,
    gain_two,
    shift_two,
    w_query,
    w_key,
    w_value,
    w_out,
    router,
    expert_in,
    expert_out,
):
    tokens, width = inputs.shape
    experts = send_counts.shape[1]
    capacity = 2 * tokens // experts
    slots = experts * capacity
    inverse = 1.0 / domain_counts.astype(F32)
    domain_weights = inverse / jnp.mean(inverse)
    ids = jnp.arange(domain_counts.shape[0], dtype=jnp.int32)
    weight = jnp.sum(jnp.where(seq_group[:, None] == ids[None, :], domain_weights[None, :], 0.0), axis=1).reshape(1, 1)
    mine = lax.axis_index("expert")
    router_row = lax.dynamic_slice_in_dim(router.T, mine, 1, axis=0).astype(F32)

    count = lax.axis_size("expert")
    g1, s1, g2, s2 = (v.reshape(1, width) for v in (gain_one, shift_one, gain_two, shift_two))
    cot_send, slot_col, slot_row = tables(experts, capacity, send_counts, weight, sort_order, cotangent)
    normed, q, k, v, mixed, lse, hidden, gate, send, cot_rows = forward(
        count, capacity, slots, inputs, g1, s1, g2, s2, w_query, w_key, w_value, w_out, router, slot_col, slot_row, cot_send
    )
    y_rows, dx_back, dx_late, grad_first, grad_second = expert_block(
        count, capacity, send, cot_rows, router_row, expert_in[0], expert_out[0]
    )
    expert_sums = (lax.psum(grad_first, "dp").astype(F32), lax.psum(grad_second, "dp").astype(F32))
    grad_inputs, dense, vec, y_back = backward(
        count, capacity, weight, inputs, cotangent, g1, g2, w_query, w_key, w_value, w_out, slot_col,
        normed, q, k, v, mixed, lse, hidden, dx_back, dx_late, y_rows,
    )
    output, dense, vec = finish(lax.axis_size("dp"), count, capacity, dense, vec, slot_col, hidden, gate, y_back, y_rows)
    dense = dense.astype(F32)
    parts = [dense[i * width : (i + 1) * width] for i in range(4)]
    vecs = [vec[i] for i in range(4)]
    return (
        output,
        grad_inputs,
        *vecs,
        *parts,
        expert_sums[0][None],
        expert_sums[1][None],
    )


def solution(mesh):
    rows = P(("dp", "expert"), None)
    split = P("expert", None, None)
    return jax.shard_map(
        local,
        mesh=mesh,
        in_specs=(rows, rows, P(("dp", "expert")), P(), rows, rows) + (P(),) * 9 + (split, split),
        out_specs=(rows, rows) + (P(),) * 8 + (split, split),
        check_vma=False,
    )
```

```python
import functools

import jax
import jax.numpy as jnp
from jax import lax
from jax.experimental import pallas as pl
from jax.experimental.pallas import tpu as pltpu
from jax.sharding import PartitionSpec as P

HEADS = 12
HEAD_DIM = 64
LEN = 1024
EPS = 1e-05
F32 = jnp.float32
BF16 = jnp.bfloat16
BLK = 256
LIMIT = 60 * 1024 * 1024

VMEM = pl.BlockSpec(memory_space=pltpu.VMEM)
SMEM = pl.BlockSpec(memory_space=pltpu.SMEM)
ANY = pl.BlockSpec(memory_space=pl.ANY)
MESH = pl.DeviceIdType.MESH


def dot(left, right, contract):
    return lax.dot_general(left, right, ((contract[0:1], contract[1:2]), ((), ())), preferred_element_type=F32)


def nn(left, right):
    return dot(left, right, (1, 0))


def nt(left, right):
    return dot(left, right, (1, 1))


def tn(left, right):
    return dot(left, right, (0, 0))


def iota(shape, axis):
    return lax.broadcasted_iota(jnp.int32, shape, axis)


def flip(index, mask, count):
    bit, out = 1, 0
    while bit < count:
        out = out + ((index // bit + mask // bit) % 2) * bit
        bit *= 2
    return out


def greet(axis, me, count):
    barrier = pltpu.get_barrier_semaphore()
    for mask in range(1, count):
        pl.semaphore_signal(barrier, inc=1, device_id={axis: flip(me, mask, count)}, device_id_type=MESH)
    pl.semaphore_wait(barrier, count - 1)


def held(count):
    return (5,) if count == 8 else ()


def send_block(me, count, capacity, mask, source, target, sends, recvs):
    peer = flip(me, mask, count)
    return pltpu.make_async_remote_copy(
        src_ref=source.at[pl.ds(pl.multiple_of(peer * capacity, capacity), capacity)],
        dst_ref=target.at[pl.ds(pl.multiple_of(mask * capacity, capacity), capacity)],
        send_sem=sends.at[mask],
        recv_sem=recvs.at[mask],
        device_id={"expert": peer},
        device_id_type=MESH,
    )


def return_block(me, count, capacity, mask, source, target, sends, recvs, shift=0):
    return pltpu.make_async_remote_copy(
        src_ref=source.at[pl.ds(pl.multiple_of((mask - shift) * capacity, capacity), capacity)],
        dst_ref=target.at[pl.ds(pl.multiple_of(me * capacity, capacity), capacity)],
        send_sem=sends.at[mask],
        recv_sem=recvs.at[mask],
        device_id={"expert": flip(me, mask, count)},
        device_id_type=MESH,
    )


def row_of(ref):
    return ref[...].reshape(1, ref.shape[0])


def domain_weight(group_ref, counts_ref):
    groups = counts_ref.shape[0]
    group = group_ref[0]
    total = jnp.zeros((1, 128), F32)
    mine = jnp.zeros((1, 128), F32)
    for index in range(groups):
        inverse = 1.0 / jnp.full((1, 128), counts_ref[index], jnp.int32).astype(F32)
        total = total + inverse
        mine = mine + jnp.where(group == index, inverse, 0.0)
    return (mine / (total / groups))[:, 0:1]


def norm_stats(rows):
    center = rows - jnp.mean(rows, axis=-1, keepdims=True)
    rstd = lax.rsqrt(jnp.mean(center * center, axis=-1, keepdims=True) + EPS)
    return center * rstd, rstd


def pack_rows(slot_row, rows_ref, send_ref):
    slots = send_ref.shape[0]
    tokens = rows_ref.shape[0]

    def step(block, carry):
        base = pl.multiple_of(block * BLK, BLK)
        slot = iota((BLK, tokens), 0) + base
        pick = jnp.where(slot == slot_row, 1.0, 0.0).astype(BF16)
        send_ref[pl.ds(base, BLK), :] = nn(pick, rows_ref[...]).astype(BF16)
        return carry

    lax.fori_loop(0, slots // BLK, step, 0)


def table_kernel(experts, capacity, counts_ref, group_ref, domain_ref, sort_ref, cot_ref, send_ref, slot_col_ref, slot_row_ref, scaled):
    tokens = cot_ref.shape[0]
    place = iota((1, tokens), 1)
    expert_at = jnp.zeros((1, tokens), jnp.int32)
    start_at = jnp.zeros((1, tokens), jnp.int32)
    end = jnp.int32(0)
    for expert in range(experts):
        count = counts_ref[0, expert]
        end = end + count
        past = place >= end
        expert_at = expert_at + jnp.where(past, 1, 0)
        start_at = start_at + jnp.where(past, count, 0)
    dest = (expert_at * capacity + place - start_at).astype(F32)
    sort_row = sort_ref[...]
    scaled[...] = (cot_ref[...].astype(F32) * domain_weight(group_ref, domain_ref)).astype(BF16)
    for block in range(tokens // BLK):
        token = iota((BLK, tokens), 0) + block * BLK
        col = jnp.sum(jnp.where(token == sort_row, dest, 0.0), axis=1, keepdims=True)
        wide = jnp.broadcast_to(col, (BLK, 128))
        slot_col_ref[pl.ds(block * BLK, BLK), :] = wide.astype(jnp.int32)
        slot_row_ref[:, pl.ds(block * BLK, BLK)] = wide.T[0:8].astype(jnp.int32)
    pack_rows(slot_row_ref[0:1, :], scaled, send_ref)


def forward_kernel(
    count,
    capacity,
    x_ref,
    gain_one_ref,
    shift_one_ref,
    gain_two_ref,
    shift_two_ref,
    wq_ref,
    wk_ref,
    wv_ref,
    wo_ref,
    router_ref,
    slot_col_ref,
    slot_row_ref,
    cot_send_ref,
    normed_ref,
    q_ref,
    k_ref,
    v_ref,
    mixed_ref,
    lse_ref,
    hidden_ref,
    gate_ref,
    send_ref,
    cot_rows_ref,
    routed,
    sends,
    recvs,
    own,
):
    tokens, width = x_ref.shape
    blocks = tokens // BLK
    me = lax.axis_index("expert")
    greet("expert", me, count)
    copies = [
        send_block(me, count, capacity, mask, cot_send_ref, cot_rows_ref, sends, recvs)
        for mask in range(1, count)
        if mask not in held(count)
    ]
    for copy in copies:
        copy.start()
    mine = pltpu.make_async_copy(
        cot_send_ref.at[pl.ds(pl.multiple_of(me * capacity, capacity), capacity)], cot_rows_ref.at[pl.ds(0, capacity)], own
    )
    mine.start()
    lane = iota((1, 128), 1)
    gain_one, shift_one, gain_two, shift_two = (row_of(r) for r in (gain_one_ref, shift_one_ref, gain_two_ref, shift_two_ref))

    def project(block, carry):
        rows = pl.ds(pl.multiple_of(block * BLK, BLK), BLK)
        hat, _ = norm_stats(x_ref[rows, :].astype(F32))
        normed = (hat * gain_one + shift_one).astype(BF16)
        normed_ref[rows, :] = normed
        q_ref[rows, :] = (nn(normed, wq_ref[...]).astype(BF16) * (HEAD_DIM ** (-0.5))).astype(BF16)
        k_ref[rows, :] = nn(normed, wk_ref[...]).astype(BF16)
        v_ref[rows, :] = nn(normed, wv_ref[...]).astype(BF16)
        return carry

    lax.fori_loop(0, blocks, project, 0)

    keep = iota((BLK, BLK), 0) <= iota((BLK, BLK), 1)

    def attend(pair, carry):
        cols = pl.ds(pl.multiple_of(pair * 128, 128), 128)
        k_pair = k_ref[:, cols]
        v_t = v_ref[:, cols].astype(F32).T.astype(BF16)
        k_head = [jnp.where(lane < 64, k_pair, 0), jnp.where(lane >= 64, k_pair, 0)]
        for block in range(blocks):
            span = (block + 1) * BLK
            query = q_ref[pl.ds(block * BLK, BLK), cols]
            outs = []
            for half in range(2):
                scores = nt(k_head[half][:span], query)
                diag = jnp.where(keep, scores[block * BLK :], -1000000000.0)
                scores = jnp.concatenate([scores[: block * BLK], diag], axis=0) if block else diag
                peak = jnp.max(scores, axis=0, keepdims=True)
                exps = jnp.exp(scores - peak)
                total = jnp.sum(exps, axis=0, keepdims=True)
                out = nn(v_t[half * 64 : half * 64 + 64, :span], exps.astype(BF16))
                outs.append(out * (1.0 / total))
                lse_ref[pair, half : half + 1, pl.ds(block * BLK, BLK)] = peak + jnp.log(total)
            mixed_ref[pl.ds(block * BLK, BLK), cols] = jnp.concatenate(outs, axis=0).T.astype(BF16)
        return carry

    lax.fori_loop(0, HEADS // 2, attend, 0)

    experts = router_ref.shape[0]

    def finish(block, carry):
        rows = pl.ds(pl.multiple_of(block * BLK, BLK), BLK)
        hidden = x_ref[rows, :].astype(F32) + nn(mixed_ref[rows, :], wo_ref[...])
        hidden_ref[rows, :] = hidden
        hat, _ = norm_stats(hidden)
        low = (hat * gain_two + shift_two).astype(BF16)
        routed[rows, :] = low
        logits = nt(low, router_ref[...])
        slot = slot_col_ref[rows, 0:1]
        first = iota((BLK, experts), 1) * capacity
        mine = (slot >= first) & (slot < first + capacity)
        logit = jnp.sum(jnp.where(mine, logits, 0.0), axis=1, keepdims=True)
        gate_ref[rows, :] = jnp.broadcast_to(jax.nn.sigmoid(logit), (BLK, 128))
        return carry

    lax.fori_loop(0, blocks, finish, 0)
    pack_rows(slot_row_ref[0:1, :], routed, send_ref)
    mine.wait()
    for copy in copies:
        copy.wait()


def gelu_parts(v):
    size = jnp.abs(v)
    t = 1.0 / (1.0 + (0.3275911 * 0.7071067811865476) * size)
    bell = jnp.exp(-0.5 * (v * v))
    poly = ((((1.061405429 * t - 1.453152027) * t + 1.421413741) * t - 0.284496736) * t + 0.254829592) * t
    tail = 0.5 * poly * bell
    return jnp.where(v >= 0.0, 1.0 - tail, tail), bell * 0.3989422804014327


def expert_kernel(
    count,
    capacity,
    chunk,
    send_ref,
    cot_send_ref,
    cot_rows_ref,
    router_ref,
    w1_hbm,
    w2_hbm,
    y_ref,
    back_ref,
    late_ref,
    gw1_ref,
    gw2_ref,
    w1_ref,
    w2_ref,
    acc1,
    acc2,
    x_rows,
    g_ref,
    dx_rows,
    y_rows,
    stage,
    load_sems,
    cot_sems,
    sends,
    recvs,
    cot_sends,
    cot_recvs,
    back_sends,
    back_recvs,
    own,
    y_sems,
    stage_sems,
):
    width, hidden = w1_ref.shape
    slots = x_rows.shape[0]
    group = BLK // capacity
    early = count - count // 4
    me = lax.axis_index("expert")
    loads = [pltpu.make_async_copy(w1_hbm, w1_ref, load_sems.at[0]), pltpu.make_async_copy(w2_hbm, w2_ref, load_sems.at[1])]
    for mask in range(count):
        if mask not in held(count):
            part = pl.ds(mask * capacity, capacity)
            loads.append(pltpu.make_async_copy(cot_rows_ref.at[part], g_ref.at[part], cot_sems.at[mask]))
    for load in loads:
        load.start()
    greet("expert", me, count)
    mine_in = pltpu.make_async_copy(
        send_ref.at[pl.ds(pl.multiple_of(me * capacity, capacity), capacity)], x_rows.at[pl.ds(0, capacity)], own.at[0]
    )
    mine_in.start()
    for mask in range(1, count):
        if mask in held(count):
            send_block(me, count, capacity, mask, cot_send_ref, g_ref, cot_sends, cot_recvs).start()
        send_block(me, count, capacity, mask, send_ref, x_rows, sends, recvs).start()
    acc1[...] = jnp.zeros_like(acc1)
    acc2[...] = jnp.zeros_like(acc2)
    for load in loads:
        load.wait()
    mine_in.wait()
    experts = router_ref.shape[0]
    router = jnp.sum(jnp.where(iota((experts, 1), 0) == me, router_ref[...].astype(F32), 0.0), axis=0, keepdims=True)

    def store_y(block):
        rows = pl.ds(pl.multiple_of(block * BLK, BLK), BLK)
        return pltpu.make_async_copy(y_rows.at[rows], y_ref.at[rows], y_sems.at[block])

    def mine_out():
        return pltpu.make_async_copy(
            dx_rows.at[pl.ds(0, capacity)], back_ref.at[pl.ds(pl.multiple_of(me * capacity, capacity), capacity)], own.at[1]
        )

    def run(block, carry):
        for item in range(group):
            mask = block * group + item

            @pl.when(mask > 0)
            def _():
                send_block(me, count, capacity, mask, send_ref, x_rows, sends, recvs).wait_recv()

            for late_mask in held(count):

                @pl.when(mask == late_mask)
                def _():
                    send_block(me, count, capacity, mask, cot_send_ref, g_ref, cot_sends, cot_recvs).wait_recv()

        rows = pl.ds(pl.multiple_of(block * BLK, BLK), BLK)
        x = x_rows[rows, :]
        logit = jnp.sum(x.astype(F32) * router, axis=1, keepdims=True)
        gate = jax.nn.sigmoid(logit)
        go = g_ref[rows, :].astype(F32)
        g = (gate * go).astype(BF16)
        x_t = x.astype(F32).T.astype(BF16)
        y = jnp.zeros(x.shape, F32)
        dx = jnp.zeros(x.shape, F32)
        for first in range(0, hidden, chunk):
            cols = pl.ds(first, chunk)
            w1 = w1_ref[:, cols]
            w2 = w2_ref[cols, :]
            pre = nn(x, w1)
            cdf, pdf = gelu_parts(pre)
            act = (pre * cdf).astype(BF16)
            slope = cdf + pre * pdf
            y = y + nn(act, w2)
            grad = (nt(g, w2) * slope).astype(BF16)
            dx = dx + nt(grad, w1)
            acc1[:, cols] += nn(x_t, grad)
            acc2[cols, :] += tn(act, g)
        y_low = y.astype(BF16)
        y_rows[rows, :] = y_low
        dlogit = jnp.sum(y_low.astype(F32) * go, axis=1, keepdims=True) * gate * (1.0 - gate)
        dx_rows[rows, :] = (dx + dlogit * router).astype(BF16)
        store_y(block).start()
        for item in range(group):
            mask = block * group + item

            @pl.when((mask > 0) & (mask < early))
            def _():
                return_block(me, count, capacity, mask, dx_rows, back_ref, back_sends, back_recvs).start()

            @pl.when(mask == 0)
            def _():
                mine_out().start()

        return carry

    lax.fori_loop(0, slots // BLK, run, 0)

    pieces = []
    for first in range(0, hidden, stage.shape[1]):
        pieces.append((acc1.at[:, pl.ds(first, stage.shape[1])], gw1_ref.at[:, pl.ds(first, stage.shape[1])]))
    for first in range(0, hidden, stage.shape[1]):
        pieces.append((acc2.at[pl.ds(first, stage.shape[1]), :], gw2_ref.at[pl.ds(first, stage.shape[1]), :]))
    writes = []
    for index, (piece, target) in enumerate(pieces):
        slot = index % 2
        if index >= 2:
            writes[index - 2].wait()
        stage[slot] = piece[...].astype(BF16)
        write = pltpu.make_async_copy(stage.at[slot], target, stage_sems.at[slot])
        write.start()
        writes.append(write)
    for write in writes[-2:]:
        write.wait()
    mine_out().wait()
    tail = pltpu.make_async_copy(dx_rows.at[pl.ds(early * capacity, (count - early) * capacity)], late_ref, own.at[0])
    tail.start()

    def settle(block, carry):
        store_y(block).wait()
        return carry

    lax.fori_loop(0, slots // BLK, settle, 0)
    tail.wait()
    for mask in range(1, count):
        send_block(me, count, capacity, mask, send_ref, x_rows, sends, recvs).wait_send()
    for mask in held(count):
        send_block(me, count, capacity, mask, cot_send_ref, g_ref, cot_sends, cot_recvs).wait_send()
    for mask in range(1, early):
        return_block(me, count, capacity, mask, dx_rows, back_ref, back_sends, back_recvs).wait()


def backward_kernel(
    count,
    capacity,
    group_ref,
    domain_ref,
    x_ref,
    cot_ref,
    gain_one_ref,
    gain_two_ref,
    wq_ref,
    wk_ref,
    wv_ref,
    wo_ref,
    slot_col_ref,
    normed_ref,
    q_ref,
    k_ref,
    v_ref,
    mixed_ref,
    lse_ref,
    hidden_ref,
    dx_hbm,
    late_ref,
    y_ref,
    grad_ref,
    dense_ref,
    vec_ref,
    y_back_ref,
    dx_ref,
    ghid,
    gmix,
    branch,
    normed_t,
    dqkv,
    sums,
    sends,
    recvs,
    late_sends,
    late_recvs,
    own,
    gets,
):
    tokens, width = x_ref.shape
    me = lax.axis_index("expert")
    early = count - count // 4
    greet("expert", me, count)
    lates = [return_block(me, count, capacity, mask, late_ref, dx_ref, late_sends, late_recvs, early) for mask in range(early, count)]
    for copy in lates:
        copy.start()
    copies = [return_block(me, count, capacity, mask, y_ref, y_back_ref, sends, recvs) for mask in range(1, count)]
    for copy in copies:
        copy.start()
    mine = pltpu.make_async_copy(
        y_ref.at[pl.ds(0, capacity)], y_back_ref.at[pl.ds(pl.multiple_of(me * capacity, capacity), capacity)], own
    )
    mine.start()
    loads = []
    for mask in range(early):
        part = pl.ds(pl.multiple_of(flip(me, mask, count) * capacity, capacity), capacity)
        loads.append(pltpu.make_async_copy(dx_hbm.at[part], dx_ref.at[part], gets.at[mask]))
        loads[-1].start()
    for load in loads:
        load.wait()
    for copy in lates:
        copy.wait()
    slots = dx_ref.shape[0]
    blocks = tokens // BLK
    lane = iota((1, 128), 1)
    weight = domain_weight(group_ref, domain_ref)
    gain_one = row_of(gain_one_ref)
    gain_two = row_of(gain_two_ref)
    sums[...] = jnp.zeros_like(sums)

    def open_block(block, carry):
        rows = pl.ds(pl.multiple_of(block * BLK, BLK), BLK)
        slot = slot_col_ref[rows, 0:1]
        pick = jnp.where(iota((BLK, slots), 1) == slot, 1.0, 0.0).astype(BF16)
        grad = nn(pick, dx_ref[...])
        hat, rstd = norm_stats(hidden_ref[rows, :])
        sums[2:3, :] += jnp.sum(grad * hat, axis=0, keepdims=True)
        sums[3:4, :] += jnp.sum(grad, axis=0, keepdims=True)
        gg = grad * gain_two
        inner = gg - jnp.mean(gg, axis=1, keepdims=True) - hat * jnp.mean(gg * hat, axis=1, keepdims=True)
        total = cot_ref[rows, :].astype(F32) * weight + rstd * inner
        ghid[rows, :] = total
        low = total.astype(BF16)
        branch[rows, :] = low
        gmix[rows, :] = nt(low, wo_ref[...]).astype(BF16)
        normed_t[:, rows] = normed_ref[rows, :].astype(F32).T.astype(BF16)
        return carry

    lax.fori_loop(0, blocks, open_block, 0)
    dense_ref[pl.ds(3 * width, width), :] = tn(mixed_ref[...], branch[...]).astype(BF16)

    keep = iota((BLK, BLK), 0) <= iota((BLK, BLK), 1)

    def attend(pair, carry):
        base = pl.multiple_of(pair * 128, 128)
        cols = pl.ds(base, 128)
        q_pair = q_ref[:, cols]
        k_pair = k_ref[:, cols]
        v_pair = v_ref[:, cols]
        o_pair = gmix[:, cols]
        low = lane < 64
        q_head = [jnp.where(low, q_pair, 0), jnp.where(low, 0, q_pair)]
        k_head = [jnp.where(low, k_pair, 0), jnp.where(low, 0, k_pair)]
        v_head = [jnp.where(low, v_pair, 0), jnp.where(low, 0, v_pair)]
        o_head = [jnp.where(low, o_pair, 0), jnp.where(low, 0, o_pair)]
        k_t = k_pair.astype(F32).T.astype(BF16)
        prod_t = (o_pair.astype(F32) * mixed_ref[:, cols].astype(F32)).T
        delta = [jnp.sum(prod_t[:64], axis=0, keepdims=True), jnp.sum(prod_t[64:], axis=0, keepdims=True)]
        dq_t = [[None] * blocks, [None] * blocks]
        for block in range(blocks):
            start = block * BLK
            dk = None
            dv = None
            for half in range(2):
                scores = nt(k_head[half][start : start + BLK], q_pair[start:])
                diag = jnp.where(keep, scores[:, :BLK], -1000000000.0)
                scores = jnp.concatenate([diag, scores[:, BLK:]], axis=1) if block < blocks - 1 else diag
                probs = jnp.exp(scores - lse_ref[pair, half : half + 1, pl.ds(start, tokens - start)])
                grad_p = nt(v_head[half][start : start + BLK], o_pair[start:])
                grad_s = (probs * (grad_p - delta[half][:, start:])).astype(BF16)
                dv_part = nn(probs.astype(BF16), o_head[half][start:])
                dk_part = nn(grad_s, q_head[half][start:])
                dv = dv_part if dv is None else dv + dv_part
                dk = dk_part if dk is None else dk + dk_part
                dq_part = nn(k_t[half * 64 : half * 64 + 64, start : start + BLK], grad_s)
                for later in range(block, blocks):
                    piece = dq_part[:, (later - block) * BLK : (later - block + 1) * BLK]
                    dq_t[half][later] = piece if dq_t[half][later] is None else dq_t[half][later] + piece
            rows = pl.ds(start, BLK)
            dqkv[rows, pl.ds(pl.multiple_of(base + width, 128), 128)] = dk.astype(BF16)
            dqkv[rows, pl.ds(pl.multiple_of(base + 2 * width, 128), 128)] = dv.astype(BF16)
        for block in range(blocks):
            both = jnp.concatenate([dq_t[0][block], dq_t[1][block]], axis=0) * (HEAD_DIM ** (-0.5))
            dqkv[pl.ds(block * BLK, BLK), cols] = both.T.astype(BF16)
        return carry

    lax.fori_loop(0, HEADS // 2, attend, 0)

    for part in range(3):
        dense_ref[pl.ds(part * width, width), :] = nn(normed_t[...], dqkv[:, pl.ds(part * width, width)]).astype(BF16)

    def close_block(block, carry):
        rows = pl.ds(pl.multiple_of(block * BLK, BLK), BLK)
        grad = nt(dqkv[rows, 0:width], wq_ref[...])
        grad = grad + nt(dqkv[rows, width : 2 * width], wk_ref[...])
        grad = grad + nt(dqkv[rows, 2 * width : 3 * width], wv_ref[...])
        hat, rstd = norm_stats(x_ref[rows, :].astype(F32))
        sums[0:1, :] += jnp.sum(grad * hat, axis=0, keepdims=True)
        sums[1:2, :] += jnp.sum(grad, axis=0, keepdims=True)
        gg = grad * gain_one
        inner = gg - jnp.mean(gg, axis=1, keepdims=True) - hat * jnp.mean(gg * hat, axis=1, keepdims=True)
        grad_ref[rows, :] = (ghid[rows, :] + rstd * inner).astype(BF16)
        return carry

    lax.fori_loop(0, blocks, close_block, 0)
    vec_ref[...] = sums[...]
    mine.wait()
    for copy in copies:
        copy.wait()


def halving_plan(dp, count, rows):
    experts = []
    mask = 2
    while 2 * mask < count:
        experts += [("expert", mask, (mask, 2 * mask)), ("expert", 3 * mask, (2 * mask,))]
        mask *= 4
    if mask < count:
        experts.append(("expert", mask, (mask,)))
    groups = [("dp", 1 << bit, (1 << bit,)) for bit in range(dp.bit_length() - 1)]
    core = [("expert", 1, (1,))]
    plans = [core + experts + groups, core + experts[::-1] + groups[::-1]]
    halvings = 0
    while halvings < len(plans[0]) and (rows >> halvings) % 32 == 0:
        halvings += 1
    return plans, halvings


def finish_kernel(
    dp,
    count,
    dense_ref,
    vec_ref,
    slot_col_ref,
    hidden_ref,
    gate_ref,
    y_ref,
    out_ref,
    full_ref,
    total_ref,
    acc,
    landing,
    full,
    vec_acc,
    vec_land,
    sends,
    recvs,
    back_sends,
    back_recvs,
    vec_sends,
    vec_recvs,
    put,
):
    tokens, width = hidden_ref.shape
    slots = y_ref.shape[0]
    rows = dense_ref.shape[0] // 2
    place = {"dp": lax.axis_index("dp"), "expert": lax.axis_index("expert")}
    size = {"dp": dp, "expert": count}
    plans, halvings = halving_plan(dp, count, rows)
    steps = len(plans[0])

    def partner(axis, mask):
        return {axis: flip(place[axis], mask, size[axis])}

    barrier = pltpu.get_barrier_semaphore()
    for axis, mask, _ in plans[0]:
        pl.semaphore_signal(barrier, inc=1, device_id=partner(axis, mask), device_id_type=MESH)
    pl.semaphore_wait(barrier, steps)

    def side(axis, masks):
        return sum(place[axis] // mask for mask in masks) % 2

    def aligned(start):
        return pl.multiple_of(start, 16)

    def remote(source, target, send, recv, device):
        return pltpu.make_async_remote_copy(
            src_ref=source, dst_ref=target, send_sem=send, recv_sem=recv, device_id=device, device_id_type=MESH
        )

    def combine(block):
        span = pl.ds(block * BLK, BLK)
        slot = slot_col_ref[span, 0:1]
        pick = jnp.where(iota((BLK, slots), 1) == slot, 1.0, 0.0).astype(BF16)
        returned = nn(pick, y_ref[...])
        out_ref[span, :] = (hidden_ref[span, :] + gate_ref[span, 0:1] * returned).astype(BF16)

    todo = list(range(tokens // BLK))
    low = [jnp.int32(stream * rows) for stream in range(2)]
    extent = rows
    offset = 0
    trail = []
    for step in range(steps):
        halve = step < halvings
        part = extent // 2 if halve else extent
        copies = []
        for stream in range(2):
            axis, mask, masks = plans[stream][step]
            mine = low[stream] + side(axis, masks) * part if halve else low[stream]
            other = low[stream] + (1 - side(axis, masks)) * part if halve else low[stream]
            source = dense_ref if step == 0 else acc.at[(step - 1) % 2]
            land = landing.at[stream, pl.ds(offset, part)]
            copy = remote(
                source.at[pl.ds(aligned(other), part)], land, sends.at[stream, step], recvs.at[stream, step], partner(axis, mask)
            )
            copy.start()
            copies.append((copy, mine, source))
        axis, mask, _ = plans[0][step]
        vec_source = vec_ref if step == 0 else vec_acc.at[step - 1]
        vec_copy = remote(vec_source, vec_land.at[step], vec_sends.at[step], vec_recvs.at[step], partner(axis, mask))
        vec_copy.start()
        if step in (1, 2):
            for block in todo[: tokens // BLK // 4]:
                combine(block)
            todo = todo[tokens // BLK // 4 :]
        trail.append((list(low), extent))
        for stream in range(2):
            copy, mine, source = copies[stream]
            copy.wait()
            span = pl.ds(aligned(mine), part)
            kept = source[span, :].astype(F32) + landing[stream, pl.ds(offset, part), :].astype(F32)
            if step < steps - 1:
                acc[step % 2, span, :] = kept.astype(BF16)
            else:
                full[span, :] = kept.astype(BF16)
            low[stream] = mine
        vec_copy.wait()
        vec_sum = vec_source[...] + vec_land[step]
        if step < steps - 1:
            vec_acc[step] = vec_sum
        else:
            total_ref[...] = vec_sum
        extent = part
        offset += part

    for step in reversed(range(halvings)):
        starts, whole = trail[step]
        copies = []
        for stream in range(2):
            axis, mask, _ = plans[stream][step]
            span = pl.ds(aligned(low[stream]), extent)
            copy = remote(
                full.at[span], full.at[span], back_sends.at[stream, step], back_recvs.at[stream, step], partner(axis, mask)
            )
            copy.start()
            copies.append(copy)
        if step in (1, 2):
            for block in todo if step == 1 else todo[: tokens // BLK // 4]:
                combine(block)
            todo = todo[tokens // BLK // 4 :]
        for stream in range(2):
            copies[stream].wait()
            low[stream] = starts[stream]
        extent = whole
    write = pltpu.make_async_copy(full, full_ref, put)
    write.start()
    write.wait()


def call(kernel, outs, in_specs, scratch, name, out_specs=None, collective=None, flops=10**9):
    remote = {} if collective is None else {"collective_id": collective, "has_side_effects": True}
    return pl.pallas_call(
        kernel,
        out_shape=outs,
        in_specs=in_specs,
        out_specs=out_specs or [VMEM] * len(outs),
        scratch_shapes=scratch,
        compiler_params=pltpu.CompilerParams(vmem_limit_bytes=LIMIT, **remote),
        cost_estimate=pl.CostEstimate(flops=flops, bytes_accessed=10**7, transcendentals=0),
        name=name,
    )


def dma(*dims):
    return pltpu.SemaphoreType.DMA(dims)


def shape(dims, kind):
    return jax.ShapeDtypeStruct(dims, kind)


def tables(experts, capacity, counts, group, domains, sort_order, cotangent):
    tokens, width = cotangent.shape
    slots = experts * capacity
    return call(
        functools.partial(table_kernel, experts, capacity),
        [shape((slots, width), BF16), shape((tokens, 128), jnp.int32), shape((8, tokens), jnp.int32)],
        [SMEM, SMEM, SMEM, VMEM, VMEM],
        [pltpu.VMEM((tokens, width), BF16)],
        "tables",
    )(counts, group, domains, sort_order, cotangent)


def forward(count, capacity, slots, inputs, g1, s1, g2, s2, wq, wk, wv, wo, router, slot_col, slot_row, cot_send):
    tokens, width = inputs.shape
    rows_low = shape((tokens, width), BF16)
    return call(
        functools.partial(forward_kernel, count, capacity),
        [
            rows_low,
            rows_low,
            rows_low,
            rows_low,
            rows_low,
            shape((HEADS // 2, 8, tokens), F32),
            shape((tokens, width), F32),
            shape((tokens, 128), F32),
            shape((slots, width), BF16),
            shape((slots, width), BF16),
        ],
        [VMEM] * 12 + [ANY],
        [pltpu.VMEM((tokens, width), BF16), dma(count), dma(count), dma()],
        "dense_forward",
        [VMEM] * 9 + [ANY],
        1,
    )(inputs, g1, s1, g2, s2, wq, wk, wv, wo, router, slot_col, slot_row, cot_send)


def expert_block(count, capacity, send, cot_send, cot_rows, router_t, w1, w2, chunk=768):
    slots, width = send.shape
    hidden = w1.shape[1]
    rows = shape((slots, width), BF16)
    keep = pltpu.VMEM((slots, width), BF16)
    return call(
        functools.partial(expert_kernel, count, capacity, chunk),
        [rows, rows, shape((slots // 4, width), BF16), shape((width, hidden), BF16), shape((hidden, width), BF16)],
        [ANY, ANY, ANY, VMEM, ANY, ANY],
        [
            pltpu.VMEM((width, hidden), BF16),
            pltpu.VMEM((hidden, width), BF16),
            pltpu.VMEM((width, hidden), F32),
            pltpu.VMEM((hidden, width), F32),
            keep,
            keep,
            keep,
            keep,
            pltpu.VMEM((2, width, width), BF16),
            dma(2),
            dma(count),
            dma(count),
            dma(count),
            dma(count),
            dma(count),
            dma(count),
            dma(count),
            dma(2),
            dma(slots // BLK),
            dma(2),
        ],
        "expert",
        [ANY] * 5,
        2,
    )(send, cot_send, cot_rows, router_t, w1, w2)


def backward(
    count, capacity, group, domains, inputs, cotangent, g1, g2, wq, wk, wv, wo, slot_col, normed, q, k, v, mixed, lse, hidden, dx, late, y
):
    tokens, width = inputs.shape
    return call(
        functools.partial(backward_kernel, count, capacity),
        [shape((tokens, width), BF16), shape((4 * width, width), BF16), shape((8, width), F32), shape(y.shape, BF16)],
        [SMEM] * 2 + [VMEM] * 16 + [ANY] * 3,
        [
            pltpu.VMEM(dx.shape, BF16),
            pltpu.VMEM((tokens, width), F32),
            pltpu.VMEM((tokens, width), BF16),
            pltpu.VMEM((tokens, width), BF16),
            pltpu.VMEM((width, tokens), BF16),
            pltpu.VMEM((tokens, 3 * width), BF16),
            pltpu.VMEM((8, width), F32),
            dma(count),
            dma(count),
            dma(count),
            dma(count),
            dma(),
            dma(count),
        ],
        "dense_backward",
        [VMEM, VMEM, VMEM, ANY],
        3,
        5 * 10**10,
    )(group, domains, inputs, cotangent, g1, g2, wq, wk, wv, wo, slot_col, normed, q, k, v, mixed, lse, hidden, dx, late, y)


def finish(dp, count, dense, vec, slot_col, hidden, gate, y_back):
    width = hidden.shape[1]
    rows = dense.shape[0]
    steps = len(halving_plan(dp, count, rows // 2)[0][0])
    return call(
        functools.partial(finish_kernel, dp, count),
        [shape(hidden.shape, BF16), shape(dense.shape, BF16), shape(vec.shape, F32)],
        [VMEM] * 6,
        [
            pltpu.VMEM((2, rows, width), BF16),
            pltpu.VMEM((2, rows, width), BF16),
            pltpu.VMEM((rows, width), BF16),
            pltpu.VMEM((steps,) + vec.shape, F32),
            pltpu.VMEM((steps,) + vec.shape, F32),
            dma(2, steps),
            dma(2, steps),
            dma(2, steps),
            dma(2, steps),
            dma(steps),
            dma(steps),
            dma(),
        ],
        "finish",
        [VMEM, ANY, VMEM],
        4,
    )(dense, vec, slot_col, hidden, gate, y_back)


def local(
    inputs,
    cotangent,
    seq_group,
    domain_counts,
    sort_order,
    send_counts,
    gain_one,
    shift_one,
    gain_two,
    shift_two,
    w_query,
    w_key,
    w_value,
    w_out,
    router,
    expert_in,
    expert_out,
):
    tokens, width = inputs.shape
    experts = send_counts.shape[1]
    capacity = 2 * tokens // experts
    slots = experts * capacity
    count = lax.axis_size("expert")
    g1, s1, g2, s2 = gain_one, shift_one, gain_two, shift_two
    router_t = router.T
    cot_send, slot_col, slot_row = tables(experts, capacity, send_counts, seq_group, domain_counts, sort_order, cotangent)
    normed, q, k, v, mixed, lse, hidden, gate, send, cot_rows = forward(
        count, capacity, slots, inputs, g1, s1, g2, s2, w_query, w_key, w_value, w_out, router_t, slot_col, slot_row, cot_send
    )
    y_rows, dx_back, dx_late, grad_first, grad_second = expert_block(
        count, capacity, send, cot_send, cot_rows, router_t, expert_in[0], expert_out[0]
    )
    expert_sums = (lax.psum(grad_first, "dp").astype(F32), lax.psum(grad_second, "dp").astype(F32))
    grad_inputs, dense, vec, y_back = backward(
        count, capacity, seq_group, domain_counts, inputs, cotangent, g1, g2, w_query, w_key, w_value, w_out, slot_col,
        normed, q, k, v, mixed, lse, hidden, dx_back, dx_late, y_rows,
    )
    output, dense, vec = finish(lax.axis_size("dp"), count, dense, vec, slot_col, hidden, gate, y_back)
    dense = dense.astype(F32)
    parts = [dense[i * width : (i + 1) * width] for i in range(4)]
    vecs = [vec[i] for i in range(4)]
    return (
        output,
        grad_inputs,
        *vecs,
        *parts,
        expert_sums[0][None],
        expert_sums[1][None],
    )


def solution(mesh):
    rows = P(("dp", "expert"), None)
    split = P("expert", None, None)
    return jax.shard_map(
        local,
        mesh=mesh,
        in_specs=(rows, rows, P(("dp", "expert")), P(), rows, rows) + (P(),) * 9 + (split, split),
        out_specs=(rows, rows) + (P(),) * 8 + (split, split),
        check_vma=False,
    )
```

```python
import functools

import jax
import jax.numpy as jnp
from jax import lax
from jax.experimental import pallas as pl
from jax.experimental.pallas import tpu as pltpu
from jax.sharding import PartitionSpec as P

HEADS = 12
HEAD_DIM = 64
LEN = 1024
EPS = 1e-05
F32 = jnp.float32
BF16 = jnp.bfloat16
BLK = 256
CODE = 4096
LIMIT = 60 * 1024 * 1024

VMEM = pl.BlockSpec(memory_space=pltpu.VMEM)
SMEM = pl.BlockSpec(memory_space=pltpu.SMEM)
ANY = pl.BlockSpec(memory_space=pl.ANY)
MESH = pl.DeviceIdType.MESH


def dot(left, right, contract):
    return lax.dot_general(left, right, ((contract[0:1], contract[1:2]), ((), ())), preferred_element_type=F32)


def nn(left, right):
    return dot(left, right, (1, 0))


def nt(left, right):
    return dot(left, right, (1, 1))


def tn(left, right):
    return dot(left, right, (0, 0))


def iota(shape, axis):
    return lax.broadcasted_iota(jnp.int32, shape, axis)


def flip(index, mask, count):
    bit, out = 1, 0
    while bit < count:
        out = out + ((index // bit + mask // bit) % 2) * bit
        bit *= 2
    return out


def greet(axis, me, count):
    barrier = pltpu.get_barrier_semaphore()
    for mask in range(1, count):
        pl.semaphore_signal(barrier, inc=1, device_id={axis: flip(me, mask, count)}, device_id_type=MESH)
    pl.semaphore_wait(barrier, count - 1)


def copy_to(source, target, send, recv, device):
    return pltpu.make_async_remote_copy(
        src_ref=source, dst_ref=target, send_sem=send, recv_sem=recv, device_id=device, device_id_type=MESH
    )


def span(start, rows):
    return pl.ds(pl.multiple_of(start, 16), rows)


def send_block(me, count, rows, mask, source, target, sends, recvs):
    peer = flip(me, mask, count)
    return copy_to(
        source.at[span(peer * rows, rows)], target.at[span(mask * rows, rows)], sends.at[mask], recvs.at[mask], {"expert": peer}
    )


def return_block(me, count, rows, mask, source, target, sends, recvs, shift=0):
    return copy_to(
        source.at[span((mask - shift) * rows, rows)],
        target.at[span(me * rows, rows)],
        sends.at[mask],
        recvs.at[mask],
        {"expert": flip(me, mask, count)},
    )


def depth_of(count):
    return count.bit_length() - 1


def gather_spare(me, count, base, rows, step, first, target, sends, recvs):
    have = rows << step
    source = first.at[pl.ds(base, rows)] if step == 0 else target.at[pl.ds(base, have)]
    return copy_to(
        source,
        target.at[pl.ds(base + have, have)],
        sends.at[step],
        recvs.at[step],
        {"expert": flip(me, count >> (step + 1), count)},
    )


def return_spare(me, count, rows, step, source, shift, landing, sends, recvs):
    half = rows << step
    return copy_to(
        source.at[pl.ds(shift + half, half)],
        landing.at[pl.ds(half, half)],
        sends.at[step],
        recvs.at[step],
        {"expert": flip(me, count >> (step + 1), count)},
    )


def row_of(ref):
    return ref[...].reshape(1, ref.shape[0])


def domain_weight(group_ref, counts_ref):
    groups = counts_ref.shape[0]
    group = group_ref[0]
    total = jnp.zeros((1, 128), F32)
    mine = jnp.zeros((1, 128), F32)
    for index in range(groups):
        inverse = 1.0 / jnp.full((1, 128), counts_ref[index], jnp.int32).astype(F32)
        total = total + inverse
        mine = mine + jnp.where(group == index, inverse, 0.0)
    return (mine / (total / groups))[:, 0:1]


def norm_stats(rows):
    center = rows - jnp.mean(rows, axis=-1, keepdims=True)
    rstd = lax.rsqrt(jnp.mean(center * center, axis=-1, keepdims=True) + EPS)
    return center * rstd, rstd


def pack_rows(slot_row, rows_ref, send_ref):
    slots = send_ref.shape[0]
    tokens = rows_ref.shape[0]

    def step(block, carry):
        base = pl.multiple_of(block * BLK, BLK)
        slot = iota((BLK, tokens), 0) + base
        pick = jnp.where(slot == slot_row, 1.0, 0.0).astype(BF16)
        send_ref[pl.ds(base, BLK), :] = nn(pick, rows_ref[...]).astype(BF16)
        return carry

    lax.fori_loop(0, slots // BLK, step, 0)


def table_kernel(experts, main, counts_ref, group_ref, domain_ref, sort_ref, cot_ref, send_ref, slot_col_ref, slot_row_ref, scaled):
    tokens = cot_ref.shape[0]
    place = iota((1, tokens), 1)
    expert_at = jnp.zeros((1, tokens), jnp.int32)
    start_at = jnp.zeros((1, tokens), jnp.int32)
    end = jnp.int32(0)
    for expert in range(experts):
        count = counts_ref[0, expert]
        end = end + count
        past = place >= end
        expert_at = expert_at + jnp.where(past, 1, 0)
        start_at = start_at + jnp.where(past, count, 0)
    slot = place - start_at
    dest = jnp.where(slot < main, expert_at * main + slot, (experts - 1) * main + slot)
    code = (expert_at * CODE + dest).astype(F32)
    sort_row = sort_ref[...]
    scaled[...] = (cot_ref[...].astype(F32) * domain_weight(group_ref, domain_ref)).astype(BF16)
    for block in range(tokens // BLK):
        token = iota((BLK, tokens), 0) + block * BLK
        col = jnp.sum(jnp.where(token == sort_row, code, 0.0), axis=1, keepdims=True)
        owner = (col * (1.0 / CODE)).astype(jnp.int32)
        where = col.astype(jnp.int32) - owner * CODE
        slot_col_ref[pl.ds(block * BLK, BLK), :] = jnp.where(iota((1, 128), 1) < 64, where, owner)
        slot_row_ref[:, pl.ds(block * BLK, BLK)] = jnp.broadcast_to(where, (BLK, 128)).astype(F32).T[0:8].astype(jnp.int32)
    pack_rows(slot_row_ref[0:1, :], scaled, send_ref)


def forward_kernel(
    count,
    main,
    spare,
    x_ref,
    gain_one_ref,
    shift_one_ref,
    gain_two_ref,
    shift_two_ref,
    wq_ref,
    wk_ref,
    wv_ref,
    wo_ref,
    router_ref,
    slot_col_ref,
    slot_row_ref,
    cot_send_ref,
    normed_ref,
    q_ref,
    k_ref,
    v_ref,
    mixed_ref,
    lse_ref,
    hidden_ref,
    gate_ref,
    send_ref,
    cot_rows_ref,
    routed,
    sends,
    recvs,
    spare_sends,
    spare_recvs,
    own,
):
    tokens, width = x_ref.shape
    blocks = tokens // BLK
    me = lax.axis_index("expert")
    greet("expert", me, count)
    base = count * main
    depth = depth_of(count)

    def gather(step):
        return gather_spare(me, count, base, spare, step, cot_send_ref, cot_rows_ref, spare_sends, spare_recvs)

    gather(0).start()
    copies = [send_block(me, count, main, mask, cot_send_ref, cot_rows_ref, sends, recvs) for mask in range(1, count)]
    for copy in copies:
        copy.start()
    mine = [
        pltpu.make_async_copy(cot_send_ref.at[span(me * main, main)], cot_rows_ref.at[pl.ds(0, main)], own.at[0]),
        pltpu.make_async_copy(cot_send_ref.at[pl.ds(base, spare)], cot_rows_ref.at[pl.ds(base, spare)], own.at[1]),
    ]
    for copy in mine:
        copy.start()
    lane = iota((1, 128), 1)
    gain_one, shift_one, gain_two, shift_two = (row_of(r) for r in (gain_one_ref, shift_one_ref, gain_two_ref, shift_two_ref))

    def project(block, carry):
        rows = pl.ds(pl.multiple_of(block * BLK, BLK), BLK)
        hat, _ = norm_stats(x_ref[rows, :].astype(F32))
        normed = (hat * gain_one + shift_one).astype(BF16)
        normed_ref[rows, :] = normed
        q_ref[rows, :] = (nn(normed, wq_ref[...]).astype(BF16) * (HEAD_DIM ** (-0.5))).astype(BF16)
        k_ref[rows, :] = nn(normed, wk_ref[...]).astype(BF16)
        v_ref[rows, :] = nn(normed, wv_ref[...]).astype(BF16)
        return carry

    lax.fori_loop(0, blocks, project, 0)
    for copy in mine:
        copy.wait()
    gather(0).wait()
    gather(1).start()

    keep = iota((BLK, BLK), 0) <= iota((BLK, BLK), 1)

    def attend(pair, carry):
        cols = pl.ds(pl.multiple_of(pair * 128, 128), 128)
        k_pair = k_ref[:, cols]
        v_t = v_ref[:, cols].astype(F32).T.astype(BF16)
        k_head = [jnp.where(lane < 64, k_pair, 0), jnp.where(lane >= 64, k_pair, 0)]
        for block in range(blocks):
            span = (block + 1) * BLK
            query = q_ref[pl.ds(block * BLK, BLK), cols]
            outs = []
            for half in range(2):
                scores = nt(k_head[half][:span], query)
                diag = jnp.where(keep, scores[block * BLK :], -1000000000.0)
                scores = jnp.concatenate([scores[: block * BLK], diag], axis=0) if block else diag
                peak = jnp.max(scores, axis=0, keepdims=True)
                exps = jnp.exp(scores - peak)
                total = jnp.sum(exps, axis=0, keepdims=True)
                out = nn(v_t[half * 64 : half * 64 + 64, :span], exps.astype(BF16))
                outs.append(out * (1.0 / total))
                lse_ref[pair, half : half + 1, pl.ds(block * BLK, BLK)] = peak + jnp.log(total)
            mixed_ref[pl.ds(block * BLK, BLK), cols] = jnp.concatenate(outs, axis=0).T.astype(BF16)
        return carry

    lax.fori_loop(0, HEADS // 2, attend, 0)
    for step in range(1, depth):
        gather(step).wait()
        if step + 1 < depth:
            gather(step + 1).start()

    experts = router_ref.shape[0]

    def finish(block, carry):
        rows = pl.ds(pl.multiple_of(block * BLK, BLK), BLK)
        hidden = x_ref[rows, :].astype(F32) + nn(mixed_ref[rows, :], wo_ref[...])
        hidden_ref[rows, :] = hidden
        hat, _ = norm_stats(hidden)
        low = (hat * gain_two + shift_two).astype(BF16)
        routed[rows, :] = low
        logits = nt(low, router_ref[...])
        owner = slot_col_ref[rows, 64:65]
        logit = jnp.sum(jnp.where(iota((BLK, experts), 1) == owner, logits, 0.0), axis=1, keepdims=True)
        gate_ref[rows, :] = jnp.broadcast_to(jax.nn.sigmoid(logit), (BLK, 128))
        return carry

    lax.fori_loop(0, blocks, finish, 0)
    pack_rows(slot_row_ref[0:1, :], routed, send_ref)
    for copy in copies:
        copy.wait()


def gelu_parts(v):
    size = jnp.abs(v)
    t = 1.0 / (1.0 + (0.3275911 * 0.7071067811865476) * size)
    bell = jnp.exp(-0.5 * (v * v))
    poly = ((((1.061405429 * t - 1.453152027) * t + 1.421413741) * t - 0.284496736) * t + 0.254829592) * t
    tail = 0.5 * poly * bell
    return jnp.where(v >= 0.0, 1.0 - tail, tail), bell * 0.3989422804014327


def expert_kernel(
    count,
    main,
    spare,
    chunk,
    counts_ref,
    send_ref,
    cot_rows_ref,
    router_ref,
    w1_hbm,
    w2_hbm,
    y_ref,
    back_ref,
    late_ref,
    gw1_ref,
    gw2_ref,
    w1_ref,
    w2_ref,
    acc1,
    acc2,
    x_rows,
    g_ref,
    dx_rows,
    y_rows,
    stage,
    load_sems,
    sends,
    recvs,
    spare_sends,
    spare_recvs,
    back_sends,
    back_recvs,
    own,
    y_sems,
    stage_sems,
):
    width, hidden = w1_ref.shape
    slots = x_rows.shape[0]
    base = count * main
    plain = base // BLK
    blocks = slots // BLK
    depth = depth_of(count)
    early = count - count // 4
    me = lax.axis_index("expert")
    loads = [
        pltpu.make_async_copy(w1_hbm, w1_ref, load_sems.at[0]),
        pltpu.make_async_copy(w2_hbm, w2_ref, load_sems.at[1]),
        pltpu.make_async_copy(cot_rows_ref, g_ref, load_sems.at[2]),
    ]
    for load in loads:
        load.start()
    greet("expert", me, count)

    def gather(step):
        return gather_spare(me, count, base, spare, step, send_ref, x_rows, spare_sends, spare_recvs)

    def arrive(mask):
        return send_block(me, count, main, mask, send_ref, x_rows, sends, recvs)

    def leave(mask):
        return return_block(me, count, main, mask, dx_rows, back_ref, back_sends, back_recvs)

    gather(0).start()
    for mask in range(1, count):
        arrive(mask).start()
    mine_in = [
        pltpu.make_async_copy(send_ref.at[span(me * main, main)], x_rows.at[pl.ds(0, main)], own.at[0]),
        pltpu.make_async_copy(send_ref.at[pl.ds(base, spare)], x_rows.at[pl.ds(base, spare)], own.at[1]),
    ]
    for copy in mine_in:
        copy.start()
    acc1[...] = jnp.zeros_like(acc1)
    acc2[...] = jnp.zeros_like(acc2)
    experts = router_ref.shape[0]
    router = jnp.sum(jnp.where(iota((experts, 1), 0) == me, router_ref[...].astype(F32), 0.0), axis=0, keepdims=True)
    hot = jnp.full((1, 128), counts_ref[0, me], jnp.int32)[:, 0:1] > main
    hot = jnp.where(hot, 1.0, 0.0)
    for copy in loads + mine_in:
        copy.wait()

    def store_y(block):
        rows = pl.ds(pl.multiple_of(block * BLK, BLK), BLK)
        return pltpu.make_async_copy(y_rows.at[rows], y_ref.at[rows], y_sems.at[block])

    def mine_out():
        return pltpu.make_async_copy(dx_rows.at[pl.ds(0, main)], back_ref.at[span(me * main, main)], own.at[0])

    def run(turn, carry):
        block = turn + turn // (plain - 1) - (turn // (blocks - 1)) * (blocks - plain + 1)
        for item in range(BLK // main + 1):
            mask = (block * BLK + main - 1) // main + item

            @pl.when((block < plain) & (mask > 0) & (mask < ((block + 1) * BLK + main - 1) // main))
            def _():
                arrive(mask).wait_recv()

        for step in range(depth):

            @pl.when(turn == (step + 1 if step + 1 < depth else plain - 1))
            def _():
                gather(step).wait_recv()
                if step + 1 < depth:
                    gather(step + 1).start()

        rows = pl.ds(pl.multiple_of(block * BLK, BLK), BLK)
        live = jnp.where(block < plain, 1.0, hot)
        x = (x_rows[rows, :].astype(F32) * live).astype(BF16)
        logit = jnp.sum(x.astype(F32) * router, axis=1, keepdims=True)
        gate = jax.nn.sigmoid(logit)
        go = g_ref[rows, :].astype(F32) * live
        g = (gate * go).astype(BF16)
        x_t = x.astype(F32).T.astype(BF16)
        y = jnp.zeros(x.shape, F32)
        dx = jnp.zeros(x.shape, F32)
        for first in range(0, hidden, chunk):
            cols = pl.ds(first, chunk)
            w1 = w1_ref[:, cols]
            w2 = w2_ref[cols, :]
            pre = nn(x, w1)
            cdf, pdf = gelu_parts(pre)
            act = (pre * cdf).astype(BF16)
            slope = cdf + pre * pdf
            y = y + nn(act, w2)
            grad = (nt(g, w2) * slope).astype(BF16)
            dx = dx + nt(grad, w1)
            acc1[:, cols] += nn(x_t, grad)
            acc2[cols, :] += tn(act, g)
        y_low = y.astype(BF16)
        y_rows[rows, :] = y_low
        dlogit = jnp.sum(y_low.astype(F32) * go, axis=1, keepdims=True) * gate * (1.0 - gate)
        dx_rows[rows, :] = (dx + dlogit * router).astype(BF16)
        store_y(block).start()
        for item in range(BLK // main + 1):
            mask = (block * BLK) // main + item
            done = (block < plain) & (mask < ((block + 1) * BLK) // main)

            @pl.when(done & (mask > 0) & (mask < early))
            def _():
                leave(mask).start()

            @pl.when(done & (mask == 0))
            def _():
                mine_out().start()

        return carry

    lax.fori_loop(0, blocks, run, 0)
    tail = pltpu.make_async_copy(dx_rows.at[pl.ds(early * main, slots - early * main)], late_ref, own.at[1])
    tail.start()

    pieces = []
    for first in range(0, hidden, stage.shape[1]):
        pieces.append((acc1.at[:, pl.ds(first, stage.shape[1])], gw1_ref.at[:, pl.ds(first, stage.shape[1])]))
    for first in range(0, hidden, stage.shape[1]):
        pieces.append((acc2.at[pl.ds(first, stage.shape[1]), :], gw2_ref.at[pl.ds(first, stage.shape[1]), :]))
    writes = []
    for index, (piece, target) in enumerate(pieces):
        slot = index % 2
        if index >= 2:
            writes[index - 2].wait()
        stage[slot] = piece[...].astype(BF16)
        write = pltpu.make_async_copy(stage.at[slot], target, stage_sems.at[slot])
        write.start()
        writes.append(write)
    for write in writes[-2:]:
        write.wait()
    mine_out().wait()
    tail.wait()

    def settle(block, carry):
        store_y(block).wait()
        return carry

    lax.fori_loop(0, blocks, settle, 0)
    for step in range(depth):
        gather(step).wait_send()
    for mask in range(1, count):
        arrive(mask).wait_send()
    for mask in range(1, early):
        leave(mask).wait()


def backward_kernel(
    count,
    main,
    spare,
    group_ref,
    domain_ref,
    x_ref,
    cot_ref,
    gain_one_ref,
    gain_two_ref,
    wq_ref,
    wk_ref,
    wv_ref,
    wo_ref,
    slot_col_ref,
    normed_ref,
    q_ref,
    k_ref,
    v_ref,
    mixed_ref,
    lse_ref,
    hidden_ref,
    dx_hbm,
    late_ref,
    y_ref,
    grad_ref,
    dense_ref,
    vec_ref,
    y_back_ref,
    dx_ref,
    spare_dx,
    spare_y,
    dx_land,
    y_land,
    ghid,
    gmix,
    branch,
    normed_t,
    dqkv,
    sums,
    sends,
    recvs,
    late_sends,
    late_recvs,
    dx_sends,
    dx_recvs,
    y_sends,
    y_recvs,
    own,
    gets,
):
    tokens, width = x_ref.shape
    me = lax.axis_index("expert")
    early = count - count // 4
    base = count * main
    late = (count - early) * main
    total = count * spare
    depth = depth_of(count)
    greet("expert", me, count)

    def sum_dx(step):
        if step == depth - 1:
            return return_spare(me, count, spare, step, late_ref, late, dx_land, dx_sends, dx_recvs)
        return return_spare(me, count, spare, step, spare_dx, 0, dx_land, dx_sends, dx_recvs)

    def sum_y(step):
        if step == depth - 1:
            return return_spare(me, count, spare, step, y_ref, base, y_land, y_sends, y_recvs)
        return return_spare(me, count, spare, step, spare_y, 0, y_land, y_sends, y_recvs)

    def settle(copy, kept, landing, step):
        copy.wait()
        half = spare << step
        kept[0:half, :] = (kept[0:half, :].astype(F32) + landing[half : 2 * half, :].astype(F32)).astype(BF16)

    sum_dx(depth - 1).start()
    lates = [return_block(me, count, main, mask, late_ref, dx_ref, late_sends, late_recvs, early) for mask in range(early, count)]
    for copy in lates:
        copy.start()
    copies = [return_block(me, count, main, mask, y_ref, y_back_ref, sends, recvs) for mask in range(1, count)]
    for copy in copies:
        copy.start()
    mine = pltpu.make_async_copy(y_ref.at[pl.ds(0, main)], y_back_ref.at[span(me * main, main)], own.at[0])
    mine.start()
    loads = [
        pltpu.make_async_copy(late_ref.at[pl.ds(late, total)], spare_dx, own.at[1]),
        pltpu.make_async_copy(y_ref.at[pl.ds(base, total)], spare_y, own.at[2]),
    ]
    for mask in range(early):
        part = span(flip(me, mask, count) * main, main)
        loads.append(pltpu.make_async_copy(dx_hbm.at[part], dx_ref.at[part], gets.at[mask]))
    for load in loads:
        load.start()
    for load in loads:
        load.wait()
    for step in reversed(range(depth)):
        settle(sum_dx(step), spare_dx, dx_land, step)
        if step:
            sum_dx(step - 1).start()
    dx_ref[pl.ds(base, BLK), :] = spare_dx[0:BLK, :]
    sum_y(depth - 1).start()
    for copy in lates:
        copy.wait()
    slots = dx_ref.shape[0]
    blocks = tokens // BLK
    lane = iota((1, 128), 1)
    weight = domain_weight(group_ref, domain_ref)
    gain_one = row_of(gain_one_ref)
    gain_two = row_of(gain_two_ref)
    sums[...] = jnp.zeros_like(sums)

    def open_block(block, carry):
        rows = pl.ds(pl.multiple_of(block * BLK, BLK), BLK)
        slot = slot_col_ref[rows, 0:1]
        pick = jnp.where(iota((BLK, slots), 1) == slot, 1.0, 0.0).astype(BF16)
        grad = nn(pick, dx_ref[...])
        hat, rstd = norm_stats(hidden_ref[rows, :])
        sums[2:3, :] += jnp.sum(grad * hat, axis=0, keepdims=True)
        sums[3:4, :] += jnp.sum(grad, axis=0, keepdims=True)
        gg = grad * gain_two
        inner = gg - jnp.mean(gg, axis=1, keepdims=True) - hat * jnp.mean(gg * hat, axis=1, keepdims=True)
        total = cot_ref[rows, :].astype(F32) * weight + rstd * inner
        ghid[rows, :] = total
        low = total.astype(BF16)
        branch[rows, :] = low
        gmix[rows, :] = nt(low, wo_ref[...]).astype(BF16)
        normed_t[:, rows] = normed_ref[rows, :].astype(F32).T.astype(BF16)
        return carry

    lax.fori_loop(0, blocks, open_block, 0)
    dense_ref[pl.ds(3 * width, width), :] = tn(mixed_ref[...], branch[...]).astype(BF16)
    settle(sum_y(depth - 1), spare_y, y_land, depth - 1)
    sum_y(depth - 2).start()

    keep = iota((BLK, BLK), 0) <= iota((BLK, BLK), 1)

    def attend(pair, carry):
        base = pl.multiple_of(pair * 128, 128)
        cols = pl.ds(base, 128)
        q_pair = q_ref[:, cols]
        k_pair = k_ref[:, cols]
        v_pair = v_ref[:, cols]
        o_pair = gmix[:, cols]
        low = lane < 64
        q_head = [jnp.where(low, q_pair, 0), jnp.where(low, 0, q_pair)]
        k_head = [jnp.where(low, k_pair, 0), jnp.where(low, 0, k_pair)]
        v_head = [jnp.where(low, v_pair, 0), jnp.where(low, 0, v_pair)]
        o_head = [jnp.where(low, o_pair, 0), jnp.where(low, 0, o_pair)]
        k_t = k_pair.astype(F32).T.astype(BF16)
        prod_t = (o_pair.astype(F32) * mixed_ref[:, cols].astype(F32)).T
        delta = [jnp.sum(prod_t[:64], axis=0, keepdims=True), jnp.sum(prod_t[64:], axis=0, keepdims=True)]
        dq_t = [[None] * blocks, [None] * blocks]
        for block in range(blocks):
            start = block * BLK
            dk = None
            dv = None
            for half in range(2):
                scores = nt(k_head[half][start : start + BLK], q_pair[start:])
                diag = jnp.where(keep, scores[:, :BLK], -1000000000.0)
                scores = jnp.concatenate([diag, scores[:, BLK:]], axis=1) if block < blocks - 1 else diag
                probs = jnp.exp(scores - lse_ref[pair, half : half + 1, pl.ds(start, tokens - start)])
                grad_p = nt(v_head[half][start : start + BLK], o_pair[start:])
                grad_s = (probs * (grad_p - delta[half][:, start:])).astype(BF16)
                dv_part = nn(probs.astype(BF16), o_head[half][start:])
                dk_part = nn(grad_s, q_head[half][start:])
                dv = dv_part if dv is None else dv + dv_part
                dk = dk_part if dk is None else dk + dk_part
                dq_part = nn(k_t[half * 64 : half * 64 + 64, start : start + BLK], grad_s)
                for later in range(block, blocks):
                    piece = dq_part[:, (later - block) * BLK : (later - block + 1) * BLK]
                    dq_t[half][later] = piece if dq_t[half][later] is None else dq_t[half][later] + piece
            rows = pl.ds(start, BLK)
            dqkv[rows, pl.ds(pl.multiple_of(base + width, 128), 128)] = dk.astype(BF16)
            dqkv[rows, pl.ds(pl.multiple_of(base + 2 * width, 128), 128)] = dv.astype(BF16)
        for block in range(blocks):
            both = jnp.concatenate([dq_t[0][block], dq_t[1][block]], axis=0) * (HEAD_DIM ** (-0.5))
            dqkv[pl.ds(block * BLK, BLK), cols] = both.T.astype(BF16)
        return carry

    lax.fori_loop(0, HEADS // 2, attend, 0)
    for step in reversed(range(depth - 1)):
        settle(sum_y(step), spare_y, y_land, step)
        if step:
            sum_y(step - 1).start()
    spare_out = pltpu.make_async_copy(spare_y.at[pl.ds(0, BLK)], y_back_ref.at[pl.ds(base, BLK)], own.at[1])
    spare_out.start()

    for part in range(3):
        dense_ref[pl.ds(part * width, width), :] = nn(normed_t[...], dqkv[:, pl.ds(part * width, width)]).astype(BF16)

    def close_block(block, carry):
        rows = pl.ds(pl.multiple_of(block * BLK, BLK), BLK)
        grad = nt(dqkv[rows, 0:width], wq_ref[...])
        grad = grad + nt(dqkv[rows, width : 2 * width], wk_ref[...])
        grad = grad + nt(dqkv[rows, 2 * width : 3 * width], wv_ref[...])
        hat, rstd = norm_stats(x_ref[rows, :].astype(F32))
        sums[0:1, :] += jnp.sum(grad * hat, axis=0, keepdims=True)
        sums[1:2, :] += jnp.sum(grad, axis=0, keepdims=True)
        gg = grad * gain_one
        inner = gg - jnp.mean(gg, axis=1, keepdims=True) - hat * jnp.mean(gg * hat, axis=1, keepdims=True)
        grad_ref[rows, :] = (ghid[rows, :] + rstd * inner).astype(BF16)
        return carry

    lax.fori_loop(0, blocks, close_block, 0)
    vec_ref[...] = sums[...]
    spare_out.wait()
    mine.wait()
    for copy in copies:
        copy.wait()


def halving_plan(dp, count, rows):
    experts = [("expert", 2 << bit) for bit in range(depth_of(count) - 1)]
    groups = [("dp", 1 << bit) for bit in range(depth_of(dp))]
    core = [("expert", 1)]
    plans = [core + groups + experts, core + experts + groups]
    halvings = 0
    while halvings < len(plans[0]) and (rows >> halvings) % 32 == 0:
        halvings += 1
    return plans, halvings


def finish_kernel(
    dp,
    count,
    dense_ref,
    vec_ref,
    slot_col_ref,
    hidden_ref,
    gate_ref,
    y_ref,
    out_ref,
    full_ref,
    total_ref,
    acc,
    landing,
    full,
    vec_acc,
    vec_land,
    sends,
    recvs,
    back_sends,
    back_recvs,
    vec_sends,
    vec_recvs,
    put,
):
    tokens, width = hidden_ref.shape
    slots = y_ref.shape[0]
    rows = dense_ref.shape[0] // 2
    place = {"dp": lax.axis_index("dp"), "expert": lax.axis_index("expert")}
    size = {"dp": dp, "expert": count}
    plans, halvings = halving_plan(dp, count, rows)
    steps = len(plans[0])

    def partner(axis, mask):
        return {axis: flip(place[axis], mask, size[axis])}

    barrier = pltpu.get_barrier_semaphore()
    for axis, mask in plans[0]:
        pl.semaphore_signal(barrier, inc=1, device_id=partner(axis, mask), device_id_type=MESH)
    pl.semaphore_wait(barrier, steps)

    def side(axis, mask):
        return (place[axis] // mask) % 2

    def combine(block):
        rows_at = pl.ds(block * BLK, BLK)
        slot = slot_col_ref[rows_at, 0:1]
        pick = jnp.where(iota((BLK, slots), 1) == slot, 1.0, 0.0).astype(BF16)
        returned = nn(pick, y_ref[...])
        out_ref[rows_at, :] = (hidden_ref[rows_at, :] + gate_ref[rows_at, 0:1] * returned).astype(BF16)

    todo = list(range(tokens // BLK))
    low = [jnp.int32(stream * rows) for stream in range(2)]
    extent = rows
    offset = 0
    trail = []
    for step in range(steps):
        halve = step < halvings
        part = extent // 2 if halve else extent
        copies = []
        for stream in range(2):
            axis, mask = plans[stream][step]
            mine = low[stream] + side(axis, mask) * part if halve else low[stream]
            other = low[stream] + (1 - side(axis, mask)) * part if halve else low[stream]
            source = dense_ref if step == 0 else acc.at[(step - 1) % 2]
            land = landing.at[stream, pl.ds(offset, part)]
            copy = copy_to(
                source.at[span(other, part)], land, sends.at[stream, step], recvs.at[stream, step], partner(axis, mask)
            )
            copy.start()
            copies.append((copy, mine, source))
        axis, mask = plans[0][step]
        vec_source = vec_ref if step == 0 else vec_acc.at[step - 1]
        vec_copy = copy_to(vec_source, vec_land.at[step], vec_sends.at[step], vec_recvs.at[step], partner(axis, mask))
        vec_copy.start()
        if step in (1, 2):
            for block in todo[: tokens // BLK // 4]:
                combine(block)
            todo = todo[tokens // BLK // 4 :]
        trail.append((list(low), extent))
        for stream in range(2):
            copy, mine, source = copies[stream]
            copy.wait()
            held = span(mine, part)
            kept = source[held, :].astype(F32) + landing[stream, pl.ds(offset, part), :].astype(F32)
            if step < steps - 1:
                acc[step % 2, held, :] = kept.astype(BF16)
            else:
                full[held, :] = kept.astype(BF16)
            low[stream] = mine
        vec_copy.wait()
        vec_sum = vec_source[...] + vec_land[step]
        if step < steps - 1:
            vec_acc[step] = vec_sum
        else:
            total_ref[...] = vec_sum
        extent = part
        offset += part

    for step in reversed(range(halvings)):
        starts, whole = trail[step]
        copies = []
        for stream in range(2):
            axis, mask = plans[stream][step]
            held = span(low[stream], extent)
            copy = copy_to(
                full.at[held], full.at[held], back_sends.at[stream, step], back_recvs.at[stream, step], partner(axis, mask)
            )
            copy.start()
            copies.append(copy)
        if step in (1, 2):
            for block in todo if step == 1 else todo[: tokens // BLK // 4]:
                combine(block)
            todo = todo[tokens // BLK // 4 :]
        for stream in range(2):
            copies[stream].wait()
            low[stream] = starts[stream]
        extent = whole
    write = pltpu.make_async_copy(full, full_ref, put)
    write.start()
    write.wait()


def call(kernel, outs, in_specs, scratch, name, out_specs=None, collective=None, flops=10**9):
    remote = {} if collective is None else {"collective_id": collective, "has_side_effects": True}
    return pl.pallas_call(
        kernel,
        out_shape=outs,
        in_specs=in_specs,
        out_specs=out_specs or [VMEM] * len(outs),
        scratch_shapes=scratch,
        compiler_params=pltpu.CompilerParams(vmem_limit_bytes=LIMIT, **remote),
        cost_estimate=pl.CostEstimate(flops=flops, bytes_accessed=10**7, transcendentals=0),
        name=name,
    )


def dma(*dims):
    return pltpu.SemaphoreType.DMA(dims)


def shape(dims, kind):
    return jax.ShapeDtypeStruct(dims, kind)


def tables(experts, main, slots, counts, group, domains, sort_order, cotangent):
    tokens, width = cotangent.shape
    return call(
        functools.partial(table_kernel, experts, main),
        [shape((slots, width), BF16), shape((tokens, 128), jnp.int32), shape((8, tokens), jnp.int32)],
        [SMEM, SMEM, SMEM, VMEM, VMEM],
        [pltpu.VMEM((tokens, width), BF16)],
        "tables",
    )(counts, group, domains, sort_order, cotangent)


def forward(count, main, spare, inputs, g1, s1, g2, s2, wq, wk, wv, wo, router, slot_col, slot_row, cot_send):
    tokens, width = inputs.shape
    rows_low = shape((tokens, width), BF16)
    return call(
        functools.partial(forward_kernel, count, main, spare),
        [
            rows_low,
            rows_low,
            rows_low,
            rows_low,
            rows_low,
            shape((HEADS // 2, 8, tokens), F32),
            shape((tokens, width), F32),
            shape((tokens, 128), F32),
            shape(cot_send.shape, BF16),
            shape((count * (main + spare), width), BF16),
        ],
        [VMEM] * 12 + [ANY],
        [pltpu.VMEM((tokens, width), BF16), dma(count), dma(count), dma(depth_of(count)), dma(depth_of(count)), dma(2)],
        "dense_forward",
        [VMEM] * 9 + [ANY],
        1,
    )(inputs, g1, s1, g2, s2, wq, wk, wv, wo, router, slot_col, slot_row, cot_send)


def expert_block(count, main, spare, counts, send, cot_rows, router_t, w1, w2, chunk=768):
    slots, width = cot_rows.shape
    hidden = w1.shape[1]
    late = slots - (count - count // 4) * main
    rows = shape((slots, width), BF16)
    keep = pltpu.VMEM((slots, width), BF16)
    depth = depth_of(count)
    return call(
        functools.partial(expert_kernel, count, main, spare, chunk),
        [
            rows,
            shape((count * main, width), BF16),
            shape((late, width), BF16),
            shape((width, hidden), BF16),
            shape((hidden, width), BF16),
        ],
        [SMEM, ANY, ANY, VMEM, ANY, ANY],
        [
            pltpu.VMEM((width, hidden), BF16),
            pltpu.VMEM((hidden, width), BF16),
            pltpu.VMEM((width, hidden), F32),
            pltpu.VMEM((hidden, width), F32),
            keep,
            keep,
            keep,
            keep,
            pltpu.VMEM((2, width, width), BF16),
            dma(3),
            dma(count),
            dma(count),
            dma(depth),
            dma(depth),
            dma(count),
            dma(count),
            dma(2),
            dma(slots // BLK),
            dma(2),
        ],
        "expert",
        [ANY] * 5,
        2,
    )(counts, send, cot_rows, router_t, w1, w2)


def backward(
    count, main, spare, group, domains, inputs, cotangent, g1, g2, wq, wk, wv, wo, slot_col, normed, q, k, v, mixed, lse, hidden, dx, late, y
):
    tokens, width = inputs.shape
    return call(
        functools.partial(backward_kernel, count, main, spare),
        [shape((tokens, width), BF16), shape((4 * width, width), BF16), shape((8, width), F32), shape((count * main + BLK, width), BF16)],
        [SMEM] * 2 + [VMEM] * 16 + [ANY] * 3,
        [
            pltpu.VMEM((count * main + BLK, width), BF16),
            pltpu.VMEM((count * spare, width), BF16),
            pltpu.VMEM((count * spare, width), BF16),
            pltpu.VMEM((count * spare, width), BF16),
            pltpu.VMEM((count * spare, width), BF16),
            pltpu.VMEM((tokens, width), F32),
            pltpu.VMEM((tokens, width), BF16),
            pltpu.VMEM((tokens, width), BF16),
            pltpu.VMEM((width, tokens), BF16),
            pltpu.VMEM((tokens, 3 * width), BF16),
            pltpu.VMEM((8, width), F32),
            dma(count),
            dma(count),
            dma(count),
            dma(count),
            dma(depth_of(count)),
            dma(depth_of(count)),
            dma(depth_of(count)),
            dma(depth_of(count)),
            dma(3),
            dma(count),
        ],
        "dense_backward",
        [VMEM, VMEM, VMEM, ANY],
        3,
        5 * 10**10,
    )(group, domains, inputs, cotangent, g1, g2, wq, wk, wv, wo, slot_col, normed, q, k, v, mixed, lse, hidden, dx, late, y)


def finish(dp, count, dense, vec, slot_col, hidden, gate, y_back):
    width = hidden.shape[1]
    rows = dense.shape[0]
    steps = len(halving_plan(dp, count, rows // 2)[0][0])
    return call(
        functools.partial(finish_kernel, dp, count),
        [shape(hidden.shape, BF16), shape(dense.shape, BF16), shape(vec.shape, F32)],
        [VMEM] * 6,
        [
            pltpu.VMEM((2, rows, width), BF16),
            pltpu.VMEM((2, rows, width), BF16),
            pltpu.VMEM((rows, width), BF16),
            pltpu.VMEM((steps,) + vec.shape, F32),
            pltpu.VMEM((steps,) + vec.shape, F32),
            dma(2, steps),
            dma(2, steps),
            dma(2, steps),
            dma(2, steps),
            dma(steps),
            dma(steps),
            dma(),
        ],
        "finish",
        [VMEM, ANY, VMEM],
        4,
    )(dense, vec, slot_col, hidden, gate, y_back)


def local(
    inputs,
    cotangent,
    seq_group,
    domain_counts,
    sort_order,
    send_counts,
    gain_one,
    shift_one,
    gain_two,
    shift_two,
    w_query,
    w_key,
    w_value,
    w_out,
    router,
    expert_in,
    expert_out,
):
    tokens, width = inputs.shape
    experts = send_counts.shape[1]
    capacity = 2 * tokens // experts
    spare = capacity // 4
    main = capacity - spare
    slots = experts * main + BLK
    count = lax.axis_size("expert")
    g1, s1, g2, s2 = gain_one, shift_one, gain_two, shift_two
    router_t = router.T
    cot_send, slot_col, slot_row = tables(experts, main, slots, send_counts, seq_group, domain_counts, sort_order, cotangent)
    normed, q, k, v, mixed, lse, hidden, gate, send, cot_rows = forward(
        count, main, spare, inputs, g1, s1, g2, s2, w_query, w_key, w_value, w_out, router_t, slot_col, slot_row, cot_send
    )
    y_rows, dx_back, dx_late, grad_first, grad_second = expert_block(
        count, main, spare, send_counts, send, cot_rows, router_t, expert_in[0], expert_out[0]
    )
    expert_sums = (lax.psum(grad_first, "dp").astype(F32), lax.psum(grad_second, "dp").astype(F32))
    grad_inputs, dense, vec, y_back = backward(
        count, main, spare, seq_group, domain_counts, inputs, cotangent, g1, g2, w_query, w_key, w_value, w_out, slot_col,
        normed, q, k, v, mixed, lse, hidden, dx_back, dx_late, y_rows,
    )
    output, dense, vec = finish(lax.axis_size("dp"), count, dense, vec, slot_col, hidden, gate, y_back)
    dense = dense.astype(F32)
    parts = [dense[i * width : (i + 1) * width] for i in range(4)]
    vecs = [vec[i] for i in range(4)]
    return (
        output,
        grad_inputs,
        *vecs,
        *parts,
        expert_sums[0][None],
        expert_sums[1][None],
    )


def solution(mesh):
    rows = P(("dp", "expert"), None)
    split = P("expert", None, None)
    return jax.shard_map(
        local,
        mesh=mesh,
        in_specs=(rows, rows, P(("dp", "expert")), P(), rows, rows) + (P(),) * 9 + (split, split),
        out_specs=(rows, rows) + (P(),) * 8 + (split, split),
        check_vma=False,
    )
```

```python
import functools

import jax
import jax.numpy as jnp
from jax import lax
from jax.experimental import pallas as pl
from jax.experimental.pallas import tpu as pltpu
from jax.sharding import PartitionSpec as P

HEADS = 12
HEAD_DIM = 64
LEN = 1024
EPS = 1e-05
F32 = jnp.float32
BF16 = jnp.bfloat16
BLK = 256
CODE = 4096
LIMIT = 60 * 1024 * 1024

VMEM = pl.BlockSpec(memory_space=pltpu.VMEM)
SMEM = pl.BlockSpec(memory_space=pltpu.SMEM)
ANY = pl.BlockSpec(memory_space=pl.ANY)
MESH = pl.DeviceIdType.MESH


def dot(left, right, contract):
    return lax.dot_general(left, right, ((contract[0:1], contract[1:2]), ((), ())), preferred_element_type=F32)


def nn(left, right):
    return dot(left, right, (1, 0))


def nt(left, right):
    return dot(left, right, (1, 1))


def tn(left, right):
    return dot(left, right, (0, 0))


def iota(shape, axis):
    return lax.broadcasted_iota(jnp.int32, shape, axis)


def flip(index, mask, count):
    bit, out = 1, 0
    while bit < count:
        out = out + ((index // bit + mask // bit) % 2) * bit
        bit *= 2
    return out


def greet(axis, me, count):
    barrier = pltpu.get_barrier_semaphore()
    for mask in range(1, count):
        pl.semaphore_signal(barrier, inc=1, device_id={axis: flip(me, mask, count)}, device_id_type=MESH)
    pl.semaphore_wait(barrier, count - 1)


def copy_to(source, target, send, recv, device):
    return pltpu.make_async_remote_copy(
        src_ref=source, dst_ref=target, send_sem=send, recv_sem=recv, device_id=device, device_id_type=MESH
    )


def span(start, rows):
    return pl.ds(pl.multiple_of(start, 16), rows)


def send_block(me, count, rows, mask, source, target, sends, recvs):
    peer = flip(me, mask, count)
    return copy_to(
        source.at[span(peer * rows, rows)], target.at[span(mask * rows, rows)], sends.at[mask], recvs.at[mask], {"expert": peer}
    )


def return_block(me, count, rows, mask, source, target, sends, recvs, shift=0):
    return copy_to(
        source.at[span((mask - shift) * rows, rows)],
        target.at[span(me * rows, rows)],
        sends.at[mask],
        recvs.at[mask],
        {"expert": flip(me, mask, count)},
    )


def depth_of(count):
    return count.bit_length() - 1


def gather_spare(me, count, base, rows, step, first, target, sends, recvs):
    have = rows << step
    source = first.at[pl.ds(base, rows)] if step == 0 else target.at[pl.ds(base, have)]
    return copy_to(
        source,
        target.at[pl.ds(base + have, have)],
        sends.at[step],
        recvs.at[step],
        {"expert": flip(me, count >> (step + 1), count)},
    )


def return_spare(me, count, rows, step, source, shift, landing, sends, recvs):
    half = rows << step
    return copy_to(
        source.at[pl.ds(shift + half, half)],
        landing.at[pl.ds(half, half)],
        sends.at[step],
        recvs.at[step],
        {"expert": flip(me, count >> (step + 1), count)},
    )


def row_of(ref):
    return ref[...].reshape(1, ref.shape[0])


def domain_weight(group_ref, counts_ref):
    groups = counts_ref.shape[0]
    group = group_ref[0]
    total = jnp.zeros((1, 128), F32)
    mine = jnp.zeros((1, 128), F32)
    for index in range(groups):
        inverse = 1.0 / jnp.full((1, 128), counts_ref[index], jnp.int32).astype(F32)
        total = total + inverse
        mine = mine + jnp.where(group == index, inverse, 0.0)
    return (mine / (total / groups))[:, 0:1]


def norm_stats(rows):
    center = rows - jnp.mean(rows, axis=-1, keepdims=True)
    rstd = lax.rsqrt(jnp.mean(center * center, axis=-1, keepdims=True) + EPS)
    return center * rstd, rstd


def pack_rows(slot_row, rows_ref, send_ref):
    slots = send_ref.shape[0]
    tokens = rows_ref.shape[0]

    def step(block, carry):
        base = pl.multiple_of(block * BLK, BLK)
        slot = iota((BLK, tokens), 0) + base
        pick = jnp.where(slot == slot_row, 1.0, 0.0).astype(BF16)
        send_ref[pl.ds(base, BLK), :] = nn(pick, rows_ref[...]).astype(BF16)
        return carry

    lax.fori_loop(0, slots // BLK, step, 0)


def table_kernel(experts, main, counts_ref, group_ref, domain_ref, sort_ref, cot_ref, send_ref, slot_col_ref, slot_row_ref, scaled):
    tokens = cot_ref.shape[0]
    place = iota((1, tokens), 1)
    expert_at = jnp.zeros((1, tokens), jnp.int32)
    start_at = jnp.zeros((1, tokens), jnp.int32)
    end = jnp.int32(0)
    for expert in range(experts):
        count = counts_ref[0, expert]
        end = end + count
        past = place >= end
        expert_at = expert_at + jnp.where(past, 1, 0)
        start_at = start_at + jnp.where(past, count, 0)
    slot = place - start_at
    dest = jnp.where(slot < main, expert_at * main + slot, (experts - 1) * main + slot)
    code = (expert_at * CODE + dest).astype(F32)
    sort_row = sort_ref[...]
    scaled[...] = (cot_ref[...].astype(F32) * domain_weight(group_ref, domain_ref)).astype(BF16)
    for block in range(tokens // BLK):
        token = iota((BLK, tokens), 0) + block * BLK
        col = jnp.sum(jnp.where(token == sort_row, code, 0.0), axis=1, keepdims=True)
        owner = (col * (1.0 / CODE)).astype(jnp.int32)
        where = col.astype(jnp.int32) - owner * CODE
        slot_col_ref[pl.ds(block * BLK, BLK), :] = jnp.where(iota((1, 128), 1) < 64, where, owner)
        slot_row_ref[:, pl.ds(block * BLK, BLK)] = jnp.broadcast_to(where, (BLK, 128)).astype(F32).T[0:8].astype(jnp.int32)
    pack_rows(slot_row_ref[0:1, :], scaled, send_ref)


def forward_kernel(
    count,
    main,
    spare,
    x_ref,
    gain_one_ref,
    shift_one_ref,
    gain_two_ref,
    shift_two_ref,
    wq_ref,
    wk_ref,
    wv_ref,
    wo_ref,
    router_ref,
    slot_col_ref,
    slot_row_ref,
    cot_send_ref,
    normed_ref,
    q_ref,
    k_ref,
    v_ref,
    mixed_ref,
    lse_ref,
    hidden_ref,
    gate_ref,
    send_ref,
    cot_rows_ref,
    routed,
    sends,
    recvs,
    spare_sends,
    spare_recvs,
    own,
):
    tokens, width = x_ref.shape
    blocks = tokens // BLK
    me = lax.axis_index("expert")
    greet("expert", me, count)
    base = count * main

    def gather(step):
        return gather_spare(me, count, base, spare, step, cot_send_ref, cot_rows_ref, spare_sends, spare_recvs)

    gather(0).start()
    copies = [send_block(me, count, main, mask, cot_send_ref, cot_rows_ref, sends, recvs) for mask in range(1, count - 1)]
    for copy in copies:
        copy.start()
    mine = [
        pltpu.make_async_copy(cot_send_ref.at[span(me * main, main)], cot_rows_ref.at[pl.ds(0, main)], own.at[0]),
        pltpu.make_async_copy(cot_send_ref.at[pl.ds(base, spare)], cot_rows_ref.at[pl.ds(base, spare)], own.at[1]),
    ]
    for copy in mine:
        copy.start()
    lane = iota((1, 128), 1)
    gain_one, shift_one, gain_two, shift_two = (row_of(r) for r in (gain_one_ref, shift_one_ref, gain_two_ref, shift_two_ref))

    def project(block, carry):
        rows = pl.ds(pl.multiple_of(block * BLK, BLK), BLK)
        hat, _ = norm_stats(x_ref[rows, :].astype(F32))
        normed = (hat * gain_one + shift_one).astype(BF16)
        normed_ref[rows, :] = normed
        q_ref[rows, :] = (nn(normed, wq_ref[...]).astype(BF16) * (HEAD_DIM ** (-0.5))).astype(BF16)
        k_ref[rows, :] = nn(normed, wk_ref[...]).astype(BF16)
        v_ref[rows, :] = nn(normed, wv_ref[...]).astype(BF16)
        return carry

    lax.fori_loop(0, blocks, project, 0)

    keep = iota((BLK, BLK), 0) <= iota((BLK, BLK), 1)

    def attend(pair, carry):
        cols = pl.ds(pl.multiple_of(pair * 128, 128), 128)
        k_pair = k_ref[:, cols]
        v_t = v_ref[:, cols].astype(F32).T.astype(BF16)
        k_head = [jnp.where(lane < 64, k_pair, 0), jnp.where(lane >= 64, k_pair, 0)]
        for block in range(blocks):
            span = (block + 1) * BLK
            query = q_ref[pl.ds(block * BLK, BLK), cols]
            outs = []
            for half in range(2):
                scores = nt(k_head[half][:span], query)
                diag = jnp.where(keep, scores[block * BLK :], -1000000000.0)
                scores = jnp.concatenate([scores[: block * BLK], diag], axis=0) if block else diag
                peak = jnp.max(scores, axis=0, keepdims=True)
                exps = jnp.exp(scores - peak)
                total = jnp.sum(exps, axis=0, keepdims=True)
                out = nn(v_t[half * 64 : half * 64 + 64, :span], exps.astype(BF16))
                outs.append(out * (1.0 / total))
                lse_ref[pair, half : half + 1, pl.ds(block * BLK, BLK)] = peak + jnp.log(total)
            mixed_ref[pl.ds(block * BLK, BLK), cols] = jnp.concatenate(outs, axis=0).T.astype(BF16)
        return carry

    lax.fori_loop(0, HEADS // 2, attend, 0)
    experts = router_ref.shape[0]

    def finish(block, carry):
        rows = pl.ds(pl.multiple_of(block * BLK, BLK), BLK)
        hidden = x_ref[rows, :].astype(F32) + nn(mixed_ref[rows, :], wo_ref[...])
        hidden_ref[rows, :] = hidden
        hat, _ = norm_stats(hidden)
        low = (hat * gain_two + shift_two).astype(BF16)
        routed[rows, :] = low
        logits = nt(low, router_ref[...])
        owner = slot_col_ref[rows, 64:65]
        logit = jnp.sum(jnp.where(iota((BLK, experts), 1) == owner, logits, 0.0), axis=1, keepdims=True)
        gate_ref[rows, :] = jnp.broadcast_to(jax.nn.sigmoid(logit), (BLK, 128))
        return carry

    lax.fori_loop(0, blocks, finish, 0)
    pack_rows(slot_row_ref[0:1, :], routed, send_ref)
    for copy in mine:
        copy.wait()
    for copy in copies + [gather(0)]:
        copy.wait()


def gelu_parts(v):
    size = jnp.abs(v)
    t = 1.0 / (1.0 + (0.3275911 * 0.7071067811865476) * size)
    bell = jnp.exp(-0.5 * (v * v))
    poly = ((((1.061405429 * t - 1.453152027) * t + 1.421413741) * t - 0.284496736) * t + 0.254829592) * t
    tail = 0.5 * poly * bell
    return jnp.where(v >= 0.0, 1.0 - tail, tail), bell * 0.3989422804014327


def expert_kernel(
    count,
    main,
    spare,
    chunk,
    counts_ref,
    send_ref,
    cot_send_ref,
    cot_rows_ref,
    router_ref,
    w1_hbm,
    w2_hbm,
    y_ref,
    back_ref,
    late_ref,
    gw1_ref,
    gw2_ref,
    w1_ref,
    w2_ref,
    acc1,
    acc2,
    x_rows,
    g_ref,
    dx_rows,
    y_rows,
    stage,
    load_sems,
    sends,
    recvs,
    spare_sends,
    spare_recvs,
    cot_sends,
    cot_recvs,
    back_sends,
    back_recvs,
    own,
    y_sems,
    stage_sems,
):
    width, hidden = w1_ref.shape
    slots = x_rows.shape[0]
    base = count * main
    plain = base // BLK
    blocks = slots // BLK
    depth = depth_of(count)
    early = count - count // 4
    me = lax.axis_index("expert")
    loads = [
        pltpu.make_async_copy(w1_hbm, w1_ref, load_sems.at[0]),
        pltpu.make_async_copy(w2_hbm, w2_ref, load_sems.at[1]),
        pltpu.make_async_copy(cot_rows_ref.at[pl.ds(0, base - main)], g_ref.at[pl.ds(0, base - main)], load_sems.at[2]),
        pltpu.make_async_copy(cot_rows_ref.at[pl.ds(base, 2 * spare)], g_ref.at[pl.ds(base, 2 * spare)], load_sems.at[3]),
    ]
    for load in loads:
        load.start()
    greet("expert", me, count)

    def gather(step):
        return gather_spare(me, count, base, spare, step, send_ref, x_rows, spare_sends, spare_recvs)

    def arrive(mask):
        return send_block(me, count, main, mask, send_ref, x_rows, sends, recvs)

    def leave(mask):
        return return_block(me, count, main, mask, dx_rows, back_ref, back_sends, back_recvs)

    def gather_cot(step):
        source = cot_rows_ref if step == 1 else g_ref
        have = spare << step
        return copy_to(
            source.at[pl.ds(base, have)],
            g_ref.at[pl.ds(base + have, have)],
            cot_sends.at[step],
            cot_recvs.at[step],
            {"expert": flip(me, count >> (step + 1), count)},
        )

    def last_cot():
        rows = span(flip(me, count - 1, count) * main, main)
        return copy_to(
            cot_send_ref.at[rows],
            g_ref.at[pl.ds(base - main, main)],
            cot_sends.at[0],
            cot_recvs.at[0],
            {"expert": flip(me, count - 1, count)},
        )

    gather_cot(1).start()
    gather(0).start()
    for mask in range(1, count):
        arrive(mask).start()
    last_cot().start()
    mine_in = [
        pltpu.make_async_copy(send_ref.at[span(me * main, main)], x_rows.at[pl.ds(0, main)], own.at[0]),
        pltpu.make_async_copy(send_ref.at[pl.ds(base, spare)], x_rows.at[pl.ds(base, spare)], own.at[1]),
    ]
    for copy in mine_in:
        copy.start()
    acc1[...] = jnp.zeros_like(acc1)
    acc2[...] = jnp.zeros_like(acc2)
    experts = router_ref.shape[0]
    router = jnp.sum(jnp.where(iota((experts, 1), 0) == me, router_ref[...].astype(F32), 0.0), axis=0, keepdims=True)
    hot = jnp.full((1, 128), counts_ref[0, me], jnp.int32)[:, 0:1] > main
    hot = jnp.where(hot, 1.0, 0.0)
    for copy in loads + mine_in:
        copy.wait()

    def store_y(block):
        rows = pl.ds(pl.multiple_of(block * BLK, BLK), BLK)
        return pltpu.make_async_copy(y_rows.at[rows], y_ref.at[rows], y_sems.at[block])

    def mine_out():
        return pltpu.make_async_copy(dx_rows.at[pl.ds(0, main)], back_ref.at[span(me * main, main)], own.at[0])

    def run(turn, carry):
        block = turn + turn // (plain - 1) - (turn // (blocks - 1)) * (blocks - plain + 1)
        for item in range(BLK // main + 1):
            mask = (block * BLK + main - 1) // main + item

            @pl.when((block < plain) & (mask > 0) & (mask < ((block + 1) * BLK + main - 1) // main))
            def _():
                arrive(mask).wait_recv()

            @pl.when((block == plain - 1) & (mask == count - 1))
            def _():
                last_cot().wait_recv()

        for step in range(depth):

            @pl.when(turn == (max(step + 1, plain - depth + step) if step else 1))
            def _():
                gather(step).wait_recv()
                if step:
                    gather_cot(step).wait_recv()
                if step + 1 < depth:
                    gather(step + 1).start()
                    if step:
                        gather_cot(step + 1).start()

        rows = pl.ds(pl.multiple_of(block * BLK, BLK), BLK)
        live = jnp.where(block < plain, 1.0, hot)
        x = (x_rows[rows, :].astype(F32) * live).astype(BF16)
        logit = jnp.sum(x.astype(F32) * router, axis=1, keepdims=True)
        gate = jax.nn.sigmoid(logit)
        go = g_ref[rows, :].astype(F32) * live
        g = (gate * go).astype(BF16)
        x_t = x.astype(F32).T.astype(BF16)
        y = jnp.zeros(x.shape, F32)
        dx = jnp.zeros(x.shape, F32)
        for first in range(0, hidden, chunk):
            cols = pl.ds(first, chunk)
            w1 = w1_ref[:, cols]
            w2 = w2_ref[cols, :]
            pre = nn(x, w1)
            cdf, pdf = gelu_parts(pre)
            act = (pre * cdf).astype(BF16)
            slope = cdf + pre * pdf
            y = y + nn(act, w2)
            grad = (nt(g, w2) * slope).astype(BF16)
            dx = dx + nt(grad, w1)
            acc1[:, cols] += nn(x_t, grad)
            acc2[cols, :] += tn(act, g)
        y_low = y.astype(BF16)
        y_rows[rows, :] = y_low
        dlogit = jnp.sum(y_low.astype(F32) * go, axis=1, keepdims=True) * gate * (1.0 - gate)
        dx_rows[rows, :] = (dx + dlogit * router).astype(BF16)
        store_y(block).start()
        for item in range(BLK // main + 1):
            mask = (block * BLK) // main + item
            done = (block < plain) & (mask < ((block + 1) * BLK) // main)

            @pl.when(done & (mask > 0) & (mask < early))
            def _():
                leave(mask).start()

            @pl.when(done & (mask == 0))
            def _():
                mine_out().start()

        return carry

    lax.fori_loop(0, blocks, run, 0)
    tail = pltpu.make_async_copy(dx_rows.at[pl.ds(early * main, slots - early * main)], late_ref, own.at[1])
    tail.start()

    pieces = []
    for first in range(0, hidden, stage.shape[1]):
        pieces.append((acc1.at[:, pl.ds(first, stage.shape[1])], gw1_ref.at[:, pl.ds(first, stage.shape[1])]))
    for first in range(0, hidden, stage.shape[1]):
        pieces.append((acc2.at[pl.ds(first, stage.shape[1]), :], gw2_ref.at[pl.ds(first, stage.shape[1]), :]))
    writes = []
    for index, (piece, target) in enumerate(pieces):
        slot = index % 2
        if index >= 2:
            writes[index - 2].wait()
        stage[slot] = piece[...].astype(BF16)
        write = pltpu.make_async_copy(stage.at[slot], target, stage_sems.at[slot])
        write.start()
        writes.append(write)
    for write in writes[-2:]:
        write.wait()
    mine_out().wait()
    tail.wait()

    def settle(block, carry):
        store_y(block).wait()
        return carry

    lax.fori_loop(0, blocks, settle, 0)
    for step in range(depth):
        gather(step).wait_send()
    for step in range(1, depth):
        gather_cot(step).wait_send()
    last_cot().wait_send()
    for mask in range(1, count):
        arrive(mask).wait_send()
    for mask in range(1, early):
        leave(mask).wait()


def backward_kernel(
    count,
    main,
    spare,
    group_ref,
    domain_ref,
    x_hbm,
    cot_hbm,
    gain_one_ref,
    gain_two_ref,
    wq_hbm,
    wk_hbm,
    wv_hbm,
    wo_hbm,
    slot_col_hbm,
    normed_hbm,
    q_hbm,
    k_hbm,
    v_hbm,
    mixed_hbm,
    lse_hbm,
    hidden_hbm,
    dx_hbm,
    late_ref,
    y_ref,
    grad_ref,
    dense_ref,
    vec_ref,
    y_back_ref,
    x_ref,
    cot_ref,
    wq_ref,
    wk_ref,
    wv_ref,
    wo_ref,
    slot_col_ref,
    normed_ref,
    q_ref,
    k_ref,
    v_ref,
    mixed_ref,
    lse_ref,
    hidden_ref,
    dx_ref,
    spare_dx,
    spare_y,
    dx_land,
    y_land,
    ghid,
    gmix,
    branch,
    normed_t,
    dqkv,
    sums,
    sends,
    recvs,
    late_sends,
    late_recvs,
    dx_sends,
    dx_recvs,
    y_sends,
    y_recvs,
    own,
    gets,
    fills,
):
    tokens, width = x_ref.shape
    me = lax.axis_index("expert")
    early = count - count // 4
    base = count * main
    late = (count - early) * main
    total = count * spare
    depth = depth_of(count)
    operands = [
        (x_hbm, x_ref),
        (cot_hbm, cot_ref),
        (wq_hbm, wq_ref),
        (wk_hbm, wk_ref),
        (wv_hbm, wv_ref),
        (wo_hbm, wo_ref),
        (slot_col_hbm, slot_col_ref),
        (normed_hbm, normed_ref),
        (q_hbm, q_ref),
        (k_hbm, k_ref),
        (v_hbm, v_ref),
        (mixed_hbm, mixed_ref),
        (lse_hbm, lse_ref),
        (hidden_hbm, hidden_ref),
    ]
    operands = [pltpu.make_async_copy(source, target, fills.at[i]) for i, (source, target) in enumerate(operands)]
    for copy in operands:
        copy.start()
    greet("expert", me, count)

    def sum_dx(step):
        if step == depth - 1:
            return return_spare(me, count, spare, step, late_ref, late, dx_land, dx_sends, dx_recvs)
        return return_spare(me, count, spare, step, spare_dx, 0, dx_land, dx_sends, dx_recvs)

    def sum_y(step):
        if step == depth - 1:
            return return_spare(me, count, spare, step, y_ref, base, y_land, y_sends, y_recvs)
        return return_spare(me, count, spare, step, spare_y, 0, y_land, y_sends, y_recvs)

    def settle(copy, kept, landing, step):
        copy.wait()
        half = spare << step
        kept[0:half, :] = (kept[0:half, :].astype(F32) + landing[half : 2 * half, :].astype(F32)).astype(BF16)

    sum_dx(depth - 1).start()
    lates = [return_block(me, count, main, mask, late_ref, dx_ref, late_sends, late_recvs, early) for mask in range(early, count)]
    for copy in lates:
        copy.start()
    copies = [return_block(me, count, main, mask, y_ref, y_back_ref, sends, recvs) for mask in range(1, count)]
    mine = pltpu.make_async_copy(y_ref.at[pl.ds(0, main)], y_back_ref.at[span(me * main, main)], own.at[0])
    mine.start()
    loads = [
        pltpu.make_async_copy(late_ref.at[pl.ds(late, total)], spare_dx, own.at[1]),
        pltpu.make_async_copy(y_ref.at[pl.ds(base, total)], spare_y, own.at[2]),
    ]
    for mask in range(early):
        part = span(flip(me, mask, count) * main, main)
        loads.append(pltpu.make_async_copy(dx_hbm.at[part], dx_ref.at[part], gets.at[mask]))
    for load in loads:
        load.start()
    for load in loads:
        load.wait()
    for step in reversed(range(depth)):
        settle(sum_dx(step), spare_dx, dx_land, step)
        if step:
            sum_dx(step - 1).start()
    dx_ref[pl.ds(base, BLK), :] = spare_dx[0:BLK, :]
    for copy in lates:
        copy.wait()
    sum_y(depth - 1).start()
    for copy in copies:
        copy.start()
    for copy in operands:
        copy.wait()
    slots = dx_ref.shape[0]
    blocks = tokens // BLK
    lane = iota((1, 128), 1)
    weight = domain_weight(group_ref, domain_ref)
    gain_one = row_of(gain_one_ref)
    gain_two = row_of(gain_two_ref)
    sums[...] = jnp.zeros_like(sums)

    def open_block(block, carry):
        rows = pl.ds(pl.multiple_of(block * BLK, BLK), BLK)
        slot = slot_col_ref[rows, 0:1]
        pick = jnp.where(iota((BLK, slots), 1) == slot, 1.0, 0.0).astype(BF16)
        grad = nn(pick, dx_ref[...])
        hat, rstd = norm_stats(hidden_ref[rows, :])
        sums[2:3, :] += jnp.sum(grad * hat, axis=0, keepdims=True)
        sums[3:4, :] += jnp.sum(grad, axis=0, keepdims=True)
        gg = grad * gain_two
        inner = gg - jnp.mean(gg, axis=1, keepdims=True) - hat * jnp.mean(gg * hat, axis=1, keepdims=True)
        total = cot_ref[rows, :].astype(F32) * weight + rstd * inner
        ghid[rows, :] = total
        low = total.astype(BF16)
        branch[rows, :] = low
        gmix[rows, :] = nt(low, wo_ref[...]).astype(BF16)
        normed_t[:, rows] = normed_ref[rows, :].astype(F32).T.astype(BF16)
        return carry

    lax.fori_loop(0, blocks, open_block, 0)
    dense_ref[pl.ds(3 * width, width), :] = tn(mixed_ref[...], branch[...]).astype(BF16)
    settle(sum_y(depth - 1), spare_y, y_land, depth - 1)
    sum_y(depth - 2).start()

    keep = iota((BLK, BLK), 0) <= iota((BLK, BLK), 1)

    def attend(pair, carry):
        base = pl.multiple_of(pair * 128, 128)
        cols = pl.ds(base, 128)
        q_pair = q_ref[:, cols]
        k_pair = k_ref[:, cols]
        v_pair = v_ref[:, cols]
        o_pair = gmix[:, cols]
        low = lane < 64
        q_head = [jnp.where(low, q_pair, 0), jnp.where(low, 0, q_pair)]
        k_head = [jnp.where(low, k_pair, 0), jnp.where(low, 0, k_pair)]
        v_head = [jnp.where(low, v_pair, 0), jnp.where(low, 0, v_pair)]
        o_head = [jnp.where(low, o_pair, 0), jnp.where(low, 0, o_pair)]
        k_t = k_pair.astype(F32).T.astype(BF16)
        prod_t = (o_pair.astype(F32) * mixed_ref[:, cols].astype(F32)).T
        delta = [jnp.sum(prod_t[:64], axis=0, keepdims=True), jnp.sum(prod_t[64:], axis=0, keepdims=True)]
        dq_t = [[None] * blocks, [None] * blocks]
        for block in range(blocks):
            start = block * BLK
            dk = None
            dv = None
            for half in range(2):
                scores = nt(k_head[half][start : start + BLK], q_pair[start:])
                diag = jnp.where(keep, scores[:, :BLK], -1000000000.0)
                scores = jnp.concatenate([diag, scores[:, BLK:]], axis=1) if block < blocks - 1 else diag
                probs = jnp.exp(scores - lse_ref[pair, half : half + 1, pl.ds(start, tokens - start)])
                grad_p = nt(v_head[half][start : start + BLK], o_pair[start:])
                grad_s = (probs * (grad_p - delta[half][:, start:])).astype(BF16)
                dv_part = nn(probs.astype(BF16), o_head[half][start:])
                dk_part = nn(grad_s, q_head[half][start:])
                dv = dv_part if dv is None else dv + dv_part
                dk = dk_part if dk is None else dk + dk_part
                dq_part = nn(k_t[half * 64 : half * 64 + 64, start : start + BLK], grad_s)
                for later in range(block, blocks):
                    piece = dq_part[:, (later - block) * BLK : (later - block + 1) * BLK]
                    dq_t[half][later] = piece if dq_t[half][later] is None else dq_t[half][later] + piece
            rows = pl.ds(start, BLK)
            dqkv[rows, pl.ds(pl.multiple_of(base + width, 128), 128)] = dk.astype(BF16)
            dqkv[rows, pl.ds(pl.multiple_of(base + 2 * width, 128), 128)] = dv.astype(BF16)
        for block in range(blocks):
            both = jnp.concatenate([dq_t[0][block], dq_t[1][block]], axis=0) * (HEAD_DIM ** (-0.5))
            dqkv[pl.ds(block * BLK, BLK), cols] = both.T.astype(BF16)
        return carry

    lax.fori_loop(0, HEADS // 2, attend, 0)

    for part in range(3):
        dense_ref[pl.ds(part * width, width), :] = nn(normed_t[...], dqkv[:, pl.ds(part * width, width)]).astype(BF16)

    def close_block(block, carry):
        rows = pl.ds(pl.multiple_of(block * BLK, BLK), BLK)
        grad = nt(dqkv[rows, 0:width], wq_ref[...])
        grad = grad + nt(dqkv[rows, width : 2 * width], wk_ref[...])
        grad = grad + nt(dqkv[rows, 2 * width : 3 * width], wv_ref[...])
        hat, rstd = norm_stats(x_ref[rows, :].astype(F32))
        sums[0:1, :] += jnp.sum(grad * hat, axis=0, keepdims=True)
        sums[1:2, :] += jnp.sum(grad, axis=0, keepdims=True)
        gg = grad * gain_one
        inner = gg - jnp.mean(gg, axis=1, keepdims=True) - hat * jnp.mean(gg * hat, axis=1, keepdims=True)
        grad_ref[rows, :] = (ghid[rows, :] + rstd * inner).astype(BF16)
        return carry

    lax.fori_loop(0, blocks, close_block, 0)
    vec_ref[...] = sums[...]
    for step in reversed(range(depth - 1)):
        settle(sum_y(step), spare_y, y_land, step)
        if step:
            sum_y(step - 1).start()
    spare_out = pltpu.make_async_copy(spare_y.at[pl.ds(0, BLK)], y_back_ref.at[pl.ds(base, BLK)], own.at[1])
    spare_out.start()
    spare_out.wait()
    mine.wait()
    for copy in copies:
        copy.wait()


def halving_plan(dp, count, rows):
    experts = [("expert", 2 << bit) for bit in range(depth_of(count) - 1)]
    groups = [("dp", 1 << bit) for bit in range(depth_of(dp))]
    core = [("expert", 1)]
    plans = [core + groups + experts, core + experts + groups]
    halvings = 0
    while halvings < len(plans[0]) and (rows >> halvings) % 32 == 0:
        halvings += 1
    return plans, halvings


def finish_kernel(
    dp,
    count,
    dense_ref,
    vec_ref,
    slot_col_ref,
    hidden_ref,
    gate_ref,
    y_ref,
    out_ref,
    full_ref,
    total_ref,
    acc,
    landing,
    full,
    vec_acc,
    vec_land,
    sends,
    recvs,
    back_sends,
    back_recvs,
    vec_sends,
    vec_recvs,
    put,
):
    tokens, width = hidden_ref.shape
    slots = y_ref.shape[0]
    rows = dense_ref.shape[0] // 2
    place = {"dp": lax.axis_index("dp"), "expert": lax.axis_index("expert")}
    size = {"dp": dp, "expert": count}
    plans, halvings = halving_plan(dp, count, rows)
    steps = len(plans[0])

    def partner(axis, mask):
        return {axis: flip(place[axis], mask, size[axis])}

    barrier = pltpu.get_barrier_semaphore()
    for axis, mask in plans[0]:
        pl.semaphore_signal(barrier, inc=1, device_id=partner(axis, mask), device_id_type=MESH)
    pl.semaphore_wait(barrier, steps)

    def side(axis, mask):
        return (place[axis] // mask) % 2

    def combine(block):
        rows_at = pl.ds(block * BLK, BLK)
        slot = slot_col_ref[rows_at, 0:1]
        pick = jnp.where(iota((BLK, slots), 1) == slot, 1.0, 0.0).astype(BF16)
        returned = nn(pick, y_ref[...])
        out_ref[rows_at, :] = (hidden_ref[rows_at, :] + gate_ref[rows_at, 0:1] * returned).astype(BF16)

    todo = list(range(tokens // BLK))
    low = [jnp.int32(stream * rows) for stream in range(2)]
    extent = rows
    offset = 0
    trail = []
    for step in range(steps):
        halve = step < halvings
        part = extent // 2 if halve else extent
        copies = []
        for stream in range(2):
            axis, mask = plans[stream][step]
            mine = low[stream] + side(axis, mask) * part if halve else low[stream]
            other = low[stream] + (1 - side(axis, mask)) * part if halve else low[stream]
            source = dense_ref if step == 0 else acc.at[(step - 1) % 2]
            land = landing.at[stream, pl.ds(offset, part)]
            copy = copy_to(
                source.at[span(other, part)], land, sends.at[stream, step], recvs.at[stream, step], partner(axis, mask)
            )
            copy.start()
            copies.append((copy, mine, source))
        axis, mask = plans[0][step]
        vec_source = vec_ref if step == 0 else vec_acc.at[step - 1]
        vec_copy = copy_to(vec_source, vec_land.at[step], vec_sends.at[step], vec_recvs.at[step], partner(axis, mask))
        vec_copy.start()
        if step in (1, 2):
            for block in todo[: tokens // BLK // 4]:
                combine(block)
            todo = todo[tokens // BLK // 4 :]
        trail.append((list(low), extent))
        for stream in range(2):
            copy, mine, source = copies[stream]
            copy.wait()
            held = span(mine, part)
            kept = source[held, :].astype(F32) + landing[stream, pl.ds(offset, part), :].astype(F32)
            if step < steps - 1:
                acc[step % 2, held, :] = kept.astype(BF16)
            else:
                full[held, :] = kept.astype(BF16)
            low[stream] = mine
        vec_copy.wait()
        vec_sum = vec_source[...] + vec_land[step]
        if step < steps - 1:
            vec_acc[step] = vec_sum
        else:
            total_ref[...] = vec_sum
        extent = part
        offset += part

    for step in reversed(range(halvings)):
        starts, whole = trail[step]
        copies = []
        for stream in range(2):
            axis, mask = plans[stream][step]
            held = span(low[stream], extent)
            copy = copy_to(
                full.at[held], full.at[held], back_sends.at[stream, step], back_recvs.at[stream, step], partner(axis, mask)
            )
            copy.start()
            copies.append(copy)
        if step in (1, 2):
            for block in todo if step == 1 else todo[: tokens // BLK // 4]:
                combine(block)
            todo = todo[tokens // BLK // 4 :]
        for stream in range(2):
            copies[stream].wait()
            low[stream] = starts[stream]
        extent = whole
    write = pltpu.make_async_copy(full, full_ref, put)
    write.start()
    write.wait()


def call(kernel, outs, in_specs, scratch, name, out_specs=None, collective=None, flops=10**9):
    remote = {} if collective is None else {"collective_id": collective, "has_side_effects": True}
    return pl.pallas_call(
        kernel,
        out_shape=outs,
        in_specs=in_specs,
        out_specs=out_specs or [VMEM] * len(outs),
        scratch_shapes=scratch,
        compiler_params=pltpu.CompilerParams(vmem_limit_bytes=LIMIT, **remote),
        cost_estimate=pl.CostEstimate(flops=flops, bytes_accessed=10**7, transcendentals=0),
        name=name,
    )


def dma(*dims):
    return pltpu.SemaphoreType.DMA(dims)


def shape(dims, kind):
    return jax.ShapeDtypeStruct(dims, kind)


def tables(experts, main, slots, counts, group, domains, sort_order, cotangent):
    tokens, width = cotangent.shape
    return call(
        functools.partial(table_kernel, experts, main),
        [shape((slots, width), BF16), shape((tokens, 128), jnp.int32), shape((8, tokens), jnp.int32)],
        [SMEM, SMEM, SMEM, VMEM, VMEM],
        [pltpu.VMEM((tokens, width), BF16)],
        "tables",
    )(counts, group, domains, sort_order, cotangent)


def forward(count, main, spare, inputs, g1, s1, g2, s2, wq, wk, wv, wo, router, slot_col, slot_row, cot_send):
    tokens, width = inputs.shape
    rows_low = shape((tokens, width), BF16)
    return call(
        functools.partial(forward_kernel, count, main, spare),
        [
            rows_low,
            rows_low,
            rows_low,
            rows_low,
            rows_low,
            shape((HEADS // 2, 8, tokens), F32),
            shape((tokens, width), F32),
            shape((tokens, 128), F32),
            shape(cot_send.shape, BF16),
            shape((count * (main + spare), width), BF16),
        ],
        [VMEM] * 12 + [ANY],
        [pltpu.VMEM((tokens, width), BF16), dma(count), dma(count), dma(depth_of(count)), dma(depth_of(count)), dma(2)],
        "dense_forward",
        [VMEM] * 9 + [ANY],
        1,
    )(inputs, g1, s1, g2, s2, wq, wk, wv, wo, router, slot_col, slot_row, cot_send)


def expert_block(count, main, spare, counts, send, cot_send, cot_rows, router_t, w1, w2, chunk=768):
    slots, width = cot_rows.shape
    hidden = w1.shape[1]
    late = slots - (count - count // 4) * main
    rows = shape((slots, width), BF16)
    keep = pltpu.VMEM((slots, width), BF16)
    depth = depth_of(count)
    return call(
        functools.partial(expert_kernel, count, main, spare, chunk),
        [
            rows,
            shape((count * main, width), BF16),
            shape((late, width), BF16),
            shape((width, hidden), BF16),
            shape((hidden, width), BF16),
        ],
        [SMEM, ANY, ANY, ANY, VMEM, ANY, ANY],
        [
            pltpu.VMEM((width, hidden), BF16),
            pltpu.VMEM((hidden, width), BF16),
            pltpu.VMEM((width, hidden), F32),
            pltpu.VMEM((hidden, width), F32),
            keep,
            keep,
            keep,
            keep,
            pltpu.VMEM((2, width, width), BF16),
            dma(4),
            dma(count),
            dma(count),
            dma(depth),
            dma(depth),
            dma(depth),
            dma(depth),
            dma(count),
            dma(count),
            dma(2),
            dma(slots // BLK),
            dma(2),
        ],
        "expert",
        [ANY] * 5,
        2,
    )(counts, send, cot_send, cot_rows, router_t, w1, w2)


def backward(
    count, main, spare, group, domains, inputs, cotangent, g1, g2, wq, wk, wv, wo, slot_col, normed, q, k, v, mixed, lse, hidden, dx, late, y
):
    tokens, width = inputs.shape
    return call(
        functools.partial(backward_kernel, count, main, spare),
        [shape((tokens, width), BF16), shape((4 * width, width), BF16), shape((8, width), F32), shape((count * main + BLK, width), BF16)],
        [SMEM] * 2 + [ANY] * 2 + [VMEM] * 2 + [ANY] * 15,
        [pltpu.VMEM(v.shape, v.dtype) for v in (inputs, cotangent, wq, wk, wv, wo, slot_col, normed, q, k, v, mixed, lse, hidden)]
        + [
            pltpu.VMEM((count * main + BLK, width), BF16),
            pltpu.VMEM((count * spare, width), BF16),
            pltpu.VMEM((count * spare, width), BF16),
            pltpu.VMEM((count * spare, width), BF16),
            pltpu.VMEM((count * spare, width), BF16),
            pltpu.VMEM((tokens, width), F32),
            pltpu.VMEM((tokens, width), BF16),
            pltpu.VMEM((tokens, width), BF16),
            pltpu.VMEM((width, tokens), BF16),
            pltpu.VMEM((tokens, 3 * width), BF16),
            pltpu.VMEM((8, width), F32),
            dma(count),
            dma(count),
            dma(count),
            dma(count),
            dma(depth_of(count)),
            dma(depth_of(count)),
            dma(depth_of(count)),
            dma(depth_of(count)),
            dma(3),
            dma(count),
            dma(14),
        ],
        "dense_backward",
        [VMEM, VMEM, VMEM, ANY],
        3,
        5 * 10**10,
    )(group, domains, inputs, cotangent, g1, g2, wq, wk, wv, wo, slot_col, normed, q, k, v, mixed, lse, hidden, dx, late, y)


def finish(dp, count, dense, vec, slot_col, hidden, gate, y_back):
    width = hidden.shape[1]
    rows = dense.shape[0]
    steps = len(halving_plan(dp, count, rows // 2)[0][0])
    return call(
        functools.partial(finish_kernel, dp, count),
        [shape(hidden.shape, BF16), shape(dense.shape, BF16), shape(vec.shape, F32)],
        [VMEM] * 6,
        [
            pltpu.VMEM((2, rows, width), BF16),
            pltpu.VMEM((2, rows, width), BF16),
            pltpu.VMEM((rows, width), BF16),
            pltpu.VMEM((steps,) + vec.shape, F32),
            pltpu.VMEM((steps,) + vec.shape, F32),
            dma(2, steps),
            dma(2, steps),
            dma(2, steps),
            dma(2, steps),
            dma(steps),
            dma(steps),
            dma(),
        ],
        "finish",
        [VMEM, ANY, VMEM],
        4,
    )(dense, vec, slot_col, hidden, gate, y_back)


def local(
    inputs,
    cotangent,
    seq_group,
    domain_counts,
    sort_order,
    send_counts,
    gain_one,
    shift_one,
    gain_two,
    shift_two,
    w_query,
    w_key,
    w_value,
    w_out,
    router,
    expert_in,
    expert_out,
):
    tokens, width = inputs.shape
    experts = send_counts.shape[1]
    capacity = 2 * tokens // experts
    spare = capacity // 4
    main = capacity - spare
    slots = experts * main + BLK
    count = lax.axis_size("expert")
    g1, s1, g2, s2 = gain_one, shift_one, gain_two, shift_two
    router_t = router.T
    cot_send, slot_col, slot_row = tables(experts, main, slots, send_counts, seq_group, domain_counts, sort_order, cotangent)
    normed, q, k, v, mixed, lse, hidden, gate, send, cot_rows = forward(
        count, main, spare, inputs, g1, s1, g2, s2, w_query, w_key, w_value, w_out, router_t, slot_col, slot_row, cot_send
    )
    y_rows, dx_back, dx_late, grad_first, grad_second = expert_block(
        count, main, spare, send_counts, send, cot_send, cot_rows, router_t, expert_in[0], expert_out[0]
    )
    expert_sums = (lax.psum(grad_first, "dp").astype(F32), lax.psum(grad_second, "dp").astype(F32))
    grad_inputs, dense, vec, y_back = backward(
        count, main, spare, seq_group, domain_counts, inputs, cotangent, g1, g2, w_query, w_key, w_value, w_out, slot_col,
        normed, q, k, v, mixed, lse, hidden, dx_back, dx_late, y_rows,
    )
    output, dense, vec = finish(lax.axis_size("dp"), count, dense, vec, slot_col, hidden, gate, y_back)
    dense = dense.astype(F32)
    parts = [dense[i * width : (i + 1) * width] for i in range(4)]
    vecs = [vec[i] for i in range(4)]
    return (
        output,
        grad_inputs,
        *vecs,
        *parts,
        expert_sums[0][None],
        expert_sums[1][None],
    )


def solution(mesh):
    rows = P(("dp", "expert"), None)
    split = P("expert", None, None)
    return jax.shard_map(
        local,
        mesh=mesh,
        in_specs=(rows, rows, P(("dp", "expert")), P(), rows, rows) + (P(),) * 9 + (split, split),
        out_specs=(rows, rows) + (P(),) * 8 + (split, split),
        check_vma=False,
    )
```

```python
import functools

import jax
import jax.numpy as jnp
from jax import lax
from jax.experimental import pallas as pl
from jax.experimental.pallas import tpu as pltpu
from jax.sharding import PartitionSpec as P

HEADS = 12
HEAD_DIM = 64
LEN = 1024
EPS = 1e-05
F32 = jnp.float32
BF16 = jnp.bfloat16
BLK = 256
CODE = 4096
LIMIT = 60 * 1024 * 1024

VMEM = pl.BlockSpec(memory_space=pltpu.VMEM)
SMEM = pl.BlockSpec(memory_space=pltpu.SMEM)
ANY = pl.BlockSpec(memory_space=pl.ANY)
MESH = pl.DeviceIdType.MESH


def dot(left, right, contract):
    return lax.dot_general(left, right, ((contract[0:1], contract[1:2]), ((), ())), preferred_element_type=F32)


def nn(left, right):
    return dot(left, right, (1, 0))


def nt(left, right):
    return dot(left, right, (1, 1))


def tn(left, right):
    return dot(left, right, (0, 0))


def iota(shape, axis):
    return lax.broadcasted_iota(jnp.int32, shape, axis)


def flip(index, mask, count):
    bit, out = 1, 0
    while bit < count:
        out = out + ((index // bit + mask // bit) % 2) * bit
        bit *= 2
    return out


def greet(axis, me, count):
    barrier = pltpu.get_barrier_semaphore()
    for mask in range(1, count):
        pl.semaphore_signal(barrier, inc=1, device_id={axis: flip(me, mask, count)}, device_id_type=MESH)
    pl.semaphore_wait(barrier, count - 1)


def copy_to(source, target, send, recv, device):
    return pltpu.make_async_remote_copy(
        src_ref=source, dst_ref=target, send_sem=send, recv_sem=recv, device_id=device, device_id_type=MESH
    )


def span(start, rows):
    return pl.ds(pl.multiple_of(start, 16), rows)


def send_block(me, count, rows, mask, source, target, sends, recvs):
    peer = flip(me, mask, count)
    return copy_to(
        source.at[span(peer * rows, rows)], target.at[span(mask * rows, rows)], sends.at[mask], recvs.at[mask], {"expert": peer}
    )


def return_block(me, count, rows, mask, source, target, sends, recvs, shift=0):
    return copy_to(
        source.at[span((mask - shift) * rows, rows)],
        target.at[span(me * rows, rows)],
        sends.at[mask],
        recvs.at[mask],
        {"expert": flip(me, mask, count)},
    )


def dp_sides():
    index = lax.axis_index("dp")
    return index, (index % 2, (index // 2) % 2)


def sum_rows(target, other, rows):
    def step(block, carry):
        part = pl.ds(pl.multiple_of(block * BLK, BLK), BLK)
        target[part, :] = (target[part, :].astype(F32) + other[part, :].astype(F32)).astype(BF16)
        return carry

    lax.fori_loop(0, rows // BLK, step, 0)


def depth_of(count):
    return count.bit_length() - 1


def gather_spare(me, count, base, rows, step, first, target, sends, recvs):
    have = rows << step
    source = first.at[pl.ds(base, rows)] if step == 0 else target.at[pl.ds(base, have)]
    return copy_to(
        source,
        target.at[pl.ds(base + have, have)],
        sends.at[step],
        recvs.at[step],
        {"expert": flip(me, count >> (step + 1), count)},
    )


def return_spare(me, count, rows, step, source, shift, landing, sends, recvs):
    half = rows << step
    return copy_to(
        source.at[pl.ds(shift + half, half)],
        landing.at[pl.ds(half, half)],
        sends.at[step],
        recvs.at[step],
        {"expert": flip(me, count >> (step + 1), count)},
    )


def row_of(ref):
    return ref[...].reshape(1, ref.shape[0])


def domain_weight(group_ref, counts_ref):
    groups = counts_ref.shape[0]
    group = group_ref[0]
    total = jnp.zeros((1, 128), F32)
    mine = jnp.zeros((1, 128), F32)
    for index in range(groups):
        inverse = 1.0 / jnp.full((1, 128), counts_ref[index], jnp.int32).astype(F32)
        total = total + inverse
        mine = mine + jnp.where(group == index, inverse, 0.0)
    return (mine / (total / groups))[:, 0:1]


def norm_stats(rows):
    center = rows - jnp.mean(rows, axis=-1, keepdims=True)
    rstd = lax.rsqrt(jnp.mean(center * center, axis=-1, keepdims=True) + EPS)
    return center * rstd, rstd


def pack_rows(slot_row, rows_ref, send_ref):
    slots = send_ref.shape[0]
    tokens = rows_ref.shape[0]

    def step(block, carry):
        base = pl.multiple_of(block * BLK, BLK)
        slot = iota((BLK, tokens), 0) + base
        pick = jnp.where(slot == slot_row, 1.0, 0.0).astype(BF16)
        send_ref[pl.ds(base, BLK), :] = nn(pick, rows_ref[...]).astype(BF16)
        return carry

    lax.fori_loop(0, slots // BLK, step, 0)


def table_kernel(experts, main, counts_ref, group_ref, domain_ref, sort_ref, cot_ref, send_ref, slot_col_ref, slot_row_ref, scaled):
    tokens = cot_ref.shape[0]
    place = iota((1, tokens), 1)
    expert_at = jnp.zeros((1, tokens), jnp.int32)
    start_at = jnp.zeros((1, tokens), jnp.int32)
    end = jnp.int32(0)
    for expert in range(experts):
        count = counts_ref[0, expert]
        end = end + count
        past = place >= end
        expert_at = expert_at + jnp.where(past, 1, 0)
        start_at = start_at + jnp.where(past, count, 0)
    slot = place - start_at
    dest = jnp.where(slot < main, expert_at * main + slot, (experts - 1) * main + slot)
    code = (expert_at * CODE + dest).astype(F32)
    sort_row = sort_ref[...]
    scaled[...] = (cot_ref[...].astype(F32) * domain_weight(group_ref, domain_ref)).astype(BF16)
    for block in range(tokens // BLK):
        token = iota((BLK, tokens), 0) + block * BLK
        col = jnp.sum(jnp.where(token == sort_row, code, 0.0), axis=1, keepdims=True)
        owner = (col * (1.0 / CODE)).astype(jnp.int32)
        where = col.astype(jnp.int32) - owner * CODE
        slot_col_ref[pl.ds(block * BLK, BLK), :] = jnp.where(iota((1, 128), 1) < 64, where, owner)
        slot_row_ref[:, pl.ds(block * BLK, BLK)] = jnp.broadcast_to(where, (BLK, 128)).astype(F32).T[0:8].astype(jnp.int32)
    pack_rows(slot_row_ref[0:1, :], scaled, send_ref)


def forward_kernel(
    count,
    main,
    spare,
    x_ref,
    gain_one_ref,
    shift_one_ref,
    gain_two_ref,
    shift_two_ref,
    wq_ref,
    wk_ref,
    wv_ref,
    wo_ref,
    router_ref,
    slot_col_ref,
    slot_row_ref,
    cot_send_ref,
    normed_ref,
    q_ref,
    k_ref,
    v_ref,
    mixed_ref,
    lse_ref,
    hidden_ref,
    gate_ref,
    send_ref,
    cot_rows_ref,
    routed,
    sends,
    recvs,
    spare_sends,
    spare_recvs,
    own,
):
    tokens, width = x_ref.shape
    blocks = tokens // BLK
    me = lax.axis_index("expert")
    greet("expert", me, count)
    base = count * main

    def gather(step):
        return gather_spare(me, count, base, spare, step, cot_send_ref, cot_rows_ref, spare_sends, spare_recvs)

    gather(0).start()
    copies = [send_block(me, count, main, mask, cot_send_ref, cot_rows_ref, sends, recvs) for mask in range(1, count - 1)]
    for copy in copies:
        copy.start()
    mine = [
        pltpu.make_async_copy(cot_send_ref.at[span(me * main, main)], cot_rows_ref.at[pl.ds(0, main)], own.at[0]),
        pltpu.make_async_copy(cot_send_ref.at[pl.ds(base, spare)], cot_rows_ref.at[pl.ds(base, spare)], own.at[1]),
    ]
    for copy in mine:
        copy.start()
    lane = iota((1, 128), 1)
    gain_one, shift_one, gain_two, shift_two = (row_of(r) for r in (gain_one_ref, shift_one_ref, gain_two_ref, shift_two_ref))

    def project(block, carry):
        rows = pl.ds(pl.multiple_of(block * BLK, BLK), BLK)
        hat, _ = norm_stats(x_ref[rows, :].astype(F32))
        normed = (hat * gain_one + shift_one).astype(BF16)
        normed_ref[rows, :] = normed
        q_ref[rows, :] = (nn(normed, wq_ref[...]).astype(BF16) * (HEAD_DIM ** (-0.5))).astype(BF16)
        k_ref[rows, :] = nn(normed, wk_ref[...]).astype(BF16)
        v_ref[rows, :] = nn(normed, wv_ref[...]).astype(BF16)
        return carry

    lax.fori_loop(0, blocks, project, 0)

    keep = iota((BLK, BLK), 0) <= iota((BLK, BLK), 1)

    def attend(pair, carry):
        cols = pl.ds(pl.multiple_of(pair * 128, 128), 128)
        k_pair = k_ref[:, cols]
        v_t = v_ref[:, cols].astype(F32).T.astype(BF16)
        k_head = [jnp.where(lane < 64, k_pair, 0), jnp.where(lane >= 64, k_pair, 0)]
        for block in range(blocks):
            span = (block + 1) * BLK
            query = q_ref[pl.ds(block * BLK, BLK), cols]
            outs = []
            for half in range(2):
                scores = nt(k_head[half][:span], query)
                diag = jnp.where(keep, scores[block * BLK :], -1000000000.0)
                scores = jnp.concatenate([scores[: block * BLK], diag], axis=0) if block else diag
                peak = jnp.max(scores, axis=0, keepdims=True)
                exps = jnp.exp(scores - peak)
                total = jnp.sum(exps, axis=0, keepdims=True)
                out = nn(v_t[half * 64 : half * 64 + 64, :span], exps.astype(BF16))
                outs.append(out * (1.0 / total))
                lse_ref[pair, half : half + 1, pl.ds(block * BLK, BLK)] = peak + jnp.log(total)
            mixed_ref[pl.ds(block * BLK, BLK), cols] = jnp.concatenate(outs, axis=0).T.astype(BF16)
        return carry

    lax.fori_loop(0, HEADS // 2, attend, 0)
    experts = router_ref.shape[0]

    def finish(block, carry):
        rows = pl.ds(pl.multiple_of(block * BLK, BLK), BLK)
        hidden = x_ref[rows, :].astype(F32) + nn(mixed_ref[rows, :], wo_ref[...])
        hidden_ref[rows, :] = hidden
        hat, _ = norm_stats(hidden)
        low = (hat * gain_two + shift_two).astype(BF16)
        routed[rows, :] = low
        logits = nt(low, router_ref[...])
        owner = slot_col_ref[rows, 64:65]
        logit = jnp.sum(jnp.where(iota((BLK, experts), 1) == owner, logits, 0.0), axis=1, keepdims=True)
        gate_ref[rows, :] = jnp.broadcast_to(jax.nn.sigmoid(logit), (BLK, 128))
        return carry

    lax.fori_loop(0, blocks, finish, 0)
    pack_rows(slot_row_ref[0:1, :], routed, send_ref)
    for copy in mine:
        copy.wait()
    for copy in copies + [gather(0)]:
        copy.wait()


def gelu_parts(v):
    size = jnp.abs(v)
    t = 1.0 / (1.0 + (0.3275911 * 0.7071067811865476) * size)
    bell = jnp.exp(-0.5 * (v * v))
    poly = ((((1.061405429 * t - 1.453152027) * t + 1.421413741) * t - 0.284496736) * t + 0.254829592) * t
    tail = 0.5 * poly * bell
    return jnp.where(v >= 0.0, 1.0 - tail, tail), bell * 0.3989422804014327


def expert_kernel(
    count,
    main,
    spare,
    chunk,
    counts_ref,
    send_ref,
    cot_send_ref,
    cot_rows_ref,
    router_ref,
    w1_hbm,
    w2_hbm,
    y_ref,
    back_ref,
    late_ref,
    grads_ref,
    w1_ref,
    w2_ref,
    acc1,
    acc2,
    x_rows,
    g_ref,
    dx_rows,
    y_rows,
    stage,
    load_sems,
    sends,
    recvs,
    spare_sends,
    spare_recvs,
    cot_sends,
    cot_recvs,
    back_sends,
    back_recvs,
    own,
    y_sems,
    stage_sems,
):
    width, hidden = w1_ref.shape
    slots = x_rows.shape[0]
    base = count * main
    plain = base // BLK
    blocks = slots // BLK
    depth = depth_of(count)
    early = count - count // 4
    me = lax.axis_index("expert")
    loads = [
        pltpu.make_async_copy(w1_hbm, w1_ref, load_sems.at[0]),
        pltpu.make_async_copy(w2_hbm, w2_ref, load_sems.at[1]),
        pltpu.make_async_copy(cot_rows_ref.at[pl.ds(0, base - main)], g_ref.at[pl.ds(0, base - main)], load_sems.at[2]),
        pltpu.make_async_copy(cot_rows_ref.at[pl.ds(base, 2 * spare)], g_ref.at[pl.ds(base, 2 * spare)], load_sems.at[3]),
    ]
    for load in loads:
        load.start()
    greet("expert", me, count)

    def gather(step):
        return gather_spare(me, count, base, spare, step, send_ref, x_rows, spare_sends, spare_recvs)

    def arrive(mask):
        return send_block(me, count, main, mask, send_ref, x_rows, sends, recvs)

    def leave(mask):
        return return_block(me, count, main, mask, dx_rows, back_ref, back_sends, back_recvs)

    def gather_cot(step):
        source = cot_rows_ref if step == 1 else g_ref
        have = spare << step
        return copy_to(
            source.at[pl.ds(base, have)],
            g_ref.at[pl.ds(base + have, have)],
            cot_sends.at[step],
            cot_recvs.at[step],
            {"expert": flip(me, count >> (step + 1), count)},
        )

    def last_cot():
        rows = span(flip(me, count - 1, count) * main, main)
        return copy_to(
            cot_send_ref.at[rows],
            g_ref.at[pl.ds(base - main, main)],
            cot_sends.at[0],
            cot_recvs.at[0],
            {"expert": flip(me, count - 1, count)},
        )

    gather_cot(1).start()
    gather(0).start()
    for mask in range(1, count):
        arrive(mask).start()
    last_cot().start()
    mine_in = [
        pltpu.make_async_copy(send_ref.at[span(me * main, main)], x_rows.at[pl.ds(0, main)], own.at[0]),
        pltpu.make_async_copy(send_ref.at[pl.ds(base, spare)], x_rows.at[pl.ds(base, spare)], own.at[1]),
    ]
    for copy in mine_in:
        copy.start()
    acc1[...] = jnp.zeros_like(acc1)
    acc2[...] = jnp.zeros_like(acc2)
    experts = router_ref.shape[0]
    router = jnp.sum(jnp.where(iota((experts, 1), 0) == me, router_ref[...].astype(F32), 0.0), axis=0, keepdims=True)
    hot = jnp.full((1, 128), counts_ref[0, me], jnp.int32)[:, 0:1] > main
    hot = jnp.where(hot, 1.0, 0.0)
    for copy in loads + mine_in:
        copy.wait()

    def store_y(block):
        rows = pl.ds(pl.multiple_of(block * BLK, BLK), BLK)
        return pltpu.make_async_copy(y_rows.at[rows], y_ref.at[rows], y_sems.at[block])

    def mine_out():
        return pltpu.make_async_copy(dx_rows.at[pl.ds(0, main)], back_ref.at[span(me * main, main)], own.at[0])

    def run(turn, carry):
        block = turn + turn // (plain - 1) - (turn // (blocks - 1)) * (blocks - plain + 1)
        for item in range(BLK // main + 1):
            mask = (block * BLK + main - 1) // main + item

            @pl.when((block < plain) & (mask > 0) & (mask < ((block + 1) * BLK + main - 1) // main))
            def _():
                arrive(mask).wait_recv()

            @pl.when((block == plain - 1) & (mask == count - 1))
            def _():
                last_cot().wait_recv()

        for step in range(depth):

            @pl.when(turn == (max(step + 1, plain - depth + step) if step else 1))
            def _():
                gather(step).wait_recv()
                if step:
                    gather_cot(step).wait_recv()
                if step + 1 < depth:
                    gather(step + 1).start()
                    if step:
                        gather_cot(step + 1).start()

        rows = pl.ds(pl.multiple_of(block * BLK, BLK), BLK)
        live = jnp.where(block < plain, 1.0, hot)
        x = (x_rows[rows, :].astype(F32) * live).astype(BF16)
        logit = jnp.sum(x.astype(F32) * router, axis=1, keepdims=True)
        gate = jax.nn.sigmoid(logit)
        go = g_ref[rows, :].astype(F32) * live
        g = (gate * go).astype(BF16)
        x_t = x.astype(F32).T.astype(BF16)
        y = jnp.zeros(x.shape, F32)
        dx = jnp.zeros(x.shape, F32)
        for first in range(0, hidden, chunk):
            cols = pl.ds(first, chunk)
            w1 = w1_ref[:, cols]
            w2 = w2_ref[cols, :]
            pre = nn(x, w1)
            cdf, pdf = gelu_parts(pre)
            act = (pre * cdf).astype(BF16)
            slope = cdf + pre * pdf
            y = y + nn(act, w2)
            grad = (nt(g, w2) * slope).astype(BF16)
            dx = dx + nt(grad, w1)
            acc1[:, cols] += nn(x_t, grad)
            acc2[cols, :] += tn(act, g)
        y_low = y.astype(BF16)
        y_rows[rows, :] = y_low
        dlogit = jnp.sum(y_low.astype(F32) * go, axis=1, keepdims=True) * gate * (1.0 - gate)
        dx_rows[rows, :] = (dx + dlogit * router).astype(BF16)
        store_y(block).start()
        for item in range(BLK // main + 1):
            mask = (block * BLK) // main + item
            done = (block < plain) & (mask < ((block + 1) * BLK) // main)

            @pl.when(done & (mask > 0) & (mask < early))
            def _():
                leave(mask).start()

            @pl.when(done & (mask == 0))
            def _():
                mine_out().start()

        return carry

    lax.fori_loop(0, blocks, run, 0)
    tail = pltpu.make_async_copy(dx_rows.at[pl.ds(early * main, slots - early * main)], late_ref, own.at[1])
    tail.start()

    pieces = []
    for first in range(0, hidden, width):
        pieces.append((acc1.at[:, pl.ds(first, width)], grads_ref.at[pl.ds(first, width)]))
    for first in range(0, hidden, width):
        pieces.append((acc2.at[pl.ds(first, width), :], grads_ref.at[pl.ds(hidden + first, width)]))
    writes = []
    for index, (piece, target) in enumerate(pieces):
        slot = index % 2
        if index >= 2:
            writes[index - 2].wait()
        stage[slot] = piece[...].astype(BF16)
        write = pltpu.make_async_copy(stage.at[slot], target, stage_sems.at[slot])
        write.start()
        writes.append(write)
    for write in writes[-2:]:
        write.wait()
    mine_out().wait()
    tail.wait()

    def settle(block, carry):
        store_y(block).wait()
        return carry

    lax.fori_loop(0, blocks, settle, 0)
    for step in range(depth):
        gather(step).wait_send()
    for step in range(1, depth):
        gather_cot(step).wait_send()
    last_cot().wait_send()
    for mask in range(1, count):
        arrive(mask).wait_send()
    for mask in range(1, early):
        leave(mask).wait()


def backward_kernel(
    dp,
    count,
    main,
    spare,
    group_ref,
    domain_ref,
    x_hbm,
    cot_hbm,
    gain_one_ref,
    gain_two_ref,
    wq_hbm,
    wk_hbm,
    wv_hbm,
    wo_hbm,
    slot_col_hbm,
    normed_hbm,
    q_hbm,
    k_hbm,
    v_hbm,
    mixed_hbm,
    lse_hbm,
    hidden_hbm,
    dx_hbm,
    late_ref,
    y_ref,
    grads_hbm,
    grad_ref,
    dense_ref,
    vec_ref,
    y_back_ref,
    piece_ref,
    x_ref,
    cot_ref,
    wq_ref,
    wk_ref,
    wv_ref,
    wo_ref,
    slot_col_ref,
    normed_ref,
    q_ref,
    k_ref,
    v_ref,
    mixed_ref,
    lse_ref,
    hidden_ref,
    dx_ref,
    spare_dx,
    spare_y,
    dx_land,
    y_land,
    kept,
    land_one,
    land_two,
    ghid,
    gmix,
    branch,
    normed_t,
    dqkv,
    sums,
    sends,
    recvs,
    late_sends,
    late_recvs,
    dx_sends,
    dx_recvs,
    y_sends,
    y_recvs,
    own,
    gets,
    fills,
    scatter_sends,
    scatter_recvs,
    keeps,
):
    tokens, width = x_ref.shape
    me = lax.axis_index("expert")
    early = count - count // 4
    base = count * main
    late = (count - early) * main
    total = count * spare
    depth = depth_of(count)
    operands = [
        (x_hbm, x_ref),
        (cot_hbm, cot_ref),
        (wq_hbm, wq_ref),
        (wk_hbm, wk_ref),
        (wv_hbm, wv_ref),
        (wo_hbm, wo_ref),
        (slot_col_hbm, slot_col_ref),
        (normed_hbm, normed_ref),
        (q_hbm, q_ref),
        (k_hbm, k_ref),
        (v_hbm, v_ref),
        (mixed_hbm, mixed_ref),
        (lse_hbm, lse_ref),
        (hidden_hbm, hidden_ref),
    ]
    operands = [pltpu.make_async_copy(source, target, fills.at[i]) for i, (source, target) in enumerate(operands)]
    for copy in operands:
        copy.start()
    barrier = pltpu.get_barrier_semaphore()
    place, bits = dp_sides()
    for mask in range(1, count):
        pl.semaphore_signal(barrier, inc=1, device_id={"expert": flip(me, mask, count)}, device_id_type=MESH)
    for mask in (1, 2):
        pl.semaphore_signal(barrier, inc=1, device_id={"dp": flip(place, mask, dp)}, device_id_type=MESH)
    pl.semaphore_wait(barrier, count + 1)
    portion = grads_hbm.shape[0] // 4
    quarter = portion // 2

    def scatter_one(stream):
        start = 2 * portion * stream + (1 - bits[stream]) * portion
        device = {"dp": flip(place, 1 << stream, dp)}
        return copy_to(
            grads_hbm.at[span(start, portion)], land_one.at[stream], scatter_sends.at[0, stream], scatter_recvs.at[0, stream], device
        )

    def keep_one(stream):
        start = 2 * portion * stream + bits[stream] * portion
        return pltpu.make_async_copy(grads_hbm.at[span(start, portion)], kept.at[stream], keeps.at[stream])

    def scatter_two(stream):
        start = (1 - bits[1 - stream]) * quarter
        device = {"dp": flip(place, 2 >> stream, dp)}
        return copy_to(
            kept.at[stream, span(start, quarter)],
            land_two.at[stream],
            scatter_sends.at[1, stream],
            scatter_recvs.at[1, stream],
            device,
        )

    def store_piece(stream):
        start = bits[1 - stream] * quarter
        return pltpu.make_async_copy(
            kept.at[stream, span(start, quarter)], piece_ref.at[pl.ds(stream * quarter, quarter)], keeps.at[stream]
        )

    for stream in range(2):
        scatter_one(stream).start()
        keep_one(stream).start()

    def sum_dx(step):
        if step == depth - 1:
            return return_spare(me, count, spare, step, late_ref, late, dx_land, dx_sends, dx_recvs)
        return return_spare(me, count, spare, step, spare_dx, 0, dx_land, dx_sends, dx_recvs)

    def sum_y(step):
        if step == depth - 1:
            return return_spare(me, count, spare, step, y_ref, base, y_land, y_sends, y_recvs)
        return return_spare(me, count, spare, step, spare_y, 0, y_land, y_sends, y_recvs)

    def settle(copy, own_rows, landing, step):
        copy.wait()
        rows = spare << step
        own_rows[0:rows, :] = (own_rows[0:rows, :].astype(F32) + landing[rows : 2 * rows, :].astype(F32)).astype(BF16)

    sum_dx(depth - 1).start()
    lates = [return_block(me, count, main, mask, late_ref, dx_ref, late_sends, late_recvs, early) for mask in range(early, count)]
    for copy in lates:
        copy.start()
    copies = [return_block(me, count, main, mask, y_ref, y_back_ref, sends, recvs) for mask in range(1, count)]
    mine = pltpu.make_async_copy(y_ref.at[pl.ds(0, main)], y_back_ref.at[span(me * main, main)], own.at[0])
    mine.start()
    loads = [
        pltpu.make_async_copy(late_ref.at[pl.ds(late, total)], spare_dx, own.at[1]),
        pltpu.make_async_copy(y_ref.at[pl.ds(base, total)], spare_y, own.at[2]),
    ]
    for mask in range(early):
        part = span(flip(me, mask, count) * main, main)
        loads.append(pltpu.make_async_copy(dx_hbm.at[part], dx_ref.at[part], gets.at[mask]))
    for load in loads:
        load.start()
    for load in loads:
        load.wait()
    for step in reversed(range(depth)):
        settle(sum_dx(step), spare_dx, dx_land, step)
        if step:
            sum_dx(step - 1).start()
    dx_ref[pl.ds(base, BLK), :] = spare_dx[0:BLK, :]
    for copy in lates:
        copy.wait()
    sum_y(depth - 1).start()
    for copy in copies:
        copy.start()
    for copy in operands:
        copy.wait()
    slots = dx_ref.shape[0]
    blocks = tokens // BLK
    lane = iota((1, 128), 1)
    weight = domain_weight(group_ref, domain_ref)
    gain_one = row_of(gain_one_ref)
    gain_two = row_of(gain_two_ref)
    sums[...] = jnp.zeros_like(sums)

    def open_block(block, carry):
        rows = pl.ds(pl.multiple_of(block * BLK, BLK), BLK)
        slot = slot_col_ref[rows, 0:1]
        pick = jnp.where(iota((BLK, slots), 1) == slot, 1.0, 0.0).astype(BF16)
        grad = nn(pick, dx_ref[...])
        hat, rstd = norm_stats(hidden_ref[rows, :])
        sums[2:3, :] += jnp.sum(grad * hat, axis=0, keepdims=True)
        sums[3:4, :] += jnp.sum(grad, axis=0, keepdims=True)
        gg = grad * gain_two
        inner = gg - jnp.mean(gg, axis=1, keepdims=True) - hat * jnp.mean(gg * hat, axis=1, keepdims=True)
        total = cot_ref[rows, :].astype(F32) * weight + rstd * inner
        ghid[rows, :] = total
        low = total.astype(BF16)
        branch[rows, :] = low
        gmix[rows, :] = nt(low, wo_ref[...]).astype(BF16)
        normed_t[:, rows] = normed_ref[rows, :].astype(F32).T.astype(BF16)
        return carry

    lax.fori_loop(0, blocks, open_block, 0)
    dense_ref[pl.ds(3 * width, width), :] = tn(mixed_ref[...], branch[...]).astype(BF16)
    settle(sum_y(depth - 1), spare_y, y_land, depth - 1)
    sum_y(depth - 2).start()

    keep = iota((BLK, BLK), 0) <= iota((BLK, BLK), 1)

    def attend(pair, carry):
        @pl.when(pair == HEADS // 4)
        def _():
            for stream in range(2):
                keep_one(stream).wait()
                scatter_one(stream).wait()
                sum_rows(kept.at[stream], land_one.at[stream], portion)
                scatter_two(stream).start()

        base = pl.multiple_of(pair * 128, 128)
        cols = pl.ds(base, 128)
        q_pair = q_ref[:, cols]
        k_pair = k_ref[:, cols]
        v_pair = v_ref[:, cols]
        o_pair = gmix[:, cols]
        low = lane < 64
        q_head = [jnp.where(low, q_pair, 0), jnp.where(low, 0, q_pair)]
        k_head = [jnp.where(low, k_pair, 0), jnp.where(low, 0, k_pair)]
        v_head = [jnp.where(low, v_pair, 0), jnp.where(low, 0, v_pair)]
        o_head = [jnp.where(low, o_pair, 0), jnp.where(low, 0, o_pair)]
        k_t = k_pair.astype(F32).T.astype(BF16)
        prod_t = (o_pair.astype(F32) * mixed_ref[:, cols].astype(F32)).T
        delta = [jnp.sum(prod_t[:64], axis=0, keepdims=True), jnp.sum(prod_t[64:], axis=0, keepdims=True)]
        dq_t = [[None] * blocks, [None] * blocks]
        for block in range(blocks):
            start = block * BLK
            dk = None
            dv = None
            for half in range(2):
                scores = nt(k_head[half][start : start + BLK], q_pair[start:])
                diag = jnp.where(keep, scores[:, :BLK], -1000000000.0)
                scores = jnp.concatenate([diag, scores[:, BLK:]], axis=1) if block < blocks - 1 else diag
                probs = jnp.exp(scores - lse_ref[pair, half : half + 1, pl.ds(start, tokens - start)])
                grad_p = nt(v_head[half][start : start + BLK], o_pair[start:])
                grad_s = (probs * (grad_p - delta[half][:, start:])).astype(BF16)
                dv_part = nn(probs.astype(BF16), o_head[half][start:])
                dk_part = nn(grad_s, q_head[half][start:])
                dv = dv_part if dv is None else dv + dv_part
                dk = dk_part if dk is None else dk + dk_part
                dq_part = nn(k_t[half * 64 : half * 64 + 64, start : start + BLK], grad_s)
                for later in range(block, blocks):
                    piece = dq_part[:, (later - block) * BLK : (later - block + 1) * BLK]
                    dq_t[half][later] = piece if dq_t[half][later] is None else dq_t[half][later] + piece
            rows = pl.ds(start, BLK)
            dqkv[rows, pl.ds(pl.multiple_of(base + width, 128), 128)] = dk.astype(BF16)
            dqkv[rows, pl.ds(pl.multiple_of(base + 2 * width, 128), 128)] = dv.astype(BF16)
        for block in range(blocks):
            both = jnp.concatenate([dq_t[0][block], dq_t[1][block]], axis=0) * (HEAD_DIM ** (-0.5))
            dqkv[pl.ds(block * BLK, BLK), cols] = both.T.astype(BF16)
        return carry

    lax.fori_loop(0, HEADS // 2, attend, 0)

    for part in range(3):
        dense_ref[pl.ds(part * width, width), :] = nn(normed_t[...], dqkv[:, pl.ds(part * width, width)]).astype(BF16)

    def close_block(block, carry):
        rows = pl.ds(pl.multiple_of(block * BLK, BLK), BLK)
        grad = nt(dqkv[rows, 0:width], wq_ref[...])
        grad = grad + nt(dqkv[rows, width : 2 * width], wk_ref[...])
        grad = grad + nt(dqkv[rows, 2 * width : 3 * width], wv_ref[...])
        hat, rstd = norm_stats(x_ref[rows, :].astype(F32))
        sums[0:1, :] += jnp.sum(grad * hat, axis=0, keepdims=True)
        sums[1:2, :] += jnp.sum(grad, axis=0, keepdims=True)
        gg = grad * gain_one
        inner = gg - jnp.mean(gg, axis=1, keepdims=True) - hat * jnp.mean(gg * hat, axis=1, keepdims=True)
        grad_ref[rows, :] = (ghid[rows, :] + rstd * inner).astype(BF16)
        return carry

    lax.fori_loop(0, blocks, close_block, 0)
    vec_ref[...] = sums[...]
    for stream in range(2):
        scatter_two(stream).wait()
        start = bits[1 - stream] * quarter
        sum_rows(kept.at[stream, span(start, quarter)], land_two.at[stream], quarter)
        store_piece(stream).start()
    for step in reversed(range(depth - 1)):
        settle(sum_y(step), spare_y, y_land, step)
        if step:
            sum_y(step - 1).start()
    spare_out = pltpu.make_async_copy(spare_y.at[pl.ds(0, BLK)], y_back_ref.at[pl.ds(base, BLK)], own.at[1])
    spare_out.start()
    spare_out.wait()
    for stream in range(2):
        store_piece(stream).wait()
    mine.wait()
    for copy in copies:
        copy.wait()


STREAMS = 3
CHUNKS = 4


def halving_plan(dp, count, rows):
    experts = [("expert", 2 << bit) for bit in range(depth_of(count) - 1)]
    groups = [("dp", 1 << bit) for bit in range(depth_of(dp))]
    core = [("expert", 1)]
    plans = [core + groups + experts, core + groups[::-1] + experts, core + experts + groups]
    halvings = 0
    while halvings < len(plans[0]) and (rows >> halvings) % 32 == 0:
        halvings += 1
    return plans, halvings


def finish_kernel(
    dp,
    count,
    dense_ref,
    vec_ref,
    slot_col_ref,
    hidden_ref,
    gate_ref,
    y_ref,
    piece_ref,
    out_ref,
    full_ref,
    total_ref,
    grads_ref,
    acc,
    landing,
    full,
    vec_acc,
    vec_land,
    sends,
    recvs,
    back_sends,
    back_recvs,
    vec_sends,
    vec_recvs,
    put,
    unit_sends,
    unit_recvs,
    own,
):
    tokens, width = hidden_ref.shape
    slots = y_ref.shape[0]
    rows = dense_ref.shape[0] // STREAMS
    place = {"dp": lax.axis_index("dp"), "expert": lax.axis_index("expert")}
    size = {"dp": dp, "expert": count}
    plans, halvings = halving_plan(dp, count, rows)
    steps = len(plans[0])

    def partner(axis, mask):
        return {axis: flip(place[axis], mask, size[axis])}

    barrier = pltpu.get_barrier_semaphore()
    for axis, mask in plans[0]:
        pl.semaphore_signal(barrier, inc=1, device_id=partner(axis, mask), device_id_type=MESH)
    pl.semaphore_wait(barrier, steps)

    def side(axis, mask):
        return (place[axis] // mask) % 2

    _, bits = dp_sides()
    quarter = piece_ref.shape[0] // 2
    chunk = quarter // CHUNKS
    starts = [
        4 * quarter * stream + bits[stream] * 2 * quarter + bits[1 - stream] * quarter for stream in range(2)
    ]
    others = [
        4 * quarter * stream + bits[stream] * 2 * quarter + (1 - bits[1 - stream]) * quarter for stream in range(2)
    ]

    def unit(index, stream):
        kind, part = index // CHUNKS, index % CHUNKS
        near, far = partner("dp", 1 << stream), partner("dp", 2 >> stream)
        if kind == 2:
            source = target = grads_ref.at[span(others[stream] + part * chunk, chunk)]
        else:
            source = piece_ref.at[pl.ds(stream * quarter + part * chunk, chunk)]
            target = grads_ref.at[span(starts[stream] + part * chunk, chunk)]
        return copy_to(
            source, target, unit_sends.at[index, stream], unit_recvs.at[index, stream], far if kind == 0 else near
        )

    pending = list(range(3 * CHUNKS))

    def advance(number):
        for _ in range(min(number, len(pending))):
            index = pending.pop(0)
            for stream in range(2):
                if index >= 2 * CHUNKS:
                    unit(index - 2 * CHUNKS, stream).wait_recv()
                unit(index, stream).start()

    mine = [
        pltpu.make_async_copy(
            piece_ref.at[pl.ds(stream * quarter, quarter)], grads_ref.at[span(starts[stream], quarter)], own.at[stream]
        )
        for stream in range(2)
    ]
    for copy in mine:
        copy.start()

    def combine(block):
        rows_at = pl.ds(block * BLK, BLK)
        slot = slot_col_ref[rows_at, 0:1]
        pick = jnp.where(iota((BLK, slots), 1) == slot, 1.0, 0.0).astype(BF16)
        returned = nn(pick, y_ref[...])
        out_ref[rows_at, :] = (hidden_ref[rows_at, :] + gate_ref[rows_at, 0:1] * returned).astype(BF16)

    todo = list(range(tokens // BLK))
    low = [jnp.int32(stream * rows) for stream in range(STREAMS)]
    extent = rows
    offset = 0
    trail = []
    for step in range(steps):
        halve = step < halvings
        part = extent // 2 if halve else extent
        copies = []
        for stream in range(STREAMS):
            axis, mask = plans[stream][step]
            kept = low[stream] + side(axis, mask) * part if halve else low[stream]
            other = low[stream] + (1 - side(axis, mask)) * part if halve else low[stream]
            source = dense_ref if step == 0 else acc.at[(step - 1) % 2]
            land = landing.at[stream, pl.ds(offset, part)]
            copy = copy_to(
                source.at[span(other, part)], land, sends.at[stream, step], recvs.at[stream, step], partner(axis, mask)
            )
            copy.start()
            copies.append((copy, kept, source))
        axis, mask = plans[0][step]
        vec_source = vec_ref if step == 0 else vec_acc.at[step - 1]
        vec_copy = copy_to(vec_source, vec_land.at[step], vec_sends.at[step], vec_recvs.at[step], partner(axis, mask))
        vec_copy.start()
        advance(1)
        if step in (1, 2):
            for block in todo[: tokens // BLK // 4]:
                combine(block)
            todo = todo[tokens // BLK // 4 :]
        trail.append((list(low), extent))
        for stream in range(STREAMS):
            copy, kept, source = copies[stream]
            copy.wait()
            held = span(kept, part)
            value = source[held, :].astype(F32) + landing[stream, pl.ds(offset, part), :].astype(F32)
            if step < steps - 1:
                acc[step % 2, held, :] = value.astype(BF16)
            else:
                full[held, :] = value.astype(BF16)
            low[stream] = kept
        vec_copy.wait()
        vec_sum = vec_source[...] + vec_land[step]
        if step < steps - 1:
            vec_acc[step] = vec_sum
        else:
            total_ref[...] = vec_sum
        extent = part
        offset += part

    for step in reversed(range(halvings)):
        origins, whole = trail[step]
        copies = []
        for stream in range(STREAMS):
            axis, mask = plans[stream][step]
            held = span(low[stream], extent)
            copy = copy_to(
                full.at[held], full.at[held], back_sends.at[stream, step], back_recvs.at[stream, step], partner(axis, mask)
            )
            copy.start()
            copies.append(copy)
        advance(2)
        if step in (1, 2):
            for block in todo if step == 1 else todo[: tokens // BLK // 4]:
                combine(block)
            todo = todo[tokens // BLK // 4 :]
        for stream in range(STREAMS):
            copies[stream].wait()
            low[stream] = origins[stream]
        extent = whole
    advance(len(pending))
    write = pltpu.make_async_copy(full, full_ref, put)
    write.start()
    for index in range(3 * CHUNKS):
        for stream in range(2):
            if index >= CHUNKS:
                unit(index, stream).wait_recv()
            unit(index, stream).wait_send()
    for copy in mine + [write]:
        copy.wait()


def widen_kernel(hidden, dense_hbm, grads_hbm, total_ref, *rest):
    outs, vecs, (low, high, gets, puts) = rest[:6], rest[6:10], rest[10:]
    width = dense_hbm.shape[1]
    jobs = []
    for block in range(hidden // width):
        part = pl.ds(block * width, width)
        jobs.append((grads_hbm.at[part], outs[4].at[:, part]))
        jobs.append((grads_hbm.at[pl.ds(hidden + block * width, width)], outs[5].at[part, :]))
    for index in range(4):
        jobs.append((dense_hbm.at[pl.ds(index * width, width)], outs[index]))
    loads = [pltpu.make_async_copy(source, low.at[i], gets.at[i]) for i, (source, _) in enumerate(jobs)]
    for load in loads:
        load.start()
    for index, vec in enumerate(vecs):
        vec[...] = total_ref[index : index + 1, :].reshape(width)
    slots = high.shape[0]
    stores = []
    for index, (_, target) in enumerate(jobs):
        loads[index].wait()
        if index >= slots:
            stores[index - slots].wait()
        high[index % slots] = low[index].astype(F32)
        stores.append(pltpu.make_async_copy(high.at[index % slots], target, puts.at[index % slots]))
        stores[-1].start()
    for store in stores[-slots:]:
        store.wait()


def call(kernel, outs, in_specs, scratch, name, out_specs=None, collective=None, flops=10**9):
    remote = {} if collective is None else {"collective_id": collective, "has_side_effects": True}
    return pl.pallas_call(
        kernel,
        out_shape=outs,
        in_specs=in_specs,
        out_specs=out_specs or [VMEM] * len(outs),
        scratch_shapes=scratch,
        compiler_params=pltpu.CompilerParams(vmem_limit_bytes=LIMIT, **remote),
        cost_estimate=pl.CostEstimate(flops=flops, bytes_accessed=10**7, transcendentals=0),
        name=name,
    )


def dma(*dims):
    return pltpu.SemaphoreType.DMA(dims)


def shape(dims, kind):
    return jax.ShapeDtypeStruct(dims, kind)


def tables(experts, main, slots, counts, group, domains, sort_order, cotangent):
    tokens, width = cotangent.shape
    return call(
        functools.partial(table_kernel, experts, main),
        [shape((slots, width), BF16), shape((tokens, 128), jnp.int32), shape((8, tokens), jnp.int32)],
        [SMEM, SMEM, SMEM, VMEM, VMEM],
        [pltpu.VMEM((tokens, width), BF16)],
        "tables",
    )(counts, group, domains, sort_order, cotangent)


def forward(count, main, spare, inputs, g1, s1, g2, s2, wq, wk, wv, wo, router, slot_col, slot_row, cot_send):
    tokens, width = inputs.shape
    rows_low = shape((tokens, width), BF16)
    return call(
        functools.partial(forward_kernel, count, main, spare),
        [
            rows_low,
            rows_low,
            rows_low,
            rows_low,
            rows_low,
            shape((HEADS // 2, 8, tokens), F32),
            shape((tokens, width), F32),
            shape((tokens, 128), F32),
            shape(cot_send.shape, BF16),
            shape((count * (main + spare), width), BF16),
        ],
        [VMEM] * 12 + [ANY],
        [pltpu.VMEM((tokens, width), BF16), dma(count), dma(count), dma(depth_of(count)), dma(depth_of(count)), dma(2)],
        "dense_forward",
        [VMEM] * 9 + [ANY],
        1,
    )(inputs, g1, s1, g2, s2, wq, wk, wv, wo, router, slot_col, slot_row, cot_send)


def expert_block(count, main, spare, counts, send, cot_send, cot_rows, router_t, w1, w2, chunk=768):
    slots, width = cot_rows.shape
    hidden = w1.shape[1]
    late = slots - (count - count // 4) * main
    rows = shape((slots, width), BF16)
    keep = pltpu.VMEM((slots, width), BF16)
    depth = depth_of(count)
    return call(
        functools.partial(expert_kernel, count, main, spare, chunk),
        [
            rows,
            shape((count * main, width), BF16),
            shape((late, width), BF16),
            shape((2 * hidden, width), BF16),
        ],
        [SMEM, ANY, ANY, ANY, VMEM, ANY, ANY],
        [
            pltpu.VMEM((width, hidden), BF16),
            pltpu.VMEM((hidden, width), BF16),
            pltpu.VMEM((width, hidden), F32),
            pltpu.VMEM((hidden, width), F32),
            keep,
            keep,
            keep,
            keep,
            pltpu.VMEM((2, width, width), BF16),
            dma(4),
            dma(count),
            dma(count),
            dma(depth),
            dma(depth),
            dma(depth),
            dma(depth),
            dma(count),
            dma(count),
            dma(2),
            dma(slots // BLK),
            dma(2),
        ],
        "expert",
        [ANY] * 4,
        2,
    )(counts, send, cot_send, cot_rows, router_t, w1, w2)


def backward(
    dp, count, main, spare, group, domains, inputs, cotangent, g1, g2, wq, wk, wv, wo, slot_col,
    normed, q, k, v, mixed, lse, hidden, dx, late, y, grads,
):
    tokens, width = inputs.shape
    half = grads.shape[0] // 4
    return call(
        functools.partial(backward_kernel, dp, count, main, spare),
        [shape((tokens, width), BF16), shape((4 * width, width), BF16), shape((8, width), F32), shape((count * main + BLK, width), BF16), shape((half, width), BF16)],
        [SMEM] * 2 + [ANY] * 2 + [VMEM] * 2 + [ANY] * 16,
        [pltpu.VMEM(v.shape, v.dtype) for v in (inputs, cotangent, wq, wk, wv, wo, slot_col, normed, q, k, v, mixed, lse, hidden)]
        + [
            pltpu.VMEM((count * main + BLK, width), BF16),
            pltpu.VMEM((count * spare, width), BF16),
            pltpu.VMEM((count * spare, width), BF16),
            pltpu.VMEM((count * spare, width), BF16),
            pltpu.VMEM((count * spare, width), BF16),
            pltpu.VMEM((2, half, width), BF16),
            pltpu.VMEM((2, half, width), BF16),
            pltpu.VMEM((2, half // 2, width), BF16),
            pltpu.VMEM((tokens, width), F32),
            pltpu.VMEM((tokens, width), BF16),
            pltpu.VMEM((tokens, width), BF16),
            pltpu.VMEM((width, tokens), BF16),
            pltpu.VMEM((tokens, 3 * width), BF16),
            pltpu.VMEM((8, width), F32),
            dma(count),
            dma(count),
            dma(count),
            dma(count),
            dma(depth_of(count)),
            dma(depth_of(count)),
            dma(depth_of(count)),
            dma(depth_of(count)),
            dma(3),
            dma(count),
            dma(14),
            dma(2, 2),
            dma(2, 2),
            dma(2),
        ],
        "dense_backward",
        [VMEM, VMEM, VMEM, ANY, ANY],
        3,
        5 * 10**10,
    )(group, domains, inputs, cotangent, g1, g2, wq, wk, wv, wo, slot_col, normed, q, k, v, mixed, lse, hidden, dx, late, y, grads)


def finish(dp, count, dense, vec, slot_col, hidden, gate, y_back, piece):
    width = hidden.shape[1]
    rows = dense.shape[0]
    steps = len(halving_plan(dp, count, rows // STREAMS)[0][0])
    return call(
        functools.partial(finish_kernel, dp, count),
        [shape(hidden.shape, BF16), shape(dense.shape, BF16), shape(vec.shape, F32), shape((4 * piece.shape[0], width), BF16)],
        [VMEM] * 6 + [ANY],
        [
            pltpu.VMEM((2, rows, width), BF16),
            pltpu.VMEM((STREAMS, rows // STREAMS + 64, width), BF16),
            pltpu.VMEM((rows, width), BF16),
            pltpu.VMEM((steps,) + vec.shape, F32),
            pltpu.VMEM((steps,) + vec.shape, F32),
            dma(STREAMS, steps),
            dma(STREAMS, steps),
            dma(STREAMS, steps),
            dma(STREAMS, steps),
            dma(steps),
            dma(steps),
            dma(),
            dma(3 * CHUNKS, 2),
            dma(3 * CHUNKS, 2),
            dma(2),
        ],
        "finish",
        [VMEM, ANY, VMEM, ANY],
        4,
    )(dense, vec, slot_col, hidden, gate, y_back, piece)


def widen(hidden, dense, grads, total):
    width = dense.shape[1]
    square = shape((width, width), F32)
    jobs = 2 * (hidden // width) + 4
    return call(
        functools.partial(widen_kernel, hidden),
        [square] * 4 + [shape((width, hidden), F32), shape((hidden, width), F32)] + [shape((width,), F32)] * 4,
        [ANY, ANY, VMEM],
        [
            pltpu.VMEM((jobs, width, width), BF16),
            pltpu.VMEM((6, width, width), F32),
            dma(jobs),
            dma(6),
        ],
        "widen",
        [ANY] * 6 + [VMEM] * 4,
    )(dense, grads, total)


def local(
    inputs,
    cotangent,
    seq_group,
    domain_counts,
    sort_order,
    send_counts,
    gain_one,
    shift_one,
    gain_two,
    shift_two,
    w_query,
    w_key,
    w_value,
    w_out,
    router,
    expert_in,
    expert_out,
):
    tokens, width = inputs.shape
    experts = send_counts.shape[1]
    capacity = 2 * tokens // experts
    spare = capacity // 4
    main = capacity - spare
    slots = experts * main + BLK
    count = lax.axis_size("expert")
    g1, s1, g2, s2 = gain_one, shift_one, gain_two, shift_two
    router_t = router.T
    cot_send, slot_col, slot_row = tables(experts, main, slots, send_counts, seq_group, domain_counts, sort_order, cotangent)
    normed, q, k, v, mixed, lse, hidden, gate, send, cot_rows = forward(
        count, main, spare, inputs, g1, s1, g2, s2, w_query, w_key, w_value, w_out, router_t, slot_col, slot_row, cot_send
    )
    y_rows, dx_back, dx_late, grads = expert_block(
        count, main, spare, send_counts, send, cot_send, cot_rows, router_t, expert_in[0], expert_out[0]
    )
    dp = lax.axis_size("dp")
    grad_inputs, dense, vec, y_back, piece = backward(
        dp, count, main, spare, seq_group, domain_counts, inputs, cotangent, g1, g2, w_query, w_key, w_value, w_out, slot_col,
        normed, q, k, v, mixed, lse, hidden, dx_back, dx_late, y_rows, grads,
    )
    output, dense, vec, grads = finish(dp, count, dense, vec, slot_col, hidden, gate, y_back, piece)
    wq, wk, wv, wo, first, second, gain_a, shift_a, gain_b, shift_b = widen(expert_in.shape[2], dense, grads, vec)
    return (output, grad_inputs, gain_a, shift_a, gain_b, shift_b, wq, wk, wv, wo, first[None], second[None])


def solution(mesh):
    rows = P(("dp", "expert"), None)
    split = P("expert", None, None)
    return jax.shard_map(
        local,
        mesh=mesh,
        in_specs=(rows, rows, P(("dp", "expert")), P(), rows, rows) + (P(),) * 9 + (split, split),
        out_specs=(rows, rows) + (P(),) * 8 + (split, split),
        check_vma=False,
    )
```

```python
import functools

import jax
import jax.numpy as jnp
from jax import lax
from jax.experimental import pallas as pl
from jax.experimental.pallas import tpu as pltpu
from jax.sharding import PartitionSpec as P

HEADS = 12
HEAD_DIM = 64
LEN = 1024
EPS = 1e-05
F32 = jnp.float32
BF16 = jnp.bfloat16
BLK = 256
CODE = 4096
LIMIT = 63 * 1024 * 1024

VMEM = pl.BlockSpec(memory_space=pltpu.VMEM)
SMEM = pl.BlockSpec(memory_space=pltpu.SMEM)
ANY = pl.BlockSpec(memory_space=pl.ANY)
MESH = pl.DeviceIdType.MESH


def dot(left, right, contract):
    return lax.dot_general(left, right, ((contract[0:1], contract[1:2]), ((), ())), preferred_element_type=F32)


def nn(left, right):
    return dot(left, right, (1, 0))


def nt(left, right):
    return dot(left, right, (1, 1))


def tn(left, right):
    return dot(left, right, (0, 0))


def iota(shape, axis):
    return lax.broadcasted_iota(jnp.int32, shape, axis)


def flip(index, mask, count):
    bit, out = 1, 0
    while bit < count:
        out = out + ((index // bit + mask // bit) % 2) * bit
        bit *= 2
    return out


def greet(axis, me, count):
    barrier = pltpu.get_barrier_semaphore()
    for mask in range(1, count):
        pl.semaphore_signal(barrier, inc=1, device_id={axis: flip(me, mask, count)}, device_id_type=MESH)
    pl.semaphore_wait(barrier, count - 1)


def copy_to(source, target, send, recv, device):
    return pltpu.make_async_remote_copy(
        src_ref=source, dst_ref=target, send_sem=send, recv_sem=recv, device_id=device, device_id_type=MESH
    )


def span(start, rows):
    return pl.ds(pl.multiple_of(start, 16), rows)


def send_block(me, count, rows, mask, source, target, sends, recvs):
    peer = flip(me, mask, count)
    return copy_to(
        source.at[span(peer * rows, rows)], target.at[span(mask * rows, rows)], sends.at[mask], recvs.at[mask], {"expert": peer}
    )


def return_block(me, count, rows, mask, source, target, sends, recvs, shift=0):
    return copy_to(
        source.at[span((mask - shift) * rows, rows)],
        target.at[span(me * rows, rows)],
        sends.at[mask],
        recvs.at[mask],
        {"expert": flip(me, mask, count)},
    )


def last_returns(count):
    return count // 8


def dp_sides():
    index = lax.axis_index("dp")
    return index, (index % 2, (index // 2) % 2)


def each_rows(rows, step, size=64):
    def body(block, carry):
        step(pl.ds(pl.multiple_of(block * size, size), size))
        return carry

    lax.fori_loop(0, rows // size, body, 0)


def sum_rows(target, other, rows):
    def step(block, carry):
        part = pl.ds(pl.multiple_of(block * BLK, BLK), BLK)
        target[part, :] = (target[part, :].astype(F32) + other[part, :].astype(F32)).astype(BF16)
        return carry

    lax.fori_loop(0, rows // BLK, step, 0)


def depth_of(count):
    return count.bit_length() - 1


def gather_spare(me, count, base, rows, step, first, target, sends, recvs):
    have = rows << step
    source = first.at[pl.ds(base, rows)] if step == 0 else target.at[pl.ds(base, have)]
    return copy_to(
        source,
        target.at[pl.ds(base + have, have)],
        sends.at[step],
        recvs.at[step],
        {"expert": flip(me, count >> (step + 1), count)},
    )


def return_spare(me, count, rows, step, source, shift, landing, sends, recvs):
    half = rows << step
    return copy_to(
        source.at[pl.ds(shift + half, half)],
        landing.at[pl.ds(half, half)],
        sends.at[step],
        recvs.at[step],
        {"expert": flip(me, count >> (step + 1), count)},
    )


def row_of(ref):
    return ref[...].reshape(1, ref.shape[0])


def domain_weight(group_ref, counts_ref):
    groups = counts_ref.shape[0]
    group = group_ref[0]
    total = jnp.zeros((1, 128), F32)
    mine = jnp.zeros((1, 128), F32)
    for index in range(groups):
        inverse = 1.0 / jnp.full((1, 128), counts_ref[index], jnp.int32).astype(F32)
        total = total + inverse
        mine = mine + jnp.where(group == index, inverse, 0.0)
    return (mine / (total / groups))[:, 0:1]


def norm_stats(rows):
    center = rows - jnp.mean(rows, axis=-1, keepdims=True)
    rstd = lax.rsqrt(jnp.mean(center * center, axis=-1, keepdims=True) + EPS)
    return center * rstd, rstd


def pack_rows(slot_row, rows_ref, send_ref):
    slots = send_ref.shape[0]
    tokens = rows_ref.shape[0]

    def step(block, carry):
        base = pl.multiple_of(block * BLK, BLK)
        slot = iota((BLK, tokens), 0) + base
        pick = jnp.where(slot == slot_row, 1.0, 0.0).astype(BF16)
        send_ref[pl.ds(base, BLK), :] = nn(pick, rows_ref[...]).astype(BF16)
        return carry

    lax.fori_loop(0, slots // BLK, step, 0)


def table_kernel(experts, main, counts_ref, group_ref, domain_ref, sort_ref, cot_ref, send_ref, slot_col_ref, slot_row_ref, scaled):
    tokens = cot_ref.shape[0]
    place = iota((1, tokens), 1)
    expert_at = jnp.zeros((1, tokens), jnp.int32)
    start_at = jnp.zeros((1, tokens), jnp.int32)
    end = jnp.int32(0)
    for expert in range(experts):
        count = counts_ref[0, expert]
        end = end + count
        past = place >= end
        expert_at = expert_at + jnp.where(past, 1, 0)
        start_at = start_at + jnp.where(past, count, 0)
    slot = place - start_at
    dest = jnp.where(slot < main, expert_at * main + slot, (experts - 1) * main + slot)
    code = (expert_at * CODE + dest).astype(F32)
    sort_row = sort_ref[...]
    scaled[...] = (cot_ref[...].astype(F32) * domain_weight(group_ref, domain_ref)).astype(BF16)
    for block in range(tokens // BLK):
        token = iota((BLK, tokens), 0) + block * BLK
        col = jnp.sum(jnp.where(token == sort_row, code, 0.0), axis=1, keepdims=True)
        owner = (col * (1.0 / CODE)).astype(jnp.int32)
        where = col.astype(jnp.int32) - owner * CODE
        slot_col_ref[pl.ds(block * BLK, BLK), :] = jnp.where(iota((1, 128), 1) < 64, where, owner)
        slot_row_ref[:, pl.ds(block * BLK, BLK)] = jnp.broadcast_to(where, (BLK, 128)).astype(F32).T[0:8].astype(jnp.int32)
    pack_rows(slot_row_ref[0:1, :], scaled, send_ref)


def forward_kernel(
    count,
    main,
    spare,
    x_ref,
    gain_one_ref,
    shift_one_ref,
    gain_two_ref,
    shift_two_ref,
    wq_ref,
    wk_ref,
    wv_ref,
    wo_ref,
    router_ref,
    slot_col_ref,
    slot_row_ref,
    cot_send_ref,
    normed_ref,
    q_ref,
    k_ref,
    v_ref,
    mixed_ref,
    hidden_ref,
    gate_ref,
    send_ref,
    cot_rows_ref,
    probs_hbm,
    routed,
    probs,
    prob_sems,
    sends,
    recvs,
    spare_sends,
    spare_recvs,
    own,
):
    tokens, width = x_ref.shape
    blocks = tokens // BLK
    me = lax.axis_index("expert")
    greet("expert", me, count)
    base = count * main

    def gather(step):
        return gather_spare(me, count, base, spare, step, cot_send_ref, cot_rows_ref, spare_sends, spare_recvs)

    gather(0).start()
    copies = [send_block(me, count, main, mask, cot_send_ref, cot_rows_ref, sends, recvs) for mask in range(1, count - 1)]
    for copy in copies:
        copy.start()
    mine = [
        pltpu.make_async_copy(cot_send_ref.at[span(me * main, main)], cot_rows_ref.at[pl.ds(0, main)], own.at[0]),
        pltpu.make_async_copy(cot_send_ref.at[pl.ds(base, spare)], cot_rows_ref.at[pl.ds(base, spare)], own.at[1]),
    ]
    for copy in mine:
        copy.start()
    lane = iota((1, 128), 1)
    gain_one, shift_one, gain_two, shift_two = (row_of(r) for r in (gain_one_ref, shift_one_ref, gain_two_ref, shift_two_ref))

    def project(block, carry):
        rows = pl.ds(pl.multiple_of(block * BLK, BLK), BLK)
        hat, _ = norm_stats(x_ref[rows, :].astype(F32))
        normed = (hat * gain_one + shift_one).astype(BF16)
        normed_ref[rows, :] = normed
        q_ref[rows, :] = (nn(normed, wq_ref[...]).astype(BF16) * (HEAD_DIM ** (-0.5))).astype(BF16)
        k_ref[rows, :] = nn(normed, wk_ref[...]).astype(BF16)
        v_ref[rows, :] = nn(normed, wv_ref[...]).astype(BF16)
        return carry

    lax.fori_loop(0, blocks, project, 0)

    keep = iota((BLK, BLK), 0) <= iota((BLK, BLK), 1)

    def keep_probs(pair):
        return pltpu.make_async_copy(probs.at[pair % 2], probs_hbm.at[pair], prob_sems.at[pair % 2])

    def attend(pair, carry):
        @pl.when(pair >= 2)
        def _():
            keep_probs(pair - 2).wait()

        cols = pl.ds(pl.multiple_of(pair * 128, 128), 128)
        k_pair = k_ref[:, cols]
        v_t = v_ref[:, cols].astype(F32).T.astype(BF16)
        k_head = [jnp.where(lane < 64, k_pair, 0), jnp.where(lane >= 64, k_pair, 0)]
        for block in range(blocks):
            span = (block + 1) * BLK
            query = q_ref[pl.ds(block * BLK, BLK), cols]
            outs = []
            for half in range(2):
                scores = nt(k_head[half][:span], query)
                diag = jnp.where(keep, scores[block * BLK :], -1000000000.0)
                scores = jnp.concatenate([scores[: block * BLK], diag], axis=0) if block else diag
                peak = jnp.max(scores, axis=0, keepdims=True)
                exps = jnp.exp(scores - peak)
                total = jnp.sum(exps, axis=0, keepdims=True)
                attention = (exps * (1.0 / total)).astype(BF16)
                probs[pair % 2, half, pl.ds(block * (block + 1) // 2 * BLK, (block + 1) * BLK), :] = attention
                outs.append(nn(v_t[half * 64 : half * 64 + 64, :span], attention))
            mixed_ref[pl.ds(block * BLK, BLK), cols] = jnp.concatenate(outs, axis=0).T.astype(BF16)
        keep_probs(pair).start()
        return carry

    lax.fori_loop(0, HEADS // 2, attend, 0)
    experts = router_ref.shape[0]

    def finish(block, carry):
        rows = pl.ds(pl.multiple_of(block * BLK, BLK), BLK)
        hidden = x_ref[rows, :].astype(F32) + nn(mixed_ref[rows, :], wo_ref[...])
        hidden_ref[rows, :] = hidden
        hat, _ = norm_stats(hidden)
        low = (hat * gain_two + shift_two).astype(BF16)
        routed[rows, :] = low
        logits = nt(low, router_ref[...])
        owner = slot_col_ref[rows, 64:65]
        logit = jnp.sum(jnp.where(iota((BLK, experts), 1) == owner, logits, 0.0), axis=1, keepdims=True)
        gate_ref[rows, :] = jnp.broadcast_to(jax.nn.sigmoid(logit), (BLK, 128))
        return carry

    lax.fori_loop(0, blocks, finish, 0)
    pack_rows(slot_row_ref[0:1, :], routed, send_ref)
    for copy in mine + [keep_probs(HEADS // 2 - 2), keep_probs(HEADS // 2 - 1)]:
        copy.wait()
    for copy in copies + [gather(0)]:
        copy.wait()


def gelu_parts(v):
    t = 1.0 / (1.0 + (0.3275911 * 0.7071067811865476) * jnp.abs(v))
    bell = jnp.exp2((-0.5 * 1.4426950408889634) * (v * v))
    poly = ((((0.5307027145 * t - 0.7265760135) * t + 0.7107068705) * t - 0.142248368) * t + 0.127414796) * t
    tail = poly * bell
    return jnp.where(v >= 0.0, 1.0 - tail, tail), bell * 0.3989422804014327


def expert_kernel(
    count,
    main,
    spare,
    chunk,
    counts_ref,
    send_ref,
    cot_send_ref,
    cot_rows_ref,
    router_ref,
    w1_hbm,
    w2_hbm,
    y_ref,
    back_ref,
    late_ref,
    grads_ref,
    w1_ref,
    w2_ref,
    acc1,
    acc2,
    x_rows,
    g_ref,
    dx_rows,
    y_rows,
    stage,
    load_sems,
    sends,
    recvs,
    spare_sends,
    spare_recvs,
    cot_sends,
    cot_recvs,
    back_sends,
    back_recvs,
    own,
    y_sems,
    stage_sems,
):
    width, hidden = w1_ref.shape
    slots = x_rows.shape[0]
    base = count * main
    plain = base // BLK
    blocks = slots // BLK
    depth = depth_of(count)
    early = count - count // 4
    me = lax.axis_index("expert")
    loads = [
        pltpu.make_async_copy(w1_hbm, w1_ref, load_sems.at[0]),
        pltpu.make_async_copy(w2_hbm, w2_ref, load_sems.at[1]),
        pltpu.make_async_copy(cot_rows_ref.at[pl.ds(0, base - main)], g_ref.at[pl.ds(0, base - main)], load_sems.at[2]),
        pltpu.make_async_copy(cot_rows_ref.at[pl.ds(base, 2 * spare)], g_ref.at[pl.ds(base, 2 * spare)], load_sems.at[3]),
    ]
    for load in loads:
        load.start()
    greet("expert", me, count)

    def gather(step):
        return gather_spare(me, count, base, spare, step, send_ref, x_rows, spare_sends, spare_recvs)

    def arrive(mask):
        return send_block(me, count, main, mask, send_ref, x_rows, sends, recvs)

    def leave(mask):
        return return_block(me, count, main, mask, dx_rows, back_ref, back_sends, back_recvs)

    def gather_cot(step):
        source = cot_rows_ref if step == 1 else g_ref
        have = spare << step
        return copy_to(
            source.at[pl.ds(base, have)],
            g_ref.at[pl.ds(base + have, have)],
            cot_sends.at[step],
            cot_recvs.at[step],
            {"expert": flip(me, count >> (step + 1), count)},
        )

    def last_cot():
        rows = span(flip(me, count - 1, count) * main, main)
        return copy_to(
            cot_send_ref.at[rows],
            g_ref.at[pl.ds(base - main, main)],
            cot_sends.at[0],
            cot_recvs.at[0],
            {"expert": flip(me, count - 1, count)},
        )

    gather_cot(1).start()
    gather(0).start()
    for mask in range(1, count):
        arrive(mask).start()
    last_cot().start()
    mine_in = [
        pltpu.make_async_copy(send_ref.at[span(me * main, main)], x_rows.at[pl.ds(0, main)], own.at[0]),
        pltpu.make_async_copy(send_ref.at[pl.ds(base, spare)], x_rows.at[pl.ds(base, spare)], own.at[1]),
    ]
    for copy in mine_in:
        copy.start()

    def clear_one(part):
        acc1[part, :] = jnp.zeros((64, hidden), F32)

    def clear_two(part):
        acc2[part, :] = jnp.zeros((64, width), F32)

    each_rows(width, clear_one)
    each_rows(hidden, clear_two)
    experts = router_ref.shape[0]
    router = jnp.sum(jnp.where(iota((experts, 1), 0) == me, router_ref[...].astype(F32), 0.0), axis=0, keepdims=True)
    hot = jnp.full((1, 128), counts_ref[0, me], jnp.int32)[:, 0:1] > main
    hot = jnp.where(hot, 1.0, 0.0)
    for copy in loads + mine_in:
        copy.wait()

    def store_y(block):
        rows = pl.ds(pl.multiple_of(block * BLK, BLK), BLK)
        return pltpu.make_async_copy(y_rows.at[rows], y_ref.at[rows], y_sems.at[block])

    def mine_out():
        return pltpu.make_async_copy(dx_rows.at[pl.ds(0, main)], back_ref.at[span(me * main, main)], own.at[0])

    def run(turn, carry):
        block = turn + turn // (plain - 1) - (turn // (blocks - 1)) * (blocks - plain + 1)
        for item in range(BLK // main + 1):
            mask = (block * BLK + main - 1) // main + item

            @pl.when((block < plain) & (mask > 0) & (mask < ((block + 1) * BLK + main - 1) // main))
            def _():
                arrive(mask).wait_recv()

            @pl.when((block == plain - 1) & (mask == count - 1))
            def _():
                last_cot().wait_recv()

        for step in range(depth):

            @pl.when(turn == (max(step + 1, plain - depth + step) if step else 1))
            def _():
                gather(step).wait_recv()
                if step:
                    gather_cot(step).wait_recv()
                if step + 1 < depth:
                    gather(step + 1).start()
                    if step:
                        gather_cot(step + 1).start()

        rows = pl.ds(pl.multiple_of(block * BLK, BLK), BLK)
        live = jnp.where(block < plain, 1.0, hot)
        x = (x_rows[rows, :].astype(F32) * live).astype(BF16)
        logit = jnp.sum(x.astype(F32) * router, axis=1, keepdims=True)
        gate = jax.nn.sigmoid(logit)
        go = g_ref[rows, :].astype(F32) * live
        g = (gate * go).astype(BF16)
        x_t = x.astype(F32).T.astype(BF16)
        y = jnp.zeros(x.shape, F32)
        dx = jnp.zeros(x.shape, F32)
        for first in range(0, hidden, chunk):
            cols = pl.ds(first, chunk)
            w1 = w1_ref[:, cols]
            w2 = w2_ref[cols, :]
            pre = nn(x, w1)
            cdf, pdf = gelu_parts(pre)
            act = (pre * cdf).astype(BF16)
            slope = cdf + pre * pdf
            y = y + nn(act, w2)
            grad = (nt(g, w2) * slope).astype(BF16)
            dx = dx + nt(grad, w1)
            acc1[:, cols] += nn(x_t, grad)
            acc2[cols, :] += tn(act, g)
        y_low = y.astype(BF16)
        y_rows[rows, :] = y_low
        dlogit = jnp.sum(y_low.astype(F32) * go, axis=1, keepdims=True) * gate * (1.0 - gate)
        dx_rows[rows, :] = (dx + dlogit * router).astype(BF16)
        store_y(block).start()
        for item in range(BLK // main + 1):
            mask = (block * BLK) // main + item
            done = (block < plain) & (mask < ((block + 1) * BLK) // main)

            @pl.when(done & (mask > 0) & (mask < early))
            def _():
                leave(mask).start()

            @pl.when(done & (mask == 0))
            def _():
                mine_out().start()

        return carry

    lax.fori_loop(0, blocks, run, 0)
    tail = pltpu.make_async_copy(dx_rows.at[pl.ds(early * main, slots - early * main)], late_ref, own.at[1])
    tail.start()

    pieces = []
    for first in range(0, hidden, width):
        pieces.append((acc1.at[:, pl.ds(first, width)], grads_ref.at[pl.ds(first, width)]))
    for first in range(0, hidden, width):
        pieces.append((acc2.at[pl.ds(first, width), :], grads_ref.at[pl.ds(hidden + first, width)]))
    writes = []
    for index, (piece, target) in enumerate(pieces):
        slot = index % 2
        if index >= 2:
            writes[index - 2].wait()

        def narrow(part):
            stage[slot, part, :] = piece[part, :].astype(BF16)

        each_rows(width, narrow)
        write = pltpu.make_async_copy(stage.at[slot], target, stage_sems.at[slot])
        write.start()
        writes.append(write)
    for write in writes[-2:]:
        write.wait()
    mine_out().wait()
    tail.wait()

    def settle(block, carry):
        store_y(block).wait()
        return carry

    lax.fori_loop(0, blocks, settle, 0)
    for step in range(depth):
        gather(step).wait_send()
    for step in range(1, depth):
        gather_cot(step).wait_send()
    last_cot().wait_send()
    for mask in range(1, count):
        arrive(mask).wait_send()
    for mask in range(1, early):
        leave(mask).wait()


def backward_kernel(
    dp,
    count,
    main,
    spare,
    group_ref,
    domain_ref,
    x_hbm,
    cot_hbm,
    gain_one_ref,
    gain_two_ref,
    wq_hbm,
    wk_hbm,
    wv_hbm,
    wo_hbm,
    slot_col_hbm,
    normed_hbm,
    q_hbm,
    k_hbm,
    v_hbm,
    mixed_hbm,
    probs_hbm,
    hidden_hbm,
    dx_hbm,
    late_ref,
    y_ref,
    grads_hbm,
    grad_ref,
    dense_ref,
    vec_ref,
    y_back_ref,
    piece_ref,
    x_ref,
    cot_ref,
    wq_ref,
    wk_ref,
    wv_ref,
    wo_ref,
    slot_col_ref,
    normed_ref,
    q_ref,
    k_ref,
    v_ref,
    mixed_ref,
    hidden_ref,
    dx_ref,
    spare_dx,
    spare_y,
    dx_land,
    y_land,
    probs,
    kept,
    land_one,
    land_two,
    gmix,
    branch,
    normed_t,
    dqkv,
    sums,
    sends,
    recvs,
    late_sends,
    late_recvs,
    dx_sends,
    dx_recvs,
    y_sends,
    y_recvs,
    own,
    gets,
    fills,
    scatter_sends,
    scatter_recvs,
    keeps,
    prob_sems,
):
    tokens, width = x_ref.shape
    me = lax.axis_index("expert")
    early = count - count // 4
    base = count * main
    late = (count - early) * main
    total = count * spare
    depth = depth_of(count)
    operands = [
        (x_hbm, x_ref),
        (cot_hbm, cot_ref),
        (wq_hbm, wq_ref),
        (wk_hbm, wk_ref),
        (wv_hbm, wv_ref),
        (wo_hbm, wo_ref),
        (slot_col_hbm, slot_col_ref),
        (normed_hbm, normed_ref),
        (q_hbm, q_ref),
        (k_hbm, k_ref),
        (v_hbm, v_ref),
        (mixed_hbm, mixed_ref),
        (hidden_hbm, hidden_ref),
    ]
    operands = [pltpu.make_async_copy(source, target, fills.at[i]) for i, (source, target) in enumerate(operands)]
    for copy in operands:
        copy.start()
    barrier = pltpu.get_barrier_semaphore()
    place, bits = dp_sides()
    for mask in range(1, count):
        pl.semaphore_signal(barrier, inc=1, device_id={"expert": flip(me, mask, count)}, device_id_type=MESH)
    for mask in (1, 2):
        pl.semaphore_signal(barrier, inc=1, device_id={"dp": flip(place, mask, dp)}, device_id_type=MESH)
    pl.semaphore_wait(barrier, count + 1)
    portion = grads_hbm.shape[0] // 4
    quarter = portion // 2

    def scatter_one(stream, second):
        side = bits[1 - stream] if second else 1 - bits[1 - stream]
        start = 2 * portion * stream + (1 - bits[stream]) * portion + side * quarter
        device = {"dp": flip(place, 1 << stream, dp)}
        return copy_to(
            grads_hbm.at[span(start, quarter)],
            land_one.at[stream, span(side * quarter, quarter)],
            scatter_sends.at[second, stream],
            scatter_recvs.at[second, stream],
            device,
        )

    def add_one(stream, second):
        side = bits[1 - stream] if second else 1 - bits[1 - stream]
        scatter_one(stream, second).wait()

        def step(rows):
            held = span(side * quarter + rows.start, 64)
            kept[stream, held, :] = (kept[stream, held, :].astype(F32) + land_one[stream, held, :].astype(F32)).astype(BF16)

        each_rows(quarter, step)

    def keep_one(stream):
        start = 2 * portion * stream + bits[stream] * portion
        return pltpu.make_async_copy(grads_hbm.at[span(start, portion)], kept.at[stream], keeps.at[stream])

    def scatter_two(stream):
        start = (1 - bits[1 - stream]) * quarter
        device = {"dp": flip(place, 2 >> stream, dp)}
        return copy_to(
            kept.at[stream, span(start, quarter)],
            land_two.at[stream],
            scatter_sends.at[2, stream],
            scatter_recvs.at[2, stream],
            device,
        )

    def store_piece(stream):
        start = bits[1 - stream] * quarter
        return pltpu.make_async_copy(
            kept.at[stream, span(start, quarter)], piece_ref.at[pl.ds(stream * quarter, quarter)], keeps.at[stream]
        )

    def load_probs(pair):
        return pltpu.make_async_copy(probs_hbm.at[pair], probs.at[pair % 2], prob_sems.at[pair % 2])

    load_probs(0).start()
    for part in range(2):
        for stream in range(2):
            scatter_one(stream, part).start()
    for stream in range(2):
        keep_one(stream).start()

    def sum_dx(step):
        if step == depth - 1:
            return return_spare(me, count, spare, step, late_ref, late, dx_land, dx_sends, dx_recvs)
        return return_spare(me, count, spare, step, spare_dx, 0, dx_land, dx_sends, dx_recvs)

    def sum_y(step):
        if step == depth - 1:
            return return_spare(me, count, spare, step, y_ref, base, y_land, y_sends, y_recvs)
        return return_spare(me, count, spare, step, spare_y, 0, y_land, y_sends, y_recvs)

    def settle(copy, own_rows, landing, step):
        copy.wait()
        rows = spare << step
        own_rows[0:rows, :] = (own_rows[0:rows, :].astype(F32) + landing[rows : 2 * rows, :].astype(F32)).astype(BF16)

    sum_dx(depth - 1).start()
    lates = [return_block(me, count, main, mask, late_ref, dx_ref, late_sends, late_recvs, early) for mask in range(early, count)]
    for copy in lates:
        copy.start()
    copies = [
        return_block(me, count, main, mask, y_ref, y_back_ref, sends, recvs) for mask in range(1, count - last_returns(count))
    ]
    mine = pltpu.make_async_copy(y_ref.at[pl.ds(0, main)], y_back_ref.at[span(me * main, main)], own.at[0])
    mine.start()
    loads = [
        pltpu.make_async_copy(late_ref.at[pl.ds(late, total)], spare_dx, own.at[1]),
        pltpu.make_async_copy(y_ref.at[pl.ds(base, total)], spare_y, own.at[2]),
    ]
    for mask in range(early):
        part = span(flip(me, mask, count) * main, main)
        loads.append(pltpu.make_async_copy(dx_hbm.at[part], dx_ref.at[part], gets.at[mask]))
    for load in loads:
        load.start()
    for load in loads:
        load.wait()
    for step in reversed(range(depth)):
        settle(sum_dx(step), spare_dx, dx_land, step)
        if step:
            sum_dx(step - 1).start()
    dx_ref[pl.ds(base, BLK), :] = spare_dx[0:BLK, :]
    for copy in lates:
        copy.wait()
    sum_y(depth - 1).start()
    for copy in copies:
        copy.start()
    for copy in operands:
        copy.wait()
    slots = dx_ref.shape[0]
    blocks = tokens // BLK
    lane = iota((1, 128), 1)
    weight = domain_weight(group_ref, domain_ref)
    gain_one = row_of(gain_one_ref)
    gain_two = row_of(gain_two_ref)
    sums[...] = jnp.zeros_like(sums)

    def open_block(block, carry):
        rows = pl.ds(pl.multiple_of(block * BLK, BLK), BLK)
        slot = slot_col_ref[rows, 0:1]
        pick = jnp.where(iota((BLK, slots), 1) == slot, 1.0, 0.0).astype(BF16)
        grad = nn(pick, dx_ref[...])
        hat, rstd = norm_stats(hidden_ref[rows, :])
        sums[2:3, :] += jnp.sum(grad * hat, axis=0, keepdims=True)
        sums[3:4, :] += jnp.sum(grad, axis=0, keepdims=True)
        gg = grad * gain_two
        inner = gg - jnp.mean(gg, axis=1, keepdims=True) - hat * jnp.mean(gg * hat, axis=1, keepdims=True)
        total = cot_ref[rows, :].astype(F32) * weight + rstd * inner
        hidden_ref[rows, :] = total
        low = total.astype(BF16)
        branch[rows, :] = low
        gmix[rows, :] = nt(low, wo_ref[...]).astype(BF16)
        normed_t[:, rows] = normed_ref[rows, :].astype(F32).T.astype(BF16)
        return carry

    lax.fori_loop(0, blocks, open_block, 0)
    dense_ref[pl.ds(3 * width, width), :] = tn(mixed_ref[...], branch[...]).astype(BF16)
    settle(sum_y(depth - 1), spare_y, y_land, depth - 1)
    sum_y(depth - 2).start()

    for stream in range(2):
        keep_one(stream).wait()
        add_one(stream, 0)
        scatter_two(stream).start()

    def attend(pair, carry):
        @pl.when(pair + 1 < HEADS // 2)
        def _():
            load_probs(pair + 1).start()

        @pl.when(pair == 4)
        def _():
            for stream in range(2):
                add_one(stream, 1)

        load_probs(pair).wait()
        base = pl.multiple_of(pair * 128, 128)
        cols = pl.ds(base, 128)
        q_pair = q_ref[:, cols]
        k_pair = k_ref[:, cols]
        v_pair = v_ref[:, cols]
        o_pair = gmix[:, cols]
        low = lane < 64
        q_head = [jnp.where(low, q_pair, 0), jnp.where(low, 0, q_pair)]
        v_head = [jnp.where(low, v_pair, 0), jnp.where(low, 0, v_pair)]
        o_head = [jnp.where(low, o_pair, 0), jnp.where(low, 0, o_pair)]
        k_t = k_pair.astype(F32).T.astype(BF16)
        prod_t = (o_pair.astype(F32) * mixed_ref[:, cols].astype(F32)).T
        delta = [jnp.sum(prod_t[:64], axis=0, keepdims=True), jnp.sum(prod_t[64:], axis=0, keepdims=True)]
        dq_t = [[None] * blocks, [None] * blocks]
        for block in range(blocks):
            start = block * BLK
            dk = None
            dv = None
            for half in range(2):
                tiles = [
                    probs[pair % 2, half, pl.ds((later * (later + 1) // 2 + block) * BLK, BLK), :]
                    for later in range(block, blocks)
                ]
                attention = jnp.concatenate(tiles, axis=1) if block < blocks - 1 else tiles[0]
                grad_p = nt(v_head[half][start : start + BLK], o_pair[start:])
                grad_s = (attention.astype(F32) * (grad_p - delta[half][:, start:])).astype(BF16)
                dv_part = nn(attention, o_head[half][start:])
                dk_part = nn(grad_s, q_head[half][start:])
                dv = dv_part if dv is None else dv + dv_part
                dk = dk_part if dk is None else dk + dk_part
                dq_part = nn(k_t[half * 64 : half * 64 + 64, start : start + BLK], grad_s)
                for later in range(block, blocks):
                    piece = dq_part[:, (later - block) * BLK : (later - block + 1) * BLK]
                    dq_t[half][later] = piece if dq_t[half][later] is None else dq_t[half][later] + piece
            rows = pl.ds(start, BLK)
            dqkv[rows, pl.ds(pl.multiple_of(base + width, 128), 128)] = dk.astype(BF16)
            dqkv[rows, pl.ds(pl.multiple_of(base + 2 * width, 128), 128)] = dv.astype(BF16)
        for block in range(blocks):
            both = jnp.concatenate([dq_t[0][block], dq_t[1][block]], axis=0) * (HEAD_DIM ** (-0.5))
            dqkv[pl.ds(block * BLK, BLK), cols] = both.T.astype(BF16)
        return carry

    lax.fori_loop(0, HEADS // 2, attend, 0)

    for part in range(3):
        dense_ref[pl.ds(part * width, width), :] = nn(normed_t[...], dqkv[:, pl.ds(part * width, width)]).astype(BF16)

    def close_block(block, carry):
        rows = pl.ds(pl.multiple_of(block * BLK, BLK), BLK)
        grad = nt(dqkv[rows, 0:width], wq_ref[...])
        grad = grad + nt(dqkv[rows, width : 2 * width], wk_ref[...])
        grad = grad + nt(dqkv[rows, 2 * width : 3 * width], wv_ref[...])
        hat, rstd = norm_stats(x_ref[rows, :].astype(F32))
        sums[0:1, :] += jnp.sum(grad * hat, axis=0, keepdims=True)
        sums[1:2, :] += jnp.sum(grad, axis=0, keepdims=True)
        gg = grad * gain_one
        inner = gg - jnp.mean(gg, axis=1, keepdims=True) - hat * jnp.mean(gg * hat, axis=1, keepdims=True)
        grad_ref[rows, :] = (hidden_ref[rows, :] + rstd * inner).astype(BF16)
        return carry

    lax.fori_loop(0, blocks, close_block, 0)
    vec_ref[...] = sums[...]
    for stream in range(2):
        scatter_two(stream).wait()
        start = bits[1 - stream] * quarter
        sum_rows(kept.at[stream, span(start, quarter)], land_two.at[stream], quarter)
        store_piece(stream).start()
    for step in reversed(range(depth - 1)):
        settle(sum_y(step), spare_y, y_land, step)
        if step:
            sum_y(step - 1).start()
    spare_out = pltpu.make_async_copy(spare_y.at[pl.ds(0, BLK)], y_back_ref.at[pl.ds(base, BLK)], own.at[1])
    spare_out.start()
    spare_out.wait()
    for stream in range(2):
        store_piece(stream).wait()
    mine.wait()
    for copy in copies:
        copy.wait()


STREAMS = 3
CHUNKS = 4


def halving_plan(dp, count, rows):
    experts = [("expert", 2 << bit) for bit in range(depth_of(count) - 1)]
    groups = [("dp", 1 << bit) for bit in range(depth_of(dp))]
    core = [("expert", 1)]
    plans = [core + groups + experts, core + groups[::-1] + experts, core + experts + groups]
    halvings = 0
    while halvings < len(plans[0]) and (rows >> halvings) % 32 == 0:
        halvings += 1
    return plans, halvings


def finish_kernel(
    dp,
    count,
    dense_ref,
    vec_ref,
    slot_col_ref,
    hidden_ref,
    gate_ref,
    y_hbm,
    y_rows_hbm,
    piece_ref,
    out_ref,
    full_ref,
    total_ref,
    grads_ref,
    y_ref,
    acc,
    landing,
    full,
    vec_acc,
    vec_land,
    sends,
    recvs,
    back_sends,
    back_recvs,
    vec_sends,
    vec_recvs,
    put,
    unit_sends,
    unit_recvs,
    own,
    y_sends,
    y_recvs,
    gets,
):
    tokens, width = hidden_ref.shape
    slots = y_ref.shape[0]
    main = (slots - BLK) // count
    early = count - last_returns(count)
    rows = dense_ref.shape[0] // STREAMS
    place = {"dp": lax.axis_index("dp"), "expert": lax.axis_index("expert")}
    size = {"dp": dp, "expert": count}
    plans, halvings = halving_plan(dp, count, rows)
    steps = len(plans[0])

    def partner(axis, mask):
        return {axis: flip(place[axis], mask, size[axis])}

    barrier = pltpu.get_barrier_semaphore()
    for axis, mask in plans[0]:
        pl.semaphore_signal(barrier, inc=1, device_id=partner(axis, mask), device_id_type=MESH)
    for mask in range(early, count):
        pl.semaphore_signal(barrier, inc=1, device_id=partner("expert", mask), device_id_type=MESH)
    pl.semaphore_wait(barrier, steps + count - early)
    me = place["expert"]
    y_copies = [return_block(me, count, main, mask, y_rows_hbm, y_ref, y_sends, y_recvs) for mask in range(early, count)]
    loads = [pltpu.make_async_copy(y_hbm.at[pl.ds(count * main, BLK)], y_ref.at[pl.ds(count * main, BLK)], gets.at[count])]
    for mask in range(early):
        part = span(flip(me, mask, count) * main, main)
        loads.append(pltpu.make_async_copy(y_hbm.at[part], y_ref.at[part], gets.at[mask]))
    for load in loads:
        load.start()

    def side(axis, mask):
        return (place[axis] // mask) % 2

    _, bits = dp_sides()
    quarter = piece_ref.shape[0] // 2
    chunk = quarter // CHUNKS
    starts = [
        4 * quarter * stream + bits[stream] * 2 * quarter + bits[1 - stream] * quarter for stream in range(2)
    ]
    others = [
        4 * quarter * stream + bits[stream] * 2 * quarter + (1 - bits[1 - stream]) * quarter for stream in range(2)
    ]

    def unit(index, stream):
        kind, part = index // CHUNKS, index % CHUNKS
        near, far = partner("dp", 1 << stream), partner("dp", 2 >> stream)
        if kind == 2:
            source = target = grads_ref.at[span(others[stream] + part * chunk, chunk)]
        else:
            source = piece_ref.at[pl.ds(stream * quarter + part * chunk, chunk)]
            target = grads_ref.at[span(starts[stream] + part * chunk, chunk)]
        return copy_to(
            source, target, unit_sends.at[index, stream], unit_recvs.at[index, stream], far if kind == 0 else near
        )

    pending = list(range(3 * CHUNKS))

    def advance(number):
        for _ in range(min(number, len(pending))):
            index = pending.pop(0)
            for stream in range(2):
                if index >= 2 * CHUNKS:
                    unit(index - 2 * CHUNKS, stream).wait_recv()
                unit(index, stream).start()

    mine = [
        pltpu.make_async_copy(
            piece_ref.at[pl.ds(stream * quarter, quarter)], grads_ref.at[span(starts[stream], quarter)], own.at[stream]
        )
        for stream in range(2)
    ]
    for copy in mine:
        copy.start()

    def combine(block):
        rows_at = pl.ds(pl.multiple_of(block * BLK, BLK), BLK)
        slot = slot_col_ref[rows_at, 0:1]
        pick = jnp.where(iota((BLK, slots), 1) == slot, 1.0, 0.0).astype(BF16)
        returned = nn(pick, y_ref[...])
        out_ref[rows_at, :] = (hidden_ref[rows_at, :] + gate_ref[rows_at, 0:1] * returned).astype(BF16)

    low = [jnp.int32(stream * rows) for stream in range(STREAMS)]
    extent = rows
    offset = 0
    trail = []
    for step in range(steps):
        halve = step < halvings
        part = extent // 2 if halve else extent
        copies = []
        for stream in range(STREAMS):
            axis, mask = plans[stream][step]
            kept = low[stream] + side(axis, mask) * part if halve else low[stream]
            other = low[stream] + (1 - side(axis, mask)) * part if halve else low[stream]
            source = dense_ref if step == 0 else acc.at[(step - 1) % 2]
            land = landing.at[stream, pl.ds(offset, part)]
            copy = copy_to(
                source.at[span(other, part)], land, sends.at[stream, step], recvs.at[stream, step], partner(axis, mask)
            )
            copy.start()
            copies.append((copy, kept, source))
        axis, mask = plans[0][step]
        vec_source = vec_ref if step == 0 else vec_acc.at[step - 1]
        vec_copy = copy_to(vec_source, vec_land.at[step], vec_sends.at[step], vec_recvs.at[step], partner(axis, mask))
        vec_copy.start()
        advance(1)
        if step == 0:
            for copy in y_copies:
                copy.start()
        trail.append((list(low), extent))
        for stream in range(STREAMS):
            copy, kept, source = copies[stream]
            copy.wait()
            target = acc.at[step % 2] if step < steps - 1 else full
            grain = min(part, 64)

            def add(rows_at):
                held = span(kept + rows_at.start, grain)
                value = source[held, :].astype(F32) + landing[stream, span(offset + rows_at.start, grain), :].astype(F32)
                target[held, :] = value.astype(BF16)

            each_rows(part, add, grain)
            low[stream] = kept
        vec_copy.wait()
        vec_sum = vec_source[...] + vec_land[step]
        if step < steps - 1:
            vec_acc[step] = vec_sum
        else:
            total_ref[...] = vec_sum
        extent = part
        offset += part

    for step in reversed(range(halvings)):
        origins, whole = trail[step]
        copies = []
        for stream in range(STREAMS):
            axis, mask = plans[stream][step]
            held = span(low[stream], extent)
            copy = copy_to(
                full.at[held], full.at[held], back_sends.at[stream, step], back_recvs.at[stream, step], partner(axis, mask)
            )
            copy.start()
            copies.append(copy)
        advance(2)
        if step == 1:
            for copy in loads + y_copies:
                copy.wait()

            def combine_block(block, carry):
                combine(block)
                return carry

            lax.fori_loop(0, tokens // BLK, combine_block, 0)
        for stream in range(STREAMS):
            copies[stream].wait()
            low[stream] = origins[stream]
        extent = whole
    advance(len(pending))
    write = pltpu.make_async_copy(full, full_ref, put)
    write.start()
    for index in range(3 * CHUNKS):
        for stream in range(2):
            if index >= CHUNKS:
                unit(index, stream).wait_recv()
            unit(index, stream).wait_send()
    for copy in mine + [write]:
        copy.wait()


def widen_kernel(hidden, dense_hbm, grads_hbm, total_ref, *rest):
    outs, vecs, (low, high, gets, puts) = rest[:6], rest[6:10], rest[10:]
    width = dense_hbm.shape[1]
    jobs = []
    for block in range(hidden // width):
        part = pl.ds(block * width, width)
        jobs.append((grads_hbm.at[part], outs[4].at[:, part]))
        jobs.append((grads_hbm.at[pl.ds(hidden + block * width, width)], outs[5].at[part, :]))
    for index in range(4):
        jobs.append((dense_hbm.at[pl.ds(index * width, width)], outs[index]))
    loads = [pltpu.make_async_copy(source, low.at[i], gets.at[i]) for i, (source, _) in enumerate(jobs)]
    for load in loads:
        load.start()
    for index, vec in enumerate(vecs):
        vec[...] = total_ref[index : index + 1, :].reshape(width)
    slots = high.shape[0]
    stores = []
    for index, (_, target) in enumerate(jobs):
        loads[index].wait()
        if index >= slots:
            stores[index - slots].wait()

        def step(part):
            high[index % slots, part, :] = low[index, part, :].astype(F32)

        each_rows(width, step)
        stores.append(pltpu.make_async_copy(high.at[index % slots], target, puts.at[index % slots]))
        stores[-1].start()
    for store in stores[-slots:]:
        store.wait()


def call(kernel, outs, in_specs, scratch, name, out_specs=None, collective=None, flops=10**9):
    remote = {} if collective is None else {"collective_id": collective, "has_side_effects": True}
    return pl.pallas_call(
        kernel,
        out_shape=outs,
        in_specs=in_specs,
        out_specs=out_specs or [VMEM] * len(outs),
        scratch_shapes=scratch,
        compiler_params=pltpu.CompilerParams(vmem_limit_bytes=LIMIT, **remote),
        cost_estimate=pl.CostEstimate(flops=flops, bytes_accessed=10**7, transcendentals=0),
        name=name,
    )


def dma(*dims):
    return pltpu.SemaphoreType.DMA(dims)


def shape(dims, kind):
    return jax.ShapeDtypeStruct(dims, kind)


def tables(experts, main, slots, counts, group, domains, sort_order, cotangent):
    tokens, width = cotangent.shape
    return call(
        functools.partial(table_kernel, experts, main),
        [shape((slots, width), BF16), shape((tokens, 128), jnp.int32), shape((8, tokens), jnp.int32)],
        [SMEM, SMEM, SMEM, VMEM, VMEM],
        [pltpu.VMEM((tokens, width), BF16)],
        "tables",
    )(counts, group, domains, sort_order, cotangent)


def forward(count, main, spare, inputs, g1, s1, g2, s2, wq, wk, wv, wo, router, slot_col, slot_row, cot_send):
    tokens, width = inputs.shape
    blocks = tokens // BLK
    prob_block = (2, blocks * (blocks + 1) // 2 * BLK, BLK)
    rows_low = shape((tokens, width), BF16)
    return call(
        functools.partial(forward_kernel, count, main, spare),
        [
            rows_low,
            rows_low,
            rows_low,
            rows_low,
            rows_low,
            shape((tokens, width), F32),
            shape((tokens, 128), F32),
            shape(cot_send.shape, BF16),
            shape((count * (main + spare), width), BF16),
            shape((HEADS // 2,) + prob_block, BF16),
        ],
        [VMEM] * 12 + [ANY],
        [
            pltpu.VMEM((tokens, width), BF16),
            pltpu.VMEM((2,) + prob_block, BF16),
            dma(2),
            dma(count),
            dma(count),
            dma(depth_of(count)),
            dma(depth_of(count)),
            dma(2),
        ],
        "dense_forward",
        [VMEM] * 8 + [ANY] * 2,
        1,
    )(inputs, g1, s1, g2, s2, wq, wk, wv, wo, router, slot_col, slot_row, cot_send)


def expert_block(count, main, spare, counts, send, cot_send, cot_rows, router_t, w1, w2, chunk=768):
    slots, width = cot_rows.shape
    hidden = w1.shape[1]
    late = slots - (count - count // 4) * main
    rows = shape((slots, width), BF16)
    keep = pltpu.VMEM((slots, width), BF16)
    depth = depth_of(count)
    return call(
        functools.partial(expert_kernel, count, main, spare, chunk),
        [
            rows,
            shape((count * main, width), BF16),
            shape((late, width), BF16),
            shape((2 * hidden, width), BF16),
        ],
        [SMEM, ANY, ANY, ANY, VMEM, ANY, ANY],
        [
            pltpu.VMEM((width, hidden), BF16),
            pltpu.VMEM((hidden, width), BF16),
            pltpu.VMEM((width, hidden), F32),
            pltpu.VMEM((hidden, width), F32),
            keep,
            keep,
            keep,
            keep,
            pltpu.VMEM((2, width, width), BF16),
            dma(4),
            dma(count),
            dma(count),
            dma(depth),
            dma(depth),
            dma(depth),
            dma(depth),
            dma(count),
            dma(count),
            dma(2),
            dma(slots // BLK),
            dma(2),
        ],
        "expert",
        [ANY] * 4,
        2,
    )(counts, send, cot_send, cot_rows, router_t, w1, w2)


def backward(
    dp, count, main, spare, group, domains, inputs, cotangent, g1, g2, wq, wk, wv, wo, slot_col,
    normed, q, k, v, mixed, probs, hidden, dx, late, y, grads,
):
    tokens, width = inputs.shape
    half = grads.shape[0] // 4
    return call(
        functools.partial(backward_kernel, dp, count, main, spare),
        [shape((tokens, width), BF16), shape((4 * width, width), BF16), shape((8, width), F32), shape((count * main + BLK, width), BF16), shape((half, width), BF16)],
        [SMEM] * 2 + [ANY] * 2 + [VMEM] * 2 + [ANY] * 16,
        [pltpu.VMEM(v.shape, v.dtype) for v in (inputs, cotangent, wq, wk, wv, wo, slot_col, normed, q, k, v, mixed, hidden)]
        + [
            pltpu.VMEM((count * main + BLK, width), BF16),
            pltpu.VMEM((count * spare, width), BF16),
            pltpu.VMEM((count * spare, width), BF16),
            pltpu.VMEM((count * spare, width), BF16),
            pltpu.VMEM((count * spare, width), BF16),
            pltpu.VMEM((2,) + probs.shape[1:], BF16),
            pltpu.VMEM((2, half, width), BF16),
            pltpu.VMEM((2, half, width), BF16),
            pltpu.VMEM((2, half // 2, width), BF16),
            pltpu.VMEM((tokens, width), BF16),
            pltpu.VMEM((tokens, width), BF16),
            pltpu.VMEM((width, tokens), BF16),
            pltpu.VMEM((tokens, 3 * width), BF16),
            pltpu.VMEM((8, width), F32),
            dma(count),
            dma(count),
            dma(count),
            dma(count),
            dma(depth_of(count)),
            dma(depth_of(count)),
            dma(depth_of(count)),
            dma(depth_of(count)),
            dma(3),
            dma(count),
            dma(13),
            dma(3, 2),
            dma(3, 2),
            dma(2),
            dma(2),
        ],
        "dense_backward",
        [VMEM, VMEM, VMEM, ANY, ANY],
        3,
        5 * 10**10,
    )(group, domains, inputs, cotangent, g1, g2, wq, wk, wv, wo, slot_col, normed, q, k, v, mixed, probs, hidden, dx, late, y, grads)


def finish(dp, count, dense, vec, slot_col, hidden, gate, y_back, y_rows, piece):
    width = hidden.shape[1]
    rows = dense.shape[0]
    steps = len(halving_plan(dp, count, rows // STREAMS)[0][0])
    return call(
        functools.partial(finish_kernel, dp, count),
        [shape(hidden.shape, BF16), shape(dense.shape, BF16), shape(vec.shape, F32), shape((4 * piece.shape[0], width), BF16)],
        [VMEM] * 5 + [ANY] * 3,
        [
            pltpu.VMEM(y_back.shape, BF16),
            pltpu.VMEM((2, rows, width), BF16),
            pltpu.VMEM((STREAMS, rows // STREAMS + 64, width), BF16),
            pltpu.VMEM((rows, width), BF16),
            pltpu.VMEM((steps,) + vec.shape, F32),
            pltpu.VMEM((steps,) + vec.shape, F32),
            dma(STREAMS, steps),
            dma(STREAMS, steps),
            dma(STREAMS, steps),
            dma(STREAMS, steps),
            dma(steps),
            dma(steps),
            dma(),
            dma(3 * CHUNKS, 2),
            dma(3 * CHUNKS, 2),
            dma(2),
            dma(count),
            dma(count),
            dma(count + 1),
        ],
        "finish",
        [VMEM, ANY, VMEM, ANY],
        4,
    )(dense, vec, slot_col, hidden, gate, y_back, y_rows, piece)


def widen(hidden, dense, grads, total):
    width = dense.shape[1]
    square = shape((width, width), F32)
    jobs = 2 * (hidden // width) + 4
    return call(
        functools.partial(widen_kernel, hidden),
        [square] * 4 + [shape((width, hidden), F32), shape((hidden, width), F32)] + [shape((width,), F32)] * 4,
        [ANY, ANY, VMEM],
        [
            pltpu.VMEM((jobs, width, width), BF16),
            pltpu.VMEM((6, width, width), F32),
            dma(jobs),
            dma(6),
        ],
        "widen",
        [ANY] * 6 + [VMEM] * 4,
    )(dense, grads, total)


def local(
    inputs,
    cotangent,
    seq_group,
    domain_counts,
    sort_order,
    send_counts,
    gain_one,
    shift_one,
    gain_two,
    shift_two,
    w_query,
    w_key,
    w_value,
    w_out,
    router,
    expert_in,
    expert_out,
):
    tokens, width = inputs.shape
    experts = send_counts.shape[1]
    capacity = 2 * tokens // experts
    spare = capacity // 4
    main = capacity - spare
    slots = experts * main + BLK
    count = lax.axis_size("expert")
    g1, s1, g2, s2 = gain_one, shift_one, gain_two, shift_two
    router_t = router.T
    cot_send, slot_col, slot_row = tables(experts, main, slots, send_counts, seq_group, domain_counts, sort_order, cotangent)
    normed, q, k, v, mixed, hidden, gate, send, cot_rows, probs = forward(
        count, main, spare, inputs, g1, s1, g2, s2, w_query, w_key, w_value, w_out, router_t, slot_col, slot_row, cot_send
    )
    y_rows, dx_back, dx_late, grads = expert_block(
        count, main, spare, send_counts, send, cot_send, cot_rows, router_t, expert_in[0], expert_out[0]
    )
    dp = lax.axis_size("dp")
    grad_inputs, dense, vec, y_back, piece = backward(
        dp, count, main, spare, seq_group, domain_counts, inputs, cotangent, g1, g2, w_query, w_key, w_value, w_out, slot_col,
        normed, q, k, v, mixed, probs, hidden, dx_back, dx_late, y_rows, grads,
    )
    output, dense, vec, grads = finish(dp, count, dense, vec, slot_col, hidden, gate, y_back, y_rows, piece)
    wq, wk, wv, wo, first, second, gain_a, shift_a, gain_b, shift_b = widen(expert_in.shape[2], dense, grads, vec)
    return (output, grad_inputs, gain_a, shift_a, gain_b, shift_b, wq, wk, wv, wo, first[None], second[None])


def solution(mesh):
    rows = P(("dp", "expert"), None)
    split = P("expert", None, None)
    return jax.shard_map(
        local,
        mesh=mesh,
        in_specs=(rows, rows, P(("dp", "expert")), P(), rows, rows) + (P(),) * 9 + (split, split),
        out_specs=(rows, rows) + (P(),) * 8 + (split, split),
        check_vma=False,
    )
```

```python
import functools

import jax
import jax.numpy as jnp
from jax import lax
from jax.experimental import pallas as pl
from jax.experimental.pallas import tpu as pltpu
from jax.sharding import PartitionSpec as P

HEADS = 12
HEAD_DIM = 64
LEN = 1024
EPS = 1e-05
F32 = jnp.float32
BF16 = jnp.bfloat16
BLK = 256
CODE = 4096
LIMIT = 63 * 1024 * 1024

VMEM = pl.BlockSpec(memory_space=pltpu.VMEM)
SMEM = pl.BlockSpec(memory_space=pltpu.SMEM)
ANY = pl.BlockSpec(memory_space=pl.ANY)
MESH = pl.DeviceIdType.MESH


def dot(left, right, contract):
    return lax.dot_general(left, right, ((contract[0:1], contract[1:2]), ((), ())), preferred_element_type=F32)


def nn(left, right):
    return dot(left, right, (1, 0))


def nt(left, right):
    return dot(left, right, (1, 1))


def tn(left, right):
    return dot(left, right, (0, 0))


def iota(shape, axis):
    return lax.broadcasted_iota(jnp.int32, shape, axis)


def flip(index, mask, count):
    bit, out = 1, 0
    while bit < count:
        out = out + ((index // bit + mask // bit) % 2) * bit
        bit *= 2
    return out


def greet(axis, me, count):
    barrier = pltpu.get_barrier_semaphore()
    for mask in range(1, count):
        pl.semaphore_signal(barrier, inc=1, device_id={axis: flip(me, mask, count)}, device_id_type=MESH)
    pl.semaphore_wait(barrier, count - 1)


def copy_to(source, target, send, recv, device):
    return pltpu.make_async_remote_copy(
        src_ref=source, dst_ref=target, send_sem=send, recv_sem=recv, device_id=device, device_id_type=MESH
    )


def span(start, rows):
    return pl.ds(pl.multiple_of(start, 16), rows)


def send_block(me, count, rows, mask, source, target, sends, recvs):
    peer = flip(me, mask, count)
    return copy_to(
        source.at[span(peer * rows, rows)], target.at[span(mask * rows, rows)], sends.at[mask], recvs.at[mask], {"expert": peer}
    )


def return_block(me, count, rows, mask, source, target, sends, recvs, shift=0):
    return copy_to(
        source.at[span((mask - shift) * rows, rows)],
        target.at[span(me * rows, rows)],
        sends.at[mask],
        recvs.at[mask],
        {"expert": flip(me, mask, count)},
    )


def last_returns(count):
    return count // 8


def dp_sides():
    index = lax.axis_index("dp")
    return index, (index % 2, (index // 2) % 2)


def each_rows(rows, step, size=64):
    def body(block, carry):
        step(pl.ds(pl.multiple_of(block * size, size), size))
        return carry

    lax.fori_loop(0, rows // size, body, 0)


def sum_rows(target, other, rows):
    def step(block, carry):
        part = pl.ds(pl.multiple_of(block * BLK, BLK), BLK)
        target[part, :] = (target[part, :].astype(F32) + other[part, :].astype(F32)).astype(BF16)
        return carry

    lax.fori_loop(0, rows // BLK, step, 0)


def depth_of(count):
    return count.bit_length() - 1


def gather_spare(me, count, base, rows, step, first, target, sends, recvs):
    have = rows << step
    source = first.at[pl.ds(base, rows)] if step == 0 else target.at[pl.ds(base, have)]
    return copy_to(
        source,
        target.at[pl.ds(base + have, have)],
        sends.at[step],
        recvs.at[step],
        {"expert": flip(me, count >> (step + 1), count)},
    )


def return_spare(me, count, rows, step, source, shift, landing, sends, recvs):
    half = rows << step
    return copy_to(
        source.at[pl.ds(shift + half, half)],
        landing.at[pl.ds(half, half)],
        sends.at[step],
        recvs.at[step],
        {"expert": flip(me, count >> (step + 1), count)},
    )


def row_of(ref):
    return ref[...].reshape(1, ref.shape[0])


def domain_weight(group_ref, counts_ref):
    groups = counts_ref.shape[0]
    group = group_ref[0]
    total = jnp.zeros((1, 128), F32)
    mine = jnp.zeros((1, 128), F32)
    for index in range(groups):
        inverse = 1.0 / jnp.full((1, 128), counts_ref[index], jnp.int32).astype(F32)
        total = total + inverse
        mine = mine + jnp.where(group == index, inverse, 0.0)
    return (mine / (total / groups))[:, 0:1]


def norm_stats(rows):
    center = rows - jnp.mean(rows, axis=-1, keepdims=True)
    rstd = lax.rsqrt(jnp.mean(center * center, axis=-1, keepdims=True) + EPS)
    return center * rstd, rstd


def pack_rows(slot_row, rows_ref, send_ref):
    slots = send_ref.shape[0]
    tokens = rows_ref.shape[0]

    def step(block, carry):
        base = pl.multiple_of(block * BLK, BLK)
        slot = iota((BLK, tokens), 0) + base
        pick = jnp.where(slot == slot_row, 1.0, 0.0).astype(BF16)
        send_ref[pl.ds(base, BLK), :] = nn(pick, rows_ref[...]).astype(BF16)
        return carry

    lax.fori_loop(0, slots // BLK, step, 0)


def table_kernel(experts, main, counts_ref, group_ref, domain_ref, sort_ref, cot_ref, send_ref, slot_col_ref, slot_row_ref, scaled):
    tokens = cot_ref.shape[0]
    place = iota((1, tokens), 1)
    expert_at = jnp.zeros((1, tokens), jnp.int32)
    start_at = jnp.zeros((1, tokens), jnp.int32)
    end = jnp.int32(0)
    for expert in range(experts):
        count = counts_ref[0, expert]
        end = end + count
        past = place >= end
        expert_at = expert_at + jnp.where(past, 1, 0)
        start_at = start_at + jnp.where(past, count, 0)
    slot = place - start_at
    dest = jnp.where(slot < main, expert_at * main + slot, (experts - 1) * main + slot)
    code = (expert_at * CODE + dest).astype(F32)
    sort_row = sort_ref[...]
    scaled[...] = (cot_ref[...].astype(F32) * domain_weight(group_ref, domain_ref)).astype(BF16)
    for block in range(tokens // BLK):
        token = iota((BLK, tokens), 0) + block * BLK
        col = jnp.sum(jnp.where(token == sort_row, code, 0.0), axis=1, keepdims=True)
        owner = (col * (1.0 / CODE)).astype(jnp.int32)
        where = col.astype(jnp.int32) - owner * CODE
        slot_col_ref[pl.ds(block * BLK, BLK), :] = jnp.where(iota((1, 128), 1) < 64, where, owner)
        slot_row_ref[:, pl.ds(block * BLK, BLK)] = jnp.broadcast_to(where, (BLK, 128)).astype(F32).T[0:8].astype(jnp.int32)
    pack_rows(slot_row_ref[0:1, :], scaled, send_ref)


def forward_kernel(
    count,
    main,
    spare,
    x_ref,
    gain_one_ref,
    shift_one_ref,
    gain_two_ref,
    shift_two_ref,
    wq_hbm,
    wk_hbm,
    wv_hbm,
    wo_hbm,
    router_ref,
    slot_col_ref,
    slot_row_ref,
    cot_send_ref,
    normed_ref,
    q_ref,
    k_ref,
    v_ref,
    mixed_ref,
    hidden_ref,
    gate_ref,
    send_ref,
    cot_rows_ref,
    probs_hbm,
    wq_ref,
    wk_ref,
    wv_ref,
    wo_ref,
    routed,
    probs,
    prob_sems,
    sends,
    recvs,
    spare_sends,
    spare_recvs,
    own,
    fills,
):
    tokens, width = x_ref.shape
    blocks = tokens // BLK
    me = lax.axis_index("expert")
    weights = [(wq_hbm, wq_ref), (wk_hbm, wk_ref), (wv_hbm, wv_ref), (wo_hbm, wo_ref)]
    weights = [pltpu.make_async_copy(source, target, fills.at[i]) for i, (source, target) in enumerate(weights)]
    for copy in weights:
        copy.start()
    greet("expert", me, count)
    base = count * main

    def gather(step):
        return gather_spare(me, count, base, spare, step, cot_send_ref, cot_rows_ref, spare_sends, spare_recvs)

    gather(0).start()
    copies = [send_block(me, count, main, mask, cot_send_ref, cot_rows_ref, sends, recvs) for mask in range(1, count - 1)]
    for copy in copies:
        copy.start()
    mine = [
        pltpu.make_async_copy(cot_send_ref.at[span(me * main, main)], cot_rows_ref.at[pl.ds(0, main)], own.at[0]),
        pltpu.make_async_copy(cot_send_ref.at[pl.ds(base, spare)], cot_rows_ref.at[pl.ds(base, spare)], own.at[1]),
    ]
    for copy in mine:
        copy.start()
    lane = iota((1, 128), 1)
    gain_one, shift_one, gain_two, shift_two = (row_of(r) for r in (gain_one_ref, shift_one_ref, gain_two_ref, shift_two_ref))

    def project(block, carry):
        rows = pl.ds(pl.multiple_of(block * BLK, BLK), BLK)
        hat, _ = norm_stats(x_ref[rows, :].astype(F32))
        normed = (hat * gain_one + shift_one).astype(BF16)
        normed_ref[rows, :] = normed
        q_ref[rows, :] = (nn(normed, wq_ref[...]).astype(BF16) * (HEAD_DIM ** (-0.5))).astype(BF16)
        k_ref[rows, :] = nn(normed, wk_ref[...]).astype(BF16)
        v_ref[rows, :] = nn(normed, wv_ref[...]).astype(BF16)
        return carry

    for copy in weights:
        copy.wait()
    lax.fori_loop(0, blocks, project, 0)

    keep = iota((BLK, BLK), 0) <= iota((BLK, BLK), 1)

    def keep_probs(pair):
        return pltpu.make_async_copy(probs.at[pair % 2], probs_hbm.at[pair], prob_sems.at[pair % 2])

    def attend(pair, carry):
        @pl.when(pair >= 2)
        def _():
            keep_probs(pair - 2).wait()

        cols = pl.ds(pl.multiple_of(pair * 128, 128), 128)
        k_pair = k_ref[:, cols]
        v_t = v_ref[:, cols].astype(F32).T.astype(BF16)
        k_head = [jnp.where(lane < 64, k_pair, 0), jnp.where(lane >= 64, k_pair, 0)]
        for block in range(blocks):
            span = (block + 1) * BLK
            query = q_ref[pl.ds(block * BLK, BLK), cols]
            outs = []
            for half in range(2):
                scores = nt(k_head[half][:span], query)
                diag = jnp.where(keep, scores[block * BLK :], -1000000000.0)
                scores = jnp.concatenate([scores[: block * BLK], diag], axis=0) if block else diag
                peak = jnp.max(scores, axis=0, keepdims=True)
                exps = jnp.exp(scores - peak)
                total = jnp.sum(exps, axis=0, keepdims=True)
                attention = (exps * (1.0 / total)).astype(BF16)
                probs[pair % 2, half, pl.ds(block * (block + 1) // 2 * BLK, (block + 1) * BLK), :] = attention
                outs.append(nn(v_t[half * 64 : half * 64 + 64, :span], attention))
            mixed_ref[pl.ds(block * BLK, BLK), cols] = jnp.concatenate(outs, axis=0).T.astype(BF16)
        keep_probs(pair).start()
        return carry

    lax.fori_loop(0, HEADS // 2, attend, 0)
    experts = router_ref.shape[0]

    def finish(block, carry):
        rows = pl.ds(pl.multiple_of(block * BLK, BLK), BLK)
        hidden = x_ref[rows, :].astype(F32) + nn(mixed_ref[rows, :], wo_ref[...])
        hidden_ref[rows, :] = hidden
        hat, _ = norm_stats(hidden)
        low = (hat * gain_two + shift_two).astype(BF16)
        routed[rows, :] = low
        logits = nt(low, router_ref[...])
        owner = slot_col_ref[rows, 64:65]
        logit = jnp.sum(jnp.where(iota((BLK, experts), 1) == owner, logits, 0.0), axis=1, keepdims=True)
        gate_ref[rows, :] = jnp.broadcast_to(jax.nn.sigmoid(logit), (BLK, 128))
        return carry

    lax.fori_loop(0, blocks, finish, 0)
    pack_rows(slot_row_ref[0:1, :], routed, send_ref)
    for copy in mine + [keep_probs(HEADS // 2 - 2), keep_probs(HEADS // 2 - 1)]:
        copy.wait()
    for copy in copies + [gather(0)]:
        copy.wait()


def gelu_parts(v):
    t = 1.0 / (1.0 + (0.3275911 * 0.7071067811865476) * jnp.abs(v))
    bell = jnp.exp2((-0.5 * 1.4426950408889634) * (v * v))
    poly = ((((0.5307027145 * t - 0.7265760135) * t + 0.7107068705) * t - 0.142248368) * t + 0.127414796) * t
    tail = poly * bell
    return jnp.where(v >= 0.0, 1.0 - tail, tail), bell * 0.3989422804014327


def expert_kernel(
    count,
    main,
    spare,
    chunk,
    counts_ref,
    send_ref,
    cot_send_ref,
    cot_rows_ref,
    router_ref,
    w1_hbm,
    w2_hbm,
    y_ref,
    back_ref,
    late_ref,
    grads_ref,
    w1_ref,
    w2_ref,
    acc1,
    acc2,
    x_rows,
    g_ref,
    dx_rows,
    y_rows,
    stage,
    load_sems,
    sends,
    recvs,
    spare_sends,
    spare_recvs,
    cot_sends,
    cot_recvs,
    back_sends,
    back_recvs,
    own,
    y_sems,
    stage_sems,
):
    width, hidden = w1_ref.shape
    slots = x_rows.shape[0]
    base = count * main
    plain = base // BLK
    blocks = slots // BLK
    depth = depth_of(count)
    early = count - count // 4
    me = lax.axis_index("expert")
    loads = [
        pltpu.make_async_copy(w1_hbm, w1_ref, load_sems.at[0]),
        pltpu.make_async_copy(w2_hbm, w2_ref, load_sems.at[1]),
        pltpu.make_async_copy(cot_rows_ref.at[pl.ds(0, base - main)], g_ref.at[pl.ds(0, base - main)], load_sems.at[2]),
        pltpu.make_async_copy(cot_rows_ref.at[pl.ds(base, 2 * spare)], g_ref.at[pl.ds(base, 2 * spare)], load_sems.at[3]),
    ]
    for load in loads:
        load.start()
    greet("expert", me, count)

    def gather(step):
        return gather_spare(me, count, base, spare, step, send_ref, x_rows, spare_sends, spare_recvs)

    def arrive(mask):
        return send_block(me, count, main, mask, send_ref, x_rows, sends, recvs)

    def leave(mask):
        return return_block(me, count, main, mask, dx_rows, back_ref, back_sends, back_recvs)

    def gather_cot(step):
        source = cot_rows_ref if step == 1 else g_ref
        have = spare << step
        return copy_to(
            source.at[pl.ds(base, have)],
            g_ref.at[pl.ds(base + have, have)],
            cot_sends.at[step],
            cot_recvs.at[step],
            {"expert": flip(me, count >> (step + 1), count)},
        )

    def last_cot():
        rows = span(flip(me, count - 1, count) * main, main)
        return copy_to(
            cot_send_ref.at[rows],
            g_ref.at[pl.ds(base - main, main)],
            cot_sends.at[0],
            cot_recvs.at[0],
            {"expert": flip(me, count - 1, count)},
        )

    gather_cot(1).start()
    gather(0).start()
    for mask in range(1, count):
        arrive(mask).start()
    last_cot().start()
    mine_in = [
        pltpu.make_async_copy(send_ref.at[span(me * main, main)], x_rows.at[pl.ds(0, main)], own.at[0]),
        pltpu.make_async_copy(send_ref.at[pl.ds(base, spare)], x_rows.at[pl.ds(base, spare)], own.at[1]),
    ]
    for copy in mine_in:
        copy.start()

    def clear_one(part):
        acc1[part, :] = jnp.zeros((64, hidden), F32)

    def clear_two(part):
        acc2[part, :] = jnp.zeros((64, width), F32)

    each_rows(width, clear_one)
    each_rows(hidden, clear_two)
    experts = router_ref.shape[0]
    router = jnp.sum(jnp.where(iota((experts, 1), 0) == me, router_ref[...].astype(F32), 0.0), axis=0, keepdims=True)
    hot = jnp.full((1, 128), counts_ref[0, me], jnp.int32)[:, 0:1] > main
    hot = jnp.where(hot, 1.0, 0.0)
    for copy in loads + mine_in:
        copy.wait()

    def store_y(block):
        rows = pl.ds(pl.multiple_of(block * BLK, BLK), BLK)
        return pltpu.make_async_copy(y_rows.at[rows], y_ref.at[rows], y_sems.at[block])

    def mine_out():
        return pltpu.make_async_copy(dx_rows.at[pl.ds(0, main)], back_ref.at[span(me * main, main)], own.at[0])

    def run(turn, carry):
        block = turn + turn // (plain - 1) - (turn // (blocks - 1)) * (blocks - plain + 1)
        for item in range(BLK // main + 1):
            mask = (block * BLK + main - 1) // main + item

            @pl.when((block < plain) & (mask > 0) & (mask < ((block + 1) * BLK + main - 1) // main))
            def _():
                arrive(mask).wait_recv()

            @pl.when((block == plain - 1) & (mask == count - 1))
            def _():
                last_cot().wait_recv()

        for step in range(depth):

            @pl.when(turn == (max(step + 1, plain - depth + step + 1) if step else 1))
            def _():
                gather(step).wait_recv()
                if step:
                    gather_cot(step).wait_recv()
                if step + 1 < depth:
                    gather(step + 1).start()
                    if step:
                        gather_cot(step + 1).start()

        rows = pl.ds(pl.multiple_of(block * BLK, BLK), BLK)
        live = jnp.where(block < plain, 1.0, hot)
        x = (x_rows[rows, :].astype(F32) * live).astype(BF16)
        logit = jnp.sum(x.astype(F32) * router, axis=1, keepdims=True)
        gate = jax.nn.sigmoid(logit)
        go = g_ref[rows, :].astype(F32) * live
        g = (gate * go).astype(BF16)
        x_t = x.astype(F32).T.astype(BF16)
        y = jnp.zeros(x.shape, F32)
        dx = jnp.zeros(x.shape, F32)
        for first in range(0, hidden, chunk):
            cols = pl.ds(first, chunk)
            w1 = w1_ref[:, cols]
            w2 = w2_ref[cols, :]
            pre = nn(x, w1)
            cdf, pdf = gelu_parts(pre)
            act = (pre * cdf).astype(BF16)
            slope = cdf + pre * pdf
            y = y + nn(act, w2)
            grad = (nt(g, w2) * slope).astype(BF16)
            dx = dx + nt(grad, w1)
            acc1[:, cols] += nn(x_t, grad)
            acc2[cols, :] += tn(act, g)
        y_low = y.astype(BF16)
        y_rows[rows, :] = y_low
        dlogit = jnp.sum(y_low.astype(F32) * go, axis=1, keepdims=True) * gate * (1.0 - gate)
        dx_rows[rows, :] = (dx + dlogit * router).astype(BF16)
        store_y(block).start()
        for item in range(BLK // main + 1):
            mask = (block * BLK) // main + item
            done = (block < plain) & (mask < ((block + 1) * BLK) // main)

            @pl.when(done & (mask > 0) & (mask < early))
            def _():
                leave(mask).start()

            @pl.when(done & (mask == 0))
            def _():
                mine_out().start()

        return carry

    lax.fori_loop(0, blocks, run, 0)
    tail = pltpu.make_async_copy(dx_rows.at[pl.ds(early * main, slots - early * main)], late_ref, own.at[1])
    tail.start()

    pieces = []
    for first in range(0, hidden, width):
        pieces.append((acc1.at[:, pl.ds(first, width)], grads_ref.at[pl.ds(first, width)]))
    for first in range(0, hidden, width):
        pieces.append((acc2.at[pl.ds(first, width), :], grads_ref.at[pl.ds(hidden + first, width)]))
    writes = []
    for index, (piece, target) in enumerate(pieces):
        slot = index % 2
        if index >= 2:
            writes[index - 2].wait()

        def narrow(part):
            stage[slot, part, :] = piece[part, :].astype(BF16)

        each_rows(width, narrow)
        write = pltpu.make_async_copy(stage.at[slot], target, stage_sems.at[slot])
        write.start()
        writes.append(write)
    for write in writes[-2:]:
        write.wait()
    mine_out().wait()
    tail.wait()

    def settle(block, carry):
        store_y(block).wait()
        return carry

    lax.fori_loop(0, blocks, settle, 0)
    for step in range(depth):
        gather(step).wait_send()
    for step in range(1, depth):
        gather_cot(step).wait_send()
    last_cot().wait_send()
    for mask in range(1, count):
        arrive(mask).wait_send()
    for mask in range(1, early):
        leave(mask).wait()


def backward_kernel(
    dp,
    count,
    main,
    spare,
    group_ref,
    domain_ref,
    x_hbm,
    cot_hbm,
    gain_one_ref,
    gain_two_ref,
    wq_hbm,
    wk_hbm,
    wv_hbm,
    wo_hbm,
    slot_col_hbm,
    normed_hbm,
    q_hbm,
    k_hbm,
    v_hbm,
    mixed_hbm,
    probs_hbm,
    hidden_hbm,
    dx_hbm,
    late_ref,
    y_ref,
    grads_hbm,
    grad_ref,
    dense_hbm,
    vec_ref,
    y_back_ref,
    piece_ref,
    x_ref,
    cot_ref,
    wq_ref,
    wk_ref,
    wv_ref,
    wo_ref,
    slot_col_ref,
    normed_ref,
    q_ref,
    k_ref,
    v_ref,
    mixed_ref,
    hidden_ref,
    dense_ref,
    dx_ref,
    spare_dx,
    spare_y,
    dx_land,
    y_land,
    probs,
    kept,
    land_one,
    land_two,
    gmix,
    branch,
    normed_t,
    dqkv,
    sums,
    sends,
    recvs,
    late_sends,
    late_recvs,
    dx_sends,
    dx_recvs,
    y_sends,
    y_recvs,
    own,
    gets,
    fills,
    scatter_sends,
    scatter_recvs,
    keeps,
    prob_sems,
    puts,
):
    tokens, width = x_ref.shape
    me = lax.axis_index("expert")
    early = count - count // 4
    base = count * main
    late = (count - early) * main
    total = count * spare
    depth = depth_of(count)
    operands = [
        (x_hbm, x_ref),
        (cot_hbm, cot_ref),
        (wq_hbm, wq_ref),
        (wk_hbm, wk_ref),
        (wv_hbm, wv_ref),
        (wo_hbm, wo_ref),
        (slot_col_hbm, slot_col_ref),
        (normed_hbm, normed_ref),
        (q_hbm, q_ref),
        (k_hbm, k_ref),
        (v_hbm, v_ref),
        (mixed_hbm, mixed_ref),
        (hidden_hbm, hidden_ref),
    ]
    operands = [pltpu.make_async_copy(source, target, fills.at[i]) for i, (source, target) in enumerate(operands)]
    for copy in operands:
        copy.start()
    barrier = pltpu.get_barrier_semaphore()
    place, bits = dp_sides()
    for mask in range(1, count):
        pl.semaphore_signal(barrier, inc=1, device_id={"expert": flip(me, mask, count)}, device_id_type=MESH)
    for mask in (1, 2):
        pl.semaphore_signal(barrier, inc=1, device_id={"dp": flip(place, mask, dp)}, device_id_type=MESH)
    pl.semaphore_wait(barrier, count + 1)
    portion = grads_hbm.shape[0] // 4
    quarter = portion // 2

    def scatter_one(stream, second):
        side = bits[1 - stream] if second else 1 - bits[1 - stream]
        start = 2 * portion * stream + (1 - bits[stream]) * portion + side * quarter
        device = {"dp": flip(place, 1 << stream, dp)}
        return copy_to(
            grads_hbm.at[span(start, quarter)],
            land_one.at[stream, span(side * quarter, quarter)],
            scatter_sends.at[second, stream],
            scatter_recvs.at[second, stream],
            device,
        )

    def add_one(stream, second):
        side = bits[1 - stream] if second else 1 - bits[1 - stream]
        scatter_one(stream, second).wait()

        def step(rows):
            held = span(side * quarter + rows.start, 64)
            kept[stream, held, :] = (kept[stream, held, :].astype(F32) + land_one[stream, held, :].astype(F32)).astype(BF16)

        each_rows(quarter, step)

    def keep_one(stream):
        start = 2 * portion * stream + bits[stream] * portion
        return pltpu.make_async_copy(grads_hbm.at[span(start, portion)], kept.at[stream], keeps.at[stream])

    def scatter_two(stream):
        start = (1 - bits[1 - stream]) * quarter
        device = {"dp": flip(place, 2 >> stream, dp)}
        return copy_to(
            kept.at[stream, span(start, quarter)],
            land_two.at[stream],
            scatter_sends.at[2, stream],
            scatter_recvs.at[2, stream],
            device,
        )

    def store_piece(stream):
        start = bits[1 - stream] * quarter
        return pltpu.make_async_copy(
            kept.at[stream, span(start, quarter)], piece_ref.at[pl.ds(stream * quarter, quarter)], keeps.at[stream]
        )

    def load_probs(pair):
        return pltpu.make_async_copy(probs_hbm.at[pair], probs.at[pair % 2], prob_sems.at[pair % 2])

    load_probs(0).start()
    for part in range(2):
        for stream in range(2):
            scatter_one(stream, part).start()
    for stream in range(2):
        keep_one(stream).start()

    def sum_dx(step):
        if step == depth - 1:
            return return_spare(me, count, spare, step, late_ref, late, dx_land, dx_sends, dx_recvs)
        return return_spare(me, count, spare, step, spare_dx, 0, dx_land, dx_sends, dx_recvs)

    def sum_y(step):
        if step == depth - 1:
            return return_spare(me, count, spare, step, y_ref, base, y_land, y_sends, y_recvs)
        return return_spare(me, count, spare, step, spare_y, 0, y_land, y_sends, y_recvs)

    def settle(copy, own_rows, landing, step):
        copy.wait()
        rows = spare << step
        own_rows[0:rows, :] = (own_rows[0:rows, :].astype(F32) + landing[rows : 2 * rows, :].astype(F32)).astype(BF16)

    sum_dx(depth - 1).start()
    lates = [return_block(me, count, main, mask, late_ref, dx_ref, late_sends, late_recvs, early) for mask in range(early, count)]
    for copy in lates:
        copy.start()
    copies = [
        return_block(me, count, main, mask, y_ref, y_back_ref, sends, recvs) for mask in range(1, count - last_returns(count))
    ]
    mine = pltpu.make_async_copy(y_ref.at[pl.ds(0, main)], y_back_ref.at[span(me * main, main)], own.at[0])
    mine.start()
    loads = [
        pltpu.make_async_copy(late_ref.at[pl.ds(late, total)], spare_dx, own.at[1]),
        pltpu.make_async_copy(y_ref.at[pl.ds(base, total)], spare_y, own.at[2]),
    ]
    for mask in range(early):
        part = span(flip(me, mask, count) * main, main)
        loads.append(pltpu.make_async_copy(dx_hbm.at[part], dx_ref.at[part], gets.at[mask]))
    for load in loads:
        load.start()
    for load in loads:
        load.wait()
    for step in reversed(range(depth)):
        settle(sum_dx(step), spare_dx, dx_land, step)
        if step:
            sum_dx(step - 1).start()
    dx_ref[pl.ds(base, BLK), :] = spare_dx[0:BLK, :]
    for copy in lates:
        copy.wait()
    sum_y(depth - 1).start()
    for copy in copies:
        copy.start()
    for copy in operands:
        copy.wait()
    slots = dx_ref.shape[0]
    blocks = tokens // BLK
    lane = iota((1, 128), 1)
    weight = domain_weight(group_ref, domain_ref)
    gain_one = row_of(gain_one_ref)
    gain_two = row_of(gain_two_ref)
    sums[...] = jnp.zeros_like(sums)

    def open_block(block, carry):
        rows = pl.ds(pl.multiple_of(block * BLK, BLK), BLK)
        slot = slot_col_ref[rows, 0:1]
        pick = jnp.where(iota((BLK, slots), 1) == slot, 1.0, 0.0).astype(BF16)
        grad = nn(pick, dx_ref[...])
        hat, rstd = norm_stats(hidden_ref[rows, :])
        sums[2:3, :] += jnp.sum(grad * hat, axis=0, keepdims=True)
        sums[3:4, :] += jnp.sum(grad, axis=0, keepdims=True)
        gg = grad * gain_two
        inner = gg - jnp.mean(gg, axis=1, keepdims=True) - hat * jnp.mean(gg * hat, axis=1, keepdims=True)
        total = cot_ref[rows, :].astype(F32) * weight + rstd * inner
        hidden_ref[rows, :] = total
        low = total.astype(BF16)
        branch[rows, :] = low
        gmix[rows, :] = nt(low, wo_ref[...]).astype(BF16)
        normed_t[:, rows] = normed_ref[rows, :].astype(F32).T.astype(BF16)
        return carry

    lax.fori_loop(0, blocks, open_block, 0)
    def put_dense(part):
        rows = pl.ds(part * width, width)
        return pltpu.make_async_copy(dense_ref.at[rows], dense_hbm.at[rows], puts.at[part])

    dense_ref[pl.ds(3 * width, width), :] = tn(mixed_ref[...], branch[...]).astype(BF16)
    put_dense(3).start()
    settle(sum_y(depth - 1), spare_y, y_land, depth - 1)
    sum_y(depth - 2).start()

    for stream in range(2):
        keep_one(stream).wait()
        add_one(stream, 0)
        scatter_two(stream).start()

    def attend(pair, carry):
        @pl.when(pair + 1 < HEADS // 2)
        def _():
            load_probs(pair + 1).start()

        @pl.when(pair == 4)
        def _():
            for stream in range(2):
                add_one(stream, 1)

        load_probs(pair).wait()
        base = pl.multiple_of(pair * 128, 128)
        cols = pl.ds(base, 128)
        q_pair = q_ref[:, cols]
        k_pair = k_ref[:, cols]
        v_pair = v_ref[:, cols]
        o_pair = gmix[:, cols]
        low = lane < 64
        q_head = [jnp.where(low, q_pair, 0), jnp.where(low, 0, q_pair)]
        v_head = [jnp.where(low, v_pair, 0), jnp.where(low, 0, v_pair)]
        o_head = [jnp.where(low, o_pair, 0), jnp.where(low, 0, o_pair)]
        k_t = k_pair.astype(F32).T.astype(BF16)
        prod_t = (o_pair.astype(F32) * mixed_ref[:, cols].astype(F32)).T
        delta = [jnp.sum(prod_t[:64], axis=0, keepdims=True), jnp.sum(prod_t[64:], axis=0, keepdims=True)]
        dq_t = [[None] * blocks, [None] * blocks]
        for block in range(blocks):
            start = block * BLK
            dk = None
            dv = None
            for half in range(2):
                tiles = [
                    probs[pair % 2, half, pl.ds((later * (later + 1) // 2 + block) * BLK, BLK), :]
                    for later in range(block, blocks)
                ]
                attention = jnp.concatenate(tiles, axis=1) if block < blocks - 1 else tiles[0]
                grad_p = nt(v_head[half][start : start + BLK], o_pair[start:])
                grad_s = (attention.astype(F32) * (grad_p - delta[half][:, start:])).astype(BF16)
                dv_part = nn(attention, o_head[half][start:])
                dk_part = nn(grad_s, q_head[half][start:])
                dv = dv_part if dv is None else dv + dv_part
                dk = dk_part if dk is None else dk + dk_part
                dq_part = nn(k_t[half * 64 : half * 64 + 64, start : start + BLK], grad_s)
                for later in range(block, blocks):
                    piece = dq_part[:, (later - block) * BLK : (later - block + 1) * BLK]
                    dq_t[half][later] = piece if dq_t[half][later] is None else dq_t[half][later] + piece
            rows = pl.ds(start, BLK)
            dqkv[rows, pl.ds(pl.multiple_of(base + width, 128), 128)] = dk.astype(BF16)
            dqkv[rows, pl.ds(pl.multiple_of(base + 2 * width, 128), 128)] = dv.astype(BF16)
        for block in range(blocks):
            both = jnp.concatenate([dq_t[0][block], dq_t[1][block]], axis=0) * (HEAD_DIM ** (-0.5))
            dqkv[pl.ds(block * BLK, BLK), cols] = both.T.astype(BF16)
        return carry

    lax.fori_loop(0, HEADS // 2, attend, 0)

    for part in range(3):
        dense_ref[pl.ds(part * width, width), :] = nn(normed_t[...], dqkv[:, pl.ds(part * width, width)]).astype(BF16)
        put_dense(part).start()

    def close_block(block, carry):
        rows = pl.ds(pl.multiple_of(block * BLK, BLK), BLK)
        grad = nt(dqkv[rows, 0:width], wq_ref[...])
        grad = grad + nt(dqkv[rows, width : 2 * width], wk_ref[...])
        grad = grad + nt(dqkv[rows, 2 * width : 3 * width], wv_ref[...])
        hat, rstd = norm_stats(x_ref[rows, :].astype(F32))
        sums[0:1, :] += jnp.sum(grad * hat, axis=0, keepdims=True)
        sums[1:2, :] += jnp.sum(grad, axis=0, keepdims=True)
        gg = grad * gain_one
        inner = gg - jnp.mean(gg, axis=1, keepdims=True) - hat * jnp.mean(gg * hat, axis=1, keepdims=True)
        grad_ref[rows, :] = (hidden_ref[rows, :] + rstd * inner).astype(BF16)
        return carry

    lax.fori_loop(0, blocks, close_block, 0)
    vec_ref[...] = sums[...]
    for stream in range(2):
        scatter_two(stream).wait()
        start = bits[1 - stream] * quarter
        sum_rows(kept.at[stream, span(start, quarter)], land_two.at[stream], quarter)
        store_piece(stream).start()
    for step in reversed(range(depth - 1)):
        settle(sum_y(step), spare_y, y_land, step)
        if step:
            sum_y(step - 1).start()
    spare_out = pltpu.make_async_copy(spare_y.at[pl.ds(0, BLK)], y_back_ref.at[pl.ds(base, BLK)], own.at[1])
    spare_out.start()
    spare_out.wait()
    for stream in range(2):
        store_piece(stream).wait()
    for part in range(4):
        put_dense(part).wait()
    mine.wait()
    for copy in copies:
        copy.wait()


STREAMS = 3
CHUNKS = 4


def halving_plan(dp, count, rows):
    experts = [("expert", 2 << bit) for bit in range(depth_of(count) - 1)]
    groups = [("dp", 1 << bit) for bit in range(depth_of(dp))]
    core = [("expert", 1)]
    plans = [core + groups + experts, core + groups[::-1] + experts, core + experts + groups]
    halvings = 0
    while halvings < len(plans[0]) and (rows >> halvings) % 32 == 0:
        halvings += 1
    return plans, halvings


def finish_kernel(
    dp,
    count,
    dense_hbm,
    vec_ref,
    slot_col_hbm,
    hidden_hbm,
    gate_hbm,
    y_hbm,
    y_rows_hbm,
    piece_ref,
    out_ref,
    full_ref,
    total_ref,
    grads_ref,
    dense_ref,
    slot_col_ref,
    hidden_ref,
    gate_ref,
    y_ref,
    acc,
    landing,
    full,
    vec_acc,
    vec_land,
    sends,
    recvs,
    back_sends,
    back_recvs,
    vec_sends,
    vec_recvs,
    put,
    unit_sends,
    unit_recvs,
    own,
    y_sends,
    y_recvs,
    gets,
    fills,
):
    tokens, width = hidden_ref.shape
    slots = y_ref.shape[0]
    main = (slots - BLK) // count
    early = count - last_returns(count)
    rows = dense_ref.shape[0] // STREAMS
    place = {"dp": lax.axis_index("dp"), "expert": lax.axis_index("expert")}
    size = {"dp": dp, "expert": count}
    plans, halvings = halving_plan(dp, count, rows)
    steps = len(plans[0])

    def partner(axis, mask):
        return {axis: flip(place[axis], mask, size[axis])}

    operands = [(dense_hbm, dense_ref), (slot_col_hbm, slot_col_ref), (hidden_hbm, hidden_ref), (gate_hbm, gate_ref)]
    operands = [pltpu.make_async_copy(source, target, fills.at[i]) for i, (source, target) in enumerate(operands)]
    for copy in operands:
        copy.start()
    barrier = pltpu.get_barrier_semaphore()
    for axis, mask in plans[0]:
        pl.semaphore_signal(barrier, inc=1, device_id=partner(axis, mask), device_id_type=MESH)
    for mask in range(early, count):
        pl.semaphore_signal(barrier, inc=1, device_id=partner("expert", mask), device_id_type=MESH)
    pl.semaphore_wait(barrier, steps + count - early)
    me = place["expert"]
    y_copies = [return_block(me, count, main, mask, y_rows_hbm, y_ref, y_sends, y_recvs) for mask in range(early, count)]
    loads = [pltpu.make_async_copy(y_hbm.at[pl.ds(count * main, BLK)], y_ref.at[pl.ds(count * main, BLK)], gets.at[count])]
    for mask in range(early):
        part = span(flip(me, mask, count) * main, main)
        loads.append(pltpu.make_async_copy(y_hbm.at[part], y_ref.at[part], gets.at[mask]))
    for load in loads:
        load.start()

    def side(axis, mask):
        return (place[axis] // mask) % 2

    _, bits = dp_sides()
    quarter = piece_ref.shape[0] // 2
    chunk = quarter // CHUNKS
    starts = [
        4 * quarter * stream + bits[stream] * 2 * quarter + bits[1 - stream] * quarter for stream in range(2)
    ]
    others = [
        4 * quarter * stream + bits[stream] * 2 * quarter + (1 - bits[1 - stream]) * quarter for stream in range(2)
    ]

    def unit(index, stream):
        kind, part = index // CHUNKS, index % CHUNKS
        near, far = partner("dp", 1 << stream), partner("dp", 2 >> stream)
        if kind == 2:
            source = target = grads_ref.at[span(others[stream] + part * chunk, chunk)]
        else:
            source = piece_ref.at[pl.ds(stream * quarter + part * chunk, chunk)]
            target = grads_ref.at[span(starts[stream] + part * chunk, chunk)]
        return copy_to(
            source, target, unit_sends.at[index, stream], unit_recvs.at[index, stream], far if kind == 0 else near
        )

    pending = list(range(3 * CHUNKS))

    def advance(number):
        for _ in range(min(number, len(pending))):
            index = pending.pop(0)
            for stream in range(2):
                if index >= 2 * CHUNKS:
                    unit(index - 2 * CHUNKS, stream).wait_recv()
                unit(index, stream).start()

    mine = [
        pltpu.make_async_copy(
            piece_ref.at[pl.ds(stream * quarter, quarter)], grads_ref.at[span(starts[stream], quarter)], own.at[stream]
        )
        for stream in range(2)
    ]
    for copy in mine:
        copy.start()

    def combine(block):
        rows_at = pl.ds(pl.multiple_of(block * BLK, BLK), BLK)
        slot = slot_col_ref[rows_at, 0:1]
        pick = jnp.where(iota((BLK, slots), 1) == slot, 1.0, 0.0).astype(BF16)
        returned = nn(pick, y_ref[...])
        out_ref[rows_at, :] = (hidden_ref[rows_at, :] + gate_ref[rows_at, 0:1] * returned).astype(BF16)

    low = [jnp.int32(stream * rows) for stream in range(STREAMS)]
    extent = rows
    offset = 0
    trail = []
    for step in range(steps):
        halve = step < halvings
        part = extent // 2 if halve else extent
        copies = []
        for stream in range(STREAMS):
            axis, mask = plans[stream][step]
            kept = low[stream] + side(axis, mask) * part if halve else low[stream]
            other = low[stream] + (1 - side(axis, mask)) * part if halve else low[stream]
            source = dense_ref if step == 0 else acc.at[(step - 1) % 2]
            land = landing.at[stream, pl.ds(offset, part)]
            copy = copy_to(
                (dense_hbm if step == 0 else source).at[span(other, part)], land, sends.at[stream, step], recvs.at[stream, step], partner(axis, mask)
            )
            copy.start()
            copies.append((copy, kept, source))
        axis, mask = plans[0][step]
        vec_source = vec_ref if step == 0 else vec_acc.at[step - 1]
        vec_copy = copy_to(vec_source, vec_land.at[step], vec_sends.at[step], vec_recvs.at[step], partner(axis, mask))
        vec_copy.start()
        advance(1)
        if step == 0:
            for copy in y_copies:
                copy.start()
        if step == 0:
            for copy in operands:
                copy.wait()
        trail.append((list(low), extent))
        for stream in range(STREAMS):
            copy, kept, source = copies[stream]
            copy.wait()
            target = acc.at[step % 2] if step < steps - 1 else full
            grain = min(part, 64)

            def add(rows_at):
                held = span(kept + rows_at.start, grain)
                value = source[held, :].astype(F32) + landing[stream, span(offset + rows_at.start, grain), :].astype(F32)
                target[held, :] = value.astype(BF16)

            each_rows(part, add, grain)
            low[stream] = kept
        vec_copy.wait()
        vec_sum = vec_source[...] + vec_land[step]
        if step < steps - 1:
            vec_acc[step] = vec_sum
        else:
            total_ref[...] = vec_sum
        extent = part
        offset += part

    for step in reversed(range(halvings)):
        origins, whole = trail[step]
        copies = []
        for stream in range(STREAMS):
            axis, mask = plans[stream][step]
            held = span(low[stream], extent)
            copy = copy_to(
                full.at[held], full.at[held], back_sends.at[stream, step], back_recvs.at[stream, step], partner(axis, mask)
            )
            copy.start()
            copies.append(copy)
        advance(2)
        if step == 1:
            for copy in loads + y_copies:
                copy.wait()

            def combine_block(block, carry):
                combine(block)
                return carry

            lax.fori_loop(0, tokens // BLK, combine_block, 0)
        for stream in range(STREAMS):
            copies[stream].wait()
            low[stream] = origins[stream]
        extent = whole
    advance(len(pending))
    write = pltpu.make_async_copy(full, full_ref, put)
    write.start()
    for index in range(3 * CHUNKS):
        for stream in range(2):
            if index >= CHUNKS:
                unit(index, stream).wait_recv()
            unit(index, stream).wait_send()
    for copy in mine + [write]:
        copy.wait()


AHEAD = 4


def widen_kernel(hidden, dense_hbm, grads_hbm, total_ref, output_hbm, inputs_hbm, *rest):
    outs, vecs, passed, (low, high, rows, gets, puts, moves) = rest[:6], rest[6:10], rest[10:12], rest[12:]
    width = dense_hbm.shape[1]
    jobs = []
    for block in range(hidden // width):
        part = pl.ds(block * width, width)
        jobs.append((grads_hbm.at[part], outs[4].at[:, part]))
        jobs.append((grads_hbm.at[pl.ds(hidden + block * width, width)], outs[5].at[part, :]))
    for index in range(4):
        jobs.append((dense_hbm.at[pl.ds(index * width, width)], outs[index]))
    loads = [pltpu.make_async_copy(source, low.at[i], gets.at[i]) for i, (source, _) in enumerate(jobs)]
    for load in loads[:AHEAD]:
        load.start()
    for index, vec in enumerate(vecs):
        vec[...] = total_ref[index : index + 1, :].reshape(width)
    taken = [pltpu.make_async_copy(source, rows.at[i], moves.at[i]) for i, source in enumerate((output_hbm, inputs_hbm))]
    given = [pltpu.make_async_copy(rows.at[i], target, moves.at[i]) for i, target in enumerate(passed)]
    slots = high.shape[0]
    stores = []
    for index, (_, target) in enumerate(jobs):
        loads[index].wait()
        if index + AHEAD < len(jobs):
            loads[index + AHEAD].start()
        if index == 1:
            for copy in taken:
                copy.start()
        if index == 4:
            for before, after in zip(taken, given):
                before.wait()
                after.start()
        if index >= slots:
            stores[index - slots].wait()

        def step(part):
            high[index % slots, part, :] = low[index, part, :].astype(F32)

        each_rows(width, step)
        stores.append(pltpu.make_async_copy(high.at[index % slots], target, puts.at[index % slots]))
        stores[-1].start()
    for copy in stores[-slots:] + given:
        copy.wait()


def call(kernel, outs, in_specs, scratch, name, out_specs=None, collective=None, flops=10**9):
    remote = {} if collective is None else {"collective_id": collective, "has_side_effects": True}
    return pl.pallas_call(
        kernel,
        out_shape=outs,
        in_specs=in_specs,
        out_specs=out_specs or [VMEM] * len(outs),
        scratch_shapes=scratch,
        compiler_params=pltpu.CompilerParams(vmem_limit_bytes=LIMIT, **remote),
        cost_estimate=pl.CostEstimate(flops=flops, bytes_accessed=10**7, transcendentals=0),
        name=name,
    )


def dma(*dims):
    return pltpu.SemaphoreType.DMA(dims)


def shape(dims, kind):
    return jax.ShapeDtypeStruct(dims, kind)


def tables(experts, main, slots, counts, group, domains, sort_order, cotangent):
    tokens, width = cotangent.shape
    return call(
        functools.partial(table_kernel, experts, main),
        [shape((slots, width), BF16), shape((tokens, 128), jnp.int32), shape((8, tokens), jnp.int32)],
        [SMEM, SMEM, SMEM, VMEM, VMEM],
        [pltpu.VMEM((tokens, width), BF16)],
        "tables",
    )(counts, group, domains, sort_order, cotangent)


def forward(count, main, spare, inputs, g1, s1, g2, s2, wq, wk, wv, wo, router, slot_col, slot_row, cot_send):
    tokens, width = inputs.shape
    blocks = tokens // BLK
    prob_block = (2, blocks * (blocks + 1) // 2 * BLK, BLK)
    rows_low = shape((tokens, width), BF16)
    return call(
        functools.partial(forward_kernel, count, main, spare),
        [
            rows_low,
            rows_low,
            rows_low,
            rows_low,
            rows_low,
            shape((tokens, width), F32),
            shape((tokens, 128), F32),
            shape(cot_send.shape, BF16),
            shape((count * (main + spare), width), BF16),
            shape((HEADS // 2,) + prob_block, BF16),
        ],
        [VMEM] * 5 + [ANY] * 4 + [VMEM] * 3 + [ANY],
        [pltpu.VMEM((width, width), BF16)] * 4
        + [
            pltpu.VMEM((tokens, width), BF16),
            pltpu.VMEM((2,) + prob_block, BF16),
            dma(2),
            dma(count),
            dma(count),
            dma(depth_of(count)),
            dma(depth_of(count)),
            dma(2),
            dma(4),
        ],
        "dense_forward",
        [VMEM] * 8 + [ANY] * 2,
        1,
    )(inputs, g1, s1, g2, s2, wq, wk, wv, wo, router, slot_col, slot_row, cot_send)


def expert_block(count, main, spare, counts, send, cot_send, cot_rows, router_t, w1, w2, chunk=768):
    slots, width = cot_rows.shape
    hidden = w1.shape[1]
    late = slots - (count - count // 4) * main
    rows = shape((slots, width), BF16)
    keep = pltpu.VMEM((slots, width), BF16)
    depth = depth_of(count)
    return call(
        functools.partial(expert_kernel, count, main, spare, chunk),
        [
            rows,
            shape((count * main, width), BF16),
            shape((late, width), BF16),
            shape((2 * hidden, width), BF16),
        ],
        [SMEM, ANY, ANY, ANY, VMEM, ANY, ANY],
        [
            pltpu.VMEM((width, hidden), BF16),
            pltpu.VMEM((hidden, width), BF16),
            pltpu.VMEM((width, hidden), F32),
            pltpu.VMEM((hidden, width), F32),
            keep,
            keep,
            keep,
            keep,
            pltpu.VMEM((2, width, width), BF16),
            dma(4),
            dma(count),
            dma(count),
            dma(depth),
            dma(depth),
            dma(depth),
            dma(depth),
            dma(count),
            dma(count),
            dma(2),
            dma(slots // BLK),
            dma(2),
        ],
        "expert",
        [ANY] * 4,
        2,
    )(counts, send, cot_send, cot_rows, router_t, w1, w2)


def backward(
    dp, count, main, spare, group, domains, inputs, cotangent, g1, g2, wq, wk, wv, wo, slot_col,
    normed, q, k, v, mixed, probs, hidden, dx, late, y, grads,
):
    tokens, width = inputs.shape
    half = grads.shape[0] // 4
    return call(
        functools.partial(backward_kernel, dp, count, main, spare),
        [shape((tokens, width), BF16), shape((4 * width, width), BF16), shape((8, width), F32), shape((count * main + BLK, width), BF16), shape((half, width), BF16)],
        [SMEM] * 2 + [ANY] * 2 + [VMEM] * 2 + [ANY] * 16,
        [pltpu.VMEM(v.shape, v.dtype) for v in (inputs, cotangent, wq, wk, wv, wo, slot_col, normed, q, k, v, mixed, hidden)]
        + [
            pltpu.VMEM((4 * width, width), BF16),
            pltpu.VMEM((count * main + BLK, width), BF16),
            pltpu.VMEM((count * spare, width), BF16),
            pltpu.VMEM((count * spare, width), BF16),
            pltpu.VMEM((count * spare, width), BF16),
            pltpu.VMEM((count * spare, width), BF16),
            pltpu.VMEM((2,) + probs.shape[1:], BF16),
            pltpu.VMEM((2, half, width), BF16),
            pltpu.VMEM((2, half, width), BF16),
            pltpu.VMEM((2, half // 2, width), BF16),
            pltpu.VMEM((tokens, width), BF16),
            pltpu.VMEM((tokens, width), BF16),
            pltpu.VMEM((width, tokens), BF16),
            pltpu.VMEM((tokens, 3 * width), BF16),
            pltpu.VMEM((8, width), F32),
            dma(count),
            dma(count),
            dma(count),
            dma(count),
            dma(depth_of(count)),
            dma(depth_of(count)),
            dma(depth_of(count)),
            dma(depth_of(count)),
            dma(3),
            dma(count),
            dma(13),
            dma(3, 2),
            dma(3, 2),
            dma(2),
            dma(2),
            dma(4),
        ],
        "dense_backward",
        [VMEM, ANY, VMEM, ANY, ANY],
        3,
        5 * 10**10,
    )(group, domains, inputs, cotangent, g1, g2, wq, wk, wv, wo, slot_col, normed, q, k, v, mixed, probs, hidden, dx, late, y, grads)


def finish(dp, count, dense, vec, slot_col, hidden, gate, y_back, y_rows, piece):
    width = hidden.shape[1]
    rows = dense.shape[0]
    steps = len(halving_plan(dp, count, rows // STREAMS)[0][0])
    return call(
        functools.partial(finish_kernel, dp, count),
        [shape(hidden.shape, BF16), shape(dense.shape, BF16), shape(vec.shape, F32), shape((4 * piece.shape[0], width), BF16)],
        [ANY, VMEM] + [ANY] * 6,
        [pltpu.VMEM(v.shape, v.dtype) for v in (dense, slot_col, hidden, gate)]
        + [
            pltpu.VMEM(y_back.shape, BF16),
            pltpu.VMEM((2, rows, width), BF16),
            pltpu.VMEM((STREAMS, rows // STREAMS + 64, width), BF16),
            pltpu.VMEM((rows, width), BF16),
            pltpu.VMEM((steps,) + vec.shape, F32),
            pltpu.VMEM((steps,) + vec.shape, F32),
            dma(STREAMS, steps),
            dma(STREAMS, steps),
            dma(STREAMS, steps),
            dma(STREAMS, steps),
            dma(steps),
            dma(steps),
            dma(),
            dma(3 * CHUNKS, 2),
            dma(3 * CHUNKS, 2),
            dma(2),
            dma(count),
            dma(count),
            dma(count + 1),
            dma(4),
        ],
        "finish",
        [VMEM, ANY, VMEM, ANY],
        4,
    )(dense, vec, slot_col, hidden, gate, y_back, y_rows, piece)


def widen(hidden, dense, grads, total, output, grad_inputs):
    width = dense.shape[1]
    square = shape((width, width), F32)
    jobs = 2 * (hidden // width) + 4
    rows = shape(output.shape, BF16)
    return call(
        functools.partial(widen_kernel, hidden),
        [square] * 4
        + [shape((width, hidden), F32), shape((hidden, width), F32)]
        + [shape((width,), F32)] * 4
        + [rows, rows],
        [ANY, ANY, VMEM, ANY, ANY],
        [
            pltpu.VMEM((jobs, width, width), BF16),
            pltpu.VMEM((6, width, width), F32),
            pltpu.VMEM((2,) + output.shape, BF16),
            dma(jobs),
            dma(6),
            dma(2),
        ],
        "widen",
        [ANY] * 6 + [VMEM] * 4 + [ANY] * 2,
    )(dense, grads, total, output, grad_inputs)


def local(
    inputs,
    cotangent,
    seq_group,
    domain_counts,
    sort_order,
    send_counts,
    gain_one,
    shift_one,
    gain_two,
    shift_two,
    w_query,
    w_key,
    w_value,
    w_out,
    router,
    expert_in,
    expert_out,
):
    tokens, width = inputs.shape
    experts = send_counts.shape[1]
    capacity = 2 * tokens // experts
    spare = capacity // 4
    main = capacity - spare
    slots = experts * main + BLK
    count = lax.axis_size("expert")
    g1, s1, g2, s2 = gain_one, shift_one, gain_two, shift_two
    router_t = router.T
    cot_send, slot_col, slot_row = tables(experts, main, slots, send_counts, seq_group, domain_counts, sort_order, cotangent)
    normed, q, k, v, mixed, hidden, gate, send, cot_rows, probs = forward(
        count, main, spare, inputs, g1, s1, g2, s2, w_query, w_key, w_value, w_out, router_t, slot_col, slot_row, cot_send
    )
    y_rows, dx_back, dx_late, grads = expert_block(
        count, main, spare, send_counts, send, cot_send, cot_rows, router_t, expert_in[0], expert_out[0]
    )
    dp = lax.axis_size("dp")
    grad_inputs, dense, vec, y_back, piece = backward(
        dp, count, main, spare, seq_group, domain_counts, inputs, cotangent, g1, g2, w_query, w_key, w_value, w_out, slot_col,
        normed, q, k, v, mixed, probs, hidden, dx_back, dx_late, y_rows, grads,
    )
    output, dense, vec, grads = finish(dp, count, dense, vec, slot_col, hidden, gate, y_back, y_rows, piece)
    wq, wk, wv, wo, first, second, gain_a, shift_a, gain_b, shift_b, output, grad_inputs = widen(
        expert_in.shape[2], dense, grads, vec, output, grad_inputs
    )
    return (output, grad_inputs, gain_a, shift_a, gain_b, shift_b, wq, wk, wv, wo, first[None], second[None])


def solution(mesh):
    rows = P(("dp", "expert"), None)
    split = P("expert", None, None)
    return jax.shard_map(
        local,
        mesh=mesh,
        in_specs=(rows, rows, P(("dp", "expert")), P(), rows, rows) + (P(),) * 9 + (split, split),
        out_specs=(rows, rows) + (P(),) * 8 + (split, split),
        check_vma=False,
    )
```

```python
import functools

import jax
import jax.numpy as jnp
from jax import lax
from jax.experimental import pallas as pl
from jax.experimental.pallas import tpu as pltpu
from jax.sharding import PartitionSpec as P

HEADS = 12
HEAD_DIM = 64
LEN = 1024
EPS = 1e-05
F32 = jnp.float32
BF16 = jnp.bfloat16
BLK = 256
CODE = 4096
LIMIT = 63 * 1024 * 1024

VMEM = pl.BlockSpec(memory_space=pltpu.VMEM)
SMEM = pl.BlockSpec(memory_space=pltpu.SMEM)
ANY = pl.BlockSpec(memory_space=pl.ANY)
MESH = pl.DeviceIdType.MESH


def dot(left, right, contract):
    return lax.dot_general(left, right, ((contract[0:1], contract[1:2]), ((), ())), preferred_element_type=F32)


def nn(left, right):
    return dot(left, right, (1, 0))


def nt(left, right):
    return dot(left, right, (1, 1))


def tn(left, right):
    return dot(left, right, (0, 0))


def iota(shape, axis):
    return lax.broadcasted_iota(jnp.int32, shape, axis)


def flip(index, mask, count):
    bit, out = 1, 0
    while bit < count:
        out = out + ((index // bit + mask // bit) % 2) * bit
        bit *= 2
    return out


def greet(axis, me, count):
    barrier = pltpu.get_barrier_semaphore()
    for mask in range(1, count):
        pl.semaphore_signal(barrier, inc=1, device_id={axis: flip(me, mask, count)}, device_id_type=MESH)
    pl.semaphore_wait(barrier, count - 1)


def copy_to(source, target, send, recv, device):
    return pltpu.make_async_remote_copy(
        src_ref=source, dst_ref=target, send_sem=send, recv_sem=recv, device_id=device, device_id_type=MESH
    )


def span(start, rows):
    return pl.ds(pl.multiple_of(start, 16), rows)


def send_block(me, count, rows, mask, source, target, sends, recvs):
    peer = flip(me, mask, count)
    return copy_to(
        source.at[span(peer * rows, rows)], target.at[span(mask * rows, rows)], sends.at[mask], recvs.at[mask], {"expert": peer}
    )


def return_block(me, count, rows, mask, source, target, sends, recvs, shift=0):
    return copy_to(
        source.at[span((mask - shift) * rows, rows)],
        target.at[span(me * rows, rows)],
        sends.at[mask],
        recvs.at[mask],
        {"expert": flip(me, mask, count)},
    )


def last_returns(count):
    return count // 8


def dp_sides():
    index = lax.axis_index("dp")
    return index, (index % 2, (index // 2) % 2)


def each_rows(rows, step, size=64):
    def body(block, carry):
        step(pl.ds(pl.multiple_of(block * size, size), size))
        return carry

    lax.fori_loop(0, rows // size, body, 0)


def sum_rows(target, other, rows):
    def step(block, carry):
        part = pl.ds(pl.multiple_of(block * BLK, BLK), BLK)
        target[part, :] = (target[part, :].astype(F32) + other[part, :].astype(F32)).astype(BF16)
        return carry

    lax.fori_loop(0, rows // BLK, step, 0)


def depth_of(count):
    return count.bit_length() - 1


def gather_spare(me, count, base, rows, step, first, target, sends, recvs):
    have = rows << step
    source = first.at[pl.ds(base, rows)] if step == 0 else target.at[pl.ds(base, have)]
    return copy_to(
        source,
        target.at[pl.ds(base + have, have)],
        sends.at[step],
        recvs.at[step],
        {"expert": flip(me, count >> (step + 1), count)},
    )


def return_spare(me, count, rows, step, source, shift, landing, sends, recvs):
    half = rows << step
    return copy_to(
        source.at[pl.ds(shift + half, half)],
        landing.at[pl.ds(half, half)],
        sends.at[step],
        recvs.at[step],
        {"expert": flip(me, count >> (step + 1), count)},
    )


def row_of(ref):
    return ref[...].reshape(1, ref.shape[0])


def domain_weight(group_ref, counts_ref):
    groups = counts_ref.shape[0]
    group = group_ref[0]
    total = jnp.zeros((1, 128), F32)
    mine = jnp.zeros((1, 128), F32)
    for index in range(groups):
        inverse = 1.0 / jnp.full((1, 128), counts_ref[index], jnp.int32).astype(F32)
        total = total + inverse
        mine = mine + jnp.where(group == index, inverse, 0.0)
    return (mine / (total / groups))[:, 0:1]


def norm_stats(rows):
    center = rows - jnp.mean(rows, axis=-1, keepdims=True)
    rstd = lax.rsqrt(jnp.mean(center * center, axis=-1, keepdims=True) + EPS)
    return center * rstd, rstd


def pack_rows(slot_row, rows_ref, send_ref):
    slots = send_ref.shape[0]
    tokens = rows_ref.shape[0]

    def step(block, carry):
        base = pl.multiple_of(block * BLK, BLK)
        slot = iota((BLK, tokens), 0) + base
        pick = jnp.where(slot == slot_row, 1.0, 0.0).astype(BF16)
        send_ref[pl.ds(base, BLK), :] = nn(pick, rows_ref[...]).astype(BF16)
        return carry

    lax.fori_loop(0, slots // BLK, step, 0)


def table_kernel(experts, main, counts_ref, group_ref, domain_ref, sort_ref, cot_ref, send_ref, slot_col_ref, slot_row_ref, scaled):
    tokens = cot_ref.shape[0]
    place = iota((1, tokens), 1)
    expert_at = jnp.zeros((1, tokens), jnp.int32)
    start_at = jnp.zeros((1, tokens), jnp.int32)
    end = jnp.int32(0)
    for expert in range(experts):
        count = counts_ref[0, expert]
        end = end + count
        past = place >= end
        expert_at = expert_at + jnp.where(past, 1, 0)
        start_at = start_at + jnp.where(past, count, 0)
    slot = place - start_at
    dest = jnp.where(slot < main, expert_at * main + slot, (experts - 1) * main + slot)
    code = (expert_at * CODE + dest).astype(F32)
    sort_row = sort_ref[...]
    scaled[...] = (cot_ref[...].astype(F32) * domain_weight(group_ref, domain_ref)).astype(BF16)
    for block in range(tokens // BLK):
        token = iota((BLK, tokens), 0) + block * BLK
        col = jnp.sum(jnp.where(token == sort_row, code, 0.0), axis=1, keepdims=True)
        owner = (col * (1.0 / CODE)).astype(jnp.int32)
        where = col.astype(jnp.int32) - owner * CODE
        slot_col_ref[pl.ds(block * BLK, BLK), :] = jnp.where(iota((1, 128), 1) < 64, where, owner)
        slot_row_ref[:, pl.ds(block * BLK, BLK)] = jnp.broadcast_to(where, (BLK, 128)).astype(F32).T[0:8].astype(jnp.int32)
    pack_rows(slot_row_ref[0:1, :], scaled, send_ref)


def forward_kernel(
    count,
    main,
    spare,
    x_ref,
    gain_one_ref,
    shift_one_ref,
    gain_two_ref,
    shift_two_ref,
    wq_hbm,
    wk_hbm,
    wv_hbm,
    wo_hbm,
    router_ref,
    slot_col_ref,
    slot_row_ref,
    cot_send_ref,
    normed_ref,
    q_ref,
    k_ref,
    v_ref,
    mixed_ref,
    hidden_ref,
    gate_ref,
    send_ref,
    cot_rows_ref,
    probs_hbm,
    wq_ref,
    wk_ref,
    wv_ref,
    wo_ref,
    routed,
    probs,
    prob_sems,
    sends,
    recvs,
    spare_sends,
    spare_recvs,
    own,
    fills,
):
    tokens, width = x_ref.shape
    blocks = tokens // BLK
    me = lax.axis_index("expert")
    weights = [(wq_hbm, wq_ref), (wk_hbm, wk_ref), (wv_hbm, wv_ref), (wo_hbm, wo_ref)]
    weights = [pltpu.make_async_copy(source, target, fills.at[i]) for i, (source, target) in enumerate(weights)]
    for copy in weights:
        copy.start()
    greet("expert", me, count)
    base = count * main

    def gather(step):
        return gather_spare(me, count, base, spare, step, cot_send_ref, cot_rows_ref, spare_sends, spare_recvs)

    gather(0).start()
    copies = [send_block(me, count, main, mask, cot_send_ref, cot_rows_ref, sends, recvs) for mask in range(1, count - 1)]
    for copy in copies:
        copy.start()
    mine = [
        pltpu.make_async_copy(cot_send_ref.at[span(me * main, main)], cot_rows_ref.at[pl.ds(0, main)], own.at[0]),
        pltpu.make_async_copy(cot_send_ref.at[pl.ds(base, spare)], cot_rows_ref.at[pl.ds(base, spare)], own.at[1]),
    ]
    for copy in mine:
        copy.start()
    lane = iota((1, 128), 1)
    gain_one, shift_one, gain_two, shift_two = (row_of(r) for r in (gain_one_ref, shift_one_ref, gain_two_ref, shift_two_ref))

    def project(block, carry):
        rows = pl.ds(pl.multiple_of(block * BLK, BLK), BLK)
        hat, _ = norm_stats(x_ref[rows, :].astype(F32))
        normed = (hat * gain_one + shift_one).astype(BF16)
        normed_ref[rows, :] = normed
        q_ref[rows, :] = (nn(normed, wq_ref[...]).astype(BF16) * (HEAD_DIM ** (-0.5))).astype(BF16)
        k_ref[rows, :] = nn(normed, wk_ref[...]).astype(BF16)
        v_ref[rows, :] = nn(normed, wv_ref[...]).astype(BF16)
        return carry

    for copy in weights:
        copy.wait()
    lax.fori_loop(0, blocks, project, 0)

    keep = iota((BLK, BLK), 0) <= iota((BLK, BLK), 1)

    def keep_probs(pair):
        return pltpu.make_async_copy(probs.at[pair % 2], probs_hbm.at[pair], prob_sems.at[pair % 2])

    def attend(pair, carry):
        @pl.when(pair >= 2)
        def _():
            keep_probs(pair - 2).wait()

        cols = pl.ds(pl.multiple_of(pair * 128, 128), 128)
        k_pair = k_ref[:, cols]
        v_t = v_ref[:, cols].astype(F32).T.astype(BF16)
        k_head = [jnp.where(lane < 64, k_pair, 0), jnp.where(lane >= 64, k_pair, 0)]
        for block in range(blocks):
            span = (block + 1) * BLK
            query = q_ref[pl.ds(block * BLK, BLK), cols]
            outs = []
            for half in range(2):
                scores = nt(k_head[half][:span], query)
                diag = jnp.where(keep, scores[block * BLK :], -1000000000.0)
                scores = jnp.concatenate([scores[: block * BLK], diag], axis=0) if block else diag
                peak = jnp.max(scores, axis=0, keepdims=True)
                exps = jnp.exp(scores - peak)
                total = jnp.sum(exps, axis=0, keepdims=True)
                attention = (exps * (1.0 / total)).astype(BF16)
                probs[pair % 2, half, pl.ds(block * (block + 1) // 2 * BLK, (block + 1) * BLK), :] = attention
                outs.append(nn(v_t[half * 64 : half * 64 + 64, :span], attention))
            mixed_ref[pl.ds(block * BLK, BLK), cols] = jnp.concatenate(outs, axis=0).T.astype(BF16)
        keep_probs(pair).start()
        return carry

    lax.fori_loop(0, HEADS // 2, attend, 0)
    experts = router_ref.shape[0]

    def finish(block, carry):
        rows = pl.ds(pl.multiple_of(block * BLK, BLK), BLK)
        hidden = x_ref[rows, :].astype(F32) + nn(mixed_ref[rows, :], wo_ref[...])
        hidden_ref[rows, :] = hidden
        hat, _ = norm_stats(hidden)
        low = (hat * gain_two + shift_two).astype(BF16)
        routed[rows, :] = low
        logits = nt(low, router_ref[...])
        owner = slot_col_ref[rows, 64:65]
        logit = jnp.sum(jnp.where(iota((BLK, experts), 1) == owner, logits, 0.0), axis=1, keepdims=True)
        gate_ref[rows, :] = jnp.broadcast_to(jax.nn.sigmoid(logit), (BLK, 128))
        return carry

    lax.fori_loop(0, blocks, finish, 0)
    pack_rows(slot_row_ref[0:1, :], routed, send_ref)
    for copy in mine + [keep_probs(HEADS // 2 - 2), keep_probs(HEADS // 2 - 1)]:
        copy.wait()
    for copy in copies + [gather(0)]:
        copy.wait()


def gelu_parts(v):
    t = 1.0 / (1.0 + (0.3275911 * 0.7071067811865476) * jnp.abs(v))
    bell = jnp.exp2((-0.5 * 1.4426950408889634) * (v * v))
    poly = ((((0.5307027145 * t - 0.7265760135) * t + 0.7107068705) * t - 0.142248368) * t + 0.127414796) * t
    tail = poly * bell
    return jnp.where(v >= 0.0, 1.0 - tail, tail), bell * 0.3989422804014327


def expert_kernel(
    count,
    main,
    spare,
    chunk,
    counts_ref,
    send_ref,
    cot_send_ref,
    cot_rows_ref,
    router_ref,
    w1_hbm,
    w2_hbm,
    y_ref,
    back_ref,
    late_ref,
    grads_ref,
    w1_ref,
    w2_ref,
    acc1,
    acc2,
    x_rows,
    g_ref,
    dx_rows,
    y_rows,
    stage,
    load_sems,
    sends,
    recvs,
    spare_sends,
    spare_recvs,
    cot_sends,
    cot_recvs,
    back_sends,
    back_recvs,
    own,
    y_sems,
    stage_sems,
):
    width, hidden = w1_ref.shape
    slots = x_rows.shape[0]
    base = count * main
    plain = base // BLK
    blocks = slots // BLK
    depth = depth_of(count)
    early = count - count // 4
    me = lax.axis_index("expert")
    loads = [
        pltpu.make_async_copy(w1_hbm, w1_ref, load_sems.at[0]),
        pltpu.make_async_copy(w2_hbm, w2_ref, load_sems.at[1]),
        pltpu.make_async_copy(cot_rows_ref.at[pl.ds(0, base - main)], g_ref.at[pl.ds(0, base - main)], load_sems.at[2]),
        pltpu.make_async_copy(cot_rows_ref.at[pl.ds(base, 2 * spare)], g_ref.at[pl.ds(base, 2 * spare)], load_sems.at[3]),
    ]
    for load in loads:
        load.start()
    greet("expert", me, count)

    def gather(step):
        return gather_spare(me, count, base, spare, step, send_ref, x_rows, spare_sends, spare_recvs)

    def arrive(mask):
        return send_block(me, count, main, mask, send_ref, x_rows, sends, recvs)

    def leave(mask):
        return return_block(me, count, main, mask, dx_rows, back_ref, back_sends, back_recvs)

    def gather_cot(step):
        source = cot_rows_ref if step == 1 else g_ref
        have = spare << step
        return copy_to(
            source.at[pl.ds(base, have)],
            g_ref.at[pl.ds(base + have, have)],
            cot_sends.at[step],
            cot_recvs.at[step],
            {"expert": flip(me, count >> (step + 1), count)},
        )

    def last_cot():
        rows = span(flip(me, count - 1, count) * main, main)
        return copy_to(
            cot_send_ref.at[rows],
            g_ref.at[pl.ds(base - main, main)],
            cot_sends.at[0],
            cot_recvs.at[0],
            {"expert": flip(me, count - 1, count)},
        )

    gather_cot(1).start()
    gather(0).start()
    for mask in range(1, count):
        arrive(mask).start()
    last_cot().start()
    mine_in = [
        pltpu.make_async_copy(send_ref.at[span(me * main, main)], x_rows.at[pl.ds(0, main)], own.at[0]),
        pltpu.make_async_copy(send_ref.at[pl.ds(base, spare)], x_rows.at[pl.ds(base, spare)], own.at[1]),
    ]
    for copy in mine_in:
        copy.start()

    def clear_one(part):
        acc1[part, :] = jnp.zeros((64, hidden), F32)

    def clear_two(part):
        acc2[part, :] = jnp.zeros((64, width), F32)

    each_rows(width, clear_one)
    each_rows(hidden, clear_two)
    experts = router_ref.shape[0]
    router = jnp.sum(jnp.where(iota((experts, 1), 0) == me, router_ref[...].astype(F32), 0.0), axis=0, keepdims=True)
    hot = jnp.full((1, 128), counts_ref[0, me], jnp.int32)[:, 0:1] > main
    hot = jnp.where(hot, 1.0, 0.0)
    for copy in loads + mine_in:
        copy.wait()

    def store_y(block):
        rows = pl.ds(pl.multiple_of(block * BLK, BLK), BLK)
        return pltpu.make_async_copy(y_rows.at[rows], y_ref.at[rows], y_sems.at[block])

    def mine_out():
        return pltpu.make_async_copy(dx_rows.at[pl.ds(0, main)], back_ref.at[span(me * main, main)], own.at[0])

    def run(turn, carry):
        block = turn + turn // (plain - 1) - (turn // (blocks - 1)) * (blocks - plain + 1)
        for item in range(BLK // main + 1):
            mask = (block * BLK + main - 1) // main + item

            @pl.when((block < plain) & (mask > 0) & (mask < ((block + 1) * BLK + main - 1) // main))
            def _():
                arrive(mask).wait_recv()

            @pl.when((block == plain - 1) & (mask == count - 1))
            def _():
                last_cot().wait_recv()

        for step in range(depth):

            @pl.when(turn == (max(step + 1, plain - depth + step + 1) if step else 1))
            def _():
                gather(step).wait_recv()
                if step:
                    gather_cot(step).wait_recv()
                if step + 1 < depth:
                    gather(step + 1).start()
                    if step:
                        gather_cot(step + 1).start()

        rows = pl.ds(pl.multiple_of(block * BLK, BLK), BLK)
        live = jnp.where(block < plain, 1.0, hot)
        x = (x_rows[rows, :].astype(F32) * live).astype(BF16)
        logit = jnp.sum(x.astype(F32) * router, axis=1, keepdims=True)
        gate = jax.nn.sigmoid(logit)
        go = g_ref[rows, :].astype(F32) * live
        g = (gate * go).astype(BF16)
        x_t = x.astype(F32).T.astype(BF16)
        y = jnp.zeros(x.shape, F32)
        dx = jnp.zeros(x.shape, F32)
        for first in range(0, hidden, chunk):
            cols = pl.ds(first, chunk)
            w1 = w1_ref[:, cols]
            w2 = w2_ref[cols, :]
            pre = nn(x, w1)
            cdf, pdf = gelu_parts(pre)
            act = (pre * cdf).astype(BF16)
            slope = cdf + pre * pdf
            y = y + nn(act, w2)
            grad = (nt(g, w2) * slope).astype(BF16)
            dx = dx + nt(grad, w1)
            acc1[:, cols] += nn(x_t, grad)
            acc2[cols, :] += tn(act, g)
        y_low = y.astype(BF16)
        y_rows[rows, :] = y_low
        dlogit = jnp.sum(y_low.astype(F32) * go, axis=1, keepdims=True) * gate * (1.0 - gate)
        dx_rows[rows, :] = (dx + dlogit * router).astype(BF16)
        store_y(block).start()
        for item in range(BLK // main + 1):
            mask = (block * BLK) // main + item
            done = (block < plain) & (mask < ((block + 1) * BLK) // main)

            @pl.when(done & (mask > 0) & (mask < early))
            def _():
                leave(mask).start()

            @pl.when(done & (mask == 0))
            def _():
                mine_out().start()

        return carry

    lax.fori_loop(0, blocks, run, 0)
    tail = pltpu.make_async_copy(dx_rows.at[pl.ds(early * main, slots - early * main)], late_ref, own.at[1])
    tail.start()

    pieces = []
    for first in range(0, hidden, width):
        pieces.append((acc1.at[:, pl.ds(first, width)], grads_ref.at[pl.ds(first, width)]))
    for first in range(0, hidden, width):
        pieces.append((acc2.at[pl.ds(first, width), :], grads_ref.at[pl.ds(hidden + first, width)]))
    writes = []
    for index, (piece, target) in enumerate(pieces):
        slot = index % 2
        if index >= 2:
            writes[index - 2].wait()

        def narrow(part):
            stage[slot, part, :] = piece[part, :].astype(BF16)

        each_rows(width, narrow)
        write = pltpu.make_async_copy(stage.at[slot], target, stage_sems.at[slot])
        write.start()
        writes.append(write)
    for write in writes[-2:]:
        write.wait()
    mine_out().wait()
    tail.wait()

    def settle(block, carry):
        store_y(block).wait()
        return carry

    lax.fori_loop(0, blocks, settle, 0)
    for step in range(depth):
        gather(step).wait_send()
    for step in range(1, depth):
        gather_cot(step).wait_send()
    last_cot().wait_send()
    for mask in range(1, count):
        arrive(mask).wait_send()
    for mask in range(1, early):
        leave(mask).wait()


def backward_kernel(
    dp,
    count,
    main,
    spare,
    group_ref,
    domain_ref,
    x_hbm,
    cot_hbm,
    gain_one_ref,
    gain_two_ref,
    wq_hbm,
    wk_hbm,
    wv_hbm,
    wo_hbm,
    slot_col_hbm,
    normed_hbm,
    q_hbm,
    k_hbm,
    v_hbm,
    mixed_hbm,
    probs_hbm,
    hidden_hbm,
    dx_hbm,
    late_ref,
    y_ref,
    grads_hbm,
    grad_ref,
    dense_hbm,
    vec_ref,
    y_back_ref,
    piece_ref,
    x_ref,
    cot_ref,
    wq_ref,
    wk_ref,
    wv_ref,
    wo_ref,
    slot_col_ref,
    normed_ref,
    q_ref,
    k_ref,
    v_ref,
    mixed_ref,
    hidden_ref,
    dense_ref,
    dx_ref,
    spare_dx,
    spare_y,
    dx_land,
    y_land,
    probs,
    kept,
    land_one,
    land_two,
    gmix,
    branch,
    normed_t,
    dqkv,
    sums,
    sends,
    recvs,
    late_sends,
    late_recvs,
    dx_sends,
    dx_recvs,
    y_sends,
    y_recvs,
    own,
    gets,
    fills,
    scatter_sends,
    scatter_recvs,
    keeps,
    prob_sems,
    puts,
):
    tokens, width = x_ref.shape
    me = lax.axis_index("expert")
    early = count - count // 4
    base = count * main
    late = (count - early) * main
    total = count * spare
    depth = depth_of(count)
    operands = [
        (x_hbm, x_ref),
        (cot_hbm, cot_ref),
        (wq_hbm, wq_ref),
        (wk_hbm, wk_ref),
        (wv_hbm, wv_ref),
        (wo_hbm, wo_ref),
        (slot_col_hbm, slot_col_ref),
        (normed_hbm, normed_ref),
        (q_hbm, q_ref),
        (k_hbm, k_ref),
        (v_hbm, v_ref),
        (mixed_hbm, mixed_ref),
        (hidden_hbm, hidden_ref),
    ]
    operands = [pltpu.make_async_copy(source, target, fills.at[i]) for i, (source, target) in enumerate(operands)]
    for copy in operands:
        copy.start()
    barrier = pltpu.get_barrier_semaphore()
    place, bits = dp_sides()
    for mask in range(1, count):
        pl.semaphore_signal(barrier, inc=1, device_id={"expert": flip(me, mask, count)}, device_id_type=MESH)
    for mask in (1, 2):
        pl.semaphore_signal(barrier, inc=1, device_id={"dp": flip(place, mask, dp)}, device_id_type=MESH)
    pl.semaphore_wait(barrier, count + 1)
    portion = grads_hbm.shape[0] // 4
    quarter = portion // 2

    def scatter_one(stream, second):
        side = bits[1 - stream] if second else 1 - bits[1 - stream]
        start = 2 * portion * stream + (1 - bits[stream]) * portion + side * quarter
        device = {"dp": flip(place, 1 << stream, dp)}
        return copy_to(
            grads_hbm.at[span(start, quarter)],
            land_one.at[stream, span(side * quarter, quarter)],
            scatter_sends.at[second, stream],
            scatter_recvs.at[second, stream],
            device,
        )

    def add_one(stream, second):
        side = bits[1 - stream] if second else 1 - bits[1 - stream]
        scatter_one(stream, second).wait()

        def step(rows):
            held = span(side * quarter + rows.start, 64)
            kept[stream, held, :] = (kept[stream, held, :].astype(F32) + land_one[stream, held, :].astype(F32)).astype(BF16)

        each_rows(quarter, step)

    def keep_one(stream):
        start = 2 * portion * stream + bits[stream] * portion
        return pltpu.make_async_copy(grads_hbm.at[span(start, portion)], kept.at[stream], keeps.at[stream])

    def scatter_two(stream):
        start = (1 - bits[1 - stream]) * quarter
        device = {"dp": flip(place, 2 >> stream, dp)}
        return copy_to(
            kept.at[stream, span(start, quarter)],
            land_two.at[stream],
            scatter_sends.at[2, stream],
            scatter_recvs.at[2, stream],
            device,
        )

    def store_piece(stream):
        start = bits[1 - stream] * quarter
        return pltpu.make_async_copy(
            kept.at[stream, span(start, quarter)], piece_ref.at[pl.ds(stream * quarter, quarter)], keeps.at[stream]
        )

    def load_probs(pair):
        return pltpu.make_async_copy(probs_hbm.at[pair], probs.at[pair % 2], prob_sems.at[pair % 2])

    load_probs(0).start()
    for part in range(2):
        for stream in range(2):
            scatter_one(stream, part).start()
    for stream in range(2):
        keep_one(stream).start()

    def sum_dx(step):
        if step == depth - 1:
            return return_spare(me, count, spare, step, late_ref, late, dx_land, dx_sends, dx_recvs)
        return return_spare(me, count, spare, step, spare_dx, 0, dx_land, dx_sends, dx_recvs)

    def sum_y(step):
        if step == depth - 1:
            return return_spare(me, count, spare, step, y_ref, base, y_land, y_sends, y_recvs)
        return return_spare(me, count, spare, step, spare_y, 0, y_land, y_sends, y_recvs)

    def settle(copy, own_rows, landing, step):
        copy.wait()
        rows = spare << step
        own_rows[0:rows, :] = (own_rows[0:rows, :].astype(F32) + landing[rows : 2 * rows, :].astype(F32)).astype(BF16)

    sum_dx(depth - 1).start()
    lates = [return_block(me, count, main, mask, late_ref, dx_ref, late_sends, late_recvs, early) for mask in range(early, count)]
    for copy in lates:
        copy.start()
    copies = [
        return_block(me, count, main, mask, y_ref, y_back_ref, sends, recvs) for mask in range(1, count - last_returns(count))
    ]
    mine = pltpu.make_async_copy(y_ref.at[pl.ds(0, main)], y_back_ref.at[span(me * main, main)], own.at[0])
    mine.start()
    loads = [
        pltpu.make_async_copy(late_ref.at[pl.ds(late, total)], spare_dx, own.at[1]),
        pltpu.make_async_copy(y_ref.at[pl.ds(base, total)], spare_y, own.at[2]),
    ]
    for mask in range(early):
        part = span(flip(me, mask, count) * main, main)
        loads.append(pltpu.make_async_copy(dx_hbm.at[part], dx_ref.at[part], gets.at[mask]))
    for load in loads:
        load.start()
    for load in loads:
        load.wait()
    for step in reversed(range(depth)):
        settle(sum_dx(step), spare_dx, dx_land, step)
        if step:
            sum_dx(step - 1).start()
    dx_ref[pl.ds(base, BLK), :] = spare_dx[0:BLK, :]
    for copy in lates:
        copy.wait()
    sum_y(depth - 1).start()
    for copy in copies[count // 2 - 1 :] + copies[: count // 2 - 1]:
        copy.start()
    for copy in operands:
        copy.wait()
    slots = dx_ref.shape[0]
    blocks = tokens // BLK
    lane = iota((1, 128), 1)
    weight = domain_weight(group_ref, domain_ref)
    gain_one = row_of(gain_one_ref)
    gain_two = row_of(gain_two_ref)
    sums[...] = jnp.zeros_like(sums)

    def open_block(block, carry):
        rows = pl.ds(pl.multiple_of(block * BLK, BLK), BLK)
        slot = slot_col_ref[rows, 0:1]
        pick = jnp.where(iota((BLK, slots), 1) == slot, 1.0, 0.0).astype(BF16)
        grad = nn(pick, dx_ref[...])
        hat, rstd = norm_stats(hidden_ref[rows, :])
        sums[2:3, :] += jnp.sum(grad * hat, axis=0, keepdims=True)
        sums[3:4, :] += jnp.sum(grad, axis=0, keepdims=True)
        gg = grad * gain_two
        inner = gg - jnp.mean(gg, axis=1, keepdims=True) - hat * jnp.mean(gg * hat, axis=1, keepdims=True)
        total = cot_ref[rows, :].astype(F32) * weight + rstd * inner
        hidden_ref[rows, :] = total
        low = total.astype(BF16)
        branch[rows, :] = low
        gmix[rows, :] = nt(low, wo_ref[...]).astype(BF16)
        normed_t[:, rows] = normed_ref[rows, :].astype(F32).T.astype(BF16)
        return carry

    lax.fori_loop(0, blocks, open_block, 0)
    def put_dense(part):
        rows = pl.ds(part * width, width)
        return pltpu.make_async_copy(dense_ref.at[rows], dense_hbm.at[rows], puts.at[part])

    dense_ref[pl.ds(3 * width, width), :] = tn(mixed_ref[...], branch[...]).astype(BF16)
    put_dense(3).start()
    settle(sum_y(depth - 1), spare_y, y_land, depth - 1)
    sum_y(depth - 2).start()

    for stream in range(2):
        keep_one(stream).wait()
        add_one(stream, 0)
        scatter_two(stream).start()

    def attend(pair, carry):
        @pl.when(pair + 1 < HEADS // 2)
        def _():
            load_probs(pair + 1).start()

        @pl.when(pair == 4)
        def _():
            for stream in range(2):
                add_one(stream, 1)

        @pl.when(pair == 5)
        def _():
            settle(sum_y(depth - 2), spare_y, y_land, depth - 2)
            sum_y(depth - 3).start()

        load_probs(pair).wait()
        base = pl.multiple_of(pair * 128, 128)
        cols = pl.ds(base, 128)
        q_pair = q_ref[:, cols]
        k_pair = k_ref[:, cols]
        v_pair = v_ref[:, cols]
        o_pair = gmix[:, cols]
        low = lane < 64
        q_head = [jnp.where(low, q_pair, 0), jnp.where(low, 0, q_pair)]
        v_head = [jnp.where(low, v_pair, 0), jnp.where(low, 0, v_pair)]
        o_head = [jnp.where(low, o_pair, 0), jnp.where(low, 0, o_pair)]
        k_t = k_pair.astype(F32).T.astype(BF16)
        prod_t = (o_pair.astype(F32) * mixed_ref[:, cols].astype(F32)).T
        delta = [jnp.sum(prod_t[:64], axis=0, keepdims=True), jnp.sum(prod_t[64:], axis=0, keepdims=True)]
        dq_t = [[None] * blocks, [None] * blocks]
        for block in range(blocks):
            start = block * BLK
            dk = None
            dv = None
            for half in range(2):
                tiles = [
                    probs[pair % 2, half, pl.ds((later * (later + 1) // 2 + block) * BLK, BLK), :]
                    for later in range(block, blocks)
                ]
                attention = jnp.concatenate(tiles, axis=1) if block < blocks - 1 else tiles[0]
                grad_p = nt(v_head[half][start : start + BLK], o_pair[start:])
                grad_s = (attention.astype(F32) * (grad_p - delta[half][:, start:])).astype(BF16)
                dv_part = nn(attention, o_head[half][start:])
                dk_part = nn(grad_s, q_head[half][start:])
                dv = dv_part if dv is None else dv + dv_part
                dk = dk_part if dk is None else dk + dk_part
                dq_part = nn(k_t[half * 64 : half * 64 + 64, start : start + BLK], grad_s)
                for later in range(block, blocks):
                    piece = dq_part[:, (later - block) * BLK : (later - block + 1) * BLK]
                    dq_t[half][later] = piece if dq_t[half][later] is None else dq_t[half][later] + piece
            rows = pl.ds(start, BLK)
            dqkv[rows, pl.ds(pl.multiple_of(base + width, 128), 128)] = dk.astype(BF16)
            dqkv[rows, pl.ds(pl.multiple_of(base + 2 * width, 128), 128)] = dv.astype(BF16)
        for block in range(blocks):
            both = jnp.concatenate([dq_t[0][block], dq_t[1][block]], axis=0) * (HEAD_DIM ** (-0.5))
            dqkv[pl.ds(block * BLK, BLK), cols] = both.T.astype(BF16)
        return carry

    lax.fori_loop(0, HEADS // 2, attend, 0)

    for part in range(3):
        dense_ref[pl.ds(part * width, width), :] = nn(normed_t[...], dqkv[:, pl.ds(part * width, width)]).astype(BF16)
        put_dense(part).start()

    def close_block(block, carry):
        rows = pl.ds(pl.multiple_of(block * BLK, BLK), BLK)
        grad = nt(dqkv[rows, 0:width], wq_ref[...])
        grad = grad + nt(dqkv[rows, width : 2 * width], wk_ref[...])
        grad = grad + nt(dqkv[rows, 2 * width : 3 * width], wv_ref[...])
        hat, rstd = norm_stats(x_ref[rows, :].astype(F32))
        sums[0:1, :] += jnp.sum(grad * hat, axis=0, keepdims=True)
        sums[1:2, :] += jnp.sum(grad, axis=0, keepdims=True)
        gg = grad * gain_one
        inner = gg - jnp.mean(gg, axis=1, keepdims=True) - hat * jnp.mean(gg * hat, axis=1, keepdims=True)
        grad_ref[rows, :] = (hidden_ref[rows, :] + rstd * inner).astype(BF16)
        return carry

    lax.fori_loop(0, blocks, close_block, 0)
    vec_ref[...] = sums[...]
    for stream in range(2):
        scatter_two(stream).wait()
        start = bits[1 - stream] * quarter
        sum_rows(kept.at[stream, span(start, quarter)], land_two.at[stream], quarter)
        store_piece(stream).start()
    for step in reversed(range(depth - 2)):
        settle(sum_y(step), spare_y, y_land, step)
        if step:
            sum_y(step - 1).start()
    spare_out = pltpu.make_async_copy(spare_y.at[pl.ds(0, BLK)], y_back_ref.at[pl.ds(base, BLK)], own.at[1])
    spare_out.start()
    spare_out.wait()
    for stream in range(2):
        store_piece(stream).wait()
    for part in range(4):
        put_dense(part).wait()
    mine.wait()
    for copy in copies:
        copy.wait()


STREAMS = 3
CHUNKS = 4


def halving_plan(dp, count, rows):
    experts = [("expert", 2 << bit) for bit in range(depth_of(count) - 1)]
    groups = [("dp", 1 << bit) for bit in range(depth_of(dp))]
    core = [("expert", 1)]
    plans = [core + groups + experts, core + groups[::-1] + experts, core + experts + groups]
    halvings = 0
    while halvings < len(plans[0]) and (rows >> halvings) % 32 == 0:
        halvings += 1
    return plans, halvings


def finish_kernel(
    dp,
    count,
    dense_hbm,
    vec_ref,
    slot_col_hbm,
    hidden_hbm,
    gate_hbm,
    y_hbm,
    y_rows_hbm,
    piece_ref,
    out_ref,
    full_ref,
    total_ref,
    grads_ref,
    dense_ref,
    slot_col_ref,
    hidden_ref,
    gate_ref,
    y_ref,
    acc,
    landing,
    full,
    vec_acc,
    vec_land,
    sends,
    recvs,
    back_sends,
    back_recvs,
    vec_sends,
    vec_recvs,
    put,
    unit_sends,
    unit_recvs,
    own,
    y_sends,
    y_recvs,
    gets,
    fills,
):
    tokens, width = hidden_ref.shape
    slots = y_ref.shape[0]
    main = (slots - BLK) // count
    early = count - last_returns(count)
    rows = dense_ref.shape[0] // STREAMS
    place = {"dp": lax.axis_index("dp"), "expert": lax.axis_index("expert")}
    size = {"dp": dp, "expert": count}
    plans, halvings = halving_plan(dp, count, rows)
    steps = len(plans[0])

    def partner(axis, mask):
        return {axis: flip(place[axis], mask, size[axis])}

    operands = [(dense_hbm, dense_ref), (slot_col_hbm, slot_col_ref), (hidden_hbm, hidden_ref), (gate_hbm, gate_ref)]
    operands = [pltpu.make_async_copy(source, target, fills.at[i]) for i, (source, target) in enumerate(operands)]
    for copy in operands:
        copy.start()
    barrier = pltpu.get_barrier_semaphore()
    for axis, mask in plans[0]:
        pl.semaphore_signal(barrier, inc=1, device_id=partner(axis, mask), device_id_type=MESH)
    for mask in range(early, count):
        pl.semaphore_signal(barrier, inc=1, device_id=partner("expert", mask), device_id_type=MESH)
    pl.semaphore_wait(barrier, steps + count - early)
    me = place["expert"]
    y_copies = [return_block(me, count, main, mask, y_rows_hbm, y_ref, y_sends, y_recvs) for mask in range(early, count)]
    loads = [pltpu.make_async_copy(y_hbm.at[pl.ds(count * main, BLK)], y_ref.at[pl.ds(count * main, BLK)], gets.at[count])]
    for mask in range(early):
        part = span(flip(me, mask, count) * main, main)
        loads.append(pltpu.make_async_copy(y_hbm.at[part], y_ref.at[part], gets.at[mask]))
    for load in loads:
        load.start()

    def side(axis, mask):
        return (place[axis] // mask) % 2

    _, bits = dp_sides()
    quarter = piece_ref.shape[0] // 2
    chunk = quarter // CHUNKS
    starts = [
        4 * quarter * stream + bits[stream] * 2 * quarter + bits[1 - stream] * quarter for stream in range(2)
    ]
    others = [
        4 * quarter * stream + bits[stream] * 2 * quarter + (1 - bits[1 - stream]) * quarter for stream in range(2)
    ]

    def unit(index, stream):
        kind, part = index // CHUNKS, index % CHUNKS
        near, far = partner("dp", 1 << stream), partner("dp", 2 >> stream)
        if kind == 2:
            source = target = grads_ref.at[span(others[stream] + part * chunk, chunk)]
        else:
            source = piece_ref.at[pl.ds(stream * quarter + part * chunk, chunk)]
            target = grads_ref.at[span(starts[stream] + part * chunk, chunk)]
        return copy_to(
            source, target, unit_sends.at[index, stream], unit_recvs.at[index, stream], far if kind == 0 else near
        )

    pending = list(range(3 * CHUNKS))

    def advance(number):
        for _ in range(min(number, len(pending))):
            index = pending.pop(0)
            for stream in range(2):
                if index >= 2 * CHUNKS:
                    unit(index - 2 * CHUNKS, stream).wait_recv()
                unit(index, stream).start()

    mine = [
        pltpu.make_async_copy(
            piece_ref.at[pl.ds(stream * quarter, quarter)], grads_ref.at[span(starts[stream], quarter)], own.at[stream]
        )
        for stream in range(2)
    ]
    for copy in mine:
        copy.start()

    def combine(block):
        rows_at = pl.ds(pl.multiple_of(block * BLK, BLK), BLK)
        slot = slot_col_ref[rows_at, 0:1]
        pick = jnp.where(iota((BLK, slots), 1) == slot, 1.0, 0.0).astype(BF16)
        returned = nn(pick, y_ref[...])
        out_ref[rows_at, :] = (hidden_ref[rows_at, :] + gate_ref[rows_at, 0:1] * returned).astype(BF16)

    low = [jnp.int32(stream * rows) for stream in range(STREAMS)]
    extent = rows
    offset = 0
    trail = []
    for step in range(steps):
        halve = step < halvings
        part = extent // 2 if halve else extent
        copies = []
        for stream in range(STREAMS):
            axis, mask = plans[stream][step]
            kept = low[stream] + side(axis, mask) * part if halve else low[stream]
            other = low[stream] + (1 - side(axis, mask)) * part if halve else low[stream]
            source = dense_ref if step == 0 else acc.at[(step - 1) % 2]
            land = landing.at[stream, pl.ds(offset, part)]
            copy = copy_to(
                (dense_hbm if step == 0 else source).at[span(other, part)], land, sends.at[stream, step], recvs.at[stream, step], partner(axis, mask)
            )
            copy.start()
            copies.append((copy, kept, source))
        axis, mask = plans[0][step]
        vec_source = vec_ref if step == 0 else vec_acc.at[step - 1]
        vec_copy = copy_to(vec_source, vec_land.at[step], vec_sends.at[step], vec_recvs.at[step], partner(axis, mask))
        vec_copy.start()
        advance(1)
        if step == 0:
            for copy in y_copies:
                copy.start()
        if step == 0:
            for copy in operands:
                copy.wait()
        trail.append((list(low), extent))
        for stream in range(STREAMS):
            copy, kept, source = copies[stream]
            copy.wait()
            target = acc.at[step % 2] if step < steps - 1 else full
            grain = min(part, 64)

            def add(rows_at):
                held = span(kept + rows_at.start, grain)
                value = source[held, :].astype(F32) + landing[stream, span(offset + rows_at.start, grain), :].astype(F32)
                target[held, :] = value.astype(BF16)

            each_rows(part, add, grain)
            low[stream] = kept
        vec_copy.wait()
        vec_sum = vec_source[...] + vec_land[step]
        if step < steps - 1:
            vec_acc[step] = vec_sum
        else:
            total_ref[...] = vec_sum
        extent = part
        offset += part

    writes = []
    for step in reversed(range(halvings)):
        origins, whole = trail[step]
        copies = []
        for stream in range(STREAMS):
            axis, mask = plans[stream][step]
            held = span(low[stream], extent)
            copy = copy_to(
                full.at[held], full.at[held], back_sends.at[stream, step], back_recvs.at[stream, step], partner(axis, mask)
            )
            copy.start()
            copies.append(copy)
        advance(2)
        if step == 1:
            for copy in loads + y_copies:
                copy.wait()

            def combine_block(block, carry):
                combine(block)
                return carry

            lax.fori_loop(0, tokens // BLK, combine_block, 0)
        for stream in range(STREAMS):
            copies[stream].wait()
            low[stream] = origins[stream]
        extent = whole
        if step == 1:
            for stream in range(STREAMS):
                held = span(low[stream], extent)
                writes.append(pltpu.make_async_copy(full.at[held], full_ref.at[held], put.at[0, stream]))
                writes[-1].start()
    advance(len(pending))
    for stream in range(STREAMS):
        held = span(stream * rows + (1 - side("expert", 1)) * (rows // 2), rows // 2)
        writes.append(pltpu.make_async_copy(full.at[held], full_ref.at[held], put.at[1, stream]))
        writes[-1].start()
    for index in range(3 * CHUNKS):
        for stream in range(2):
            if index >= CHUNKS:
                unit(index, stream).wait_recv()
            unit(index, stream).wait_send()
    for copy in mine + writes:
        copy.wait()


AHEAD = 6


def widen_kernel(hidden, dense_hbm, grads_hbm, total_ref, output_hbm, inputs_hbm, *rest):
    outs, vecs, passed, (low, high, rows, gets, puts, moves) = rest[:6], rest[6:10], rest[10:12], rest[12:]
    width = dense_hbm.shape[1]
    jobs = []
    for block in range(hidden // width):
        part = pl.ds(block * width, width)
        jobs.append((grads_hbm.at[part], outs[4].at[:, part]))
        jobs.append((grads_hbm.at[pl.ds(hidden + block * width, width)], outs[5].at[part, :]))
    for index in range(4):
        jobs.append((dense_hbm.at[pl.ds(index * width, width)], outs[index]))
    loads = [pltpu.make_async_copy(source, low.at[i], gets.at[i]) for i, (source, _) in enumerate(jobs)]
    for load in loads[:AHEAD]:
        load.start()
    for index, vec in enumerate(vecs):
        vec[...] = total_ref[index : index + 1, :].reshape(width)
    taken = [pltpu.make_async_copy(source, rows.at[i], moves.at[i]) for i, source in enumerate((output_hbm, inputs_hbm))]
    given = [pltpu.make_async_copy(rows.at[i], target, moves.at[i]) for i, target in enumerate(passed)]
    slots = high.shape[0]
    stores = []
    for index, (_, target) in enumerate(jobs):
        loads[index].wait()
        if index + AHEAD < len(jobs):
            loads[index + AHEAD].start()
        if index == 1:
            for copy in taken:
                copy.start()
        if index == 4:
            for before, after in zip(taken, given):
                before.wait()
                after.start()
        if index >= slots:
            stores[index - slots].wait()

        def step(part):
            high[index % slots, part, :] = low[index, part, :].astype(F32)

        each_rows(width, step)
        stores.append(pltpu.make_async_copy(high.at[index % slots], target, puts.at[index % slots]))
        stores[-1].start()
    for copy in stores[-slots:] + given:
        copy.wait()


def call(kernel, outs, in_specs, scratch, name, out_specs=None, collective=None, flops=10**9):
    remote = {} if collective is None else {"collective_id": collective, "has_side_effects": True}
    return pl.pallas_call(
        kernel,
        out_shape=outs,
        in_specs=in_specs,
        out_specs=out_specs or [VMEM] * len(outs),
        scratch_shapes=scratch,
        compiler_params=pltpu.CompilerParams(vmem_limit_bytes=LIMIT, **remote),
        cost_estimate=pl.CostEstimate(flops=flops, bytes_accessed=10**7, transcendentals=0),
        name=name,
    )


def dma(*dims):
    return pltpu.SemaphoreType.DMA(dims)


def shape(dims, kind):
    return jax.ShapeDtypeStruct(dims, kind)


def tables(experts, main, slots, counts, group, domains, sort_order, cotangent):
    tokens, width = cotangent.shape
    return call(
        functools.partial(table_kernel, experts, main),
        [shape((slots, width), BF16), shape((tokens, 128), jnp.int32), shape((8, tokens), jnp.int32)],
        [SMEM, SMEM, SMEM, VMEM, VMEM],
        [pltpu.VMEM((tokens, width), BF16)],
        "tables",
    )(counts, group, domains, sort_order, cotangent)


def forward(count, main, spare, inputs, g1, s1, g2, s2, wq, wk, wv, wo, router, slot_col, slot_row, cot_send):
    tokens, width = inputs.shape
    blocks = tokens // BLK
    prob_block = (2, blocks * (blocks + 1) // 2 * BLK, BLK)
    rows_low = shape((tokens, width), BF16)
    return call(
        functools.partial(forward_kernel, count, main, spare),
        [
            rows_low,
            rows_low,
            rows_low,
            rows_low,
            rows_low,
            shape((tokens, width), F32),
            shape((tokens, 128), F32),
            shape(cot_send.shape, BF16),
            shape((count * (main + spare), width), BF16),
            shape((HEADS // 2,) + prob_block, BF16),
        ],
        [VMEM] * 5 + [ANY] * 4 + [VMEM] * 3 + [ANY],
        [pltpu.VMEM((width, width), BF16)] * 4
        + [
            pltpu.VMEM((tokens, width), BF16),
            pltpu.VMEM((2,) + prob_block, BF16),
            dma(2),
            dma(count),
            dma(count),
            dma(depth_of(count)),
            dma(depth_of(count)),
            dma(2),
            dma(4),
        ],
        "dense_forward",
        [VMEM] * 8 + [ANY] * 2,
        1,
    )(inputs, g1, s1, g2, s2, wq, wk, wv, wo, router, slot_col, slot_row, cot_send)


def expert_block(count, main, spare, counts, send, cot_send, cot_rows, router_t, w1, w2, chunk=768):
    slots, width = cot_rows.shape
    hidden = w1.shape[1]
    late = slots - (count - count // 4) * main
    rows = shape((slots, width), BF16)
    keep = pltpu.VMEM((slots, width), BF16)
    depth = depth_of(count)
    return call(
        functools.partial(expert_kernel, count, main, spare, chunk),
        [
            rows,
            shape((count * main, width), BF16),
            shape((late, width), BF16),
            shape((2 * hidden, width), BF16),
        ],
        [SMEM, ANY, ANY, ANY, VMEM, ANY, ANY],
        [
            pltpu.VMEM((width, hidden), BF16),
            pltpu.VMEM((hidden, width), BF16),
            pltpu.VMEM((width, hidden), F32),
            pltpu.VMEM((hidden, width), F32),
            keep,
            keep,
            keep,
            keep,
            pltpu.VMEM((2, width, width), BF16),
            dma(4),
            dma(count),
            dma(count),
            dma(depth),
            dma(depth),
            dma(depth),
            dma(depth),
            dma(count),
            dma(count),
            dma(2),
            dma(slots // BLK),
            dma(2),
        ],
        "expert",
        [ANY] * 4,
        2,
    )(counts, send, cot_send, cot_rows, router_t, w1, w2)


def backward(
    dp, count, main, spare, group, domains, inputs, cotangent, g1, g2, wq, wk, wv, wo, slot_col,
    normed, q, k, v, mixed, probs, hidden, dx, late, y, grads,
):
    tokens, width = inputs.shape
    half = grads.shape[0] // 4
    return call(
        functools.partial(backward_kernel, dp, count, main, spare),
        [shape((tokens, width), BF16), shape((4 * width, width), BF16), shape((8, width), F32), shape((count * main + BLK, width), BF16), shape((half, width), BF16)],
        [SMEM] * 2 + [ANY] * 2 + [VMEM] * 2 + [ANY] * 16,
        [pltpu.VMEM(v.shape, v.dtype) for v in (inputs, cotangent, wq, wk, wv, wo, slot_col, normed, q, k, v, mixed, hidden)]
        + [
            pltpu.VMEM((4 * width, width), BF16),
            pltpu.VMEM((count * main + BLK, width), BF16),
            pltpu.VMEM((count * spare, width), BF16),
            pltpu.VMEM((count * spare, width), BF16),
            pltpu.VMEM((count * spare, width), BF16),
            pltpu.VMEM((count * spare, width), BF16),
            pltpu.VMEM((2,) + probs.shape[1:], BF16),
            pltpu.VMEM((2, half, width), BF16),
            pltpu.VMEM((2, half, width), BF16),
            pltpu.VMEM((2, half // 2, width), BF16),
            pltpu.VMEM((tokens, width), BF16),
            pltpu.VMEM((tokens, width), BF16),
            pltpu.VMEM((width, tokens), BF16),
            pltpu.VMEM((tokens, 3 * width), BF16),
            pltpu.VMEM((8, width), F32),
            dma(count),
            dma(count),
            dma(count),
            dma(count),
            dma(depth_of(count)),
            dma(depth_of(count)),
            dma(depth_of(count)),
            dma(depth_of(count)),
            dma(3),
            dma(count),
            dma(13),
            dma(3, 2),
            dma(3, 2),
            dma(2),
            dma(2),
            dma(4),
        ],
        "dense_backward",
        [VMEM, ANY, VMEM, ANY, ANY],
        3,
        5 * 10**10,
    )(group, domains, inputs, cotangent, g1, g2, wq, wk, wv, wo, slot_col, normed, q, k, v, mixed, probs, hidden, dx, late, y, grads)


def finish(dp, count, dense, vec, slot_col, hidden, gate, y_back, y_rows, piece):
    width = hidden.shape[1]
    rows = dense.shape[0]
    steps = len(halving_plan(dp, count, rows // STREAMS)[0][0])
    return call(
        functools.partial(finish_kernel, dp, count),
        [shape(hidden.shape, BF16), shape(dense.shape, BF16), shape(vec.shape, F32), shape((4 * piece.shape[0], width), BF16)],
        [ANY, VMEM] + [ANY] * 6,
        [pltpu.VMEM(v.shape, v.dtype) for v in (dense, slot_col, hidden, gate)]
        + [
            pltpu.VMEM(y_back.shape, BF16),
            pltpu.VMEM((2, rows, width), BF16),
            pltpu.VMEM((STREAMS, rows // STREAMS + 64, width), BF16),
            pltpu.VMEM((rows, width), BF16),
            pltpu.VMEM((steps,) + vec.shape, F32),
            pltpu.VMEM((steps,) + vec.shape, F32),
            dma(STREAMS, steps),
            dma(STREAMS, steps),
            dma(STREAMS, steps),
            dma(STREAMS, steps),
            dma(steps),
            dma(steps),
            dma(2, STREAMS),
            dma(3 * CHUNKS, 2),
            dma(3 * CHUNKS, 2),
            dma(2),
            dma(count),
            dma(count),
            dma(count + 1),
            dma(4),
        ],
        "finish",
        [VMEM, ANY, VMEM, ANY],
        4,
    )(dense, vec, slot_col, hidden, gate, y_back, y_rows, piece)


def widen(hidden, dense, grads, total, output, grad_inputs):
    width = dense.shape[1]
    square = shape((width, width), F32)
    jobs = 2 * (hidden // width) + 4
    rows = shape(output.shape, BF16)
    return call(
        functools.partial(widen_kernel, hidden),
        [square] * 4
        + [shape((width, hidden), F32), shape((hidden, width), F32)]
        + [shape((width,), F32)] * 4
        + [rows, rows],
        [ANY, ANY, VMEM, ANY, ANY],
        [
            pltpu.VMEM((jobs, width, width), BF16),
            pltpu.VMEM((6, width, width), F32),
            pltpu.VMEM((2,) + output.shape, BF16),
            dma(jobs),
            dma(6),
            dma(2),
        ],
        "widen",
        [ANY] * 6 + [VMEM] * 4 + [ANY] * 2,
    )(dense, grads, total, output, grad_inputs)


def local(
    inputs,
    cotangent,
    seq_group,
    domain_counts,
    sort_order,
    send_counts,
    gain_one,
    shift_one,
    gain_two,
    shift_two,
    w_query,
    w_key,
    w_value,
    w_out,
    router,
    expert_in,
    expert_out,
):
    tokens, width = inputs.shape
    experts = send_counts.shape[1]
    capacity = 2 * tokens // experts
    spare = capacity // 4
    main = capacity - spare
    slots = experts * main + BLK
    count = lax.axis_size("expert")
    g1, s1, g2, s2 = gain_one, shift_one, gain_two, shift_two
    router_t = router.T
    cot_send, slot_col, slot_row = tables(experts, main, slots, send_counts, seq_group, domain_counts, sort_order, cotangent)
    normed, q, k, v, mixed, hidden, gate, send, cot_rows, probs = forward(
        count, main, spare, inputs, g1, s1, g2, s2, w_query, w_key, w_value, w_out, router_t, slot_col, slot_row, cot_send
    )
    y_rows, dx_back, dx_late, grads = expert_block(
        count, main, spare, send_counts, send, cot_send, cot_rows, router_t, expert_in[0], expert_out[0]
    )
    dp = lax.axis_size("dp")
    grad_inputs, dense, vec, y_back, piece = backward(
        dp, count, main, spare, seq_group, domain_counts, inputs, cotangent, g1, g2, w_query, w_key, w_value, w_out, slot_col,
        normed, q, k, v, mixed, probs, hidden, dx_back, dx_late, y_rows, grads,
    )
    output, dense, vec, grads = finish(dp, count, dense, vec, slot_col, hidden, gate, y_back, y_rows, piece)
    wq, wk, wv, wo, first, second, gain_a, shift_a, gain_b, shift_b, output, grad_inputs = widen(
        expert_in.shape[2], dense, grads, vec, output, grad_inputs
    )
    return (output, grad_inputs, gain_a, shift_a, gain_b, shift_b, wq, wk, wv, wo, first[None], second[None])


def solution(mesh):
    rows = P(("dp", "expert"), None)
    split = P("expert", None, None)
    return jax.shard_map(
        local,
        mesh=mesh,
        in_specs=(rows, rows, P(("dp", "expert")), P(), rows, rows) + (P(),) * 9 + (split, split),
        out_specs=(rows, rows) + (P(),) * 8 + (split, split),
        check_vma=False,
    )
```

```python
import functools

import jax
import jax.numpy as jnp
from jax import lax
from jax.experimental import pallas as pl
from jax.experimental.pallas import tpu as pltpu
from jax.sharding import PartitionSpec as P

HEADS = 12
HEAD_DIM = 64
LEN = 1024
EPS = 1e-05
F32 = jnp.float32
BF16 = jnp.bfloat16
BLK = 256
CODE = 4096
LIMIT = 63 * 1024 * 1024

VMEM = pl.BlockSpec(memory_space=pltpu.VMEM)
SMEM = pl.BlockSpec(memory_space=pltpu.SMEM)
ANY = pl.BlockSpec(memory_space=pl.ANY)
MESH = pl.DeviceIdType.MESH


def dot(left, right, contract):
    return lax.dot_general(left, right, ((contract[0:1], contract[1:2]), ((), ())), preferred_element_type=F32)


def nn(left, right):
    return dot(left, right, (1, 0))


def nt(left, right):
    return dot(left, right, (1, 1))


def tn(left, right):
    return dot(left, right, (0, 0))


def iota(shape, axis):
    return lax.broadcasted_iota(jnp.int32, shape, axis)


def flip(index, mask, count):
    bit, out = 1, 0
    while bit < count:
        out = out + ((index // bit + mask // bit) % 2) * bit
        bit *= 2
    return out


def greet(axis, me, count):
    barrier = pltpu.get_barrier_semaphore()
    for mask in range(1, count):
        pl.semaphore_signal(barrier, inc=1, device_id={axis: flip(me, mask, count)}, device_id_type=MESH)
    pl.semaphore_wait(barrier, count - 1)


def copy_to(source, target, send, recv, device):
    return pltpu.make_async_remote_copy(
        src_ref=source, dst_ref=target, send_sem=send, recv_sem=recv, device_id=device, device_id_type=MESH
    )


def span(start, rows):
    return pl.ds(pl.multiple_of(start, 16), rows)


def send_block(me, count, rows, mask, source, target, sends, recvs):
    peer = flip(me, mask, count)
    return copy_to(
        source.at[span(peer * rows, rows)], target.at[span(mask * rows, rows)], sends.at[mask], recvs.at[mask], {"expert": peer}
    )


def return_block(me, count, rows, mask, source, target, sends, recvs, shift=0):
    return copy_to(
        source.at[span((mask - shift) * rows, rows)],
        target.at[span(me * rows, rows)],
        sends.at[mask],
        recvs.at[mask],
        {"expert": flip(me, mask, count)},
    )


def last_returns(count):
    return count // 8


def dp_sides():
    index = lax.axis_index("dp")
    return index, (index % 2, (index // 2) % 2)


def each_rows(rows, step, size=64):
    def body(block, carry):
        step(pl.ds(pl.multiple_of(block * size, size), size))
        return carry

    lax.fori_loop(0, rows // size, body, 0)


def sum_rows(target, other, rows):
    def step(block, carry):
        part = pl.ds(pl.multiple_of(block * BLK, BLK), BLK)
        target[part, :] = (target[part, :].astype(F32) + other[part, :].astype(F32)).astype(BF16)
        return carry

    lax.fori_loop(0, rows // BLK, step, 0)


def depth_of(count):
    return count.bit_length() - 1


def gather_spare(me, count, base, rows, step, first, target, sends, recvs):
    have = rows << step
    source = first.at[pl.ds(base, rows)] if step == 0 else target.at[pl.ds(base, have)]
    return copy_to(
        source,
        target.at[pl.ds(base + have, have)],
        sends.at[step],
        recvs.at[step],
        {"expert": flip(me, count >> (step + 1), count)},
    )


def return_spare(me, count, rows, step, source, shift, landing, sends, recvs):
    half = rows << step
    return copy_to(
        source.at[pl.ds(shift + half, half)],
        landing.at[pl.ds(half, half)],
        sends.at[step],
        recvs.at[step],
        {"expert": flip(me, count >> (step + 1), count)},
    )


def row_of(ref):
    return ref[...].reshape(1, ref.shape[0])


def domain_weight(group_ref, counts_ref):
    groups = counts_ref.shape[0]
    group = group_ref[0]
    total = jnp.zeros((1, 128), F32)
    mine = jnp.zeros((1, 128), F32)
    for index in range(groups):
        inverse = 1.0 / jnp.full((1, 128), counts_ref[index], jnp.int32).astype(F32)
        total = total + inverse
        mine = mine + jnp.where(group == index, inverse, 0.0)
    return (mine / (total / groups))[:, 0:1]


def norm_stats(rows):
    center = rows - jnp.mean(rows, axis=-1, keepdims=True)
    rstd = lax.rsqrt(jnp.mean(center * center, axis=-1, keepdims=True) + EPS)
    return center * rstd, rstd


def pack_rows(slot_row, rows_ref, send_ref):
    slots = send_ref.shape[0]
    tokens = rows_ref.shape[0]

    def step(block, carry):
        base = pl.multiple_of(block * BLK, BLK)
        slot = iota((BLK, tokens), 0) + base
        pick = jnp.where(slot == slot_row, 1.0, 0.0).astype(BF16)
        send_ref[pl.ds(base, BLK), :] = nn(pick, rows_ref[...]).astype(BF16)
        return carry

    lax.fori_loop(0, slots // BLK, step, 0, unroll=True)


def table_kernel(experts, main, counts_ref, group_ref, domain_ref, sort_ref, cot_ref, send_ref, slot_col_ref, slot_row_ref, scaled):
    tokens = cot_ref.shape[0]
    place = iota((1, tokens), 1)
    expert_at = jnp.zeros((1, tokens), jnp.int32)
    start_at = jnp.zeros((1, tokens), jnp.int32)
    end = jnp.int32(0)
    for expert in range(experts):
        count = counts_ref[0, expert]
        end = end + count
        past = place >= end
        expert_at = expert_at + jnp.where(past, 1, 0)
        start_at = start_at + jnp.where(past, count, 0)
    slot = place - start_at
    dest = jnp.where(slot < main, expert_at * main + slot, (experts - 1) * main + slot)
    code = (expert_at * CODE + dest).astype(F32)
    sort_row = sort_ref[...]
    scaled[...] = (cot_ref[...].astype(F32) * domain_weight(group_ref, domain_ref)).astype(BF16)
    for block in range(tokens // BLK):
        token = iota((BLK, tokens), 0) + block * BLK
        col = jnp.sum(jnp.where(token == sort_row, code, 0.0), axis=1, keepdims=True)
        owner = (col * (1.0 / CODE)).astype(jnp.int32)
        where = col.astype(jnp.int32) - owner * CODE
        slot_col_ref[pl.ds(block * BLK, BLK), :] = jnp.where(iota((1, 128), 1) < 64, where, owner)
        slot_row_ref[:, pl.ds(block * BLK, BLK)] = jnp.broadcast_to(where, (BLK, 128)).astype(F32).T[0:8].astype(jnp.int32)
    pack_rows(slot_row_ref[0:1, :], scaled, send_ref)


def forward_kernel(
    count,
    main,
    spare,
    x_ref,
    gain_one_ref,
    shift_one_ref,
    gain_two_ref,
    shift_two_ref,
    wq_hbm,
    wk_hbm,
    wv_hbm,
    wo_hbm,
    router_ref,
    slot_col_ref,
    slot_row_ref,
    cot_send_ref,
    normed_ref,
    q_ref,
    k_ref,
    v_ref,
    mixed_ref,
    hidden_ref,
    gate_ref,
    send_ref,
    cot_rows_ref,
    probs_hbm,
    wq_ref,
    wk_ref,
    wv_ref,
    wo_ref,
    routed,
    probs,
    prob_sems,
    sends,
    recvs,
    spare_sends,
    spare_recvs,
    own,
    fills,
):
    tokens, width = x_ref.shape
    blocks = tokens // BLK
    me = lax.axis_index("expert")
    weights = [(wq_hbm, wq_ref), (wk_hbm, wk_ref), (wv_hbm, wv_ref), (wo_hbm, wo_ref)]
    weights = [pltpu.make_async_copy(source, target, fills.at[i]) for i, (source, target) in enumerate(weights)]
    for copy in weights:
        copy.start()
    greet("expert", me, count)
    base = count * main

    def gather(step):
        return gather_spare(me, count, base, spare, step, cot_send_ref, cot_rows_ref, spare_sends, spare_recvs)

    gather(0).start()
    copies = [send_block(me, count, main, mask, cot_send_ref, cot_rows_ref, sends, recvs) for mask in range(1, count - 1)]
    for copy in copies:
        copy.start()
    mine = [
        pltpu.make_async_copy(cot_send_ref.at[span(me * main, main)], cot_rows_ref.at[pl.ds(0, main)], own.at[0]),
        pltpu.make_async_copy(cot_send_ref.at[pl.ds(base, spare)], cot_rows_ref.at[pl.ds(base, spare)], own.at[1]),
    ]
    for copy in mine:
        copy.start()
    lane = iota((1, 128), 1)
    gain_one, shift_one, gain_two, shift_two = (row_of(r) for r in (gain_one_ref, shift_one_ref, gain_two_ref, shift_two_ref))

    def project(block, carry):
        rows = pl.ds(pl.multiple_of(block * BLK, BLK), BLK)
        hat, _ = norm_stats(x_ref[rows, :].astype(F32))
        normed = (hat * gain_one + shift_one).astype(BF16)
        normed_ref[rows, :] = normed
        q_ref[rows, :] = (nn(normed, wq_ref[...]).astype(BF16) * (HEAD_DIM ** (-0.5))).astype(BF16)
        k_ref[rows, :] = nn(normed, wk_ref[...]).astype(BF16)
        v_ref[rows, :] = nn(normed, wv_ref[...]).astype(BF16)
        return carry

    for copy in weights:
        copy.wait()
    lax.fori_loop(0, blocks, project, 0, unroll=2)

    keep = iota((BLK, BLK), 0) <= iota((BLK, BLK), 1)

    def keep_probs(pair):
        return pltpu.make_async_copy(probs.at[pair % 2], probs_hbm.at[pair], prob_sems.at[pair % 2])

    def attend(pair, carry):
        @pl.when(pair >= 2)
        def _():
            keep_probs(pair - 2).wait()

        cols = pl.ds(pl.multiple_of(pair * 128, 128), 128)
        k_pair = k_ref[:, cols]
        v_t = v_ref[:, cols].astype(F32).T.astype(BF16)
        k_head = [jnp.where(lane < 64, k_pair, 0), jnp.where(lane >= 64, k_pair, 0)]
        for block in range(blocks):
            span = (block + 1) * BLK
            query = q_ref[pl.ds(block * BLK, BLK), cols]
            outs = []
            for half in range(2):
                scores = nt(k_head[half][:span], query)
                diag = jnp.where(keep, scores[block * BLK :], -1000000000.0)
                scores = jnp.concatenate([scores[: block * BLK], diag], axis=0) if block else diag
                peak = jnp.max(scores, axis=0, keepdims=True)
                exps = jnp.exp(scores - peak)
                total = jnp.sum(exps, axis=0, keepdims=True)
                attention = (exps * (1.0 / total)).astype(BF16)
                probs[pair % 2, half, pl.ds(block * (block + 1) // 2 * BLK, (block + 1) * BLK), :] = attention
                outs.append(nn(v_t[half * 64 : half * 64 + 64, :span], attention))
            mixed_ref[pl.ds(block * BLK, BLK), cols] = jnp.concatenate(outs, axis=0).T.astype(BF16)
        keep_probs(pair).start()
        return carry

    lax.fori_loop(0, HEADS // 2, attend, 0)
    experts = router_ref.shape[0]

    def finish(block, carry):
        rows = pl.ds(pl.multiple_of(block * BLK, BLK), BLK)
        hidden = x_ref[rows, :].astype(F32) + nn(mixed_ref[rows, :], wo_ref[...])
        hidden_ref[rows, :] = hidden
        hat, _ = norm_stats(hidden)
        low = (hat * gain_two + shift_two).astype(BF16)
        routed[rows, :] = low
        logits = nt(low, router_ref[...])
        owner = slot_col_ref[rows, 64:65]
        logit = jnp.sum(jnp.where(iota((BLK, experts), 1) == owner, logits, 0.0), axis=1, keepdims=True)
        gate_ref[rows, :] = jnp.broadcast_to(jax.nn.sigmoid(logit), (BLK, 128))
        return carry

    lax.fori_loop(0, blocks, finish, 0, unroll=2)
    pack_rows(slot_row_ref[0:1, :], routed, send_ref)
    for copy in mine + [keep_probs(HEADS // 2 - 2), keep_probs(HEADS // 2 - 1)]:
        copy.wait()
    for copy in copies + [gather(0)]:
        copy.wait()


def gelu_parts(v):
    t = 1.0 / (1.0 + (0.3275911 * 0.7071067811865476) * jnp.abs(v))
    bell = jnp.exp2((-0.5 * 1.4426950408889634) * (v * v))
    poly = ((((0.5307027145 * t - 0.7265760135) * t + 0.7107068705) * t - 0.142248368) * t + 0.127414796) * t
    tail = poly * bell
    return jnp.where(v >= 0.0, 1.0 - tail, tail), bell * 0.3989422804014327


def expert_kernel(
    count,
    main,
    spare,
    chunk,
    counts_ref,
    send_ref,
    cot_send_ref,
    cot_rows_ref,
    router_ref,
    w1_hbm,
    w2_hbm,
    y_ref,
    back_ref,
    late_ref,
    grads_ref,
    w1_ref,
    w2_ref,
    acc1,
    acc2,
    x_rows,
    g_ref,
    dx_rows,
    y_rows,
    stage,
    load_sems,
    sends,
    recvs,
    spare_sends,
    spare_recvs,
    cot_sends,
    cot_recvs,
    back_sends,
    back_recvs,
    own,
    y_sems,
    stage_sems,
):
    width, hidden = w1_ref.shape
    slots = x_rows.shape[0]
    base = count * main
    plain = base // BLK
    blocks = slots // BLK
    depth = depth_of(count)
    early = count - count // 4
    me = lax.axis_index("expert")
    loads = [
        pltpu.make_async_copy(w1_hbm, w1_ref, load_sems.at[0]),
        pltpu.make_async_copy(w2_hbm, w2_ref, load_sems.at[1]),
        pltpu.make_async_copy(cot_rows_ref.at[pl.ds(0, base - main)], g_ref.at[pl.ds(0, base - main)], load_sems.at[2]),
        pltpu.make_async_copy(cot_rows_ref.at[pl.ds(base, 2 * spare)], g_ref.at[pl.ds(base, 2 * spare)], load_sems.at[3]),
    ]
    for load in loads:
        load.start()
    greet("expert", me, count)

    def gather(step):
        return gather_spare(me, count, base, spare, step, send_ref, x_rows, spare_sends, spare_recvs)

    def arrive(mask):
        return send_block(me, count, main, mask, send_ref, x_rows, sends, recvs)

    def leave(mask):
        return return_block(me, count, main, mask, dx_rows, back_ref, back_sends, back_recvs)

    def gather_cot(step):
        source = cot_rows_ref if step == 1 else g_ref
        have = spare << step
        return copy_to(
            source.at[pl.ds(base, have)],
            g_ref.at[pl.ds(base + have, have)],
            cot_sends.at[step],
            cot_recvs.at[step],
            {"expert": flip(me, count >> (step + 1), count)},
        )

    def last_cot():
        rows = span(flip(me, count - 1, count) * main, main)
        return copy_to(
            cot_send_ref.at[rows],
            g_ref.at[pl.ds(base - main, main)],
            cot_sends.at[0],
            cot_recvs.at[0],
            {"expert": flip(me, count - 1, count)},
        )

    gather_cot(1).start()
    gather(0).start()
    for mask in range(1, count):
        arrive(mask).start()
    last_cot().start()
    mine_in = [
        pltpu.make_async_copy(send_ref.at[span(me * main, main)], x_rows.at[pl.ds(0, main)], own.at[0]),
        pltpu.make_async_copy(send_ref.at[pl.ds(base, spare)], x_rows.at[pl.ds(base, spare)], own.at[1]),
    ]
    for copy in mine_in:
        copy.start()

    def clear_one(part):
        acc1[part, :] = jnp.zeros((64, hidden), F32)

    def clear_two(part):
        acc2[part, :] = jnp.zeros((64, width), F32)

    each_rows(width, clear_one)
    each_rows(hidden, clear_two)
    experts = router_ref.shape[0]
    router = jnp.sum(jnp.where(iota((experts, 1), 0) == me, router_ref[...].astype(F32), 0.0), axis=0, keepdims=True)
    hot = jnp.full((1, 128), counts_ref[0, me], jnp.int32)[:, 0:1] > main
    hot = jnp.where(hot, 1.0, 0.0)
    for copy in loads + mine_in:
        copy.wait()

    def store_y(block):
        rows = pl.ds(pl.multiple_of(block * BLK, BLK), BLK)
        return pltpu.make_async_copy(y_rows.at[rows], y_ref.at[rows], y_sems.at[block])

    def mine_out():
        return pltpu.make_async_copy(dx_rows.at[pl.ds(0, main)], back_ref.at[span(me * main, main)], own.at[0])

    def run(turn, carry):
        block = turn + turn // (plain - 1) - (turn // (blocks - 1)) * (blocks - plain + 1)
        for item in range(BLK // main + 1):
            mask = (block * BLK + main - 1) // main + item

            @pl.when((block < plain) & (mask > 0) & (mask < ((block + 1) * BLK + main - 1) // main))
            def _():
                arrive(mask).wait_recv()

            @pl.when((block == plain - 1) & (mask == count - 1))
            def _():
                last_cot().wait_recv()

        for step in range(depth):

            @pl.when(turn == (max(step + 1, plain - depth + step + 1) if step else 1))
            def _():
                gather(step).wait_recv()
                if step:
                    gather_cot(step).wait_recv()
                if step + 1 < depth:
                    gather(step + 1).start()
                    if step:
                        gather_cot(step + 1).start()

        rows = pl.ds(pl.multiple_of(block * BLK, BLK), BLK)
        live = jnp.where(block < plain, 1.0, hot)
        x = (x_rows[rows, :].astype(F32) * live).astype(BF16)
        logit = jnp.sum(x.astype(F32) * router, axis=1, keepdims=True)
        gate = jax.nn.sigmoid(logit)
        go = g_ref[rows, :].astype(F32) * live
        g = (gate * go).astype(BF16)
        x_t = x.astype(F32).T.astype(BF16)
        y = jnp.zeros(x.shape, F32)
        dx = jnp.zeros(x.shape, F32)
        for first in range(0, hidden, chunk):
            cols = pl.ds(first, chunk)
            w1 = w1_ref[:, cols]
            w2 = w2_ref[cols, :]
            pre = nn(x, w1)
            cdf, pdf = gelu_parts(pre)
            act = (pre * cdf).astype(BF16)
            slope = cdf + pre * pdf
            y = y + nn(act, w2)
            grad = (nt(g, w2) * slope).astype(BF16)
            dx = dx + nt(grad, w1)
            acc1[:, cols] += nn(x_t, grad)
            acc2[cols, :] += tn(act, g)
        y_low = y.astype(BF16)
        y_rows[rows, :] = y_low
        dlogit = jnp.sum(y_low.astype(F32) * go, axis=1, keepdims=True) * gate * (1.0 - gate)
        dx_rows[rows, :] = (dx + dlogit * router).astype(BF16)
        store_y(block).start()
        for item in range(BLK // main + 1):
            mask = (block * BLK) // main + item
            done = (block < plain) & (mask < ((block + 1) * BLK) // main)

            @pl.when(done & (mask > 0) & (mask < early))
            def _():
                leave(mask).start()

            @pl.when(done & (mask == 0))
            def _():
                mine_out().start()

        return carry

    lax.fori_loop(0, blocks, run, 0)
    tail = pltpu.make_async_copy(dx_rows.at[pl.ds(early * main, slots - early * main)], late_ref, own.at[1])
    tail.start()

    pieces = []
    for first in range(0, hidden, width):
        pieces.append((acc1.at[:, pl.ds(first, width)], grads_ref.at[pl.ds(first, width)]))
    for first in range(0, hidden, width):
        pieces.append((acc2.at[pl.ds(first, width), :], grads_ref.at[pl.ds(hidden + first, width)]))
    writes = []
    for index, (piece, target) in enumerate(pieces):
        slot = index % 2
        if index >= 2:
            writes[index - 2].wait()

        def narrow(part):
            stage[slot, part, :] = piece[part, :].astype(BF16)

        each_rows(width, narrow)
        write = pltpu.make_async_copy(stage.at[slot], target, stage_sems.at[slot])
        write.start()
        writes.append(write)
    for write in writes[-2:]:
        write.wait()
    mine_out().wait()
    tail.wait()

    def settle(block, carry):
        store_y(block).wait()
        return carry

    lax.fori_loop(0, blocks, settle, 0)
    for step in range(depth):
        gather(step).wait_send()
    for step in range(1, depth):
        gather_cot(step).wait_send()
    last_cot().wait_send()
    for mask in range(1, count):
        arrive(mask).wait_send()
    for mask in range(1, early):
        leave(mask).wait()


def backward_kernel(
    dp,
    count,
    main,
    spare,
    group_ref,
    domain_ref,
    x_hbm,
    cot_hbm,
    gain_one_ref,
    gain_two_ref,
    wq_hbm,
    wk_hbm,
    wv_hbm,
    wo_hbm,
    slot_col_hbm,
    normed_hbm,
    q_hbm,
    k_hbm,
    v_hbm,
    mixed_hbm,
    probs_hbm,
    hidden_hbm,
    dx_hbm,
    late_ref,
    y_ref,
    grads_hbm,
    grad_ref,
    dense_hbm,
    vec_ref,
    y_back_ref,
    piece_ref,
    x_ref,
    cot_ref,
    wq_ref,
    wk_ref,
    wv_ref,
    wo_ref,
    slot_col_ref,
    normed_ref,
    q_ref,
    k_ref,
    v_ref,
    mixed_ref,
    hidden_ref,
    dense_ref,
    dx_ref,
    spare_dx,
    spare_y,
    dx_land,
    y_land,
    probs,
    kept,
    land_one,
    land_two,
    gmix,
    branch,
    normed_t,
    dqkv,
    sums,
    sends,
    recvs,
    late_sends,
    late_recvs,
    dx_sends,
    dx_recvs,
    y_sends,
    y_recvs,
    own,
    gets,
    fills,
    scatter_sends,
    scatter_recvs,
    keeps,
    prob_sems,
    puts,
):
    tokens, width = x_ref.shape
    me = lax.axis_index("expert")
    early = count - count // 4
    base = count * main
    late = (count - early) * main
    total = count * spare
    depth = depth_of(count)
    operands = [
        (x_hbm, x_ref),
        (cot_hbm, cot_ref),
        (wq_hbm, wq_ref),
        (wk_hbm, wk_ref),
        (wv_hbm, wv_ref),
        (wo_hbm, wo_ref),
        (slot_col_hbm, slot_col_ref),
        (normed_hbm, normed_ref),
        (q_hbm, q_ref),
        (k_hbm, k_ref),
        (v_hbm, v_ref),
        (mixed_hbm, mixed_ref),
        (hidden_hbm, hidden_ref),
    ]
    operands = [pltpu.make_async_copy(source, target, fills.at[i]) for i, (source, target) in enumerate(operands)]
    for copy in operands:
        copy.start()
    barrier = pltpu.get_barrier_semaphore()
    place, bits = dp_sides()
    for mask in range(1, count):
        pl.semaphore_signal(barrier, inc=1, device_id={"expert": flip(me, mask, count)}, device_id_type=MESH)
    for mask in (1, 2):
        pl.semaphore_signal(barrier, inc=1, device_id={"dp": flip(place, mask, dp)}, device_id_type=MESH)
    pl.semaphore_wait(barrier, count + 1)
    portion = grads_hbm.shape[0] // 4
    quarter = portion // 2

    def scatter_one(stream, second):
        side = bits[1 - stream] if second else 1 - bits[1 - stream]
        start = 2 * portion * stream + (1 - bits[stream]) * portion + side * quarter
        device = {"dp": flip(place, 1 << stream, dp)}
        return copy_to(
            grads_hbm.at[span(start, quarter)],
            land_one.at[stream, span(side * quarter, quarter)],
            scatter_sends.at[second, stream],
            scatter_recvs.at[second, stream],
            device,
        )

    def add_one(stream, second):
        side = bits[1 - stream] if second else 1 - bits[1 - stream]
        scatter_one(stream, second).wait()

        def step(rows):
            held = span(side * quarter + rows.start, 64)
            kept[stream, held, :] = (kept[stream, held, :].astype(F32) + land_one[stream, held, :].astype(F32)).astype(BF16)

        each_rows(quarter, step)

    def keep_one(stream):
        start = 2 * portion * stream + bits[stream] * portion
        return pltpu.make_async_copy(grads_hbm.at[span(start, portion)], kept.at[stream], keeps.at[stream])

    def scatter_two(stream):
        start = (1 - bits[1 - stream]) * quarter
        device = {"dp": flip(place, 2 >> stream, dp)}
        return copy_to(
            kept.at[stream, span(start, quarter)],
            land_two.at[stream],
            scatter_sends.at[2, stream],
            scatter_recvs.at[2, stream],
            device,
        )

    def store_piece(stream):
        start = bits[1 - stream] * quarter
        return pltpu.make_async_copy(
            kept.at[stream, span(start, quarter)], piece_ref.at[pl.ds(stream * quarter, quarter)], keeps.at[stream]
        )

    def load_probs(pair):
        return pltpu.make_async_copy(probs_hbm.at[pair], probs.at[pair % 2], prob_sems.at[pair % 2])

    load_probs(0).start()
    for part in range(2):
        for stream in range(2):
            scatter_one(stream, part).start()
    for stream in range(2):
        keep_one(stream).start()

    def sum_dx(step):
        if step == depth - 1:
            return return_spare(me, count, spare, step, late_ref, late, dx_land, dx_sends, dx_recvs)
        return return_spare(me, count, spare, step, spare_dx, 0, dx_land, dx_sends, dx_recvs)

    def sum_y(step):
        if step == depth - 1:
            return return_spare(me, count, spare, step, y_ref, base, y_land, y_sends, y_recvs)
        return return_spare(me, count, spare, step, spare_y, 0, y_land, y_sends, y_recvs)

    def settle(copy, own_rows, landing, step):
        copy.wait()
        rows = spare << step
        own_rows[0:rows, :] = (own_rows[0:rows, :].astype(F32) + landing[rows : 2 * rows, :].astype(F32)).astype(BF16)

    sum_dx(depth - 1).start()
    lates = [return_block(me, count, main, mask, late_ref, dx_ref, late_sends, late_recvs, early) for mask in range(early, count)]
    for copy in lates:
        copy.start()
    copies = [
        return_block(me, count, main, mask, y_ref, y_back_ref, sends, recvs) for mask in range(1, count - last_returns(count))
    ]
    mine = pltpu.make_async_copy(y_ref.at[pl.ds(0, main)], y_back_ref.at[span(me * main, main)], own.at[0])
    mine.start()
    loads = [
        pltpu.make_async_copy(late_ref.at[pl.ds(late, total)], spare_dx, own.at[1]),
        pltpu.make_async_copy(y_ref.at[pl.ds(base, total)], spare_y, own.at[2]),
    ]
    for mask in range(early):
        part = span(flip(me, mask, count) * main, main)
        loads.append(pltpu.make_async_copy(dx_hbm.at[part], dx_ref.at[part], gets.at[mask]))
    for load in loads:
        load.start()
    for load in loads:
        load.wait()
    for step in reversed(range(depth)):
        settle(sum_dx(step), spare_dx, dx_land, step)
        if step:
            sum_dx(step - 1).start()
    dx_ref[pl.ds(base, BLK), :] = spare_dx[0:BLK, :]
    for copy in lates:
        copy.wait()
    sum_y(depth - 1).start()
    for copy in copies[count // 2 - 1 :] + copies[: count // 2 - 1]:
        copy.start()
    for copy in operands:
        copy.wait()
    slots = dx_ref.shape[0]
    blocks = tokens // BLK
    lane = iota((1, 128), 1)
    weight = domain_weight(group_ref, domain_ref)
    gain_one = row_of(gain_one_ref)
    gain_two = row_of(gain_two_ref)
    sums[...] = jnp.zeros_like(sums)

    def open_block(block, carry):
        rows = pl.ds(pl.multiple_of(block * BLK, BLK), BLK)
        slot = slot_col_ref[rows, 0:1]
        pick = jnp.where(iota((BLK, slots), 1) == slot, 1.0, 0.0).astype(BF16)
        grad = nn(pick, dx_ref[...])
        hat, rstd = norm_stats(hidden_ref[rows, :])
        sums[2:3, :] += jnp.sum(grad * hat, axis=0, keepdims=True)
        sums[3:4, :] += jnp.sum(grad, axis=0, keepdims=True)
        gg = grad * gain_two
        inner = gg - jnp.mean(gg, axis=1, keepdims=True) - hat * jnp.mean(gg * hat, axis=1, keepdims=True)
        total = cot_ref[rows, :].astype(F32) * weight + rstd * inner
        hidden_ref[rows, :] = total
        low = total.astype(BF16)
        branch[rows, :] = low
        gmix[rows, :] = nt(low, wo_ref[...]).astype(BF16)
        normed_t[:, rows] = normed_ref[rows, :].astype(F32).T.astype(BF16)
        return carry

    lax.fori_loop(0, blocks, open_block, 0)
    def put_dense(part):
        rows = pl.ds(part * width, width)
        return pltpu.make_async_copy(dense_ref.at[rows], dense_hbm.at[rows], puts.at[part])

    dense_ref[pl.ds(3 * width, width), :] = tn(mixed_ref[...], branch[...]).astype(BF16)
    put_dense(3).start()
    settle(sum_y(depth - 1), spare_y, y_land, depth - 1)
    sum_y(depth - 2).start()

    for stream in range(2):
        keep_one(stream).wait()
        add_one(stream, 0)
        scatter_two(stream).start()

    def attend(pair, carry):
        @pl.when(pair + 1 < HEADS // 2)
        def _():
            load_probs(pair + 1).start()

        @pl.when(pair == 4)
        def _():
            for stream in range(2):
                add_one(stream, 1)

        @pl.when(pair == 5)
        def _():
            settle(sum_y(depth - 2), spare_y, y_land, depth - 2)
            sum_y(depth - 3).start()

        load_probs(pair).wait()
        base = pl.multiple_of(pair * 128, 128)
        cols = pl.ds(base, 128)
        q_pair = q_ref[:, cols]
        k_pair = k_ref[:, cols]
        v_pair = v_ref[:, cols]
        o_pair = gmix[:, cols]
        low = lane < 64
        q_head = [jnp.where(low, q_pair, 0), jnp.where(low, 0, q_pair)]
        v_head = [jnp.where(low, v_pair, 0), jnp.where(low, 0, v_pair)]
        o_head = [jnp.where(low, o_pair, 0), jnp.where(low, 0, o_pair)]
        k_t = k_pair.astype(F32).T.astype(BF16)
        prod_t = (o_pair.astype(F32) * mixed_ref[:, cols].astype(F32)).T
        delta = [jnp.sum(prod_t[:64], axis=0, keepdims=True), jnp.sum(prod_t[64:], axis=0, keepdims=True)]
        dq_t = [[None] * blocks, [None] * blocks]
        for block in range(blocks):
            start = block * BLK
            dk = None
            dv = None
            for half in range(2):
                tiles = [
                    probs[pair % 2, half, pl.ds((later * (later + 1) // 2 + block) * BLK, BLK), :]
                    for later in range(block, blocks)
                ]
                attention = jnp.concatenate(tiles, axis=1) if block < blocks - 1 else tiles[0]
                grad_p = nt(v_head[half][start : start + BLK], o_pair[start:])
                grad_s = (attention.astype(F32) * (grad_p - delta[half][:, start:])).astype(BF16)
                dv_part = nn(attention, o_head[half][start:])
                dk_part = nn(grad_s, q_head[half][start:])
                dv = dv_part if dv is None else dv + dv_part
                dk = dk_part if dk is None else dk + dk_part
                dq_part = nn(k_t[half * 64 : half * 64 + 64, start : start + BLK], grad_s)
                for later in range(block, blocks):
                    piece = dq_part[:, (later - block) * BLK : (later - block + 1) * BLK]
                    dq_t[half][later] = piece if dq_t[half][later] is None else dq_t[half][later] + piece
            rows = pl.ds(start, BLK)
            dqkv[rows, pl.ds(pl.multiple_of(base + width, 128), 128)] = dk.astype(BF16)
            dqkv[rows, pl.ds(pl.multiple_of(base + 2 * width, 128), 128)] = dv.astype(BF16)
        for block in range(blocks):
            both = jnp.concatenate([dq_t[0][block], dq_t[1][block]], axis=0) * (HEAD_DIM ** (-0.5))
            dqkv[pl.ds(block * BLK, BLK), cols] = both.T.astype(BF16)
        return carry

    lax.fori_loop(0, HEADS // 2, attend, 0)

    for part in range(3):
        dense_ref[pl.ds(part * width, width), :] = nn(normed_t[...], dqkv[:, pl.ds(part * width, width)]).astype(BF16)
        put_dense(part).start()

    def close_block(block, carry):
        rows = pl.ds(pl.multiple_of(block * BLK, BLK), BLK)
        grad = nt(dqkv[rows, 0:width], wq_ref[...])
        grad = grad + nt(dqkv[rows, width : 2 * width], wk_ref[...])
        grad = grad + nt(dqkv[rows, 2 * width : 3 * width], wv_ref[...])
        hat, rstd = norm_stats(x_ref[rows, :].astype(F32))
        sums[0:1, :] += jnp.sum(grad * hat, axis=0, keepdims=True)
        sums[1:2, :] += jnp.sum(grad, axis=0, keepdims=True)
        gg = grad * gain_one
        inner = gg - jnp.mean(gg, axis=1, keepdims=True) - hat * jnp.mean(gg * hat, axis=1, keepdims=True)
        grad_ref[rows, :] = (hidden_ref[rows, :] + rstd * inner).astype(BF16)
        return carry

    lax.fori_loop(0, blocks, close_block, 0)
    vec_ref[...] = sums[...]
    for stream in range(2):
        scatter_two(stream).wait()
        start = bits[1 - stream] * quarter
        sum_rows(kept.at[stream, span(start, quarter)], land_two.at[stream], quarter)
        store_piece(stream).start()
    for step in reversed(range(depth - 2)):
        settle(sum_y(step), spare_y, y_land, step)
        if step:
            sum_y(step - 1).start()
    spare_out = pltpu.make_async_copy(spare_y.at[pl.ds(0, BLK)], y_back_ref.at[pl.ds(base, BLK)], own.at[1])
    spare_out.start()
    spare_out.wait()
    for stream in range(2):
        store_piece(stream).wait()
    for part in range(4):
        put_dense(part).wait()
    mine.wait()
    for copy in copies:
        copy.wait()


STREAMS = 3
CHUNKS = 4


def halving_plan(dp, count, rows):
    experts = [("expert", 2 << bit) for bit in range(depth_of(count) - 1)]
    groups = [("dp", 1 << bit) for bit in range(depth_of(dp))]
    core = [("expert", 1)]
    plans = [core + groups + experts, core + groups[::-1] + experts, core + experts + groups]
    halvings = 0
    while halvings < len(plans[0]) and (rows >> halvings) % 32 == 0:
        halvings += 1
    return plans, halvings


def finish_kernel(
    dp,
    count,
    dense_hbm,
    vec_ref,
    slot_col_hbm,
    hidden_hbm,
    gate_hbm,
    y_hbm,
    y_rows_hbm,
    piece_ref,
    out_ref,
    full_ref,
    total_ref,
    grads_ref,
    dense_ref,
    slot_col_ref,
    hidden_ref,
    gate_ref,
    y_ref,
    acc,
    landing,
    full,
    vec_acc,
    vec_land,
    sends,
    recvs,
    back_sends,
    back_recvs,
    vec_sends,
    vec_recvs,
    put,
    unit_sends,
    unit_recvs,
    own,
    y_sends,
    y_recvs,
    gets,
    fills,
):
    tokens, width = hidden_ref.shape
    slots = y_ref.shape[0]
    main = (slots - BLK) // count
    early = count - last_returns(count)
    rows = dense_ref.shape[0] // STREAMS
    place = {"dp": lax.axis_index("dp"), "expert": lax.axis_index("expert")}
    size = {"dp": dp, "expert": count}
    plans, halvings = halving_plan(dp, count, rows)
    steps = len(plans[0])

    def partner(axis, mask):
        return {axis: flip(place[axis], mask, size[axis])}

    operands = [(dense_hbm, dense_ref), (slot_col_hbm, slot_col_ref), (hidden_hbm, hidden_ref), (gate_hbm, gate_ref)]
    operands = [pltpu.make_async_copy(source, target, fills.at[i]) for i, (source, target) in enumerate(operands)]
    for copy in operands:
        copy.start()
    barrier = pltpu.get_barrier_semaphore()
    for axis, mask in plans[0]:
        pl.semaphore_signal(barrier, inc=1, device_id=partner(axis, mask), device_id_type=MESH)
    for mask in range(early, count):
        pl.semaphore_signal(barrier, inc=1, device_id=partner("expert", mask), device_id_type=MESH)
    pl.semaphore_wait(barrier, steps + count - early)
    me = place["expert"]
    y_copies = [return_block(me, count, main, mask, y_rows_hbm, y_ref, y_sends, y_recvs) for mask in range(early, count)]
    loads = [pltpu.make_async_copy(y_hbm.at[pl.ds(count * main, BLK)], y_ref.at[pl.ds(count * main, BLK)], gets.at[count])]
    for mask in range(early):
        part = span(flip(me, mask, count) * main, main)
        loads.append(pltpu.make_async_copy(y_hbm.at[part], y_ref.at[part], gets.at[mask]))
    for load in loads:
        load.start()

    def side(axis, mask):
        return (place[axis] // mask) % 2

    _, bits = dp_sides()
    quarter = piece_ref.shape[0] // 2
    chunk = quarter // CHUNKS
    starts = [
        4 * quarter * stream + bits[stream] * 2 * quarter + bits[1 - stream] * quarter for stream in range(2)
    ]
    others = [
        4 * quarter * stream + bits[stream] * 2 * quarter + (1 - bits[1 - stream]) * quarter for stream in range(2)
    ]

    def unit(index, stream):
        kind, part = index // CHUNKS, index % CHUNKS
        near, far = partner("dp", 1 << stream), partner("dp", 2 >> stream)
        if kind == 2:
            source = target = grads_ref.at[span(others[stream] + part * chunk, chunk)]
        else:
            source = piece_ref.at[pl.ds(stream * quarter + part * chunk, chunk)]
            target = grads_ref.at[span(starts[stream] + part * chunk, chunk)]
        return copy_to(
            source, target, unit_sends.at[index, stream], unit_recvs.at[index, stream], far if kind == 0 else near
        )

    pending = list(range(3 * CHUNKS))

    def advance(number):
        for _ in range(min(number, len(pending))):
            index = pending.pop(0)
            for stream in range(2):
                if index >= 2 * CHUNKS:
                    unit(index - 2 * CHUNKS, stream).wait_recv()
                unit(index, stream).start()

    mine = [
        pltpu.make_async_copy(
            piece_ref.at[pl.ds(stream * quarter, quarter)], grads_ref.at[span(starts[stream], quarter)], own.at[stream]
        )
        for stream in range(2)
    ]
    for copy in mine:
        copy.start()

    def combine(block):
        rows_at = pl.ds(pl.multiple_of(block * BLK, BLK), BLK)
        slot = slot_col_ref[rows_at, 0:1]
        pick = jnp.where(iota((BLK, slots), 1) == slot, 1.0, 0.0).astype(BF16)
        returned = nn(pick, y_ref[...])
        out_ref[rows_at, :] = (hidden_ref[rows_at, :] + gate_ref[rows_at, 0:1] * returned).astype(BF16)

    low = [jnp.int32(stream * rows) for stream in range(STREAMS)]
    extent = rows
    offset = 0
    trail = []
    for step in range(steps):
        halve = step < halvings
        part = extent // 2 if halve else extent
        copies = []
        for stream in range(STREAMS):
            axis, mask = plans[stream][step]
            kept = low[stream] + side(axis, mask) * part if halve else low[stream]
            other = low[stream] + (1 - side(axis, mask)) * part if halve else low[stream]
            source = dense_ref if step == 0 else acc.at[(step - 1) % 2]
            land = landing.at[stream, pl.ds(offset, part)]
            copy = copy_to(
                (dense_hbm if step == 0 else source).at[span(other, part)], land, sends.at[stream, step], recvs.at[stream, step], partner(axis, mask)
            )
            copy.start()
            copies.append((copy, kept, source))
        axis, mask = plans[0][step]
        vec_source = vec_ref if step == 0 else vec_acc.at[step - 1]
        vec_copy = copy_to(vec_source, vec_land.at[step], vec_sends.at[step], vec_recvs.at[step], partner(axis, mask))
        vec_copy.start()
        advance(1)
        if step == 0:
            for copy in y_copies:
                copy.start()
        if step == 0:
            for copy in operands:
                copy.wait()
        trail.append((list(low), extent))
        for stream in range(STREAMS):
            copy, kept, source = copies[stream]
            copy.wait()
            target = acc.at[step % 2] if step < steps - 1 else full
            grain = min(part, 64)

            def add(rows_at):
                held = span(kept + rows_at.start, grain)
                value = source[held, :].astype(F32) + landing[stream, span(offset + rows_at.start, grain), :].astype(F32)
                target[held, :] = value.astype(BF16)

            each_rows(part, add, grain)
            low[stream] = kept
        vec_copy.wait()
        vec_sum = vec_source[...] + vec_land[step]
        if step < steps - 1:
            vec_acc[step] = vec_sum
        else:
            total_ref[...] = vec_sum
        extent = part
        offset += part

    writes = []
    for step in reversed(range(halvings)):
        origins, whole = trail[step]
        copies = []
        for stream in range(STREAMS):
            axis, mask = plans[stream][step]
            held = span(low[stream], extent)
            copy = copy_to(
                full.at[held], full.at[held], back_sends.at[stream, step], back_recvs.at[stream, step], partner(axis, mask)
            )
            copy.start()
            copies.append(copy)
        advance(2)
        if step == 1:
            for copy in loads + y_copies:
                copy.wait()

            def combine_block(block, carry):
                combine(block)
                return carry

            lax.fori_loop(0, tokens // BLK, combine_block, 0)
        for stream in range(STREAMS):
            copies[stream].wait()
            low[stream] = origins[stream]
        extent = whole
        if step == 1:
            for stream in range(STREAMS):
                held = span(low[stream], extent)
                writes.append(pltpu.make_async_copy(full.at[held], full_ref.at[held], put.at[0, stream]))
                writes[-1].start()
    advance(len(pending))
    for stream in range(STREAMS):
        held = span(stream * rows + (1 - side("expert", 1)) * (rows // 2), rows // 2)
        writes.append(pltpu.make_async_copy(full.at[held], full_ref.at[held], put.at[1, stream]))
        writes[-1].start()
    for index in range(3 * CHUNKS):
        for stream in range(2):
            if index >= CHUNKS:
                unit(index, stream).wait_recv()
            unit(index, stream).wait_send()
    for copy in mine + writes:
        copy.wait()


AHEAD = 6


def widen_kernel(hidden, dense_hbm, grads_hbm, total_ref, output_hbm, inputs_hbm, *rest):
    outs, vecs, passed, (low, high, rows, gets, puts, moves) = rest[:6], rest[6:10], rest[10:12], rest[12:]
    width = dense_hbm.shape[1]
    jobs = []
    for block in range(hidden // width):
        part = pl.ds(block * width, width)
        jobs.append((grads_hbm.at[part], outs[4].at[:, part]))
        jobs.append((grads_hbm.at[pl.ds(hidden + block * width, width)], outs[5].at[part, :]))
    for index in range(4):
        jobs.append((dense_hbm.at[pl.ds(index * width, width)], outs[index]))
    loads = [pltpu.make_async_copy(source, low.at[i], gets.at[i]) for i, (source, _) in enumerate(jobs)]
    for load in loads[:AHEAD]:
        load.start()
    for index, vec in enumerate(vecs):
        vec[...] = total_ref[index : index + 1, :].reshape(width)
    taken = [pltpu.make_async_copy(source, rows.at[i], moves.at[i]) for i, source in enumerate((output_hbm, inputs_hbm))]
    given = [pltpu.make_async_copy(rows.at[i], target, moves.at[i]) for i, target in enumerate(passed)]
    slots = high.shape[0]
    stores = []
    for index, (_, target) in enumerate(jobs):
        loads[index].wait()
        if index + AHEAD < len(jobs):
            loads[index + AHEAD].start()
        if index == 1:
            for copy in taken:
                copy.start()
        if index == 4:
            for before, after in zip(taken, given):
                before.wait()
                after.start()
        if index >= slots:
            stores[index - slots].wait()

        def step(part):
            high[index % slots, part, :] = low[index, part, :].astype(F32)

        each_rows(width, step)
        stores.append(pltpu.make_async_copy(high.at[index % slots], target, puts.at[index % slots]))
        stores[-1].start()
    for copy in stores[-slots:] + given:
        copy.wait()


def call(kernel, outs, in_specs, scratch, name, out_specs=None, collective=None, flops=10**9):
    remote = {} if collective is None else {"collective_id": collective, "has_side_effects": True}
    return pl.pallas_call(
        kernel,
        out_shape=outs,
        in_specs=in_specs,
        out_specs=out_specs or [VMEM] * len(outs),
        scratch_shapes=scratch,
        compiler_params=pltpu.CompilerParams(vmem_limit_bytes=LIMIT, **remote),
        cost_estimate=pl.CostEstimate(flops=flops, bytes_accessed=10**7, transcendentals=0),
        name=name,
    )


def dma(*dims):
    return pltpu.SemaphoreType.DMA(dims)


def shape(dims, kind):
    return jax.ShapeDtypeStruct(dims, kind)


def tables(experts, main, slots, counts, group, domains, sort_order, cotangent):
    tokens, width = cotangent.shape
    return call(
        functools.partial(table_kernel, experts, main),
        [shape((slots, width), BF16), shape((tokens, 128), jnp.int32), shape((8, tokens), jnp.int32)],
        [SMEM, SMEM, SMEM, VMEM, VMEM],
        [pltpu.VMEM((tokens, width), BF16)],
        "tables",
    )(counts, group, domains, sort_order, cotangent)


def forward(count, main, spare, inputs, g1, s1, g2, s2, wq, wk, wv, wo, router, slot_col, slot_row, cot_send):
    tokens, width = inputs.shape
    blocks = tokens // BLK
    prob_block = (2, blocks * (blocks + 1) // 2 * BLK, BLK)
    rows_low = shape((tokens, width), BF16)
    return call(
        functools.partial(forward_kernel, count, main, spare),
        [
            rows_low,
            rows_low,
            rows_low,
            rows_low,
            rows_low,
            shape((tokens, width), F32),
            shape((tokens, 128), F32),
            shape(cot_send.shape, BF16),
            shape((count * (main + spare), width), BF16),
            shape((HEADS // 2,) + prob_block, BF16),
        ],
        [VMEM] * 5 + [ANY] * 4 + [VMEM] * 3 + [ANY],
        [pltpu.VMEM((width, width), BF16)] * 4
        + [
            pltpu.VMEM((tokens, width), BF16),
            pltpu.VMEM((2,) + prob_block, BF16),
            dma(2),
            dma(count),
            dma(count),
            dma(depth_of(count)),
            dma(depth_of(count)),
            dma(2),
            dma(4),
        ],
        "dense_forward",
        [VMEM] * 8 + [ANY] * 2,
        1,
    )(inputs, g1, s1, g2, s2, wq, wk, wv, wo, router, slot_col, slot_row, cot_send)


def expert_block(count, main, spare, counts, send, cot_send, cot_rows, router_t, w1, w2, chunk=768):
    slots, width = cot_rows.shape
    hidden = w1.shape[1]
    late = slots - (count - count // 4) * main
    rows = shape((slots, width), BF16)
    keep = pltpu.VMEM((slots, width), BF16)
    depth = depth_of(count)
    return call(
        functools.partial(expert_kernel, count, main, spare, chunk),
        [
            rows,
            shape((count * main, width), BF16),
            shape((late, width), BF16),
            shape((2 * hidden, width), BF16),
        ],
        [SMEM, ANY, ANY, ANY, VMEM, ANY, ANY],
        [
            pltpu.VMEM((width, hidden), BF16),
            pltpu.VMEM((hidden, width), BF16),
            pltpu.VMEM((width, hidden), F32),
            pltpu.VMEM((hidden, width), F32),
            keep,
            keep,
            keep,
            keep,
            pltpu.VMEM((2, width, width), BF16),
            dma(4),
            dma(count),
            dma(count),
            dma(depth),
            dma(depth),
            dma(depth),
            dma(depth),
            dma(count),
            dma(count),
            dma(2),
            dma(slots // BLK),
            dma(2),
        ],
        "expert",
        [ANY] * 4,
        2,
    )(counts, send, cot_send, cot_rows, router_t, w1, w2)


def backward(
    dp, count, main, spare, group, domains, inputs, cotangent, g1, g2, wq, wk, wv, wo, slot_col,
    normed, q, k, v, mixed, probs, hidden, dx, late, y, grads,
):
    tokens, width = inputs.shape
    half = grads.shape[0] // 4
    return call(
        functools.partial(backward_kernel, dp, count, main, spare),
        [shape((tokens, width), BF16), shape((4 * width, width), BF16), shape((8, width), F32), shape((count * main + BLK, width), BF16), shape((half, width), BF16)],
        [SMEM] * 2 + [ANY] * 2 + [VMEM] * 2 + [ANY] * 16,
        [pltpu.VMEM(v.shape, v.dtype) for v in (inputs, cotangent, wq, wk, wv, wo, slot_col, normed, q, k, v, mixed, hidden)]
        + [
            pltpu.VMEM((4 * width, width), BF16),
            pltpu.VMEM((count * main + BLK, width), BF16),
            pltpu.VMEM((count * spare, width), BF16),
            pltpu.VMEM((count * spare, width), BF16),
            pltpu.VMEM((count * spare, width), BF16),
            pltpu.VMEM((count * spare, width), BF16),
            pltpu.VMEM((2,) + probs.shape[1:], BF16),
            pltpu.VMEM((2, half, width), BF16),
            pltpu.VMEM((2, half, width), BF16),
            pltpu.VMEM((2, half // 2, width), BF16),
            pltpu.VMEM((tokens, width), BF16),
            pltpu.VMEM((tokens, width), BF16),
            pltpu.VMEM((width, tokens), BF16),
            pltpu.VMEM((tokens, 3 * width), BF16),
            pltpu.VMEM((8, width), F32),
            dma(count),
            dma(count),
            dma(count),
            dma(count),
            dma(depth_of(count)),
            dma(depth_of(count)),
            dma(depth_of(count)),
            dma(depth_of(count)),
            dma(3),
            dma(count),
            dma(13),
            dma(3, 2),
            dma(3, 2),
            dma(2),
            dma(2),
            dma(4),
        ],
        "dense_backward",
        [VMEM, ANY, VMEM, ANY, ANY],
        3,
        5 * 10**10,
    )(group, domains, inputs, cotangent, g1, g2, wq, wk, wv, wo, slot_col, normed, q, k, v, mixed, probs, hidden, dx, late, y, grads)


def finish(dp, count, dense, vec, slot_col, hidden, gate, y_back, y_rows, piece):
    width = hidden.shape[1]
    rows = dense.shape[0]
    steps = len(halving_plan(dp, count, rows // STREAMS)[0][0])
    return call(
        functools.partial(finish_kernel, dp, count),
        [shape(hidden.shape, BF16), shape(dense.shape, BF16), shape(vec.shape, F32), shape((4 * piece.shape[0], width), BF16)],
        [ANY, VMEM] + [ANY] * 6,
        [pltpu.VMEM(v.shape, v.dtype) for v in (dense, slot_col, hidden, gate)]
        + [
            pltpu.VMEM(y_back.shape, BF16),
            pltpu.VMEM((2, rows, width), BF16),
            pltpu.VMEM((STREAMS, rows // STREAMS + 64, width), BF16),
            pltpu.VMEM((rows, width), BF16),
            pltpu.VMEM((steps,) + vec.shape, F32),
            pltpu.VMEM((steps,) + vec.shape, F32),
            dma(STREAMS, steps),
            dma(STREAMS, steps),
            dma(STREAMS, steps),
            dma(STREAMS, steps),
            dma(steps),
            dma(steps),
            dma(2, STREAMS),
            dma(3 * CHUNKS, 2),
            dma(3 * CHUNKS, 2),
            dma(2),
            dma(count),
            dma(count),
            dma(count + 1),
            dma(4),
        ],
        "finish",
        [VMEM, ANY, VMEM, ANY],
        4,
    )(dense, vec, slot_col, hidden, gate, y_back, y_rows, piece)


def widen(hidden, dense, grads, total, output, grad_inputs):
    width = dense.shape[1]
    square = shape((width, width), F32)
    jobs = 2 * (hidden // width) + 4
    rows = shape(output.shape, BF16)
    return call(
        functools.partial(widen_kernel, hidden),
        [square] * 4
        + [shape((width, hidden), F32), shape((hidden, width), F32)]
        + [shape((width,), F32)] * 4
        + [rows, rows],
        [ANY, ANY, VMEM, ANY, ANY],
        [
            pltpu.VMEM((jobs, width, width), BF16),
            pltpu.VMEM((6, width, width), F32),
            pltpu.VMEM((2,) + output.shape, BF16),
            dma(jobs),
            dma(6),
            dma(2),
        ],
        "widen",
        [ANY] * 6 + [VMEM] * 4 + [ANY] * 2,
    )(dense, grads, total, output, grad_inputs)


def local(
    inputs,
    cotangent,
    seq_group,
    domain_counts,
    sort_order,
    send_counts,
    gain_one,
    shift_one,
    gain_two,
    shift_two,
    w_query,
    w_key,
    w_value,
    w_out,
    router,
    expert_in,
    expert_out,
):
    tokens, width = inputs.shape
    experts = send_counts.shape[1]
    capacity = 2 * tokens // experts
    spare = capacity // 4
    main = capacity - spare
    slots = experts * main + BLK
    count = lax.axis_size("expert")
    g1, s1, g2, s2 = gain_one, shift_one, gain_two, shift_two
    router_t = router.T
    cot_send, slot_col, slot_row = tables(experts, main, slots, send_counts, seq_group, domain_counts, sort_order, cotangent)
    normed, q, k, v, mixed, hidden, gate, send, cot_rows, probs = forward(
        count, main, spare, inputs, g1, s1, g2, s2, w_query, w_key, w_value, w_out, router_t, slot_col, slot_row, cot_send
    )
    y_rows, dx_back, dx_late, grads = expert_block(
        count, main, spare, send_counts, send, cot_send, cot_rows, router_t, expert_in[0], expert_out[0]
    )
    dp = lax.axis_size("dp")
    grad_inputs, dense, vec, y_back, piece = backward(
        dp, count, main, spare, seq_group, domain_counts, inputs, cotangent, g1, g2, w_query, w_key, w_value, w_out, slot_col,
        normed, q, k, v, mixed, probs, hidden, dx_back, dx_late, y_rows, grads,
    )
    output, dense, vec, grads = finish(dp, count, dense, vec, slot_col, hidden, gate, y_back, y_rows, piece)
    wq, wk, wv, wo, first, second, gain_a, shift_a, gain_b, shift_b, output, grad_inputs = widen(
        expert_in.shape[2], dense, grads, vec, output, grad_inputs
    )
    return (output, grad_inputs, gain_a, shift_a, gain_b, shift_b, wq, wk, wv, wo, first[None], second[None])


def solution(mesh):
    rows = P(("dp", "expert"), None)
    split = P("expert", None, None)
    return jax.shard_map(
        local,
        mesh=mesh,
        in_specs=(rows, rows, P(("dp", "expert")), P(), rows, rows) + (P(),) * 9 + (split, split),
        out_specs=(rows, rows) + (P(),) * 8 + (split, split),
        check_vma=False,
    )
```

```python
import functools

import jax
import jax.numpy as jnp
from jax import lax
from jax.experimental import pallas as pl
from jax.experimental.pallas import tpu as pltpu
from jax.sharding import PartitionSpec as P

HEADS = 12
HEAD_DIM = 64
LEN = 1024
EPS = 1e-05
F32 = jnp.float32
BF16 = jnp.bfloat16
BLK = 256
CODE = 4096
LIMIT = 63 * 1024 * 1024

VMEM = pl.BlockSpec(memory_space=pltpu.VMEM)
SMEM = pl.BlockSpec(memory_space=pltpu.SMEM)
ANY = pl.BlockSpec(memory_space=pl.ANY)
MESH = pl.DeviceIdType.MESH


def dot(left, right, contract):
    return lax.dot_general(left, right, ((contract[0:1], contract[1:2]), ((), ())), preferred_element_type=F32)


def nn(left, right):
    return dot(left, right, (1, 0))


def nt(left, right):
    return dot(left, right, (1, 1))


def tn(left, right):
    return dot(left, right, (0, 0))


def iota(shape, axis):
    return lax.broadcasted_iota(jnp.int32, shape, axis)


def flip(index, mask, count):
    bit, out = 1, 0
    while bit < count:
        out = out + ((index // bit + mask // bit) % 2) * bit
        bit *= 2
    return out


def greet(axis, me, count):
    barrier = pltpu.get_barrier_semaphore()
    for mask in range(1, count):
        pl.semaphore_signal(barrier, inc=1, device_id={axis: flip(me, mask, count)}, device_id_type=MESH)
    pl.semaphore_wait(barrier, count - 1)


def copy_to(source, target, send, recv, device):
    return pltpu.make_async_remote_copy(
        src_ref=source, dst_ref=target, send_sem=send, recv_sem=recv, device_id=device, device_id_type=MESH
    )


def span(start, rows):
    return pl.ds(pl.multiple_of(start, 16), rows)


def send_block(me, count, rows, mask, source, target, sends, recvs):
    peer = flip(me, mask, count)
    return copy_to(
        source.at[span(peer * rows, rows)], target.at[span(mask * rows, rows)], sends.at[mask], recvs.at[mask], {"expert": peer}
    )


def return_block(me, count, rows, mask, source, target, sends, recvs, shift=0):
    return copy_to(
        source.at[span((mask - shift) * rows, rows)],
        target.at[span(me * rows, rows)],
        sends.at[mask],
        recvs.at[mask],
        {"expert": flip(me, mask, count)},
    )


def last_returns(count):
    return count // 8


def dp_sides():
    index = lax.axis_index("dp")
    return index, (index % 2, (index // 2) % 2)


def each_rows(rows, step, size=64):
    def body(block, carry):
        step(pl.ds(pl.multiple_of(block * size, size), size))
        return carry

    lax.fori_loop(0, rows // size, body, 0)


def sum_rows(target, other, rows):
    def step(block, carry):
        part = pl.ds(pl.multiple_of(block * BLK, BLK), BLK)
        target[part, :] = (target[part, :].astype(F32) + other[part, :].astype(F32)).astype(BF16)
        return carry

    lax.fori_loop(0, rows // BLK, step, 0)


def depth_of(count):
    return count.bit_length() - 1


def gather_spare(me, count, base, rows, step, first, target, sends, recvs):
    have = rows << step
    source = first.at[pl.ds(base, rows)] if step == 0 else target.at[pl.ds(base, have)]
    return copy_to(
        source,
        target.at[pl.ds(base + have, have)],
        sends.at[step],
        recvs.at[step],
        {"expert": flip(me, count >> (step + 1), count)},
    )


def return_spare(me, count, rows, step, source, shift, landing, sends, recvs):
    half = rows << step
    return copy_to(
        source.at[pl.ds(shift + half, half)],
        landing.at[pl.ds(half, half)],
        sends.at[step],
        recvs.at[step],
        {"expert": flip(me, count >> (step + 1), count)},
    )


def row_of(ref):
    return ref[...].reshape(1, ref.shape[0])


def domain_weight(group_ref, counts_ref):
    groups = counts_ref.shape[0]
    group = group_ref[0]
    total = jnp.zeros((1, 128), F32)
    mine = jnp.zeros((1, 128), F32)
    for index in range(groups):
        inverse = 1.0 / jnp.full((1, 128), counts_ref[index], jnp.int32).astype(F32)
        total = total + inverse
        mine = mine + jnp.where(group == index, inverse, 0.0)
    return (mine / (total / groups))[:, 0:1]


def norm_stats(rows):
    center = rows - jnp.mean(rows, axis=-1, keepdims=True)
    rstd = lax.rsqrt(jnp.mean(center * center, axis=-1, keepdims=True) + EPS)
    return center * rstd, rstd


def pack_rows(slot_row, rows_ref, send_ref):
    slots = send_ref.shape[0]
    tokens = rows_ref.shape[0]

    def step(block, carry):
        base = pl.multiple_of(block * BLK, BLK)
        slot = iota((BLK, tokens), 0) + base
        pick = jnp.where(slot == slot_row, 1.0, 0.0).astype(BF16)
        send_ref[pl.ds(base, BLK), :] = nn(pick, rows_ref[...]).astype(BF16)
        return carry

    lax.fori_loop(0, slots // BLK, step, 0, unroll=True)


def table_kernel(experts, main, counts_ref, group_ref, domain_ref, sort_ref, cot_ref, send_ref, slot_col_ref, slot_row_ref, scaled):
    tokens = cot_ref.shape[0]
    place = iota((1, tokens), 1)
    expert_at = jnp.zeros((1, tokens), jnp.int32)
    start_at = jnp.zeros((1, tokens), jnp.int32)
    end = jnp.int32(0)
    for expert in range(experts):
        count = counts_ref[0, expert]
        end = end + count
        past = place >= end
        expert_at = expert_at + jnp.where(past, 1, 0)
        start_at = start_at + jnp.where(past, count, 0)
    slot = place - start_at
    dest = jnp.where(slot < main, expert_at * main + slot, (experts - 1) * main + slot)
    code = (expert_at * CODE + dest).astype(F32)
    sort_row = sort_ref[...]
    scaled[...] = (cot_ref[...].astype(F32) * domain_weight(group_ref, domain_ref)).astype(BF16)
    for block in range(tokens // BLK):
        token = iota((BLK, tokens), 0) + block * BLK
        col = jnp.sum(jnp.where(token == sort_row, code, 0.0), axis=1, keepdims=True)
        owner = (col * (1.0 / CODE)).astype(jnp.int32)
        where = col.astype(jnp.int32) - owner * CODE
        slot_col_ref[pl.ds(block * BLK, BLK), :] = jnp.where(iota((1, 128), 1) < 64, where, owner)
        slot_row_ref[:, pl.ds(block * BLK, BLK)] = jnp.broadcast_to(where, (BLK, 128)).astype(F32).T[0:8].astype(jnp.int32)
    pack_rows(slot_row_ref[0:1, :], scaled, send_ref)


def forward_kernel(
    count,
    main,
    spare,
    x_ref,
    gain_one_ref,
    shift_one_ref,
    gain_two_ref,
    shift_two_ref,
    wq_hbm,
    wk_hbm,
    wv_hbm,
    wo_hbm,
    router_ref,
    slot_col_ref,
    slot_row_ref,
    cot_send_ref,
    normed_ref,
    q_ref,
    k_ref,
    v_ref,
    mixed_ref,
    hidden_ref,
    gate_ref,
    send_ref,
    cot_rows_ref,
    probs_hbm,
    wq_ref,
    wk_ref,
    wv_ref,
    wo_ref,
    routed,
    probs,
    prob_sems,
    sends,
    recvs,
    spare_sends,
    spare_recvs,
    own,
    fills,
):
    tokens, width = x_ref.shape
    blocks = tokens // BLK
    me = lax.axis_index("expert")
    weights = [(wq_hbm, wq_ref), (wk_hbm, wk_ref), (wv_hbm, wv_ref), (wo_hbm, wo_ref)]
    weights = [pltpu.make_async_copy(source, target, fills.at[i]) for i, (source, target) in enumerate(weights)]
    for copy in weights:
        copy.start()
    greet("expert", me, count)
    base = count * main

    def gather(step):
        return gather_spare(me, count, base, spare, step, cot_send_ref, cot_rows_ref, spare_sends, spare_recvs)

    gather(0).start()
    copies = [send_block(me, count, main, mask, cot_send_ref, cot_rows_ref, sends, recvs) for mask in range(1, count - 1)]
    for copy in copies:
        copy.start()
    mine = [
        pltpu.make_async_copy(cot_send_ref.at[span(me * main, main)], cot_rows_ref.at[pl.ds(0, main)], own.at[0]),
        pltpu.make_async_copy(cot_send_ref.at[pl.ds(base, spare)], cot_rows_ref.at[pl.ds(base, spare)], own.at[1]),
    ]
    for copy in mine:
        copy.start()
    lane = iota((1, 128), 1)
    gain_one, shift_one, gain_two, shift_two = (row_of(r) for r in (gain_one_ref, shift_one_ref, gain_two_ref, shift_two_ref))

    def project(block, carry):
        rows = pl.ds(pl.multiple_of(block * BLK, BLK), BLK)
        hat, _ = norm_stats(x_ref[rows, :].astype(F32))
        normed = (hat * gain_one + shift_one).astype(BF16)
        normed_ref[rows, :] = normed
        q_ref[rows, :] = (nn(normed, wq_ref[...]).astype(BF16) * (HEAD_DIM ** (-0.5))).astype(BF16)
        k_ref[rows, :] = nn(normed, wk_ref[...]).astype(BF16)
        v_ref[rows, :] = nn(normed, wv_ref[...]).astype(BF16)
        return carry

    for copy in weights:
        copy.wait()
    lax.fori_loop(0, blocks, project, 0, unroll=2)

    keep = iota((BLK, BLK), 0) <= iota((BLK, BLK), 1)

    def keep_probs(pair):
        return pltpu.make_async_copy(probs.at[pair % 2], probs_hbm.at[pair], prob_sems.at[pair % 2])

    def attend(pair, carry):
        @pl.when(pair >= 2)
        def _():
            keep_probs(pair - 2).wait()

        cols = pl.ds(pl.multiple_of(pair * 128, 128), 128)
        k_pair = k_ref[:, cols]
        v_t = v_ref[:, cols].astype(F32).T.astype(BF16)
        k_head = [jnp.where(lane < 64, k_pair, 0), jnp.where(lane >= 64, k_pair, 0)]
        for block in range(blocks):
            span = (block + 1) * BLK
            query = q_ref[pl.ds(block * BLK, BLK), cols]
            outs = []
            for half in range(2):
                scores = nt(k_head[half][:span], query)
                diag = jnp.where(keep, scores[block * BLK :], -1000000000.0)
                scores = jnp.concatenate([scores[: block * BLK], diag], axis=0) if block else diag
                peak = jnp.max(scores, axis=0, keepdims=True)
                exps = jnp.exp(scores - peak)
                total = jnp.sum(exps, axis=0, keepdims=True)
                attention = (exps * (1.0 / total)).astype(BF16)
                probs[pair % 2, half, pl.ds(block * (block + 1) // 2 * BLK, (block + 1) * BLK), :] = attention
                outs.append(nn(v_t[half * 64 : half * 64 + 64, :span], attention))
            mixed_ref[pl.ds(block * BLK, BLK), cols] = jnp.concatenate(outs, axis=0).T.astype(BF16)
        keep_probs(pair).start()
        return carry

    lax.fori_loop(0, HEADS // 2, attend, 0)
    experts = router_ref.shape[0]

    def finish(block, carry):
        rows = pl.ds(pl.multiple_of(block * BLK, BLK), BLK)
        hidden = x_ref[rows, :].astype(F32) + nn(mixed_ref[rows, :], wo_ref[...])
        hidden_ref[rows, :] = hidden
        hat, _ = norm_stats(hidden)
        low = (hat * gain_two + shift_two).astype(BF16)
        routed[rows, :] = low
        logits = nt(low, router_ref[...])
        owner = slot_col_ref[rows, 64:65]
        logit = jnp.sum(jnp.where(iota((BLK, experts), 1) == owner, logits, 0.0), axis=1, keepdims=True)
        gate_ref[rows, :] = jnp.broadcast_to(jax.nn.sigmoid(logit), (BLK, 128))
        return carry

    lax.fori_loop(0, blocks, finish, 0, unroll=2)
    pack_rows(slot_row_ref[0:1, :], routed, send_ref)
    for copy in mine + [keep_probs(HEADS // 2 - 2), keep_probs(HEADS // 2 - 1)]:
        copy.wait()
    for copy in copies + [gather(0)]:
        copy.wait()


def gelu_parts(v):
    t = 1.0 / (1.0 + (0.3275911 * 0.7071067811865476) * jnp.abs(v))
    bell = jnp.exp2((-0.5 * 1.4426950408889634) * (v * v))
    poly = ((((0.5307027145 * t - 0.7265760135) * t + 0.7107068705) * t - 0.142248368) * t + 0.127414796) * t
    tail = poly * bell
    return jnp.where(v >= 0.0, 1.0 - tail, tail), bell * 0.3989422804014327


def expert_kernel(
    count,
    main,
    spare,
    chunk,
    counts_ref,
    send_ref,
    cot_send_ref,
    cot_rows_ref,
    router_ref,
    w1_hbm,
    w2_hbm,
    y_ref,
    back_ref,
    late_ref,
    grads_ref,
    w1_ref,
    w2_ref,
    acc1,
    acc2,
    x_rows,
    g_ref,
    dx_rows,
    y_rows,
    stage,
    load_sems,
    sends,
    recvs,
    spare_sends,
    spare_recvs,
    cot_sends,
    cot_recvs,
    back_sends,
    back_recvs,
    own,
    y_sems,
    stage_sems,
):
    width, hidden = w1_ref.shape
    slots = x_rows.shape[0]
    base = count * main
    plain = base // BLK
    blocks = slots // BLK
    depth = depth_of(count)
    early = count - count // 4
    me = lax.axis_index("expert")
    loads = [
        pltpu.make_async_copy(w1_hbm, w1_ref, load_sems.at[0]),
        pltpu.make_async_copy(w2_hbm, w2_ref, load_sems.at[1]),
        pltpu.make_async_copy(cot_rows_ref.at[pl.ds(0, base - main)], g_ref.at[pl.ds(0, base - main)], load_sems.at[2]),
        pltpu.make_async_copy(cot_rows_ref.at[pl.ds(base, 2 * spare)], g_ref.at[pl.ds(base, 2 * spare)], load_sems.at[3]),
    ]
    for load in loads:
        load.start()
    greet("expert", me, count)

    def gather(step):
        return gather_spare(me, count, base, spare, step, send_ref, x_rows, spare_sends, spare_recvs)

    def arrive(mask):
        return send_block(me, count, main, mask, send_ref, x_rows, sends, recvs)

    def leave(mask):
        return return_block(me, count, main, mask, dx_rows, back_ref, back_sends, back_recvs)

    def gather_cot(step):
        source = cot_rows_ref if step == 1 else g_ref
        have = spare << step
        return copy_to(
            source.at[pl.ds(base, have)],
            g_ref.at[pl.ds(base + have, have)],
            cot_sends.at[step],
            cot_recvs.at[step],
            {"expert": flip(me, count >> (step + 1), count)},
        )

    def last_cot():
        rows = span(flip(me, count - 1, count) * main, main)
        return copy_to(
            cot_send_ref.at[rows],
            g_ref.at[pl.ds(base - main, main)],
            cot_sends.at[0],
            cot_recvs.at[0],
            {"expert": flip(me, count - 1, count)},
        )

    gather_cot(1).start()
    gather(0).start()
    for mask in range(1, count):
        arrive(mask).start()
    last_cot().start()
    mine_in = [
        pltpu.make_async_copy(send_ref.at[span(me * main, main)], x_rows.at[pl.ds(0, main)], own.at[0]),
        pltpu.make_async_copy(send_ref.at[pl.ds(base, spare)], x_rows.at[pl.ds(base, spare)], own.at[1]),
    ]
    for copy in mine_in:
        copy.start()

    def clear_one(part):
        acc1[part, :] = jnp.zeros((64, hidden), F32)

    def clear_two(part):
        acc2[part, :] = jnp.zeros((64, width), F32)

    each_rows(width, clear_one)
    each_rows(hidden, clear_two)
    experts = router_ref.shape[0]
    router = jnp.sum(jnp.where(iota((experts, 1), 0) == me, router_ref[...].astype(F32), 0.0), axis=0, keepdims=True)
    hot = jnp.full((1, 128), counts_ref[0, me], jnp.int32)[:, 0:1] > main
    hot = jnp.where(hot, 1.0, 0.0)
    for copy in loads + mine_in:
        copy.wait()

    def store_y(block):
        rows = pl.ds(pl.multiple_of(block * BLK, BLK), BLK)
        return pltpu.make_async_copy(y_rows.at[rows], y_ref.at[rows], y_sems.at[block])

    def mine_out():
        return pltpu.make_async_copy(dx_rows.at[pl.ds(0, main)], back_ref.at[span(me * main, main)], own.at[0])

    def run(turn, carry):
        block = turn + turn // (plain - 1) - (turn // (blocks - 1)) * (blocks - plain + 1)
        for item in range(BLK // main + 1):
            mask = (block * BLK + main - 1) // main + item

            @pl.when((block < plain) & (mask > 0) & (mask < ((block + 1) * BLK + main - 1) // main))
            def _():
                arrive(mask).wait_recv()

            @pl.when((block == plain - 1) & (mask == count - 1))
            def _():
                last_cot().wait_recv()

        for step in range(depth):

            @pl.when(turn == (max(step + 1, plain - depth + step + 1) if step else 1))
            def _():
                gather(step).wait_recv()
                if step:
                    gather_cot(step).wait_recv()
                if step + 1 < depth:
                    gather(step + 1).start()
                    if step:
                        gather_cot(step + 1).start()

        rows = pl.ds(pl.multiple_of(block * BLK, BLK), BLK)
        live = jnp.where(block < plain, 1.0, hot)
        x = (x_rows[rows, :].astype(F32) * live).astype(BF16)
        logit = jnp.sum(x.astype(F32) * router, axis=1, keepdims=True)
        gate = jax.nn.sigmoid(logit)
        go = g_ref[rows, :].astype(F32) * live
        g = (gate * go).astype(BF16)
        x_t = x.astype(F32).T.astype(BF16)
        y = jnp.zeros(x.shape, F32)
        dx = jnp.zeros(x.shape, F32)
        for first in range(0, hidden, chunk):
            cols = pl.ds(first, chunk)
            w1 = w1_ref[:, cols]
            w2 = w2_ref[cols, :]
            pre = nn(x, w1)
            cdf, pdf = gelu_parts(pre)
            act = (pre * cdf).astype(BF16)
            slope = cdf + pre * pdf
            y = y + nn(act, w2)
            grad = (nt(g, w2) * slope).astype(BF16)
            dx = dx + nt(grad, w1)
            acc1[:, cols] += nn(x_t, grad)
            acc2[cols, :] += tn(act, g)
        y_low = y.astype(BF16)
        y_rows[rows, :] = y_low
        dlogit = jnp.sum(y_low.astype(F32) * go, axis=1, keepdims=True) * gate * (1.0 - gate)
        dx_rows[rows, :] = (dx + dlogit * router).astype(BF16)
        store_y(block).start()
        for item in range(BLK // main + 1):
            mask = (block * BLK) // main + item
            done = (block < plain) & (mask < ((block + 1) * BLK) // main)

            @pl.when(done & (mask > 0) & (mask < early))
            def _():
                leave(mask).start()

            @pl.when(done & (mask == 0))
            def _():
                mine_out().start()

        return carry

    lax.fori_loop(0, blocks, run, 0)
    tail = pltpu.make_async_copy(dx_rows.at[pl.ds(early * main, slots - early * main)], late_ref, own.at[1])
    tail.start()

    pieces = []
    for first in range(0, hidden, width):
        pieces.append((acc1.at[:, pl.ds(first, width)], grads_ref.at[pl.ds(first, width)]))
    for first in range(0, hidden, width):
        pieces.append((acc2.at[pl.ds(first, width), :], grads_ref.at[pl.ds(hidden + first, width)]))
    writes = []
    for index, (piece, target) in enumerate(pieces):
        slot = index % 4
        if index >= 4:
            writes[index - 4].wait()

        def narrow(part):
            stage[slot, part, :] = piece[part, :].astype(BF16)

        each_rows(width, narrow)
        write = pltpu.make_async_copy(stage.at[slot], target, stage_sems.at[slot])
        write.start()
        writes.append(write)
    for write in writes[-4:]:
        write.wait()
    mine_out().wait()
    tail.wait()

    def settle(block, carry):
        store_y(block).wait()
        return carry

    lax.fori_loop(0, blocks, settle, 0)
    for step in range(depth):
        gather(step).wait_send()
    for step in range(1, depth):
        gather_cot(step).wait_send()
    last_cot().wait_send()
    for mask in range(1, count):
        arrive(mask).wait_send()
    for mask in range(1, early):
        leave(mask).wait()


def backward_kernel(
    dp,
    count,
    main,
    spare,
    group_ref,
    domain_ref,
    x_hbm,
    cot_hbm,
    gain_one_ref,
    gain_two_ref,
    wq_hbm,
    wk_hbm,
    wv_hbm,
    wo_hbm,
    slot_col_hbm,
    normed_hbm,
    q_hbm,
    k_hbm,
    v_hbm,
    mixed_hbm,
    probs_hbm,
    hidden_hbm,
    dx_hbm,
    late_ref,
    y_ref,
    grads_hbm,
    grad_ref,
    dense_hbm,
    vec_ref,
    y_back_ref,
    piece_ref,
    x_ref,
    cot_ref,
    wq_ref,
    wk_ref,
    wv_ref,
    wo_ref,
    slot_col_ref,
    normed_ref,
    q_ref,
    k_ref,
    v_ref,
    mixed_ref,
    hidden_ref,
    dense_ref,
    dx_ref,
    spare_dx,
    spare_y,
    dx_land,
    y_land,
    probs,
    kept,
    land_one,
    land_two,
    gmix,
    branch,
    normed_t,
    dqkv,
    sums,
    sends,
    recvs,
    late_sends,
    late_recvs,
    dx_sends,
    dx_recvs,
    y_sends,
    y_recvs,
    own,
    gets,
    fills,
    scatter_sends,
    scatter_recvs,
    keeps,
    prob_sems,
    puts,
):
    tokens, width = x_ref.shape
    me = lax.axis_index("expert")
    early = count - count // 4
    base = count * main
    late = (count - early) * main
    total = count * spare
    depth = depth_of(count)
    operands = [
        (x_hbm, x_ref),
        (cot_hbm, cot_ref),
        (wq_hbm, wq_ref),
        (wk_hbm, wk_ref),
        (wv_hbm, wv_ref),
        (wo_hbm, wo_ref),
        (slot_col_hbm, slot_col_ref),
        (normed_hbm, normed_ref),
        (q_hbm, q_ref),
        (k_hbm, k_ref),
        (v_hbm, v_ref),
        (mixed_hbm, mixed_ref),
        (hidden_hbm, hidden_ref),
    ]
    operands = [pltpu.make_async_copy(source, target, fills.at[i]) for i, (source, target) in enumerate(operands)]
    for copy in operands:
        copy.start()
    barrier = pltpu.get_barrier_semaphore()
    place, bits = dp_sides()
    for mask in range(1, count):
        pl.semaphore_signal(barrier, inc=1, device_id={"expert": flip(me, mask, count)}, device_id_type=MESH)
    for mask in (1, 2):
        pl.semaphore_signal(barrier, inc=1, device_id={"dp": flip(place, mask, dp)}, device_id_type=MESH)
    pl.semaphore_wait(barrier, count + 1)
    portion = grads_hbm.shape[0] // 4
    quarter = portion // 2

    def scatter_one(stream, second):
        side = bits[1 - stream] if second else 1 - bits[1 - stream]
        start = 2 * portion * stream + (1 - bits[stream]) * portion + side * quarter
        device = {"dp": flip(place, 1 << stream, dp)}
        return copy_to(
            grads_hbm.at[span(start, quarter)],
            land_one.at[stream, span(side * quarter, quarter)],
            scatter_sends.at[second, stream],
            scatter_recvs.at[second, stream],
            device,
        )

    def add_one(stream, second):
        side = bits[1 - stream] if second else 1 - bits[1 - stream]
        scatter_one(stream, second).wait()

        def step(rows):
            held = span(side * quarter + rows.start, 64)
            kept[stream, held, :] = (kept[stream, held, :].astype(F32) + land_one[stream, held, :].astype(F32)).astype(BF16)

        each_rows(quarter, step)

    def keep_one(stream):
        start = 2 * portion * stream + bits[stream] * portion
        return pltpu.make_async_copy(grads_hbm.at[span(start, portion)], kept.at[stream], keeps.at[stream])

    def scatter_two(stream):
        start = (1 - bits[1 - stream]) * quarter
        device = {"dp": flip(place, 2 >> stream, dp)}
        return copy_to(
            kept.at[stream, span(start, quarter)],
            land_two.at[stream],
            scatter_sends.at[2, stream],
            scatter_recvs.at[2, stream],
            device,
        )

    def store_piece(stream):
        start = bits[1 - stream] * quarter
        return pltpu.make_async_copy(
            kept.at[stream, span(start, quarter)], piece_ref.at[pl.ds(stream * quarter, quarter)], keeps.at[stream]
        )

    def load_probs(pair):
        return pltpu.make_async_copy(probs_hbm.at[pair], probs.at[pair % 2], prob_sems.at[pair % 2])

    load_probs(0).start()
    for part in range(2):
        for stream in range(2):
            scatter_one(stream, part).start()
    for stream in range(2):
        keep_one(stream).start()

    def sum_dx(step):
        if step == depth - 1:
            return return_spare(me, count, spare, step, late_ref, late, dx_land, dx_sends, dx_recvs)
        return return_spare(me, count, spare, step, spare_dx, 0, dx_land, dx_sends, dx_recvs)

    def sum_y(step):
        if step == depth - 1:
            return return_spare(me, count, spare, step, y_ref, base, y_land, y_sends, y_recvs)
        return return_spare(me, count, spare, step, spare_y, 0, y_land, y_sends, y_recvs)

    def settle(copy, own_rows, landing, step):
        copy.wait()
        rows = spare << step
        own_rows[0:rows, :] = (own_rows[0:rows, :].astype(F32) + landing[rows : 2 * rows, :].astype(F32)).astype(BF16)

    sum_dx(depth - 1).start()
    lates = [return_block(me, count, main, mask, late_ref, dx_ref, late_sends, late_recvs, early) for mask in range(early, count)]
    for copy in lates:
        copy.start()
    copies = [
        return_block(me, count, main, mask, y_ref, y_back_ref, sends, recvs) for mask in range(1, count - last_returns(count))
    ]
    mine = pltpu.make_async_copy(y_ref.at[pl.ds(0, main)], y_back_ref.at[span(me * main, main)], own.at[0])
    mine.start()
    loads = [
        pltpu.make_async_copy(late_ref.at[pl.ds(late, total)], spare_dx, own.at[1]),
        pltpu.make_async_copy(y_ref.at[pl.ds(base, total)], spare_y, own.at[2]),
    ]
    for mask in range(early):
        part = span(flip(me, mask, count) * main, main)
        loads.append(pltpu.make_async_copy(dx_hbm.at[part], dx_ref.at[part], gets.at[mask]))
    for load in loads:
        load.start()
    for load in loads:
        load.wait()
    for step in reversed(range(depth)):
        settle(sum_dx(step), spare_dx, dx_land, step)
        if step:
            sum_dx(step - 1).start()
    dx_ref[pl.ds(base, BLK), :] = spare_dx[0:BLK, :]
    for copy in lates:
        copy.wait()
    sum_y(depth - 1).start()
    for copy in copies[count // 2 - 1 :] + copies[: count // 2 - 1]:
        copy.start()
    for copy in operands:
        copy.wait()
    slots = dx_ref.shape[0]
    blocks = tokens // BLK
    lane = iota((1, 128), 1)
    weight = domain_weight(group_ref, domain_ref)
    gain_one = row_of(gain_one_ref)
    gain_two = row_of(gain_two_ref)
    sums[...] = jnp.zeros_like(sums)

    def open_block(block, carry):
        rows = pl.ds(pl.multiple_of(block * BLK, BLK), BLK)
        slot = slot_col_ref[rows, 0:1]
        pick = jnp.where(iota((BLK, slots), 1) == slot, 1.0, 0.0).astype(BF16)
        grad = nn(pick, dx_ref[...])
        hat, rstd = norm_stats(hidden_ref[rows, :])
        sums[2:3, :] += jnp.sum(grad * hat, axis=0, keepdims=True)
        sums[3:4, :] += jnp.sum(grad, axis=0, keepdims=True)
        gg = grad * gain_two
        inner = gg - jnp.mean(gg, axis=1, keepdims=True) - hat * jnp.mean(gg * hat, axis=1, keepdims=True)
        total = cot_ref[rows, :].astype(F32) * weight + rstd * inner
        hidden_ref[rows, :] = total
        low = total.astype(BF16)
        branch[rows, :] = low
        gmix[rows, :] = nt(low, wo_ref[...]).astype(BF16)
        normed_t[:, rows] = normed_ref[rows, :].astype(F32).T.astype(BF16)
        return carry

    lax.fori_loop(0, blocks, open_block, 0)
    def put_dense(part):
        rows = pl.ds(part * width, width)
        return pltpu.make_async_copy(dense_ref.at[rows], dense_hbm.at[rows], puts.at[part])

    dense_ref[pl.ds(3 * width, width), :] = tn(mixed_ref[...], branch[...]).astype(BF16)
    put_dense(3).start()
    settle(sum_y(depth - 1), spare_y, y_land, depth - 1)
    sum_y(depth - 2).start()

    for stream in range(2):
        keep_one(stream).wait()
        add_one(stream, 0)
        scatter_two(stream).start()

    def attend(pair, carry):
        @pl.when(pair + 1 < HEADS // 2)
        def _():
            load_probs(pair + 1).start()

        @pl.when(pair == 4)
        def _():
            for stream in range(2):
                add_one(stream, 1)

        @pl.when(pair == 5)
        def _():
            settle(sum_y(depth - 2), spare_y, y_land, depth - 2)
            sum_y(depth - 3).start()

        load_probs(pair).wait()
        base = pl.multiple_of(pair * 128, 128)
        cols = pl.ds(base, 128)
        q_pair = q_ref[:, cols]
        k_pair = k_ref[:, cols]
        v_pair = v_ref[:, cols]
        o_pair = gmix[:, cols]
        low = lane < 64
        q_head = [jnp.where(low, q_pair, 0), jnp.where(low, 0, q_pair)]
        v_head = [jnp.where(low, v_pair, 0), jnp.where(low, 0, v_pair)]
        o_head = [jnp.where(low, o_pair, 0), jnp.where(low, 0, o_pair)]
        k_t = k_pair.astype(F32).T.astype(BF16)
        prod_t = (o_pair.astype(F32) * mixed_ref[:, cols].astype(F32)).T
        delta = [jnp.sum(prod_t[:64], axis=0, keepdims=True), jnp.sum(prod_t[64:], axis=0, keepdims=True)]
        dq_t = [[None] * blocks, [None] * blocks]
        for block in range(blocks):
            start = block * BLK
            dk = None
            dv = None
            for half in range(2):
                tiles = [
                    probs[pair % 2, half, pl.ds((later * (later + 1) // 2 + block) * BLK, BLK), :]
                    for later in range(block, blocks)
                ]
                attention = jnp.concatenate(tiles, axis=1) if block < blocks - 1 else tiles[0]
                grad_p = nt(v_head[half][start : start + BLK], o_pair[start:])
                grad_s = (attention.astype(F32) * (grad_p - delta[half][:, start:])).astype(BF16)
                dv_part = nn(attention, o_head[half][start:])
                dk_part = nn(grad_s, q_head[half][start:])
                dv = dv_part if dv is None else dv + dv_part
                dk = dk_part if dk is None else dk + dk_part
                dq_part = nn(k_t[half * 64 : half * 64 + 64, start : start + BLK], grad_s)
                for later in range(block, blocks):
                    piece = dq_part[:, (later - block) * BLK : (later - block + 1) * BLK]
                    dq_t[half][later] = piece if dq_t[half][later] is None else dq_t[half][later] + piece
            rows = pl.ds(start, BLK)
            dqkv[rows, pl.ds(pl.multiple_of(base + width, 128), 128)] = dk.astype(BF16)
            dqkv[rows, pl.ds(pl.multiple_of(base + 2 * width, 128), 128)] = dv.astype(BF16)
        for block in range(blocks):
            both = jnp.concatenate([dq_t[0][block], dq_t[1][block]], axis=0) * (HEAD_DIM ** (-0.5))
            dqkv[pl.ds(block * BLK, BLK), cols] = both.T.astype(BF16)
        return carry

    lax.fori_loop(0, HEADS // 2, attend, 0)

    for part in range(3):
        dense_ref[pl.ds(part * width, width), :] = nn(normed_t[...], dqkv[:, pl.ds(part * width, width)]).astype(BF16)
        put_dense(part).start()

    def close_block(block, carry):
        rows = pl.ds(pl.multiple_of(block * BLK, BLK), BLK)
        grad = nt(dqkv[rows, 0:width], wq_ref[...])
        grad = grad + nt(dqkv[rows, width : 2 * width], wk_ref[...])
        grad = grad + nt(dqkv[rows, 2 * width : 3 * width], wv_ref[...])
        hat, rstd = norm_stats(x_ref[rows, :].astype(F32))
        sums[0:1, :] += jnp.sum(grad * hat, axis=0, keepdims=True)
        sums[1:2, :] += jnp.sum(grad, axis=0, keepdims=True)
        gg = grad * gain_one
        inner = gg - jnp.mean(gg, axis=1, keepdims=True) - hat * jnp.mean(gg * hat, axis=1, keepdims=True)
        grad_ref[rows, :] = (hidden_ref[rows, :] + rstd * inner).astype(BF16)
        return carry

    lax.fori_loop(0, blocks, close_block, 0)
    vec_ref[...] = sums[...]
    for stream in range(2):
        scatter_two(stream).wait()
        start = bits[1 - stream] * quarter
        sum_rows(kept.at[stream, span(start, quarter)], land_two.at[stream], quarter)
        store_piece(stream).start()
    for step in reversed(range(depth - 2)):
        settle(sum_y(step), spare_y, y_land, step)
        if step:
            sum_y(step - 1).start()
    spare_out = pltpu.make_async_copy(spare_y.at[pl.ds(0, BLK)], y_back_ref.at[pl.ds(base, BLK)], own.at[1])
    spare_out.start()
    spare_out.wait()
    for stream in range(2):
        store_piece(stream).wait()
    for part in range(4):
        put_dense(part).wait()
    mine.wait()
    for copy in copies:
        copy.wait()


STREAMS = 3
CHUNKS = 4


def halving_plan(dp, count, rows):
    experts = [("expert", 2 << bit) for bit in range(depth_of(count) - 1)]
    groups = [("dp", 1 << bit) for bit in range(depth_of(dp))]
    core = [("expert", 1)]
    plans = [core + groups + experts, core + groups[::-1] + experts, core + experts + groups]
    halvings = 0
    while halvings < len(plans[0]) and (rows >> halvings) % 32 == 0:
        halvings += 1
    return plans, halvings


def finish_kernel(
    dp,
    count,
    dense_hbm,
    vec_ref,
    slot_col_hbm,
    hidden_hbm,
    gate_hbm,
    y_hbm,
    y_rows_hbm,
    piece_ref,
    out_ref,
    full_ref,
    total_ref,
    grads_ref,
    dense_ref,
    slot_col_ref,
    hidden_ref,
    gate_ref,
    y_ref,
    acc,
    landing,
    full,
    vec_acc,
    vec_land,
    sends,
    recvs,
    back_sends,
    back_recvs,
    vec_sends,
    vec_recvs,
    put,
    unit_sends,
    unit_recvs,
    own,
    y_sends,
    y_recvs,
    gets,
    fills,
):
    tokens, width = hidden_ref.shape
    slots = y_ref.shape[0]
    main = (slots - BLK) // count
    early = count - last_returns(count)
    rows = dense_ref.shape[0] // STREAMS
    place = {"dp": lax.axis_index("dp"), "expert": lax.axis_index("expert")}
    size = {"dp": dp, "expert": count}
    plans, halvings = halving_plan(dp, count, rows)
    steps = len(plans[0])

    def partner(axis, mask):
        return {axis: flip(place[axis], mask, size[axis])}

    operands = [(dense_hbm, dense_ref), (slot_col_hbm, slot_col_ref), (hidden_hbm, hidden_ref), (gate_hbm, gate_ref)]
    operands = [pltpu.make_async_copy(source, target, fills.at[i]) for i, (source, target) in enumerate(operands)]
    for copy in operands:
        copy.start()
    barrier = pltpu.get_barrier_semaphore()
    for axis, mask in plans[0]:
        pl.semaphore_signal(barrier, inc=1, device_id=partner(axis, mask), device_id_type=MESH)
    for mask in range(early, count):
        pl.semaphore_signal(barrier, inc=1, device_id=partner("expert", mask), device_id_type=MESH)
    pl.semaphore_wait(barrier, steps + count - early)
    me = place["expert"]
    y_copies = [return_block(me, count, main, mask, y_rows_hbm, y_ref, y_sends, y_recvs) for mask in range(early, count)]
    loads = [pltpu.make_async_copy(y_hbm.at[pl.ds(count * main, BLK)], y_ref.at[pl.ds(count * main, BLK)], gets.at[count])]
    for mask in range(early):
        part = span(flip(me, mask, count) * main, main)
        loads.append(pltpu.make_async_copy(y_hbm.at[part], y_ref.at[part], gets.at[mask]))
    for load in loads:
        load.start()

    def side(axis, mask):
        return (place[axis] // mask) % 2

    _, bits = dp_sides()
    quarter = piece_ref.shape[0] // 2
    chunk = quarter // CHUNKS
    starts = [
        4 * quarter * stream + bits[stream] * 2 * quarter + bits[1 - stream] * quarter for stream in range(2)
    ]
    others = [
        4 * quarter * stream + bits[stream] * 2 * quarter + (1 - bits[1 - stream]) * quarter for stream in range(2)
    ]

    def unit(index, stream):
        kind, part = index // CHUNKS, index % CHUNKS
        near, far = partner("dp", 1 << stream), partner("dp", 2 >> stream)
        if kind == 2:
            source = target = grads_ref.at[span(others[stream] + part * chunk, chunk)]
        else:
            source = piece_ref.at[pl.ds(stream * quarter + part * chunk, chunk)]
            target = grads_ref.at[span(starts[stream] + part * chunk, chunk)]
        return copy_to(
            source, target, unit_sends.at[index, stream], unit_recvs.at[index, stream], far if kind == 0 else near
        )

    pending = list(range(3 * CHUNKS))

    def advance(number):
        for _ in range(min(number, len(pending))):
            index = pending.pop(0)
            for stream in range(2):
                if index >= 2 * CHUNKS:
                    unit(index - 2 * CHUNKS, stream).wait_recv()
                unit(index, stream).start()

    mine = [
        pltpu.make_async_copy(
            piece_ref.at[pl.ds(stream * quarter, quarter)], grads_ref.at[span(starts[stream], quarter)], own.at[stream]
        )
        for stream in range(2)
    ]
    for copy in mine:
        copy.start()

    def combine(block):
        rows_at = pl.ds(pl.multiple_of(block * BLK, BLK), BLK)
        slot = slot_col_ref[rows_at, 0:1]
        pick = jnp.where(iota((BLK, slots), 1) == slot, 1.0, 0.0).astype(BF16)
        returned = nn(pick, y_ref[...])
        out_ref[rows_at, :] = (hidden_ref[rows_at, :] + gate_ref[rows_at, 0:1] * returned).astype(BF16)

    low = [jnp.int32(stream * rows) for stream in range(STREAMS)]
    extent = rows
    offset = 0
    trail = []
    for step in range(steps):
        halve = step < halvings
        part = extent // 2 if halve else extent
        copies = []
        for stream in range(STREAMS):
            axis, mask = plans[stream][step]
            kept = low[stream] + side(axis, mask) * part if halve else low[stream]
            other = low[stream] + (1 - side(axis, mask)) * part if halve else low[stream]
            source = dense_ref if step == 0 else acc.at[(step - 1) % 2]
            land = landing.at[stream, pl.ds(offset, part)]
            copy = copy_to(
                (dense_hbm if step == 0 else source).at[span(other, part)], land, sends.at[stream, step], recvs.at[stream, step], partner(axis, mask)
            )
            copy.start()
            copies.append((copy, kept, source))
        axis, mask = plans[0][step]
        vec_source = vec_ref if step == 0 else vec_acc.at[step - 1]
        vec_copy = copy_to(vec_source, vec_land.at[step], vec_sends.at[step], vec_recvs.at[step], partner(axis, mask))
        vec_copy.start()
        advance(1)
        if step == 0:
            for copy in y_copies:
                copy.start()
        if step == 0:
            for copy in operands:
                copy.wait()
        trail.append((list(low), extent))
        for stream in range(STREAMS):
            copy, kept, source = copies[stream]
            copy.wait()
            target = acc.at[step % 2] if step < steps - 1 else full
            grain = min(part, 64)

            def add(rows_at):
                held = span(kept + rows_at.start, grain)
                value = source[held, :].astype(F32) + landing[stream, span(offset + rows_at.start, grain), :].astype(F32)
                target[held, :] = value.astype(BF16)

            each_rows(part, add, grain)
            low[stream] = kept
        vec_copy.wait()
        vec_sum = vec_source[...] + vec_land[step]
        if step < steps - 1:
            vec_acc[step] = vec_sum
        else:
            total_ref[...] = vec_sum
        extent = part
        offset += part

    writes = []
    for step in reversed(range(halvings)):
        origins, whole = trail[step]
        copies = []
        for stream in range(STREAMS):
            axis, mask = plans[stream][step]
            held = span(low[stream], extent)
            copy = copy_to(
                full.at[held], full.at[held], back_sends.at[stream, step], back_recvs.at[stream, step], partner(axis, mask)
            )
            copy.start()
            copies.append(copy)
        advance(2)
        if step == 1:
            for copy in loads + y_copies:
                copy.wait()

            def combine_block(block, carry):
                combine(block)
                return carry

            lax.fori_loop(0, tokens // BLK, combine_block, 0)
        for stream in range(STREAMS):
            copies[stream].wait()
            low[stream] = origins[stream]
        extent = whole
        if step == 1:
            for stream in range(STREAMS):
                held = span(low[stream], extent)
                writes.append(pltpu.make_async_copy(full.at[held], full_ref.at[held], put.at[0, stream]))
                writes[-1].start()
    advance(len(pending))
    for stream in range(STREAMS):
        held = span(stream * rows + (1 - side("expert", 1)) * (rows // 2), rows // 2)
        writes.append(pltpu.make_async_copy(full.at[held], full_ref.at[held], put.at[1, stream]))
        writes[-1].start()
    for index in range(3 * CHUNKS):
        for stream in range(2):
            if index >= CHUNKS:
                unit(index, stream).wait_recv()
            unit(index, stream).wait_send()
    for copy in mine + writes:
        copy.wait()


AHEAD = 6


def widen_kernel(hidden, dense_hbm, grads_hbm, total_ref, output_hbm, inputs_hbm, *rest):
    outs, vecs, passed, (low, high, rows, gets, puts, moves) = rest[:6], rest[6:10], rest[10:12], rest[12:]
    width = dense_hbm.shape[1]
    jobs = []
    for block in range(hidden // width):
        part = pl.ds(block * width, width)
        jobs.append((grads_hbm.at[part], outs[4].at[:, part]))
        jobs.append((grads_hbm.at[pl.ds(hidden + block * width, width)], outs[5].at[part, :]))
    for index in range(4):
        jobs.append((dense_hbm.at[pl.ds(index * width, width)], outs[index]))
    loads = [pltpu.make_async_copy(source, low.at[i], gets.at[i]) for i, (source, _) in enumerate(jobs)]
    for load in loads[:AHEAD]:
        load.start()
    for index, vec in enumerate(vecs):
        vec[...] = total_ref[index : index + 1, :].reshape(width)
    taken = [pltpu.make_async_copy(source, rows.at[i], moves.at[i]) for i, source in enumerate((output_hbm, inputs_hbm))]
    given = [pltpu.make_async_copy(rows.at[i], target, moves.at[i]) for i, target in enumerate(passed)]
    slots = high.shape[0]
    stores = []
    for index, (_, target) in enumerate(jobs):
        loads[index].wait()
        if index + AHEAD < len(jobs):
            loads[index + AHEAD].start()
        if index == 1:
            for copy in taken:
                copy.start()
        if index == 4:
            for before, after in zip(taken, given):
                before.wait()
                after.start()
        if index >= slots:
            stores[index - slots].wait()

        def step(part):
            high[index % slots, part, :] = low[index, part, :].astype(F32)

        each_rows(width, step)
        stores.append(pltpu.make_async_copy(high.at[index % slots], target, puts.at[index % slots]))
        stores[-1].start()
    for copy in stores[-slots:] + given:
        copy.wait()


def call(kernel, outs, in_specs, scratch, name, out_specs=None, collective=None, flops=10**9):
    remote = {} if collective is None else {"collective_id": collective, "has_side_effects": True}
    return pl.pallas_call(
        kernel,
        out_shape=outs,
        in_specs=in_specs,
        out_specs=out_specs or [VMEM] * len(outs),
        scratch_shapes=scratch,
        compiler_params=pltpu.CompilerParams(vmem_limit_bytes=LIMIT, **remote),
        cost_estimate=pl.CostEstimate(flops=flops, bytes_accessed=10**7, transcendentals=0),
        name=name,
    )


def dma(*dims):
    return pltpu.SemaphoreType.DMA(dims)


def shape(dims, kind):
    return jax.ShapeDtypeStruct(dims, kind)


def tables(experts, main, slots, counts, group, domains, sort_order, cotangent):
    tokens, width = cotangent.shape
    return call(
        functools.partial(table_kernel, experts, main),
        [shape((slots, width), BF16), shape((tokens, 128), jnp.int32), shape((8, tokens), jnp.int32)],
        [SMEM, SMEM, SMEM, VMEM, VMEM],
        [pltpu.VMEM((tokens, width), BF16)],
        "tables",
    )(counts, group, domains, sort_order, cotangent)


def forward(count, main, spare, inputs, g1, s1, g2, s2, wq, wk, wv, wo, router, slot_col, slot_row, cot_send):
    tokens, width = inputs.shape
    blocks = tokens // BLK
    prob_block = (2, blocks * (blocks + 1) // 2 * BLK, BLK)
    rows_low = shape((tokens, width), BF16)
    return call(
        functools.partial(forward_kernel, count, main, spare),
        [
            rows_low,
            rows_low,
            rows_low,
            rows_low,
            rows_low,
            shape((tokens, width), F32),
            shape((tokens, 128), F32),
            shape(cot_send.shape, BF16),
            shape((count * (main + spare), width), BF16),
            shape((HEADS // 2,) + prob_block, BF16),
        ],
        [VMEM] * 5 + [ANY] * 4 + [VMEM] * 3 + [ANY],
        [pltpu.VMEM((width, width), BF16)] * 4
        + [
            pltpu.VMEM((tokens, width), BF16),
            pltpu.VMEM((2,) + prob_block, BF16),
            dma(2),
            dma(count),
            dma(count),
            dma(depth_of(count)),
            dma(depth_of(count)),
            dma(2),
            dma(4),
        ],
        "dense_forward",
        [VMEM] * 8 + [ANY] * 2,
        1,
    )(inputs, g1, s1, g2, s2, wq, wk, wv, wo, router, slot_col, slot_row, cot_send)


def expert_block(count, main, spare, counts, send, cot_send, cot_rows, router_t, w1, w2, chunk=768):
    slots, width = cot_rows.shape
    hidden = w1.shape[1]
    late = slots - (count - count // 4) * main
    rows = shape((slots, width), BF16)
    keep = pltpu.VMEM((slots, width), BF16)
    depth = depth_of(count)
    return call(
        functools.partial(expert_kernel, count, main, spare, chunk),
        [
            rows,
            shape((count * main, width), BF16),
            shape((late, width), BF16),
            shape((2 * hidden, width), BF16),
        ],
        [SMEM, ANY, ANY, ANY, VMEM, ANY, ANY],
        [
            pltpu.VMEM((width, hidden), BF16),
            pltpu.VMEM((hidden, width), BF16),
            pltpu.VMEM((width, hidden), F32),
            pltpu.VMEM((hidden, width), F32),
            keep,
            keep,
            keep,
            keep,
            pltpu.VMEM((4, width, width), BF16),
            dma(4),
            dma(count),
            dma(count),
            dma(depth),
            dma(depth),
            dma(depth),
            dma(depth),
            dma(count),
            dma(count),
            dma(2),
            dma(slots // BLK),
            dma(4),
        ],
        "expert",
        [ANY] * 4,
        2,
    )(counts, send, cot_send, cot_rows, router_t, w1, w2)


def backward(
    dp, count, main, spare, group, domains, inputs, cotangent, g1, g2, wq, wk, wv, wo, slot_col,
    normed, q, k, v, mixed, probs, hidden, dx, late, y, grads,
):
    tokens, width = inputs.shape
    half = grads.shape[0] // 4
    return call(
        functools.partial(backward_kernel, dp, count, main, spare),
        [shape((tokens, width), BF16), shape((4 * width, width), BF16), shape((8, width), F32), shape((count * main + BLK, width), BF16), shape((half, width), BF16)],
        [SMEM] * 2 + [ANY] * 2 + [VMEM] * 2 + [ANY] * 16,
        [pltpu.VMEM(v.shape, v.dtype) for v in (inputs, cotangent, wq, wk, wv, wo, slot_col, normed, q, k, v, mixed, hidden)]
        + [
            pltpu.VMEM((4 * width, width), BF16),
            pltpu.VMEM((count * main + BLK, width), BF16),
            pltpu.VMEM((count * spare, width), BF16),
            pltpu.VMEM((count * spare, width), BF16),
            pltpu.VMEM((count * spare, width), BF16),
            pltpu.VMEM((count * spare, width), BF16),
            pltpu.VMEM((2,) + probs.shape[1:], BF16),
            pltpu.VMEM((2, half, width), BF16),
            pltpu.VMEM((2, half, width), BF16),
            pltpu.VMEM((2, half // 2, width), BF16),
            pltpu.VMEM((tokens, width), BF16),
            pltpu.VMEM((tokens, width), BF16),
            pltpu.VMEM((width, tokens), BF16),
            pltpu.VMEM((tokens, 3 * width), BF16),
            pltpu.VMEM((8, width), F32),
            dma(count),
            dma(count),
            dma(count),
            dma(count),
            dma(depth_of(count)),
            dma(depth_of(count)),
            dma(depth_of(count)),
            dma(depth_of(count)),
            dma(3),
            dma(count),
            dma(13),
            dma(3, 2),
            dma(3, 2),
            dma(2),
            dma(2),
            dma(4),
        ],
        "dense_backward",
        [VMEM, ANY, VMEM, ANY, ANY],
        3,
        5 * 10**10,
    )(group, domains, inputs, cotangent, g1, g2, wq, wk, wv, wo, slot_col, normed, q, k, v, mixed, probs, hidden, dx, late, y, grads)


def finish(dp, count, dense, vec, slot_col, hidden, gate, y_back, y_rows, piece):
    width = hidden.shape[1]
    rows = dense.shape[0]
    steps = len(halving_plan(dp, count, rows // STREAMS)[0][0])
    return call(
        functools.partial(finish_kernel, dp, count),
        [shape(hidden.shape, BF16), shape(dense.shape, BF16), shape(vec.shape, F32), shape((4 * piece.shape[0], width), BF16)],
        [ANY, VMEM] + [ANY] * 6,
        [pltpu.VMEM(v.shape, v.dtype) for v in (dense, slot_col, hidden, gate)]
        + [
            pltpu.VMEM(y_back.shape, BF16),
            pltpu.VMEM((2, rows, width), BF16),
            pltpu.VMEM((STREAMS, rows // STREAMS + 64, width), BF16),
            pltpu.VMEM((rows, width), BF16),
            pltpu.VMEM((steps,) + vec.shape, F32),
            pltpu.VMEM((steps,) + vec.shape, F32),
            dma(STREAMS, steps),
            dma(STREAMS, steps),
            dma(STREAMS, steps),
            dma(STREAMS, steps),
            dma(steps),
            dma(steps),
            dma(2, STREAMS),
            dma(3 * CHUNKS, 2),
            dma(3 * CHUNKS, 2),
            dma(2),
            dma(count),
            dma(count),
            dma(count + 1),
            dma(4),
        ],
        "finish",
        [VMEM, ANY, VMEM, ANY],
        4,
    )(dense, vec, slot_col, hidden, gate, y_back, y_rows, piece)


def widen(hidden, dense, grads, total, output, grad_inputs):
    width = dense.shape[1]
    square = shape((width, width), F32)
    jobs = 2 * (hidden // width) + 4
    rows = shape(output.shape, BF16)
    return call(
        functools.partial(widen_kernel, hidden),
        [square] * 4
        + [shape((width, hidden), F32), shape((hidden, width), F32)]
        + [shape((width,), F32)] * 4
        + [rows, rows],
        [ANY, ANY, VMEM, ANY, ANY],
        [
            pltpu.VMEM((jobs, width, width), BF16),
            pltpu.VMEM((6, width, width), F32),
            pltpu.VMEM((2,) + output.shape, BF16),
            dma(jobs),
            dma(6),
            dma(2),
        ],
        "widen",
        [ANY] * 6 + [VMEM] * 4 + [ANY] * 2,
    )(dense, grads, total, output, grad_inputs)


def local(
    inputs,
    cotangent,
    seq_group,
    domain_counts,
    sort_order,
    send_counts,
    gain_one,
    shift_one,
    gain_two,
    shift_two,
    w_query,
    w_key,
    w_value,
    w_out,
    router,
    expert_in,
    expert_out,
):
    tokens, width = inputs.shape
    experts = send_counts.shape[1]
    capacity = 2 * tokens // experts
    spare = capacity // 4
    main = capacity - spare
    slots = experts * main + BLK
    count = lax.axis_size("expert")
    g1, s1, g2, s2 = gain_one, shift_one, gain_two, shift_two
    router_t = router.T
    cot_send, slot_col, slot_row = tables(experts, main, slots, send_counts, seq_group, domain_counts, sort_order, cotangent)
    normed, q, k, v, mixed, hidden, gate, send, cot_rows, probs = forward(
        count, main, spare, inputs, g1, s1, g2, s2, w_query, w_key, w_value, w_out, router_t, slot_col, slot_row, cot_send
    )
    y_rows, dx_back, dx_late, grads = expert_block(
        count, main, spare, send_counts, send, cot_send, cot_rows, router_t, expert_in[0], expert_out[0]
    )
    dp = lax.axis_size("dp")
    grad_inputs, dense, vec, y_back, piece = backward(
        dp, count, main, spare, seq_group, domain_counts, inputs, cotangent, g1, g2, w_query, w_key, w_value, w_out, slot_col,
        normed, q, k, v, mixed, probs, hidden, dx_back, dx_late, y_rows, grads,
    )
    output, dense, vec, grads = finish(dp, count, dense, vec, slot_col, hidden, gate, y_back, y_rows, piece)
    wq, wk, wv, wo, first, second, gain_a, shift_a, gain_b, shift_b, output, grad_inputs = widen(
        expert_in.shape[2], dense, grads, vec, output, grad_inputs
    )
    return (output, grad_inputs, gain_a, shift_a, gain_b, shift_b, wq, wk, wv, wo, first[None], second[None])


def solution(mesh):
    rows = P(("dp", "expert"), None)
    split = P("expert", None, None)
    return jax.shard_map(
        local,
        mesh=mesh,
        in_specs=(rows, rows, P(("dp", "expert")), P(), rows, rows) + (P(),) * 9 + (split, split),
        out_specs=(rows, rows) + (P(),) * 8 + (split, split),
        check_vma=False,
    )
```
